32 devices in a mesh: seq: 16 (over z, y, x), ch: 2 (over core).
Axes of the slice: x: 2, y: 2, z: 4, core: 2. Of those that a mesh axis runs over, the one named last changes fastest.
Arguments:
- tokens: bfloat16 [16384, 768], P('seq', 'ch'), may hold values from -6 to 6
- seg_ids: int32 [16384], replicated, may hold values from 0 to 7, never falling along the last dimension, each value on 1 to 8192 neighbouring positions
- norm1_gain: float32 [768], P('ch'), may hold values from 0.5 to 1.5
- in_weight: bfloat16 [768, 3, 768], P(None, None, 'ch'), may hold values from -0.21875 to 0.21875
- short_weight: float32 [3, 3, 768], P(None, None, 'ch'), may hold values from -3.5 to 3.5
- filt_w1: float32 [33, 64], replicated, may hold values from -1 to 1
- filt_b1: float32 [64], replicated, may hold values from -3.140625 to 3.140625
- filt_w2: float32 [64, 64], replicated, may hold values from -0.75 to 0.75
- filt_w3: float32 [64, 768], P(None, 'ch'), may hold values from -0.25 to 0.25
- long_bias: float32 [768], P('ch'), may hold values from -6 to 6
- tail_gain: float32 [768], P('ch'), may hold values from -6 to 6
- tail_rate: float32 [768], P('ch'), may hold values from 1.2207031e-05 to 0.05
- out_weight: bfloat16 [768, 768], P('ch'), may hold values from -0.21875 to 0.21875
- norm2_gain: float32 [768], P('ch'), may hold values from 0.5 to 1.5
- up_weight: bfloat16 [768, 3072], P(None, 'ch'), may hold values from -0.21875 to 0.21875
- down_weight: bfloat16 [3072, 768], P('ch'), may hold values from -0.109375 to 0.109375
- grad_out: bfloat16 [16384, 768], P('seq', 'ch'), may hold values from -8 to 8
Outputs:
- output: float32 [16384, 768], P('seq', 'ch')
- grad_tokens: float32 [16384, 768], P('seq', 'ch')
- grad_norm1_gain: float32 [768], replicated
- grad_in_weight: float32 [768, 3, 768], P('seq', None, 'ch')
- grad_short_weight: float32 [3, 3, 768], replicated
- grad_filt_w1: float32 [33, 64], replicated
- grad_filt_b1: float32 [64], replicated
- grad_filt_w2: float32 [64, 64], replicated
- grad_filt_w3: float32 [64, 768], replicated
- grad_long_bias: float32 [768], replicated
- grad_tail_gain: float32 [768], replicated
- grad_tail_rate: float32 [768], replicated
- grad_out_weight: float32 [768, 768], P('ch', 'seq')
- grad_norm2_gain: float32 [768], replicated
- grad_up_weight: float32 [768, 3072], P('seq', 'ch')
- grad_down_weight: float32 [3072, 768], P('ch', 'seq')
The draws below stay inside these ranges and needn't reach their ends.
Inputs may be any that keep to these rules, and one draw needn't show every extreme that they name: `seg_ids`: document numbers over all 16384 tokens: never falling, rising by one where a new document starts; each document has 1 to 8192 tokens and one has exactly 8192.
All inputs are finite; a program needn't handle non-finite values.
Results may differ from the reference program's by a relative error of at most 0.013.
Values may be sent and summed in bfloat16 or wider, within the bound.
A program may use at most 256 MiB of HBM per device.

```python
import math
import jax
import jax.numpy as jnp
import numpy as np
from jax import lax

D = 768
FF = 3072
EMB = 33
FILT_HID = 64
FIR = 32
TOKENS = 16384
LENGTH = 16384
DOCS = 8
DOC_MOST = 8192


def with_spikes(values, key, source, target, shards_of, factor):
    owner, partner = [(jnp.arange(values.shape[dim]) // (values.shape[dim] // shards_of)).reshape([-1 if axis == dim else 1 for axis in range(values.ndim)]) for dim in (source, target)]
    chosen = jax.random.permutation(key, shards_of)[partner]
    strong = (owner == chosen) | (owner == (partner + shards_of // 2) % shards_of)
    return jnp.where(strong, factor * values, values)


def steps_of(rng, shape, split, low, top_value):
    level = 1.0
    for dim, blocks in split:
        heights = jax.random.uniform(jax.random.fold_in(jax.random.fold_in(rng, 6), dim), (blocks,), jnp.float32, low / len(split), top_value / len(split))
        level = level * jnp.repeat(jnp.exp(heights), shape[dim] // blocks).reshape((-1,) + (1,) * (len(shape) - 1 - dim))
    return level


def length_profile(count, total, most, skew):
    portions = [(1 << 20) // math.isqrt(rank ** skew) + 1 for rank in range(2, count + 1)]
    surplus, given = total - most - (count - 1), [1] * (count - 1)
    while surplus > 0:
        candidates = [i for i in range(count - 1) if given[i] < most]
        whole, left = sum([portions[i] for i in candidates]), surplus
        for i in candidates:
            addition = min(most - given[i], max(1, left * portions[i] // whole), surplus)
            given[i] = given[i] + addition
            surplus = surplus - addition
    return np.array([most] + given)


def ragged_sizes(own_key, amount, total, reach, lean):
    if amount == 2:
        one = jax.random.randint(own_key, (), max(1, total - reach), min(reach, total - 1) + 1)
        return jnp.stack([one, total - one])
    sizes = jnp.asarray(length_profile(amount, total, reach, lean), jnp.int32)
    pairs = (amount - 1) // 2
    source_of, sink = sizes[1:1 + 2 * pairs:2], sizes[2:2 + 2 * pairs:2]
    margin = jnp.minimum(source_of - 1, reach - sink)
    passed = jax.random.randint(jax.random.fold_in(own_key, 1), (pairs,), 0, 1 << 20) % (margin + 1)
    sizes = sizes.at[1:1 + 2 * pairs:2].set(source_of - passed).at[2:2 + 2 * pairs:2].set(sink + passed)
    return sizes[jax.random.permutation(jax.random.fold_in(own_key, 2), amount)]


def normal_values(rng, shape, scale, most, shards=(), kind=jnp.bfloat16):
    values = jax.random.normal(rng, shape, jnp.float32) * scale
    if len(shards) > 0:
        values = steps_of(rng, shape, shards, -0.22, 0.18) * values
    return jnp.clip(values, min=-most, max=most).astype(kind)


def gaussian_with(stream_key, shape, scale, bound, split, heavy, held_as=jnp.bfloat16):
    array = scale * jax.random.normal(stream_key, shape, jnp.float32)
    if split:
        array = array * steps_of(stream_key, shape, split, -0.22, 0.18)
    return jnp.clip(with_spikes(array, jax.random.fold_in(stream_key, 3), *heavy), -bound, bound).astype(held_as)


def setup_inputs(seed: int = 0) -> dict:
    key_of = jax.random.split(jax.random.key(seed), 18)
    tokens = normal_values(key_of[0], (TOKENS, D), 1.0, 6.0, ((0, 16), (1, 2)))
    seg_ids = jnp.searchsorted(jnp.cumsum(ragged_sizes(key_of[1], DOCS, TOKENS, DOC_MOST, 2)), jnp.arange(TOKENS), side="right").astype(jnp.int32)
    norm1_gain = jnp.clip(1.0 + 0.1 * jax.random.normal(key_of[2], (D,), jnp.float32), 0.5, 1.5)
    in_weight = normal_values(key_of[3], (D, 3, D), D ** -0.5, 0.21875, ((2, 2),))
    short_weight = normal_values(key_of[4], (3, 3, D), 0.6, 3.5, ((2, 2),), jnp.float32)
    filt_w1 = normal_values(key_of[5], (EMB, FILT_HID), EMB ** -0.5, 1.0, (), jnp.float32)
    filt_b1 = jnp.clip(jax.random.uniform(key_of[6], (FILT_HID,), jnp.float32, -3.140625, 3.140625), -3.140625, 3.140625)
    filt_w2 = normal_values(key_of[7], (FILT_HID, FILT_HID), FILT_HID ** -0.5, 0.75, (), jnp.float32)
    filt_w3 = normal_values(key_of[8], (FILT_HID, D), 0.04, 0.25, ((1, 2),), jnp.float32)
    long_bias = normal_values(key_of[9], (D,), 1.0, 6.0, ((0, 2),), jnp.float32)
    tail_gain = normal_values(key_of[10], (D,), 1.0, 6.0, ((0, 2),), jnp.float32)
    tail_rate = jnp.clip(jnp.exp(math.log(0.05) - 8.317766 * jax.random.uniform(key_of[11], (D,), jnp.float32) ** steps_of(key_of[11], (D,), ((0, 2),), -0.2, 0.2)), 1.220703143189894e-05, 0.05)
    out_weight = normal_values(key_of[12], (D, D), D ** -0.5, 0.21875, ((0, 2),))
    norm2_gain = jnp.clip(1.0 + 0.1 * jax.random.normal(key_of[13], (D,), jnp.float32), 0.5, 1.5)
    up_weight = normal_values(key_of[14], (D, FF), D ** -0.5, 0.21875, ((1, 2),))
    down_weight = normal_values(key_of[15], (FF, D), FF ** -0.5, 0.109375, ((0, 2),))
    grad_out = gaussian_with(key_of[16], (TOKENS, D), 1.0, 8.0, ((0, 16), (1, 2)), (0, 1, 16, 2.0))
    return dict(tokens=tokens, seg_ids=seg_ids, norm1_gain=norm1_gain, in_weight=in_weight, short_weight=short_weight, filt_w1=filt_w1, filt_b1=filt_b1, filt_w2=filt_w2, filt_w3=filt_w3, long_bias=long_bias, tail_gain=tail_gain, tail_rate=tail_rate, out_weight=out_weight, norm2_gain=norm2_gain, up_weight=up_weight, down_weight=down_weight, grad_out=grad_out)


EPSILON = 1e-05
FREQUENCY = 0.4
HIGHEST = lax.Precision.HIGHEST

@jax.custom_vjp
def low(v):
    return lax.optimization_barrier(v.astype(jnp.bfloat16)).astype(jnp.float32)

@jax.custom_vjp
def low_back(v):
    return v

def low_keep(v):
    return (low(v), None)

def low_pass(kept, grad):
    return (grad,)

def back_keep(v):
    return (v, None)

def back_low(kept, grad):
    return (low(grad),)
low.defvjp(low_keep, low_pass)
low_back.defvjp(back_keep, back_low)

def affine_pair(earlier, follower):
    return (earlier[0] * follower[0], follower[0] * earlier[1] + follower[1])

def position_table(filter_len, band_count):
    places = jnp.arange(filter_len, dtype=jnp.float32)
    harmonics = jnp.arange(1, band_count + 1, dtype=jnp.float32)
    angles = FREQUENCY * places[:, None] * harmonics[None, :]
    return jnp.concatenate([places[:, None] / filter_len, jnp.cos(angles), jnp.sin(angles)], axis=1)

def gelu_tanh(values):
    return 0.5 * values * (1.0 + jnp.tanh(0.7978845608028654 * (values + 0.044715 * values * values * values)))

def layer_norm(hidden, gain_vec):
    center = lax.optimization_barrier(jnp.mean(hidden, axis=-1, keepdims=True))
    spread = lax.optimization_barrier(jnp.mean(jnp.square(hidden - center), axis=-1, keepdims=True))
    return (hidden - center) * lax.rsqrt(spread + EPSILON) * gain_vec

def lagged(values, lag_step):
    if lag_step == 0:
        return values
    return jnp.concatenate([jnp.zeros((lag_step,) + values.shape[1:], values.dtype), values[:values.shape[0] - lag_step]])

def build_masks(segment):
    length = segment.shape[0]
    position = jnp.arange(length, dtype=jnp.int32)
    result = []
    for lag_step in range(FIR):
        prior_ids = jnp.concatenate([jnp.full((lag_step,), -1, jnp.int32), segment[:length - lag_step]])
        result.append(((segment == prior_ids) & (position >= lag_step)).astype(jnp.float32))
    return result

def mixer_conv(projected, short_weight, doc_masks):
    return sum((short_weight[lag_step] * doc_masks[lag_step][:, None, None] * lagged(projected, lag_step) for lag_step in range(3)))

def explicit_part(long_taps, doc_masks, stream):
    return sum((long_taps[lag_step] * doc_masks[lag_step][:, None] * lagged(stream, lag_step) for lag_step in range(FIR)))

def filter_taps(filt_w1, filt_b1, filt_w2, filt_w3, full_width):
    pos_table = position_table(FIR, (filt_w1.shape[0] - 1) // 2)
    pre_one = jnp.dot(pos_table, filt_w1, precision=HIGHEST) + filt_b1
    pre_two = jnp.dot(jnp.sin(pre_one), filt_w2, precision=HIGHEST)
    raw_taps = jnp.dot(jnp.sin(pre_two), filt_w3, precision=HIGHEST)
    channel = jnp.arange(filt_w3.shape[1], dtype=jnp.float32)
    window = jnp.exp(-(0.5 + 3.0 * channel / full_width)[None, :] * jnp.arange(FIR, dtype=jnp.float32)[:, None] / FIR)
    return raw_taps * window

def block_forward(params, tokens, segment):
    norm1_gain, in_weight, short_weight, filt_w1, filt_b1, filt_w2, filt_w3, long_bias, tail_gain, tail_rate, out_weight, norm2_gain, up_weight, down_weight = params
    length, full_width = tokens.shape
    doc_masks = build_masks(segment)
    norm_one = low(layer_norm(tokens, norm1_gain))
    projected = low_back(low(jnp.dot(norm_one, in_weight.reshape(full_width, 3 * full_width), precision=HIGHEST)))
    projected = projected.reshape(length, 3, full_width)
    conv_out = jax.checkpoint(mixer_conv)(projected, short_weight, doc_masks)
    stream = low(conv_out[:, 0] * conv_out[:, 2])
    long_taps = filter_taps(filt_w1, filt_b1, filt_w2, filt_w3, full_width)
    explicit = jax.checkpoint(explicit_part)(long_taps, doc_masks, stream)
    factor = jnp.exp(-tail_rate)
    norm_tail = jnp.sqrt(-jnp.expm1(-2.0 * tail_rate))
    decay_step = doc_masks[1][:, None] * factor[None, :]
    state_sum = lax.associative_scan(affine_pair, (decay_step, stream), axis=0)[1]
    carried = decay_step * lagged(state_sum, 1)
    long_mix = long_bias * stream + explicit + tail_gain * norm_tail * carried
    mixed_out = low(long_mix * conv_out[:, 1])
    middle = tokens + low_back(jnp.dot(mixed_out, out_weight, precision=HIGHEST))
    norm_two = low(layer_norm(middle, norm2_gain))
    upward = low_back(jnp.dot(norm_two, up_weight, precision=HIGHEST))
    active = low(gelu_tanh(upward))
    return middle + low_back(jnp.dot(active, down_weight, precision=HIGHEST))

def reference(tokens, seg_ids, norm1_gain, in_weight, short_weight, filt_w1, filt_b1, filt_w2, filt_w3, long_bias, tail_gain, tail_rate, out_weight, norm2_gain, up_weight, down_weight, grad_out):
    full_width = tokens.shape[1]
    params = tuple((weight.astype(jnp.float32) for weight in (norm1_gain, in_weight, short_weight, filt_w1, filt_b1, filt_w2, filt_w3, long_bias, tail_gain, tail_rate, out_weight, norm2_gain, up_weight, down_weight)))
    seq_count = tokens.shape[0] // LENGTH
    pieces = tokens.astype(jnp.float32).reshape(seq_count, LENGTH, full_width)
    segments = seg_ids.reshape(seq_count, LENGTH)
    cotangents = grad_out.astype(jnp.float32).reshape(seq_count, LENGTH, full_width)

    def one_sequence(totals, seq_item):
        seq_piece, segment, cotangent = seq_item

        def forward(weights, inputs):
            return block_forward(weights, inputs, segment)
        output_piece, pullback = jax.vjp(forward, params, seq_piece)
        weight_grads, input_grad = pullback(cotangent)
        return (jax.tree.map(jnp.add, totals, weight_grads), (output_piece, input_grad))
    totals, (outputs, input_grads) = lax.scan(one_sequence, jax.tree.map(jnp.zeros_like, params), (pieces, segments, cotangents))
    return (outputs.reshape(-1, full_width), input_grads.reshape(-1, full_width), totals[0], totals[1], totals[2], totals[3], totals[4], totals[5], totals[6], totals[7], totals[8], totals[9], totals[10], totals[11], totals[12], totals[13])
```

```python
import functools

import jax
import jax.numpy as jnp
from jax import lax
from jax.experimental import pallas as pl
from jax.experimental.pallas import tpu as pltpu
from jax.sharding import PartitionSpec as P

FIR = 32
SEQ_LEN = 16384
DOC_MOST = 8192
EPSILON = 1e-05
FREQUENCY = 0.4
HIGHEST = lax.Precision.HIGHEST
MESH = pl.DeviceIdType.MESH
F32, BF16 = jnp.float32, jnp.bfloat16

BEFORE = 48
AFTER = 80
LANES = 128
BLOCK = 256
CHUNK = 64
SUMS = 48
HEAD = 16
FF_TILE = 512
VMEM_LIMIT = 56 << 20
ROOT_TWO_OVER_PI = 0.7978845608028654


def position_table(filter_len, band_count):
    places = jnp.arange(filter_len, dtype=F32)
    harmonics = jnp.arange(1, band_count + 1, dtype=F32)
    angles = FREQUENCY * places[:, None] * harmonics[None, :]
    return jnp.concatenate([places[:, None] / filter_len, jnp.cos(angles), jnp.sin(angles)], axis=1)


def of(ref, start, size):
    return pl.ds(pl.multiple_of(start, size), size)


def exchange_kernel(sizes, tokens, gout, w_in, w_out, w_up, w_down, head, taps, filt,
                    tok_o, g_o, in_o, out_o, up_o, down_o, vec_o, local_sem, send_sem, recv_sem):
    n, rows, width, hidden = sizes
    block = rows // 2
    s, c = lax.axis_index("seq"), lax.axis_index("ch")
    barrier = pltpu.get_barrier_semaphore()
    pl.semaphore_signal(barrier, inc=1, device_id=(s, 1 - c), device_id_type=MESH)

    @pl.when((c == 0) & (s > 0))
    def _():
        for k in range(2):
            pl.semaphore_signal(barrier, inc=1, device_id=(s - 1, k), device_id_type=MESH)

    @pl.when(s < n - 1)
    def _():
        pl.semaphore_wait(barrier, 2)

    @pl.when(s == n - 1)
    def _():
        pl.semaphore_wait(barrier, 1)

    cols = pl.ds(pl.multiple_of(c * width, width), width)
    hid = pl.ds(pl.multiple_of(c * hidden, hidden), hidden)
    pairs = [
        (w_in, in_o.at[:, :, cols]),
        (head, vec_o.at[pl.ds(0, HEAD), cols]),
        (taps, vec_o.at[pl.ds(HEAD, FIR), cols]),
        (filt, vec_o.at[pl.ds(HEAD + FIR, filt.shape[0]), cols]),
        (w_out, out_o.at[cols, :]),
        (w_up, up_o.at[:, hid]),
        (w_down, down_o.at[hid, :]),
    ]

    def remote(src, dst, k, target):
        return pltpu.make_async_remote_copy(
            src_ref=src, dst_ref=dst, send_sem=send_sem.at[k], recv_sem=recv_sem.at[k],
            device_id=target, device_id_type=MESH)

    partner = (s, 1 - c)
    left, right = pl.ds(0, width), pl.ds(width, width)
    first, second = pl.ds(0, block), pl.ds(block, block)
    early = pl.ds(block - BEFORE, block + BEFORE)
    tail = pl.ds(rows - BEFORE, BEFORE)

    @pl.when(c == 0)
    def _():
        remote(tokens.at[early, :], tok_o.at[:, left], 0, partner).start()
        remote(gout.at[second, :], g_o.at[:, left], 1, partner).start()
        pltpu.make_async_copy(tokens.at[first, :], tok_o.at[pl.ds(BEFORE, block), left], local_sem.at[0]).start()
        pltpu.make_async_copy(gout.at[first, :], g_o.at[:, left], local_sem.at[1]).start()

        @pl.when(s < n - 1)
        def _():
            remote(tokens.at[tail, :], tok_o.at[pl.ds(0, BEFORE), left], 2, (s + 1, 0)).start()

    @pl.when(c == 1)
    def _():
        remote(tokens.at[first, :], tok_o.at[pl.ds(BEFORE, block), right], 0, partner).start()
        remote(gout.at[first, :], g_o.at[:, right], 1, partner).start()
        pltpu.make_async_copy(tokens.at[early, :], tok_o.at[:, right], local_sem.at[0]).start()
        pltpu.make_async_copy(gout.at[second, :], g_o.at[:, right], local_sem.at[1]).start()

        @pl.when(s < n - 1)
        def _():
            remote(tokens.at[tail, :], tok_o.at[pl.ds(0, BEFORE), right], 3, (s + 1, 0)).start()

    for k, (src, dst) in enumerate(pairs):
        remote(src, dst, 4 + k, partner).start()
        pltpu.make_async_copy(src, dst, local_sem.at[2 + k]).start()

    for k, (src, dst) in enumerate(pairs):
        pltpu.make_async_copy(src, dst, local_sem.at[2 + k]).wait()
        remote(src, dst, 4 + k, partner).wait()

    @pl.when(c == 0)
    def _():
        remote(tokens.at[early, :], tok_o.at[:, left], 0, partner).wait_send()
        remote(gout.at[second, :], g_o.at[:, left], 1, partner).wait_send()
        remote(tokens.at[first, :], tok_o.at[pl.ds(BEFORE, block), right], 0, partner).wait_recv()
        remote(gout.at[first, :], g_o.at[:, right], 1, partner).wait_recv()
        pltpu.make_async_copy(tokens.at[first, :], tok_o.at[pl.ds(BEFORE, block), left], local_sem.at[0]).wait()
        pltpu.make_async_copy(gout.at[first, :], g_o.at[:, left], local_sem.at[1]).wait()

        @pl.when(s < n - 1)
        def _():
            remote(tokens.at[tail, :], tok_o.at[pl.ds(0, BEFORE), left], 2, (s + 1, 0)).wait_send()

        @pl.when(s > 0)
        def _():
            remote(tokens.at[tail, :], tok_o.at[pl.ds(0, BEFORE), left], 2, partner).wait_recv()
            remote(tokens.at[tail, :], tok_o.at[pl.ds(0, BEFORE), right], 3, partner).wait_recv()

    @pl.when(c == 1)
    def _():
        remote(tokens.at[first, :], tok_o.at[pl.ds(BEFORE, block), right], 0, partner).wait_send()
        remote(gout.at[first, :], g_o.at[:, right], 1, partner).wait_send()
        remote(tokens.at[early, :], tok_o.at[:, left], 0, partner).wait_recv()
        remote(gout.at[second, :], g_o.at[:, left], 1, partner).wait_recv()
        pltpu.make_async_copy(tokens.at[early, :], tok_o.at[:, right], local_sem.at[0]).wait()
        pltpu.make_async_copy(gout.at[second, :], g_o.at[:, right], local_sem.at[1]).wait()

        @pl.when(s < n - 1)
        def _():
            remote(tokens.at[tail, :], tok_o.at[pl.ds(0, BEFORE), right], 3, (s + 1, 0)).wait_send()


def exchange(n, tokens, gout, w_in, w_out, w_up, w_down, *vec):
    rows, width = tokens.shape
    hidden = w_up.shape[1]
    full, block = 2 * width, rows // 2
    anywhere = pl.BlockSpec(memory_space=pl.ANY)
    return pl.pallas_call(
        functools.partial(exchange_kernel, (n, rows, width, hidden)),
        name="exchange",
        out_shape=(
            jax.ShapeDtypeStruct((BEFORE + block, full), BF16),
            jax.ShapeDtypeStruct((block, full), BF16),
            jax.ShapeDtypeStruct((3, full, full), BF16),
            jax.ShapeDtypeStruct((full, full), BF16),
            jax.ShapeDtypeStruct((full, 2 * hidden), BF16),
            jax.ShapeDtypeStruct((2 * hidden, full), BF16),
            jax.ShapeDtypeStruct((sum(part.shape[0] for part in vec), full), F32),
        ),
        in_specs=[anywhere] * 9,
        out_specs=[pl.BlockSpec(memory_space=pltpu.VMEM)] * 7,
        scratch_shapes=[pltpu.SemaphoreType.DMA((9,)), pltpu.SemaphoreType.DMA((11,)), pltpu.SemaphoreType.DMA((11,))],
        compiler_params=pltpu.CompilerParams(collective_id=0, has_side_effects=True, vmem_limit_bytes=VMEM_LIMIT),
    )(tokens, gout, w_in, w_out, w_up, w_down, *vec)


def row_stats(values):
    center = jnp.mean(values, axis=1, keepdims=True)
    shifted = values - center
    inverse = lax.rsqrt(jnp.mean(shifted * shifted, axis=1, keepdims=True) + EPSILON)
    return shifted * inverse, inverse


def mixer_kernel(block, ids_s, tok, win, vec, vblk, ids, n1_o, proj_o, v_o, x0_o, x1_o, u_o, long_o, car_o, end_o,
                 n1_s, proj_s, u_s, state_s):
    rows = BEFORE + block
    lane_blocks = BLOCK // LANES

    @pl.when(pl.program_id(0) == 0)
    def _():
        gain = vec[0:1, :]

        def normed(j, _):
            at = pl.ds(pl.multiple_of(j * 16, 16), 16)
            values = jnp.where(ids[at, 0:1] >= 0.0, tok[at, :].astype(F32), 0.0)
            n1_s[at, :] = (row_stats(values)[0] * gain).astype(BF16)
            return 0

        lax.fori_loop(0, rows // 16, normed, 0)
        n1_o[...] = n1_s[pl.ds(BEFORE, block), :]

    for s in range(3):
        part = jnp.dot(n1_s[...], win[s], preferred_element_type=F32).astype(BF16)
        proj_o[s] = part
        for b in range(lane_blocks):
            proj_s[s, b] = part[:, b * LANES : (b + 1) * LANES].astype(F32)

    def convolved(start, size):
        own = ids[pl.ds(start, size), :]
        same = [None] + [own == ids[pl.ds(start - j, size), :] for j in (1, 2)]
        results = []
        for b in range(lane_blocks):
            lanes = slice(b * LANES, (b + 1) * LANES)
            streams = []
            for s in range(3):
                value = vblk[6 + s : 7 + s, lanes] * proj_s[s, b, pl.ds(start, size), :]
                for j in (1, 2):
                    tap = vblk[6 + 3 * j + s : 7 + 3 * j + s, lanes]
                    value += jnp.where(same[j], tap * proj_s[s, b, pl.ds(start - j, size), :], 0.0)
                streams.append(value)
            gated = (streams[0] * streams[2]).astype(BF16)
            u_s[b, pl.ds(start, size), :] = gated.astype(F32)
            results.append((streams, gated))
        return results

    head = convolved(16, 32)
    for b in range(lane_blocks):
        lanes = slice(b * LANES, (b + 1) * LANES)
        u_o[0:16, lanes] = jnp.zeros((16, LANES), BF16)
        u_o[16:48, lanes] = head[b][1]

    def conv_chunk(j, _):
        start = pl.multiple_of(BEFORE + j * 32, 16)
        to = pl.ds(pl.multiple_of(j * 32, 32), 32)
        for b, (streams, gated) in enumerate(convolved(start, 32)):
            lanes = slice(b * LANES, (b + 1) * LANES)
            v_o[to, lanes] = streams[0]
            x0_o[to, lanes] = streams[1]
            x1_o[to, lanes] = streams[2]
            u_o[pl.ds(start, 32), lanes] = gated
        return 0

    lax.fori_loop(0, block // 32, conv_chunk, 0)

    row_id = lax.broadcasted_iota(jnp.int32, (8, LANES), 0)
    rates = [vblk[4:5, b * LANES : (b + 1) * LANES] for b in range(lane_blocks)]
    powers = [jnp.exp(-rate * (row_id + 1).astype(F32)) for rate in rates]
    lams = [[jnp.exp(-rate * float(step)) for step in (1, 2, 4)] for rate in rates]
    for b in range(lane_blocks):
        state_s[b, 0:8, :] = jnp.zeros((8, LANES), F32)

    def scan_group(g, carry):
        start = pl.multiple_of(BEFORE + g * 8, 8)
        own = ids[pl.ds(start, 8), :]
        masks = [(own == ids[pl.ds(start - step, 8), :]) & (row_id >= step) for step in (1, 2, 4)]
        joined = own == jnp.broadcast_to(ids[pl.ds(start - 1, 1), :], (8, LANES))
        result = []
        for b in range(lane_blocks):
            value = u_s[b, pl.ds(start, 8), :]
            for mask, lam, step in zip(masks, lams[b], (1, 2, 4)):
                value += jnp.where(mask, lam * pltpu.roll(value, step, 0), 0.0)
            value += jnp.where(joined, powers[b] * carry[b], 0.0)
            state_s[b, pl.ds(pl.multiple_of(8 + g * 8, 8), 8), :] = value
            result.append(jnp.broadcast_to(value[7:8, :], (8, LANES)))
        return tuple(result)

    zero = jnp.zeros((8, LANES), F32)
    final = lax.fori_loop(0, block // 8, scan_group, (zero,) * lane_blocks, unroll=4)
    for b in range(lane_blocks):
        end_o[:, b * LANES : (b + 1) * LANES] = final[b][0:1, :]

    for b in range(lane_blocks):
        lanes = slice(b * LANES, (b + 1) * LANES)
        bias, gain, lam = vblk[2:3, lanes], vblk[3:4, lanes], lams[b][0]
        nu = vblk[5:6, lanes]

        def long_chunk(j, _):
            start = pl.multiple_of(BEFORE + j * CHUNK, 16)
            to = pl.ds(pl.multiple_of(j * CHUNK, CHUNK), CHUNK)
            own = ids[pl.ds(start, CHUNK), :]
            here = u_s[b, pl.ds(start, CHUNK), :]
            previous = state_s[b, pl.ds(7 + j * CHUNK, CHUNK), :]
            carried = jnp.where(own == ids[pl.ds(start - 1, CHUNK), :], lam * previous, 0.0)
            car_o[to, lanes] = carried
            base = bias * here + (gain * nu) * carried
            whole = ids_s[start + CHUNK - 1] == ids_s[start - FIR + 1]

            @pl.when(whole)
            def _():
                total = base
                for k in range(FIR):
                    total += vblk[16 + k : 17 + k, lanes] * u_s[b, pl.ds(start - k, CHUNK), :]
                long_o[to, lanes] = total

            @pl.when(jnp.logical_not(whole))
            def _():
                total = base
                for k in range(FIR):
                    term = vblk[16 + k : 17 + k, lanes] * u_s[b, pl.ds(start - k, CHUNK), :]
                    total += jnp.where(own == ids[pl.ds(start - k, CHUNK), :], term, 0.0)
                long_o[to, lanes] = total

            return 0

        lax.fori_loop(0, block // CHUNK, long_chunk, 0)


def mixer(ids_s, tok, win, vec, ids):
    rows, full = tok.shape
    block = rows - BEFORE
    lane_blocks = BLOCK // LANES
    whole = lambda *shape: pl.BlockSpec(shape, lambda i: (0,) * len(shape))
    by_channel = lambda count: pl.BlockSpec((count, BLOCK), lambda i: (0, i))
    return pl.pallas_call(
        functools.partial(mixer_kernel, block),
        name="mixer",
        grid=(full // BLOCK,),
        out_shape=(
            jax.ShapeDtypeStruct((block, full), BF16),
            jax.ShapeDtypeStruct((3, rows, full), BF16),
            jax.ShapeDtypeStruct((block, full), F32),
            jax.ShapeDtypeStruct((block, full), F32),
            jax.ShapeDtypeStruct((block, full), F32),
            jax.ShapeDtypeStruct((rows, full), BF16),
            jax.ShapeDtypeStruct((block, full), F32),
            jax.ShapeDtypeStruct((block, full), F32),
            jax.ShapeDtypeStruct((1, full), F32),
        ),
        in_specs=[
            pl.BlockSpec(memory_space=pltpu.SMEM),
            whole(rows, full),
            pl.BlockSpec((3, full, BLOCK), lambda i: (0, 0, i)),
            whole(*vec.shape),
            by_channel(vec.shape[0]),
            whole(*ids.shape),
        ],
        out_specs=(
            whole(block, full),
            pl.BlockSpec((3, rows, BLOCK), lambda i: (0, 0, i)),
            by_channel(block),
            by_channel(block),
            by_channel(block),
            by_channel(rows),
            by_channel(block),
            by_channel(block),
            by_channel(1),
        ),
        scratch_shapes=[
            pltpu.VMEM((rows, full), BF16),
            pltpu.VMEM((3, lane_blocks, rows, LANES), F32),
            pltpu.VMEM((lane_blocks, rows, LANES), F32),
            pltpu.VMEM((lane_blocks, 8 + block, LANES), F32),
        ],
        compiler_params=pltpu.CompilerParams(vmem_limit_bytes=VMEM_LIMIT),
    )(ids_s, tok, win, vec, vec, ids)


def push_kernel(n, reach, backward, halo_in, *refs):
    if halo_in:
        end, halo, weights, joined_o, halo_o, slots, send_sem, recv_sem, halo_sem = refs
    else:
        end, weights, joined_o, slots, send_sem, recv_sem = refs
    s, c = lax.axis_index("seq"), lax.axis_index("ch")
    total, me = 2 * n, 2 * s + c
    ahead = -1 if backward else 1
    place = total - 1 - me if backward else me
    barrier = pltpu.get_barrier_semaphore()

    def device(index):
        return (index // 2, index % 2)

    for k in range(reach):

        @pl.when(place - 1 - k >= 0)
        def _():
            pl.semaphore_signal(barrier, inc=1, device_id=device(me - ahead * (1 + k)), device_id_type=MESH)

    for count in range(1, reach + 1):

        @pl.when((total - 1 - place >= count) if count == reach else (total - 1 - place == count))
        def _():
            pl.semaphore_wait(barrier, count)

    def copy(k):
        return pltpu.make_async_remote_copy(
            src_ref=end, dst_ref=slots.at[k], send_sem=send_sem.at[k], recv_sem=recv_sem.at[k],
            device_id=device(me + ahead * (1 + k)), device_id_type=MESH)

    def halo_copy():
        return pltpu.make_async_remote_copy(
            src_ref=halo, dst_ref=halo_o, send_sem=halo_sem.at[0], recv_sem=halo_sem.at[1],
            device_id=device(me + ahead), device_id_type=MESH)

    for k in range(reach):

        @pl.when(place + 1 + k < total)
        def _():
            copy(k).start()
            if halo_in and k == 0:
                halo_copy().start()

    joined_o[...] = jnp.zeros_like(joined_o)
    for k in range(reach):

        @pl.when(place - 1 - k >= 0)
        def _():
            copy(k).wait_recv()
            for row in range(joined_o.shape[0]):
                joined_o[row : row + 1, :] += weights[row, k : k + 1, :] * slots[k]

    for k in range(reach):

        @pl.when(place + 1 + k < total)
        def _():
            copy(k).wait_send()

    if halo_in:

        @pl.when(place + 1 < total)
        def _():
            halo_copy().wait_send()

        @pl.when(place - 1 >= 0)
        def _():
            halo_copy().wait_recv()


def push(n, end, weights, backward, collective_id, halo=None):
    results, reach, full = weights.shape
    vmem = pl.BlockSpec(memory_space=pltpu.VMEM)
    out_shape = [jax.ShapeDtypeStruct((results, full), F32)]
    scratch = [pltpu.VMEM((reach, 1, full), F32), pltpu.SemaphoreType.DMA((reach,)), pltpu.SemaphoreType.DMA((reach,))]
    operands = [end]
    if halo is not None:
        out_shape.append(jax.ShapeDtypeStruct(halo.shape, halo.dtype))
        scratch.append(pltpu.SemaphoreType.DMA((2,)))
        operands.append(halo)
    operands.append(weights)
    return pl.pallas_call(
        functools.partial(push_kernel, n, reach, backward, halo is not None),
        name="push_back" if backward else "push_on",
        out_shape=out_shape,
        in_specs=[vmem] * len(operands),
        out_specs=[vmem] * len(out_shape),
        scratch_shapes=scratch,
        compiler_params=pltpu.CompilerParams(collective_id=collective_id, has_side_effects=True),
    )(*operands)


def contract(left, right, dims):
    return lax.dot_general(left, right, (dims, ((), ())), preferred_element_type=F32)


def ffn_kernel(block, tiles, tok, x0, base, car, ids, enter, g, vec, wout, wup, wdn,
               out_o, long_o, car_o, gmid_o, gmix_o, gout_w_o, gup_o, gdn_o, gain_o,
               mixed_s, middle_s, n2_s, gn2_s, gout_s):
    step = pl.program_id(0)
    rows16 = block // 32

    @pl.when(step == 0)
    def _():
        rate, tail = vec[4:5, :], vec[3:4, :] * vec[5:6, :]
        state = enter[0:1, :]
        last = ids[pl.ds(BEFORE - 1, 1), 0:1]

        def mix(j, _):
            at = pl.ds(pl.multiple_of(j * 32, 32), 32)
            steps = (lax.broadcasted_iota(jnp.int32, (32, 1), 0) + (j * 32 + 1)).astype(F32)
            same = ids[pl.ds(pl.multiple_of(BEFORE + j * 32, 16), 32), 0:1] == last
            entered = jnp.where(same, jnp.exp(-rate * steps) * state, 0.0)
            car_o[at, :] = car[at, :] + entered
            long = base[at, :] + tail * entered
            long_o[at, :] = long
            mixed_s[at, :] = (long * x0[at, :]).astype(BF16)
            return 0

        lax.fori_loop(0, rows16, mix, 0)
        middle_s[...] = jnp.dot(mixed_s[...], wout[...], preferred_element_type=F32)

        def norm(j, _):
            at = pl.ds(pl.multiple_of(j * 32, 32), 32)
            values = middle_s[at, :] + tok[pl.ds(pl.multiple_of(BEFORE + j * 32, 16), 32), :].astype(F32)
            middle_s[at, :] = values
            out_o[at, :] = values
            n2_s[at, :] = (row_stats(values)[0] * vec[1:2, :]).astype(BF16)
            gn2_s[at, :] = jnp.zeros_like(values)
            return 0

        lax.fori_loop(0, rows16, norm, 0)

    n2, rows = n2_s[...], g[...]
    up = jnp.dot(n2, wup[...], preferred_element_type=F32)
    pulled = contract(rows, wdn[...], ((1,), (1,)))
    square = up * up
    inner = ROOT_TWO_OVER_PI * up * (1.0 + 0.044715 * square)
    bent = jnp.tanh(inner)
    half = 0.5 * (1.0 + bent)
    active = (up * half).astype(BF16)
    slope = half + (0.5 * ROOT_TWO_OVER_PI) * up * (1.0 - bent * bent) * (1.0 + 0.134145 * square)
    g_up = (pulled * slope).astype(BF16)
    out_o[...] += jnp.dot(active, wdn[...], preferred_element_type=F32)
    gn2_s[...] += contract(g_up, wup[...], ((1,), (1,)))
    gdn_o[...] = contract(rows, active, ((0,), (0,))).astype(BF16)
    gup_o[...] = contract(n2, g_up, ((0,), (0,))).astype(BF16)

    @pl.when(step == tiles - 1)
    def _():
        def back(j, total):
            at = pl.ds(pl.multiple_of(j * 32, 32), 32)
            normal, inverse = row_stats(middle_s[at, :])
            grad = gn2_s[at, :]
            total += jnp.sum(grad * normal, axis=0, keepdims=True)
            scaled = grad * vec[1:2, :]
            cross = jnp.mean(scaled * normal, axis=1, keepdims=True)
            result = g[at, :].astype(F32) + inverse * (
                scaled - jnp.mean(scaled, axis=1, keepdims=True) - normal * cross)
            gmid_o[at, :] = result
            gout_s[at, :] = result.astype(BF16)
            return total

        gain_o[...] = lax.fori_loop(0, rows16, back, jnp.zeros_like(gain_o))
        gmix_o[...] = contract(gout_s[...], wout[...], ((1,), (1,)))
        gout_w_o[...] = contract(gout_s[...], mixed_s[...], ((0,), (0,))).astype(BF16)


def ffn(tok, x0, base, car, ids, enter, g, vec, wout, wup, wdn):
    block, full = g.shape
    hidden = wup.shape[1]
    tiles = hidden // FF_TILE
    whole = lambda *shape: pl.BlockSpec(shape, lambda i: (0,) * len(shape))
    wide = lambda dtype: jax.ShapeDtypeStruct((block, full), dtype)
    return pl.pallas_call(
        functools.partial(ffn_kernel, block, tiles),
        name="ffn",
        grid=(tiles,),
        out_shape=(
            wide(F32), wide(F32), wide(F32), wide(F32), wide(F32),
            jax.ShapeDtypeStruct((full, full), BF16),
            jax.ShapeDtypeStruct((full, hidden), BF16),
            jax.ShapeDtypeStruct((full, hidden), BF16),
            jax.ShapeDtypeStruct((1, full), F32),
        ),
        in_specs=[
            whole(*tok.shape), whole(block, full), whole(block, full), whole(block, full), whole(*ids.shape),
            whole(*enter.shape), whole(block, full), whole(*vec.shape), whole(full, full),
            pl.BlockSpec((full, FF_TILE), lambda i: (0, i)),
            pl.BlockSpec((FF_TILE, full), lambda i: (i, 0)),
        ],
        out_specs=(
            whole(block, full), whole(block, full), whole(block, full), whole(block, full), whole(block, full),
            whole(full, full),
            pl.BlockSpec((full, FF_TILE), lambda i: (0, i)),
            pl.BlockSpec((full, FF_TILE), lambda i: (0, i)),
            whole(1, full),
        ),
        scratch_shapes=[
            pltpu.VMEM((block, full), BF16),
            pltpu.VMEM((block, full), F32),
            pltpu.VMEM((block, full), BF16),
            pltpu.VMEM((block, full), F32),
            pltpu.VMEM((block, full), BF16),
        ],
        compiler_params=pltpu.CompilerParams(vmem_limit_bytes=VMEM_LIMIT),
    )(tok, x0, base, car, ids, enter, g, vec, wout, wup, wdn)


def gate_kernel(block, gmix, x0, x1, v, long, car, u, vblk, ids, glong_o, q_o, first_o, halo_o, sums_o, gc_s):
    lane_blocks = BLOCK // LANES
    row_id = lax.broadcasted_iota(jnp.int32, (8, LANES), 0)
    lam_of, power_of, zero = [], [], jnp.zeros((8, LANES), F32)
    for b in range(lane_blocks):
        lanes = slice(b * LANES, (b + 1) * LANES)
        rate = vblk[4:5, lanes]
        tail = vblk[3:4, lanes] * vblk[5:6, lanes]
        lam_of.append([jnp.exp(-rate * float(step)) for step in (1, 2, 4)])
        power_of.append(jnp.exp(-rate * (8 - row_id).astype(F32)))

        def gated(j, totals):
            at = pl.ds(pl.multiple_of(j * 32, 32), 32)
            grad = gmix[at, lanes] * x0[at, lanes]
            glong_o[at, lanes] = grad
            gc_s[b, at, :] = grad * tail
            here = u[pl.ds(pl.multiple_of(BEFORE + j * 32, 16), 32), lanes].astype(F32)
            return (
                totals[0] + jnp.sum((grad * here).reshape(4, 8, LANES), axis=0),
                totals[1] + jnp.sum((grad * car[at, lanes]).reshape(4, 8, LANES), axis=0),
            )

        for row, total in enumerate(lax.fori_loop(0, block // 32, gated, (zero, zero))):
            sums_o[row : row + 1, lanes] = jnp.sum(total, axis=0, keepdims=True)
        halo_o[56:64, lanes] = x1[0:8, lanes]
        halo_o[64:72, lanes] = v[0:8, lanes]
        halo_o[72:80, lanes] = gmix[0:8, lanes] * long[0:8, lanes]

    def scan_group(i, carry):
        g = block // 8 - 1 - i
        to = pl.ds(pl.multiple_of(g * 8, 8), 8)
        start = pl.multiple_of(BEFORE + g * 8, 8)
        own = ids[pl.ds(start, 8), :]
        masks = [(own == ids[pl.ds(start + step, 8), :]) & (row_id < 8 - step) for step in (1, 2, 4)]
        joined = own == jnp.broadcast_to(ids[pl.ds(start + 8, 1), :], (8, LANES))
        result = []
        for b in range(lane_blocks):
            value = gc_s[b, to, :]
            for mask, lam, step in zip(masks, lam_of[b], (1, 2, 4)):
                value += jnp.where(mask, lam * pltpu.roll(value, 8 - step, 0), 0.0)
            value += jnp.where(joined, power_of[b] * carry[b], 0.0)
            q_o[to, b * LANES : (b + 1) * LANES] = value
            result.append(jnp.broadcast_to(value[0:1, :], (8, LANES)))
        return tuple(result)

    final = lax.fori_loop(0, block // 8, scan_group, (zero,) * lane_blocks, unroll=4)
    for b in range(lane_blocks):
        first_o[:, b * LANES : (b + 1) * LANES] = final[b][0:1, :]
    halo_o[0:48, :] = glong_o[0:48, :]
    halo_o[48:56, :] = q_o[0:8, :]


def gate(gmix, x0, x1, v, long, car, u, vec, ids):
    block, full = gmix.shape
    by_channel = lambda count: pl.BlockSpec((count, BLOCK), lambda i: (0, i))
    return pl.pallas_call(
        functools.partial(gate_kernel, block),
        name="gate",
        grid=(full // BLOCK,),
        out_shape=(
            jax.ShapeDtypeStruct((block, full), F32),
            jax.ShapeDtypeStruct((block, full), F32),
            jax.ShapeDtypeStruct((1, full), F32),
            jax.ShapeDtypeStruct((80, full), F32),
            jax.ShapeDtypeStruct((2, full), F32),
        ),
        in_specs=[by_channel(block)] * 6 + [
            by_channel(u.shape[0]), by_channel(vec.shape[0]), pl.BlockSpec(ids.shape, lambda i: (0, 0))],
        out_specs=(by_channel(block), by_channel(block), by_channel(1), by_channel(80), by_channel(2)),
        scratch_shapes=[pltpu.VMEM((BLOCK // LANES, block, LANES), F32)],
        compiler_params=pltpu.CompilerParams(vmem_limit_bytes=VMEM_LIMIT),
    )(gmix, x0, x1, v, long, car, u, vec, ids)


def back_kernel(block, steps, ids_s, glong, q, halo, joined, gmix, long, car, x1, v, u, proj, vec, vblk, ids,
                n1, win, tok, gmid, gw_o, gtok_o, sums_o, gain_o, gl_s, u_s, proj_s, gc_s, gp_s, gn1_s, taps_s):
    lane_blocks = BLOCK // LANES
    step = pl.program_id(0)
    zero = jnp.zeros((8, LANES), F32)

    @pl.when(step == 0)
    def _():
        gn1_s[...] = jnp.zeros_like(gn1_s)

    for b in range(lane_blocks):
        lanes = slice(b * LANES, (b + 1) * LANES)
        gl_s[b, 0:block, :] = glong[:, lanes]
        gl_s[b, block : block + 48, :] = halo[0:48, lanes]
        u_s[b] = u[:, lanes].astype(F32)
        for s in range(3):
            proj_s[s, b] = proj[s, :, lanes].astype(F32)
        taps_s[b] = jnp.zeros_like(taps_s[b])

    for b in range(lane_blocks):
        lanes = slice(b * LANES, (b + 1) * LANES)
        rate, bias = vblk[4:5, lanes], vblk[2:3, lanes]
        tail = vblk[3:4, lanes] * vblk[5:6, lanes]
        mine, following = joined[0:1, lanes], joined[1:2, lanes]
        last = ids[pl.ds(BEFORE + block - 1, 1), :]

        def chunk(j, total):
            at = pl.ds(pl.multiple_of(j * CHUNK, CHUNK), CHUNK)
            start = pl.multiple_of(BEFORE + j * CHUNK, 16)
            own = ids[pl.ds(start, CHUNK), :]
            here = gl_s[b, at, :]
            left = (block - 1 - j * CHUNK - lax.broadcasted_iota(jnp.int32, (CHUNK, LANES), 0)).astype(F32)
            state = q[at, lanes] + jnp.where(own == last, jnp.exp(-rate * left) * mine, 0.0)
            total += jnp.sum((car[at, lanes] * state).reshape(CHUNK // 8, 8, LANES), axis=0)
            base = (bias - tail) * here + state
            after = ids_s[start] == ids_s[start + CHUNK - 1 + FIR - 1]
            before = ids_s[start + CHUNK - 1] == ids_s[start - FIR + 1]

            def finish(grad):
                gc_s[0, b, at, :] = grad * x1[at, lanes]
                gc_s[1, b, at, :] = gmix[at, lanes] * long[at, lanes]
                gc_s[2, b, at, :] = grad * v[at, lanes]

            @pl.when(after)
            def _():
                grad = base
                for k in range(FIR):
                    grad += vblk[16 + k : 17 + k, lanes] * gl_s[b, pl.ds(j * CHUNK + k, CHUNK), :]
                finish(grad)

            @pl.when(jnp.logical_not(after))
            def _():
                grad = base
                for k in range(FIR):
                    term = vblk[16 + k : 17 + k, lanes] * gl_s[b, pl.ds(j * CHUNK + k, CHUNK), :]
                    grad += jnp.where(own == ids[pl.ds(start + k, CHUNK), :], term, 0.0)
                finish(grad)

            @pl.when(before)
            def _():
                for k in range(FIR):
                    term = here * u_s[b, pl.ds(start - k, CHUNK), :]
                    taps_s[b, k] += jnp.sum(term.reshape(CHUNK // 8, 8, LANES), axis=0)

            @pl.when(jnp.logical_not(before))
            def _():
                for k in range(FIR):
                    term = here * u_s[b, pl.ds(start - k, CHUNK), :]
                    term = jnp.where(own == ids[pl.ds(start - k, CHUNK), :], term, 0.0)
                    taps_s[b, k] += jnp.sum(term.reshape(CHUNK // 8, 8, LANES), axis=0)

            return total

        total = lax.fori_loop(0, block // CHUNK, chunk, zero)
        sums_o[41:42, lanes] = jnp.sum(total, axis=0, keepdims=True)
        for k in range(FIR):
            sums_o[k : k + 1, lanes] = jnp.sum(taps_s[b, k], axis=0, keepdims=True)

        start = BEFORE + block
        own = ids[pl.ds(start, 8), :]
        end_id = ids_s[BEFORE + block + AFTER].astype(F32)
        left = (block - 1 - lax.broadcasted_iota(jnp.int32, (8, LANES), 0)).astype(F32)
        state = halo[48:56, lanes] + jnp.where(own == end_id, jnp.exp(-rate * left) * following, 0.0)
        grad = (bias - tail) * gl_s[b, block : block + 8, :] + state
        for k in range(FIR):
            term = vblk[16 + k : 17 + k, lanes] * gl_s[b, block + k : block + k + 8, :]
            grad += jnp.where(own == ids[pl.ds(start + k, 8), :], term, 0.0)
        gc_s[0, b, block : block + 8, :] = grad * halo[56:64, lanes]
        gc_s[1, b, block : block + 8, :] = halo[72:80, lanes]
        gc_s[2, b, block : block + 8, :] = grad * halo[64:72, lanes]

        def short(j, totals):
            at = pl.ds(pl.multiple_of(j * 32, 32), 32)
            start = pl.multiple_of(BEFORE + j * 32, 16)
            own = ids[pl.ds(start, 32), :]
            same = [own == ids[pl.ds(start - k, 32), :] for k in (1, 2)]
            later = [own == ids[pl.ds(start + k, 32), :] for k in (1, 2)]
            result = []
            for s in range(3):
                here = gc_s[s, b, at, :]
                value = vblk[6 + s : 7 + s, lanes] * here
                for k in (1, 2):
                    tap = vblk[6 + 3 * k + s : 7 + 3 * k + s, lanes]
                    value += jnp.where(later[k - 1], tap * gc_s[s, b, pl.ds(j * 32 + k, 32), :], 0.0)
                gp_s[s, at, lanes] = value.astype(BF16)
                for k in range(3):
                    term = here * proj_s[s, b, pl.ds(start - k, 32), :]
                    if k:
                        term = jnp.where(same[k - 1], term, 0.0)
                    result.append(totals[3 * s + k] + jnp.sum(term.reshape(4, 8, LANES), axis=0))
            return tuple(result)

        totals = lax.fori_loop(0, block // 32, short, (zero,) * 9)
        for s in range(3):
            for k in range(3):
                sums_o[32 + 3 * k + s : 33 + 3 * k + s, lanes] = jnp.sum(totals[3 * s + k], axis=0, keepdims=True)
        sums_o[42:SUMS, lanes] = jnp.zeros((SUMS - 42, LANES), F32)

    for s in range(3):
        part = gp_s[s]
        gw_o[s] = contract(n1[...], part, ((0,), (0,))).astype(BF16)
        gn1_s[...] += contract(part, win[s], ((1,), (1,)))

    @pl.when(step == steps - 1)
    def _():
        def back(j, total):
            at = pl.ds(pl.multiple_of(j * 32, 32), 32)
            normal, inverse = row_stats(tok[pl.ds(pl.multiple_of(BEFORE + j * 32, 16), 32), :].astype(F32))
            grad = gn1_s[at, :]
            total += jnp.sum(grad * normal, axis=0, keepdims=True)
            scaled = grad * vec[0:1, :]
            cross = jnp.mean(scaled * normal, axis=1, keepdims=True)
            gtok_o[at, :] = gmid[at, :] + inverse * (
                scaled - jnp.mean(scaled, axis=1, keepdims=True) - normal * cross)
            return total

        gain_o[...] = lax.fori_loop(0, block // 32, back, jnp.zeros_like(gain_o))


def back(ids_s, glong, q, halo, joined, gmix, long, car, x1, v, u, proj, vec, ids, n1, win, tok, gmid):
    block, full = glong.shape
    rows, steps = BEFORE + block, full // BLOCK
    lane_blocks = BLOCK // LANES
    whole = lambda *shape: pl.BlockSpec(shape, lambda i: (0,) * len(shape))
    by_channel = lambda count: pl.BlockSpec((count, BLOCK), lambda i: (0, i))
    stacked = lambda count: pl.BlockSpec((3, count, BLOCK), lambda i: (0, 0, i))
    return pl.pallas_call(
        functools.partial(back_kernel, block, steps),
        name="back",
        grid=(steps,),
        out_shape=(
            jax.ShapeDtypeStruct((3, full, full), BF16),
            jax.ShapeDtypeStruct((block, full), F32),
            jax.ShapeDtypeStruct((SUMS, full), F32),
            jax.ShapeDtypeStruct((1, full), F32),
        ),
        in_specs=[
            pl.BlockSpec(memory_space=pltpu.SMEM),
            by_channel(block), by_channel(block), by_channel(80), by_channel(2),
            by_channel(block), by_channel(block), by_channel(block), by_channel(block), by_channel(block),
            by_channel(rows), stacked(rows), whole(*vec.shape), by_channel(vec.shape[0]), whole(*ids.shape),
            whole(block, full), stacked(full), whole(*tok.shape), whole(block, full),
        ],
        out_specs=(stacked(full), whole(block, full), by_channel(SUMS), whole(1, full)),
        scratch_shapes=[
            pltpu.VMEM((lane_blocks, block + 48, LANES), F32),
            pltpu.VMEM((lane_blocks, rows, LANES), F32),
            pltpu.VMEM((3, lane_blocks, rows, LANES), F32),
            pltpu.VMEM((3, lane_blocks, block + 8, LANES), F32),
            pltpu.VMEM((3, block, BLOCK), BF16),
            pltpu.VMEM((block, full), F32),
            pltpu.VMEM((lane_blocks, FIR, 8, LANES), F32),
        ],
        compiler_params=pltpu.CompilerParams(vmem_limit_bytes=VMEM_LIMIT),
    )(ids_s, glong, q, halo, joined, gmix, long, car, x1, v, u, proj, vec, vec, ids, n1, win, tok, gmid)


def reduce_kernel(sizes, g_in, g_out, g_up, g_dn, small, out, gtok,
                  total_o, small_o, out_full, gtok_full,
                  held, first, arrived, small_s, small_r, local_sem, send_sem, recv_sem, block_send, block_recv):
    n, width, hidden, block = sizes
    bits = n.bit_length() - 1
    s, c = lax.axis_index("seq"), lax.axis_index("ch")
    half = held.shape[2] // 2
    partner = (s, 1 - c)
    peers = []
    for bit in range(bits):
        flipped = s + (1 - 2 * ((s // (1 << bit)) % 2)) * (1 << bit)
        peers.append((flipped, c))
    barrier = pltpu.get_barrier_semaphore()
    for peer in [partner] + peers:
        pl.semaphore_signal(barrier, inc=1, device_id=peer, device_id_type=MESH)
    pl.semaphore_wait(barrier, 1 + bits)

    def columns(which, size):
        return pl.ds(pl.multiple_of(which * size, size), size)

    def remote(src, dst, k, target):
        return pltpu.make_async_remote_copy(
            src_ref=src, dst_ref=dst, send_sem=send_sem.at[k], recv_sem=recv_sem.at[k],
            device_id=target, device_id_type=MESH)

    def segments(which):
        parts, start = [], 0
        for stream in range(3):
            parts.append((g_in.at[stream, :, :, columns(which, width)], pl.ds(start, width)))
            start += width
        parts.append((g_out.at[:, :, columns(which, width)], pl.ds(start, width)))
        start += width
        for ref in (g_up, g_dn):
            parts.append((ref.at[:, :, columns(which, hidden)], pl.ds(start, hidden)))
            start += hidden
        return parts

    started = []
    for k, (src, at) in enumerate(segments(1 - c)):
        copy = remote(src, first.at[:, :, at], k, partner)
        copy.start()
        started.append(copy)
    copies = [remote(small, small_r.at[0], 6, partner)]
    copies[0].start()
    own_rows = columns(c, block)
    tails = []
    for k, (src, dst) in enumerate(((out, out_full), (gtok, gtok_full))):
        copy = remote(src.at[:, columns(1 - c, width)], dst.at[own_rows, :], 7 + k, partner)
        copy.start()
        tails.append(copy)
    locals_ = []
    for k, (src, at) in enumerate(segments(c)):
        copy = pltpu.make_async_copy(src, held.at[:, :, at], local_sem.at[k])
        copy.start()
        locals_.append(copy)
    for k, (src, dst) in enumerate(((out, out_full), (gtok, gtok_full))):
        copy = pltpu.make_async_copy(src.at[:, columns(c, width)], dst.at[own_rows, :], local_sem.at[6 + k])
        copy.start()
        locals_.append(copy)
    copies[0].wait()
    small_s[0] = small[...] + small_r[0]
    for copy in locals_ + started:
        copy.wait()

    def add_first(b, _):
        held[b] = (held[b].astype(F32) + first[b].astype(F32)).astype(BF16)
        return 0

    lax.fori_loop(0, n, add_first, 0)

    orders = [list(range(bits)), [1, 0] + list(range(2, bits))]
    slot_of, count = [], 0
    for k in range(bits):
        slot_of.append(count)
        count += n >> (k + 1)

    def places(part, k, mine):
        order = orders[part]
        bit, open_bits = order[k], order[k + 1 :]
        fixed = 0
        for done in order[:k]:
            fixed += ((s // (1 << done)) % 2) * (1 << done)
        own = (s // (1 << bit)) % 2
        fixed += (own if mine else 1 - own) * (1 << bit)
        return [fixed + sum(((e >> i) & 1) << b for i, b in enumerate(open_bits)) for e in range(1 << len(open_bits))]

    def block_copy(part, k, e, place):
        slot = slot_of[k] + e
        return pltpu.make_async_remote_copy(
            src_ref=held.at[place, :, pl.ds(part * half, half)], dst_ref=arrived.at[part, slot],
            send_sem=block_send.at[part, slot], recv_sem=block_recv.at[part, slot],
            device_id=peers[orders[part][k]], device_id_type=MESH)

    sent = []
    for k in range(bits):
        for part in range(2):
            if k:
                for e, place in enumerate(places(part, k - 1, True)):
                    block_copy(part, k - 1, e, place).wait_recv()
                    mine = held.at[place, :, pl.ds(part * half, half)]
                    mine[...] = (mine[...].astype(F32) + arrived[part, slot_of[k - 1] + e].astype(F32)).astype(BF16)
            for e, place in enumerate(places(part, k, False)):
                copy = block_copy(part, k, e, place)
                copy.start()
                sent.append(copy)
        if k:
            copies[k].wait()
            small_s[k] = small_s[k - 1] + small_r[k]
        copy = remote(small_s.at[k], small_r.at[k + 1], 9 + k, peers[k])
        copy.start()
        copies.append(copy)
    copies[bits].wait()
    small_o[...] = small_s[bits - 1] + small_r[bits]
    for part in range(2):
        place = places(part, bits - 1, True)[0]
        block_copy(part, bits - 1, 0, place).wait_recv()
        at = pl.ds(part * half, half)
        total_o[:, at] = held[place, :, at].astype(F32) + arrived[part, slot_of[bits - 1]].astype(F32)
    for copy in sent:
        copy.wait_send()
    for copy in tails:
        copy.wait()


def reduce(n, g_in, g_out, g_up, g_dn, small, out, gtok):
    full, block = out.shape[1], out.shape[0]
    width, hidden = full // 2, g_up.shape[1] // 2
    rows = full // n
    columns = 4 * width + 2 * hidden
    bits = n.bit_length() - 1
    anywhere = pl.BlockSpec(memory_space=pl.ANY)
    vmem = pl.BlockSpec(memory_space=pltpu.VMEM)
    return pl.pallas_call(
        functools.partial(reduce_kernel, (n, width, hidden, block)),
        name="reduce",
        out_shape=(
            jax.ShapeDtypeStruct((rows, columns), F32),
            jax.ShapeDtypeStruct(small.shape, F32),
            jax.ShapeDtypeStruct((2 * block, width), F32),
            jax.ShapeDtypeStruct((2 * block, width), F32),
        ),
        in_specs=[anywhere] * 4 + [vmem] + [anywhere] * 2,
        out_specs=(vmem, vmem, anywhere, anywhere),
        scratch_shapes=[
            pltpu.VMEM((n, rows, columns), BF16),
            pltpu.VMEM((n, rows, columns), BF16),
            pltpu.VMEM((2, n - 1, rows, columns // 2), BF16),
            pltpu.VMEM((bits,) + small.shape, F32),
            pltpu.VMEM((bits + 1,) + small.shape, F32),
            pltpu.SemaphoreType.DMA((8,)),
            pltpu.SemaphoreType.DMA((9 + bits,)),
            pltpu.SemaphoreType.DMA((9 + bits,)),
            pltpu.SemaphoreType.DMA((2, n - 1)),
            pltpu.SemaphoreType.DMA((2, n - 1)),
        ],
        compiler_params=pltpu.CompilerParams(collective_id=3, has_side_effects=True, vmem_limit_bytes=VMEM_LIMIT),
    )(g_in.reshape(3, n, rows, full), g_out.reshape(n, rows, full), g_up.reshape(n, rows, 2 * hidden),
      g_dn.reshape(n, rows, 2 * hidden), small, out, gtok)


def reduce_plain(n, g_in, g_out, g_up, g_dn, small, out, gtok):
    full = out.shape[1]
    width, hidden = full // 2, g_up.shape[1] // 2
    parts = []
    for stream in range(3):
        parts.append((g_in[stream], width))
    parts += [(g_out, width), (g_up, hidden), (g_dn, hidden)]
    halves = [
        jnp.concatenate([part[:, k * size : (k + 1) * size] for part, size in parts], axis=1).astype(F32)
        for k in range(2)
    ]
    both = lax.psum_scatter(jnp.stack(halves), "ch", scatter_dimension=0, tiled=False)
    total = lax.psum_scatter(both, "seq", scatter_dimension=0, tiled=True)
    swap = lambda whole: lax.all_to_all(whole, "ch", split_axis=1, concat_axis=0, tiled=True)
    return total, lax.psum(small, ("seq", "ch")), swap(out), swap(gtok)


def on_device(tokens, seg_ids, norm1_gain, in_weight, short_weight, filt_w1, filt_b1, filt_w2, filt_w3,
              long_bias, tail_gain, tail_rate, out_weight, norm2_gain, up_weight, down_weight, grad_out):
    rows, width = tokens.shape
    full, block = 2 * width, rows // 2
    n = lax.axis_size("seq")
    devices = 2 * n
    me = 2 * lax.axis_index("seq") + lax.axis_index("ch")
    row_start = me * block
    total_rows = seg_ids.shape[0]
    length = min(SEQ_LEN, total_rows)

    keys = seg_ids + (jnp.arange(total_rows, dtype=jnp.int32) // length) * 65536
    padded = jnp.concatenate([jnp.full((BEFORE,), -1, jnp.int32), keys, jnp.full((block + AFTER,), -2, jnp.int32)])
    near = lax.dynamic_slice_in_dim(padded, row_start, BEFORE + 2 * block)
    window = near[: BEFORE + block + AFTER]
    ids_s = jnp.concatenate([window, jnp.full((8,), 1, jnp.int32) * near[BEFORE + 2 * block - 1]])
    ids = jnp.broadcast_to(window.astype(F32)[:, None], (window.shape[0], LANES))

    channel_start = lax.axis_index("ch") * width
    pos_table = position_table(FIR, (filt_w1.shape[0] - 1) // 2)
    pre_one = jnp.dot(pos_table, filt_w1, precision=HIGHEST) + filt_b1
    hidden_one = jnp.sin(pre_one)
    pre_two = jnp.dot(hidden_one, filt_w2, precision=HIGHEST)
    hidden_two = jnp.sin(pre_two)
    channel = channel_start.astype(F32) + jnp.arange(width, dtype=F32)
    window_of = lambda channels: jnp.exp(
        -(0.5 + 3.0 * channels / full)[None, :] * jnp.arange(FIR, dtype=F32)[:, None] / FIR)
    taps = jnp.dot(hidden_two, filt_w3, precision=HIGHEST) * window_of(channel)
    norm_tail = jnp.sqrt(-jnp.expm1(-2.0 * tail_rate))
    rows_of = [norm1_gain, norm2_gain, long_bias, tail_gain, tail_rate, norm_tail]
    rows_of += [short_weight[j, s] for j in range(3) for s in range(3)]
    row_index = jnp.arange(HEAD)[:, None]
    head = jnp.zeros((HEAD, width), F32)
    for k, row in enumerate(rows_of):
        head = jnp.where(row_index == k, row[None, :], head)

    tok, g, win, wout, wup, wdn, vec = exchange(
        n, tokens, grad_out, jnp.transpose(in_weight, (1, 0, 2)), out_weight, up_weight, down_weight, head, taps, filt_w3)
    rate, gain, nu = vec[4], vec[3], vec[5]

    n1, proj, v, x0, x1, u, base, car, end = mixer(ids_s, tok, win, vec, ids)

    firsts, lasts = keys[::block], keys[block - 1 :: block]
    reach = min(DOC_MOST // block, devices - 1)
    order = jnp.arange(reach)
    source = jnp.clip(me - 1 - order, 0, devices - 1)
    valid = (me - 1 - order >= 0) & (lasts[source] == lasts[jnp.clip(me - 1, 0, devices - 1)])
    weights = jnp.where(valid[:, None], jnp.exp(-rate[None, :] * (block * order.astype(F32))[:, None]), 0.0)
    (enter,) = push(n, end, weights[None], False, 1)

    out, long, car, gmid, gmix, gw_out, gw_up, gw_dn, gain_two = ffn(tok, x0, base, car, ids, enter, g, vec, wout, wup, wdn)

    glong, q, first, halo, sums = gate(gmix, x0, x1, v, long, car, u, vec, ids)
    reach = min(DOC_MOST // block + 1, devices - 1)
    order = jnp.arange(reach)
    source = jnp.clip(me + 1 + order, 0, devices - 1)
    weights = []
    for later in range(2):
        valid = (me + 1 + order < devices) & (order >= later) & (
            firsts[source] == lasts[jnp.clip(me + later, 0, devices - 1)])
        distance = (block * (order - later) + 1).astype(F32)
        weights.append(jnp.where(valid[:, None], jnp.exp(-rate[None, :] * jnp.maximum(distance, 0.0)[:, None]), 0.0))
    joined, halo = push(n, first, jnp.stack(weights), True, 2, halo)

    gw_in, gtok, sums_two, gain_one = back(
        ids_s, glong, q, halo, joined, gmix, long, car, x1, v, u, proj, vec, ids, n1, win, tok, gmid)

    small = jnp.concatenate([sums_two[:42], sums, gain_one, gain_two, jnp.zeros((2, full), F32)])
    reducer = reduce if (full // n) % 16 == 0 else reduce_plain
    total, small, out, gtok = reducer(n, gw_in, gw_out, gw_up, gw_dn, small, out, gtok)

    taps_grad, short_grad = small[:FIR], small[FIR : FIR + 9].reshape(3, 3, full)
    carried_q, bias_grad, long_car = small[41], small[42], small[43]
    factor = jnp.exp(-rate)
    rate_grad = gain * long_car * factor * factor / nu - carried_q
    raw_grad = taps_grad * window_of(jnp.arange(full, dtype=F32))
    w3_grad = jnp.dot(hidden_two.T, raw_grad, precision=HIGHEST)
    pre_two_grad = jnp.dot(raw_grad, vec[48:].T, precision=HIGHEST) * jnp.cos(pre_two)
    w2_grad = jnp.dot(hidden_one.T, pre_two_grad, precision=HIGHEST)
    pre_one_grad = jnp.dot(pre_two_grad, filt_w2.T, precision=HIGHEST) * jnp.cos(pre_one)
    w1_grad = jnp.dot(pos_table.T, pre_one_grad, precision=HIGHEST)
    hidden = up_weight.shape[1]
    in_grad = jnp.stack([total[:, k * width : (k + 1) * width] for k in range(3)], axis=1)
    return (
        out,
        gtok,
        small[44],
        in_grad,
        short_grad,
        w1_grad,
        jnp.sum(pre_one_grad, axis=0),
        w2_grad,
        w3_grad,
        bias_grad,
        nu * long_car,
        rate_grad,
        total[:, 3 * width : 4 * width].T,
        small[45],
        total[:, 4 * width : 4 * width + hidden],
        total[:, 4 * width + hidden :].T,
    )


def solution(mesh):
    placed = (
        P("seq", "ch"),
        P(),
        P("ch"),
        P(None, None, "ch"),
        P(None, None, "ch"),
        P(),
        P(),
        P(),
        P(None, "ch"),
        P("ch"),
        P("ch"),
        P("ch"),
        P("ch", None),
        P("ch"),
        P(None, "ch"),
        P("ch", None),
        P("seq", "ch"),
    )
    return jax.shard_map(
        on_device,
        mesh=mesh,
        in_specs=placed,
        out_specs=(
            P("seq", "ch"),
            P("seq", "ch"),
            P(),
            P("seq", None, "ch"),
            P(),
            P(),
            P(),
            P(),
            P(),
            P(),
            P(),
            P(),
            P("ch", "seq"),
            P(),
            P("seq", "ch"),
            P("ch", "seq"),
        ),
        check_vma=False,
    )
```

```python
import functools

import jax
import jax.numpy as jnp
from jax import lax
from jax.experimental import pallas as pl
from jax.experimental.pallas import tpu as pltpu
from jax.sharding import PartitionSpec as P

FIR = 32
SEQ_LEN = 16384
DOC_MOST = 8192
EPSILON = 1e-05
FREQUENCY = 0.4
HIGHEST = lax.Precision.HIGHEST
MESH = pl.DeviceIdType.MESH
F32, BF16 = jnp.float32, jnp.bfloat16

BEFORE = 48
AFTER = 80
LANES = 128
BLOCK = 256
CHUNK = 64
SUMS = 48
HEAD = 16
VMEM_LIMIT = 56 << 20
ROOT_TWO_OVER_PI = 0.7978845608028654


def position_table(filter_len, band_count):
    places = jnp.arange(filter_len, dtype=F32)
    harmonics = jnp.arange(1, band_count + 1, dtype=F32)
    angles = FREQUENCY * places[:, None] * harmonics[None, :]
    return jnp.concatenate([places[:, None] / filter_len, jnp.cos(angles), jnp.sin(angles)], axis=1)


def of(ref, start, size):
    return pl.ds(pl.multiple_of(start, size), size)


def exchange_kernel(sizes, tokens, gout, w_in, w_out, w_up, w_down, head, taps, filt,
                    tok_o, g_o, in_o, out_o, up_o, down_o, vec_o, local_sem, send_sem, recv_sem):
    n, rows, width, hidden = sizes
    block = rows // 2
    s, c = lax.axis_index("seq"), lax.axis_index("ch")
    barrier = pltpu.get_barrier_semaphore()
    pl.semaphore_signal(barrier, inc=1, device_id=(s, 1 - c), device_id_type=MESH)

    @pl.when((c == 0) & (s > 0))
    def _():
        for k in range(2):
            pl.semaphore_signal(barrier, inc=1, device_id=(s - 1, k), device_id_type=MESH)

    @pl.when(s < n - 1)
    def _():
        pl.semaphore_wait(barrier, 2)

    @pl.when(s == n - 1)
    def _():
        pl.semaphore_wait(barrier, 1)

    cols = pl.ds(pl.multiple_of(c * width, width), width)
    hid = pl.ds(pl.multiple_of(c * hidden, hidden), hidden)
    pairs = [
        (w_in, in_o.at[:, :, cols]),
        (head, vec_o.at[pl.ds(0, HEAD), cols]),
        (taps, vec_o.at[pl.ds(HEAD, FIR), cols]),
        (filt, vec_o.at[pl.ds(HEAD + FIR, filt.shape[0]), cols]),
        (w_out, out_o.at[cols, :]),
        (w_up, up_o.at[:, hid]),
        (w_down, down_o.at[hid, :]),
    ]

    def remote(src, dst, k, target):
        return pltpu.make_async_remote_copy(
            src_ref=src, dst_ref=dst, send_sem=send_sem.at[k], recv_sem=recv_sem.at[k],
            device_id=target, device_id_type=MESH)

    partner = (s, 1 - c)
    left, right = pl.ds(0, width), pl.ds(width, width)
    first, second = pl.ds(0, block), pl.ds(block, block)
    early = pl.ds(block - BEFORE, block + BEFORE)
    tail = pl.ds(rows - BEFORE, BEFORE)

    @pl.when(c == 0)
    def _():
        remote(tokens.at[early, :], tok_o.at[:, left], 0, partner).start()
        remote(gout.at[second, :], g_o.at[:, left], 1, partner).start()
        pltpu.make_async_copy(tokens.at[first, :], tok_o.at[pl.ds(BEFORE, block), left], local_sem.at[0]).start()
        pltpu.make_async_copy(gout.at[first, :], g_o.at[:, left], local_sem.at[1]).start()

        @pl.when(s < n - 1)
        def _():
            remote(tokens.at[tail, :], tok_o.at[pl.ds(0, BEFORE), left], 2, (s + 1, 0)).start()

    @pl.when(c == 1)
    def _():
        remote(tokens.at[first, :], tok_o.at[pl.ds(BEFORE, block), right], 0, partner).start()
        remote(gout.at[first, :], g_o.at[:, right], 1, partner).start()
        pltpu.make_async_copy(tokens.at[early, :], tok_o.at[:, right], local_sem.at[0]).start()
        pltpu.make_async_copy(gout.at[second, :], g_o.at[:, right], local_sem.at[1]).start()

        @pl.when(s < n - 1)
        def _():
            remote(tokens.at[tail, :], tok_o.at[pl.ds(0, BEFORE), right], 3, (s + 1, 0)).start()

    for k, (src, dst) in enumerate(pairs):
        remote(src, dst, 4 + k, partner).start()
        pltpu.make_async_copy(src, dst, local_sem.at[2 + k]).start()

    for k, (src, dst) in enumerate(pairs):
        pltpu.make_async_copy(src, dst, local_sem.at[2 + k]).wait()
        remote(src, dst, 4 + k, partner).wait()

    @pl.when(c == 0)
    def _():
        remote(tokens.at[early, :], tok_o.at[:, left], 0, partner).wait_send()
        remote(gout.at[second, :], g_o.at[:, left], 1, partner).wait_send()
        remote(tokens.at[first, :], tok_o.at[pl.ds(BEFORE, block), right], 0, partner).wait_recv()
        remote(gout.at[first, :], g_o.at[:, right], 1, partner).wait_recv()
        pltpu.make_async_copy(tokens.at[first, :], tok_o.at[pl.ds(BEFORE, block), left], local_sem.at[0]).wait()
        pltpu.make_async_copy(gout.at[first, :], g_o.at[:, left], local_sem.at[1]).wait()

        @pl.when(s < n - 1)
        def _():
            remote(tokens.at[tail, :], tok_o.at[pl.ds(0, BEFORE), left], 2, (s + 1, 0)).wait_send()

        @pl.when(s > 0)
        def _():
            remote(tokens.at[tail, :], tok_o.at[pl.ds(0, BEFORE), left], 2, partner).wait_recv()
            remote(tokens.at[tail, :], tok_o.at[pl.ds(0, BEFORE), right], 3, partner).wait_recv()

    @pl.when(c == 1)
    def _():
        remote(tokens.at[first, :], tok_o.at[pl.ds(BEFORE, block), right], 0, partner).wait_send()
        remote(gout.at[first, :], g_o.at[:, right], 1, partner).wait_send()
        remote(tokens.at[early, :], tok_o.at[:, left], 0, partner).wait_recv()
        remote(gout.at[second, :], g_o.at[:, left], 1, partner).wait_recv()
        pltpu.make_async_copy(tokens.at[early, :], tok_o.at[:, right], local_sem.at[0]).wait()
        pltpu.make_async_copy(gout.at[second, :], g_o.at[:, right], local_sem.at[1]).wait()

        @pl.when(s < n - 1)
        def _():
            remote(tokens.at[tail, :], tok_o.at[pl.ds(0, BEFORE), right], 3, (s + 1, 0)).wait_send()


def exchange(n, tokens, gout, w_in, w_out, w_up, w_down, *vec):
    rows, width = tokens.shape
    hidden = w_up.shape[1]
    full, block = 2 * width, rows // 2
    anywhere = pl.BlockSpec(memory_space=pl.ANY)
    return pl.pallas_call(
        functools.partial(exchange_kernel, (n, rows, width, hidden)),
        name="exchange",
        out_shape=(
            jax.ShapeDtypeStruct((BEFORE + block, full), BF16),
            jax.ShapeDtypeStruct((block, full), BF16),
            jax.ShapeDtypeStruct((3, full, full), BF16),
            jax.ShapeDtypeStruct((full, full), BF16),
            jax.ShapeDtypeStruct((full, 2 * hidden), BF16),
            jax.ShapeDtypeStruct((2 * hidden, full), BF16),
            jax.ShapeDtypeStruct((sum(part.shape[0] for part in vec), full), F32),
        ),
        in_specs=[anywhere] * 9,
        out_specs=[pl.BlockSpec(memory_space=pltpu.VMEM)] * 7,
        scratch_shapes=[pltpu.SemaphoreType.DMA((9,)), pltpu.SemaphoreType.DMA((11,)), pltpu.SemaphoreType.DMA((11,))],
        compiler_params=pltpu.CompilerParams(collective_id=0, has_side_effects=True, vmem_limit_bytes=VMEM_LIMIT),
    )(tokens, gout, w_in, w_out, w_up, w_down, *vec)


def row_stats(values):
    center = jnp.mean(values, axis=1, keepdims=True)
    shifted = values - center
    inverse = lax.rsqrt(jnp.mean(shifted * shifted, axis=1, keepdims=True) + EPSILON)
    return shifted * inverse, inverse


def mixer_kernel(block, ids_s, tok, win, vec, vblk, ids, n1_o, proj_o, v_o, x0_o, x1_o, u_o, long_o, car_o, end_o,
                 n1_s, proj_s, u_s, state_s):
    rows = BEFORE + block
    lane_blocks = BLOCK // LANES

    @pl.when(pl.program_id(0) == 0)
    def _():
        gain = vec[0:1, :]

        def normed(j, _):
            at = pl.ds(pl.multiple_of(j * 16, 16), 16)
            values = jnp.where(ids[at, 0:1] >= 0.0, tok[at, :].astype(F32), 0.0)
            n1_s[at, :] = (row_stats(values)[0] * gain).astype(BF16)
            return 0

        lax.fori_loop(0, rows // 16, normed, 0)
        n1_o[...] = n1_s[pl.ds(BEFORE, block), :]

    for s in range(3):
        part = jnp.dot(n1_s[...], win[s], preferred_element_type=F32).astype(BF16)
        proj_o[s] = part
        for b in range(lane_blocks):
            proj_s[s, b] = part[:, b * LANES : (b + 1) * LANES].astype(F32)

    def convolved(start, size):
        own = ids[pl.ds(start, size), :]
        same = [None] + [own == ids[pl.ds(start - j, size), :] for j in (1, 2)]
        results = []
        for b in range(lane_blocks):
            lanes = slice(b * LANES, (b + 1) * LANES)
            streams = []
            for s in range(3):
                value = vblk[6 + s : 7 + s, lanes] * proj_s[s, b, pl.ds(start, size), :]
                for j in (1, 2):
                    tap = vblk[6 + 3 * j + s : 7 + 3 * j + s, lanes]
                    value += jnp.where(same[j], tap * proj_s[s, b, pl.ds(start - j, size), :], 0.0)
                streams.append(value)
            gated = (streams[0] * streams[2]).astype(BF16)
            u_s[b, pl.ds(start, size), :] = gated.astype(F32)
            results.append((streams, gated))
        return results

    head = convolved(16, 32)
    for b in range(lane_blocks):
        lanes = slice(b * LANES, (b + 1) * LANES)
        u_o[0:16, lanes] = jnp.zeros((16, LANES), BF16)
        u_o[16:48, lanes] = head[b][1]

    def conv_chunk(j, _):
        start = pl.multiple_of(BEFORE + j * 32, 16)
        to = pl.ds(pl.multiple_of(j * 32, 32), 32)
        for b, (streams, gated) in enumerate(convolved(start, 32)):
            lanes = slice(b * LANES, (b + 1) * LANES)
            v_o[to, lanes] = streams[0]
            x0_o[to, lanes] = streams[1]
            x1_o[to, lanes] = streams[2]
            u_o[pl.ds(start, 32), lanes] = gated
        return 0

    lax.fori_loop(0, block // 32, conv_chunk, 0)

    row_id = lax.broadcasted_iota(jnp.int32, (8, LANES), 0)
    rates = [vblk[4:5, b * LANES : (b + 1) * LANES] for b in range(lane_blocks)]
    powers = [jnp.exp(-rate * (row_id + 1).astype(F32)) for rate in rates]
    lams = [[jnp.exp(-rate * float(step)) for step in (1, 2, 4)] for rate in rates]
    for b in range(lane_blocks):
        state_s[b, 0:8, :] = jnp.zeros((8, LANES), F32)

    def scan_group(g, carry):
        start = pl.multiple_of(BEFORE + g * 8, 8)
        own = ids[pl.ds(start, 8), :]
        masks = [(own == ids[pl.ds(start - step, 8), :]) & (row_id >= step) for step in (1, 2, 4)]
        joined = own == jnp.broadcast_to(ids[pl.ds(start - 1, 1), :], (8, LANES))
        result = []
        for b in range(lane_blocks):
            value = u_s[b, pl.ds(start, 8), :]
            for mask, lam, step in zip(masks, lams[b], (1, 2, 4)):
                value += jnp.where(mask, lam * pltpu.roll(value, step, 0), 0.0)
            value += jnp.where(joined, powers[b] * carry[b], 0.0)
            state_s[b, pl.ds(pl.multiple_of(8 + g * 8, 8), 8), :] = value
            result.append(jnp.broadcast_to(value[7:8, :], (8, LANES)))
        return tuple(result)

    zero = jnp.zeros((8, LANES), F32)
    final = lax.fori_loop(0, block // 8, scan_group, (zero,) * lane_blocks, unroll=4)
    for b in range(lane_blocks):
        end_o[:, b * LANES : (b + 1) * LANES] = final[b][0:1, :]

    for b in range(lane_blocks):
        lanes = slice(b * LANES, (b + 1) * LANES)
        bias, gain, lam = vblk[2:3, lanes], vblk[3:4, lanes], lams[b][0]
        nu = vblk[5:6, lanes]

        def long_chunk(j, _):
            start = pl.multiple_of(BEFORE + j * CHUNK, 16)
            to = pl.ds(pl.multiple_of(j * CHUNK, CHUNK), CHUNK)
            own = ids[pl.ds(start, CHUNK), :]
            here = u_s[b, pl.ds(start, CHUNK), :]
            previous = state_s[b, pl.ds(7 + j * CHUNK, CHUNK), :]
            carried = jnp.where(own == ids[pl.ds(start - 1, CHUNK), :], lam * previous, 0.0)
            car_o[to, lanes] = carried
            base = bias * here + (gain * nu) * carried
            whole = ids_s[start + CHUNK - 1] == ids_s[start - FIR + 1]

            @pl.when(whole)
            def _():
                total = base
                for k in range(FIR):
                    total += vblk[16 + k : 17 + k, lanes] * u_s[b, pl.ds(start - k, CHUNK), :]
                long_o[to, lanes] = total

            @pl.when(jnp.logical_not(whole))
            def _():
                total = base
                for k in range(FIR):
                    term = vblk[16 + k : 17 + k, lanes] * u_s[b, pl.ds(start - k, CHUNK), :]
                    total += jnp.where(own == ids[pl.ds(start - k, CHUNK), :], term, 0.0)
                long_o[to, lanes] = total

            return 0

        lax.fori_loop(0, block // CHUNK, long_chunk, 0)


def mixer(ids_s, tok, win, vec, ids):
    rows, full = tok.shape
    block = rows - BEFORE
    lane_blocks = BLOCK // LANES
    whole = lambda *shape: pl.BlockSpec(shape, lambda i: (0,) * len(shape))
    by_channel = lambda count: pl.BlockSpec((count, BLOCK), lambda i: (0, i))
    return pl.pallas_call(
        functools.partial(mixer_kernel, block),
        name="mixer",
        grid=(full // BLOCK,),
        out_shape=(
            jax.ShapeDtypeStruct((block, full), BF16),
            jax.ShapeDtypeStruct((3, rows, full), BF16),
            jax.ShapeDtypeStruct((block, full), F32),
            jax.ShapeDtypeStruct((block, full), F32),
            jax.ShapeDtypeStruct((block, full), F32),
            jax.ShapeDtypeStruct((rows, full), BF16),
            jax.ShapeDtypeStruct((block, full), F32),
            jax.ShapeDtypeStruct((block, full), F32),
            jax.ShapeDtypeStruct((1, full), F32),
        ),
        in_specs=[
            pl.BlockSpec(memory_space=pltpu.SMEM),
            whole(rows, full),
            pl.BlockSpec((3, full, BLOCK), lambda i: (0, 0, i)),
            whole(*vec.shape),
            by_channel(vec.shape[0]),
            whole(*ids.shape),
        ],
        out_specs=(
            whole(block, full),
            pl.BlockSpec((3, rows, BLOCK), lambda i: (0, 0, i)),
            by_channel(block),
            by_channel(block),
            by_channel(block),
            by_channel(rows),
            by_channel(block),
            by_channel(block),
            by_channel(1),
        ),
        scratch_shapes=[
            pltpu.VMEM((rows, full), BF16),
            pltpu.VMEM((3, lane_blocks, rows, LANES), F32),
            pltpu.VMEM((lane_blocks, rows, LANES), F32),
            pltpu.VMEM((lane_blocks, 8 + block, LANES), F32),
        ],
        compiler_params=pltpu.CompilerParams(vmem_limit_bytes=VMEM_LIMIT),
    )(ids_s, tok, win, vec, vec, ids)


def push_kernel(n, reach, backward, halo_in, *refs):
    if halo_in:
        end, halo, weights, joined_o, halo_o, slots, send_sem, recv_sem, halo_sem = refs
    else:
        end, weights, joined_o, slots, send_sem, recv_sem = refs
    s, c = lax.axis_index("seq"), lax.axis_index("ch")
    total, me = 2 * n, 2 * s + c
    ahead = -1 if backward else 1
    place = total - 1 - me if backward else me
    barrier = pltpu.get_barrier_semaphore()

    def device(index):
        return (index // 2, index % 2)

    for k in range(reach):

        @pl.when(place - 1 - k >= 0)
        def _():
            pl.semaphore_signal(barrier, inc=1, device_id=device(me - ahead * (1 + k)), device_id_type=MESH)

    for count in range(1, reach + 1):

        @pl.when((total - 1 - place >= count) if count == reach else (total - 1 - place == count))
        def _():
            pl.semaphore_wait(barrier, count)

    def copy(k):
        return pltpu.make_async_remote_copy(
            src_ref=end, dst_ref=slots.at[k], send_sem=send_sem.at[k], recv_sem=recv_sem.at[k],
            device_id=device(me + ahead * (1 + k)), device_id_type=MESH)

    def halo_copy():
        return pltpu.make_async_remote_copy(
            src_ref=halo, dst_ref=halo_o, send_sem=halo_sem.at[0], recv_sem=halo_sem.at[1],
            device_id=device(me + ahead), device_id_type=MESH)

    for k in range(reach):

        @pl.when(place + 1 + k < total)
        def _():
            copy(k).start()
            if halo_in and k == 0:
                halo_copy().start()

    joined_o[...] = jnp.zeros_like(joined_o)
    for k in range(reach):

        @pl.when(place - 1 - k >= 0)
        def _():
            copy(k).wait_recv()
            for row in range(joined_o.shape[0]):
                joined_o[row : row + 1, :] += weights[row, k : k + 1, :] * slots[k]

    for k in range(reach):

        @pl.when(place + 1 + k < total)
        def _():
            copy(k).wait_send()

    if halo_in:

        @pl.when(place + 1 < total)
        def _():
            halo_copy().wait_send()

        @pl.when(place - 1 >= 0)
        def _():
            halo_copy().wait_recv()


def push(n, end, weights, backward, collective_id, halo=None):
    results, reach, full = weights.shape
    vmem = pl.BlockSpec(memory_space=pltpu.VMEM)
    out_shape = [jax.ShapeDtypeStruct((results, full), F32)]
    scratch = [pltpu.VMEM((reach, 1, full), F32), pltpu.SemaphoreType.DMA((reach,)), pltpu.SemaphoreType.DMA((reach,))]
    operands = [end]
    if halo is not None:
        out_shape.append(jax.ShapeDtypeStruct(halo.shape, halo.dtype))
        scratch.append(pltpu.SemaphoreType.DMA((2,)))
        operands.append(halo)
    operands.append(weights)
    return pl.pallas_call(
        functools.partial(push_kernel, n, reach, backward, halo is not None),
        name="push_back" if backward else "push_on",
        out_shape=out_shape,
        in_specs=[vmem] * len(operands),
        out_specs=[vmem] * len(out_shape),
        scratch_shapes=scratch,
        compiler_params=pltpu.CompilerParams(collective_id=collective_id, has_side_effects=True),
    )(*operands)


TILE = 512
PART = TILE // 2
STAGES = 5


class Summing:
    def __init__(self, tiles, rows, staged, first, second, third, fourth, fifth, send_sem, recv_sem):
        self.tiles, self.rows, self.staged = tiles, rows, staged
        self.first, self.second, self.third, self.fourth, self.fifth = first, second, third, fourth, fifth
        self.send_sem, self.recv_sem = send_sem, recv_sem
        self.s, self.c = lax.axis_index("seq"), lax.axis_index("ch")
        self.bits = [(self.s // (1 << b)) % 2 for b in range(4)]
        self.peers = [(self.s + (1 - 2 * bit) * (1 << b), self.c) for b, bit in enumerate(self.bits)]
        self.partner = (self.s, 1 - self.c)
        self.order = ((0, 1, 2, 3), (1, 0, 2, 3))

    @staticmethod
    def scratch(tiles, rows):
        return [
            pltpu.VMEM((2, 2, 2, 2, 2, 2, rows, TILE), BF16),
            pltpu.VMEM((tiles, 2, 2, 2, 2, rows, TILE), BF16),
            pltpu.VMEM((tiles, 2, 2, 2, 2, rows, PART), BF16),
            pltpu.VMEM((tiles, 2, 2, 2, rows, PART), BF16),
            pltpu.VMEM((tiles, 2, 2, rows, PART), BF16),
            pltpu.VMEM((tiles, 2, rows, PART), BF16),
            pltpu.SemaphoreType.DMA((tiles, 1 + 2 * 4)),
            pltpu.SemaphoreType.DMA((tiles, 1 + 2 * 4)),
        ]

    def greet(self, barrier):
        for peer in [self.partner] + self.peers:
            pl.semaphore_signal(barrier, inc=1, device_id=peer, device_id_type=MESH)
        pl.semaphore_wait(barrier, 5)

    def remote(self, src, dst, tile, k, target):
        return pltpu.make_async_remote_copy(
            src_ref=src, dst_ref=dst, send_sem=self.send_sem.at[tile, k], recv_sem=self.recv_sem.at[tile, k],
            device_id=target, device_id_type=MESH)

    def copies(self, tile, stage):
        if stage == 0:
            return [self.remote(self.staged.at[tile % 2, 1], self.first.at[tile], tile, 0, self.partner)]
        result = []
        for part in range(2):
            bit = self.order[part][stage - 1]
            away = 1 - self.bits[bit]
            at = pl.ds(part * PART, PART)
            if stage == 1:
                src = self.first.at[tile, :, :, :, away, :, at] if part == 0 else self.first.at[tile, :, :, away, :, :, at]
                dst = self.second.at[tile, part]
            elif stage == 2:
                src, dst = self.second.at[tile, part, :, :, away], self.third.at[tile, part]
            elif stage == 3:
                src, dst = self.third.at[tile, part, :, away], self.fourth.at[tile, part]
            else:
                src, dst = self.fourth.at[tile, part, away], self.fifth.at[tile, part]
            result.append(self.remote(src, dst, tile, 1 + 2 * (stage - 1) + part, self.peers[bit]))
        return result

    def start(self, tile, stage):
        for copy in self.copies(tile, stage):
            copy.start()

    def advance(self, tile, stage, total):
        for copy in self.copies(tile, stage):
            copy.wait()
        x, y, low, high = self.bits
        if stage == 0:
            def add(i, _):
                for h in range(2):
                    for j in range(2):
                        for k in range(2):
                            self.first[tile, h, i, j, k] += self.staged[tile % 2, 0, h, i, j, k]
                return 0
            lax.fori_loop(0, 2, add, 0)
        elif stage == 1:
            def add(i, _):
                for h in range(2):
                    for k in range(2):
                        self.second[tile, 0, h, i, k] += self.first[tile, h, i, k, x, :, 0:PART]
                        self.second[tile, 1, h, i, k] += self.first[tile, h, i, y, k, :, PART:TILE]
                return 0
            lax.fori_loop(0, 2, add, 0)
        elif stage == 2:
            for i in range(2):
                for k in range(2):
                    self.third[tile, 0, i, k] += self.second[tile, 0, i, k, y]
                    self.third[tile, 1, i, k] += self.second[tile, 1, i, k, x]
        elif stage == 3:
            for part in range(2):
                for i in range(2):
                    self.fourth[tile, part, i] += self.third[tile, part, i, low]
        else:
            for part in range(2):
                mine = self.fourth[tile, part, high].astype(F32)
                total(tile, part, mine + self.fifth[tile, part].astype(F32))
            return
        self.start(tile, stage + 1)


def contract(left, right, dims):
    return lax.dot_general(left, right, (dims, ((), ())), preferred_element_type=F32)


def ffn_kernel(block, tiles, summed, tok, x0, base, car, ids, enter, g, vec, wout, *refs):
    if summed:
        (wup_a, wup_b, wdn_a, wdn_b, out_o, long_o, car_o, gmid_o, gmix_o, gout_w_o, gup_o, gdn_o, gain_o,
         mixed_s, middle_s, n2_s, gn2_s, gout_s, *buffers) = refs
    else:
        (wup, wdn, out_o, long_o, car_o, gmid_o, gmix_o, gout_w_o, gup_o, gdn_o, gain_o,
         mixed_s, middle_s, n2_s, gn2_s, gout_s) = refs
    step = pl.program_id(0)
    rows16 = block // 32

    if summed:
        full = g.shape[1]
        sums = Summing(tiles, full // 16, *buffers)

        @pl.when(step == 0)
        def _():
            sums.greet(pltpu.get_barrier_semaphore())

        def total(tile, part, value):
            ref = (gup_o, gdn_o)[part]
            ref[:, pl.ds(pl.multiple_of(tile * PART, PART), PART)] = value

        for stage in range(STAGES - 1, -1, -1):

            @pl.when((step - 1 - stage >= 0) & (step - 1 - stage < tiles))
            def _():
                sums.advance(step - 1 - stage, stage, total)

    @pl.when(step == 0)
    def _():
        rate, tail = vec[4:5, :], vec[3:4, :] * vec[5:6, :]
        state = enter[0:1, :]
        last = ids[pl.ds(BEFORE - 1, 1), 0:1]

        def mix(j, _):
            at = pl.ds(pl.multiple_of(j * 32, 32), 32)
            steps = (lax.broadcasted_iota(jnp.int32, (32, 1), 0) + (j * 32 + 1)).astype(F32)
            same = ids[pl.ds(pl.multiple_of(BEFORE + j * 32, 16), 32), 0:1] == last
            entered = jnp.where(same, jnp.exp(-rate * steps) * state, 0.0)
            car_o[at, :] = car[at, :] + entered
            long = base[at, :] + tail * entered
            long_o[at, :] = long
            mixed_s[at, :] = (long * x0[at, :]).astype(BF16)
            return 0

        lax.fori_loop(0, rows16, mix, 0)
        middle_s[...] = jnp.dot(mixed_s[...], wout[...], preferred_element_type=F32)

        def norm(j, _):
            at = pl.ds(pl.multiple_of(j * 32, 32), 32)
            values = middle_s[at, :] + tok[pl.ds(pl.multiple_of(BEFORE + j * 32, 16), 32), :].astype(F32)
            middle_s[at, :] = values
            out_o[at, :] = values
            n2_s[at, :] = (row_stats(values)[0] * vec[1:2, :]).astype(BF16)
            gn2_s[at, :] = jnp.zeros_like(values)
            return 0

        lax.fori_loop(0, rows16, norm, 0)

    def feed(wup, wdn):
        n2, rows = n2_s[...], g[...]
        up = jnp.dot(n2, wup[...], preferred_element_type=F32)
        pulled = contract(rows, wdn[...], ((1,), (1,)))
        square = up * up
        inner = ROOT_TWO_OVER_PI * up * (1.0 + 0.044715 * square)
        bent = jnp.tanh(inner)
        half = 0.5 * (1.0 + bent)
        active = (up * half).astype(BF16)
        slope = half + (0.5 * ROOT_TWO_OVER_PI) * up * (1.0 - bent * bent) * (1.0 + 0.134145 * square)
        g_up = (pulled * slope).astype(BF16)
        out_o[...] += jnp.dot(active, wdn[...], preferred_element_type=F32)
        gn2_s[...] += contract(g_up, wup[...], ((1,), (1,)))
        return contract(n2, g_up, ((0,), (0,))).astype(BF16), contract(rows, active, ((0,), (0,))).astype(BF16)

    if summed:

        @pl.when(step < tiles)
        def _():
            for half, (wup, wdn) in enumerate(((wup_a, wdn_a), (wup_b, wdn_b))):
                whose = (half + sums.c) % 2
                for part, grad in enumerate(feed(wup, wdn)):
                    cols = slice(part * PART, (part + 1) * PART)
                    for q in range(16):
                        at = (step % 2, whose, q // 8, q // 4 % 2, q // 2 % 2, q % 2, slice(None), cols)
                        sums.staged[at] = grad[q * sums.rows : (q + 1) * sums.rows]
            sums.start(step, 0)
    else:
        gup_o[...], gdn_o[...] = feed(wup, wdn)

    @pl.when(step == (tiles if summed else tiles - 1))
    def _():
        def back(j, total):
            at = pl.ds(pl.multiple_of(j * 32, 32), 32)
            normal, inverse = row_stats(middle_s[at, :])
            grad = gn2_s[at, :]
            total += jnp.sum(grad * normal, axis=0, keepdims=True)
            scaled = grad * vec[1:2, :]
            cross = jnp.mean(scaled * normal, axis=1, keepdims=True)
            result = g[at, :].astype(F32) + inverse * (
                scaled - jnp.mean(scaled, axis=1, keepdims=True) - normal * cross)
            gmid_o[at, :] = result
            gout_s[at, :] = result.astype(BF16)
            return total

        gain_o[...] = lax.fori_loop(0, rows16, back, jnp.zeros_like(gain_o))
        gmix_o[...] = contract(gout_s[...], wout[...], ((1,), (1,)))
        gout_w_o[...] = contract(gout_s[...], mixed_s[...], ((0,), (0,))).astype(BF16)


def ffn(summed, tok, x0, base, car, ids, enter, g, vec, wout, wup, wdn):
    block, full = g.shape
    hidden = wup.shape[1]
    tiles = hidden // TILE
    whole = lambda *shape: pl.BlockSpec(shape, lambda i: (0,) * len(shape), pipeline_mode=pl.Buffered(1))
    wide = lambda dtype: jax.ShapeDtypeStruct((block, full), dtype)
    if summed:
        rows = full // 16
        at = lambda i, half: jnp.minimum(i, tiles - 1) + half * tiles
        weight_specs = [pl.BlockSpec((full, PART), lambda i, half=half: (0, at(i, half))) for half in range(2)]
        weight_specs += [pl.BlockSpec((PART, full), lambda i, half=half: (at(i, half), 0)) for half in range(2)]
        grads = [jax.ShapeDtypeStruct((rows, hidden // 2), F32)] * 2
        grad_specs = [whole(rows, hidden // 2)] * 2
        scratch = Summing.scratch(tiles, rows)
        params = dict(collective_id=4, has_side_effects=True)
        weights = (wup, wup, wdn, wdn)
    else:
        weight_specs = [pl.BlockSpec((full, TILE), lambda i: (0, i)), pl.BlockSpec((TILE, full), lambda i: (i, 0))]
        grads = [jax.ShapeDtypeStruct((full, hidden), BF16)] * 2
        grad_specs = [pl.BlockSpec((full, TILE), lambda i: (0, i))] * 2
        scratch, params, weights = [], {}, (wup, wdn)
    return pl.pallas_call(
        functools.partial(ffn_kernel, block, tiles, summed),
        name="ffn",
        grid=(tiles + STAGES if summed else tiles,),
        out_shape=(
            wide(F32), wide(F32), wide(F32), wide(F32), wide(F32),
            jax.ShapeDtypeStruct((full, full), BF16),
            *grads,
            jax.ShapeDtypeStruct((1, full), F32),
        ),
        in_specs=[
            whole(*tok.shape), whole(block, full), whole(block, full), whole(block, full), whole(*ids.shape),
            whole(*enter.shape), whole(block, full), whole(*vec.shape), whole(full, full),
            *weight_specs,
        ],
        out_specs=(
            whole(block, full), whole(block, full), whole(block, full), whole(block, full), whole(block, full),
            whole(full, full),
            *grad_specs,
            whole(1, full),
        ),
        scratch_shapes=[
            pltpu.VMEM((block, full), BF16),
            pltpu.VMEM((block, full), F32),
            pltpu.VMEM((block, full), BF16),
            pltpu.VMEM((block, full), F32),
            pltpu.VMEM((block, full), BF16),
            *scratch,
        ],
        compiler_params=pltpu.CompilerParams(vmem_limit_bytes=VMEM_LIMIT, **params),
    )(tok, x0, base, car, ids, enter, g, vec, wout, *weights)


def gate_kernel(block, gmix, x0, x1, v, long, car, u, vblk, ids, glong_o, q_o, first_o, halo_o, sums_o, gc_s):
    lane_blocks = BLOCK // LANES
    row_id = lax.broadcasted_iota(jnp.int32, (8, LANES), 0)
    lam_of, power_of, zero = [], [], jnp.zeros((8, LANES), F32)
    for b in range(lane_blocks):
        lanes = slice(b * LANES, (b + 1) * LANES)
        rate = vblk[4:5, lanes]
        tail = vblk[3:4, lanes] * vblk[5:6, lanes]
        lam_of.append([jnp.exp(-rate * float(step)) for step in (1, 2, 4)])
        power_of.append(jnp.exp(-rate * (8 - row_id).astype(F32)))

        def gated(j, totals):
            at = pl.ds(pl.multiple_of(j * 32, 32), 32)
            grad = gmix[at, lanes] * x0[at, lanes]
            glong_o[at, lanes] = grad
            gc_s[b, at, :] = grad * tail
            here = u[pl.ds(pl.multiple_of(BEFORE + j * 32, 16), 32), lanes].astype(F32)
            return (
                totals[0] + jnp.sum((grad * here).reshape(4, 8, LANES), axis=0),
                totals[1] + jnp.sum((grad * car[at, lanes]).reshape(4, 8, LANES), axis=0),
            )

        for row, total in enumerate(lax.fori_loop(0, block // 32, gated, (zero, zero))):
            sums_o[row : row + 1, lanes] = jnp.sum(total, axis=0, keepdims=True)
        halo_o[56:64, lanes] = x1[0:8, lanes]
        halo_o[64:72, lanes] = v[0:8, lanes]
        halo_o[72:80, lanes] = gmix[0:8, lanes] * long[0:8, lanes]

    def scan_group(i, carry):
        g = block // 8 - 1 - i
        to = pl.ds(pl.multiple_of(g * 8, 8), 8)
        start = pl.multiple_of(BEFORE + g * 8, 8)
        own = ids[pl.ds(start, 8), :]
        masks = [(own == ids[pl.ds(start + step, 8), :]) & (row_id < 8 - step) for step in (1, 2, 4)]
        joined = own == jnp.broadcast_to(ids[pl.ds(start + 8, 1), :], (8, LANES))
        result = []
        for b in range(lane_blocks):
            value = gc_s[b, to, :]
            for mask, lam, step in zip(masks, lam_of[b], (1, 2, 4)):
                value += jnp.where(mask, lam * pltpu.roll(value, 8 - step, 0), 0.0)
            value += jnp.where(joined, power_of[b] * carry[b], 0.0)
            q_o[to, b * LANES : (b + 1) * LANES] = value
            result.append(jnp.broadcast_to(value[0:1, :], (8, LANES)))
        return tuple(result)

    final = lax.fori_loop(0, block // 8, scan_group, (zero,) * lane_blocks, unroll=4)
    for b in range(lane_blocks):
        first_o[:, b * LANES : (b + 1) * LANES] = final[b][0:1, :]
    halo_o[0:48, :] = glong_o[0:48, :]
    halo_o[48:56, :] = q_o[0:8, :]


def gate(gmix, x0, x1, v, long, car, u, vec, ids):
    block, full = gmix.shape
    by_channel = lambda count: pl.BlockSpec((count, BLOCK), lambda i: (0, i))
    return pl.pallas_call(
        functools.partial(gate_kernel, block),
        name="gate",
        grid=(full // BLOCK,),
        out_shape=(
            jax.ShapeDtypeStruct((block, full), F32),
            jax.ShapeDtypeStruct((block, full), F32),
            jax.ShapeDtypeStruct((1, full), F32),
            jax.ShapeDtypeStruct((80, full), F32),
            jax.ShapeDtypeStruct((2, full), F32),
        ),
        in_specs=[by_channel(block)] * 6 + [
            by_channel(u.shape[0]), by_channel(vec.shape[0]), pl.BlockSpec(ids.shape, lambda i: (0, 0))],
        out_specs=(by_channel(block), by_channel(block), by_channel(1), by_channel(80), by_channel(2)),
        scratch_shapes=[pltpu.VMEM((BLOCK // LANES, block, LANES), F32)],
        compiler_params=pltpu.CompilerParams(vmem_limit_bytes=VMEM_LIMIT),
    )(gmix, x0, x1, v, long, car, u, vec, ids)


def back_kernel(block, steps, ids_s, glong, q, halo, joined, gmix, long, car, x1, v, u, proj, vec, vblk, ids,
                n1, win, tok, gmid, gw_o, gtok_o, sums_o, gain_o, gl_s, u_s, proj_s, gc_s, gp_s, gn1_s, taps_s):
    lane_blocks = BLOCK // LANES
    step = pl.program_id(0)
    zero = jnp.zeros((8, LANES), F32)

    @pl.when(step == 0)
    def _():
        gn1_s[...] = jnp.zeros_like(gn1_s)

    for b in range(lane_blocks):
        lanes = slice(b * LANES, (b + 1) * LANES)
        gl_s[b, 0:block, :] = glong[:, lanes]
        gl_s[b, block : block + 48, :] = halo[0:48, lanes]
        u_s[b] = u[:, lanes].astype(F32)
        for s in range(3):
            proj_s[s, b] = proj[s, :, lanes].astype(F32)
        taps_s[b] = jnp.zeros_like(taps_s[b])

    for b in range(lane_blocks):
        lanes = slice(b * LANES, (b + 1) * LANES)
        rate, bias = vblk[4:5, lanes], vblk[2:3, lanes]
        tail = vblk[3:4, lanes] * vblk[5:6, lanes]
        mine, following = joined[0:1, lanes], joined[1:2, lanes]
        last = ids[pl.ds(BEFORE + block - 1, 1), :]

        def chunk(j, total):
            at = pl.ds(pl.multiple_of(j * CHUNK, CHUNK), CHUNK)
            start = pl.multiple_of(BEFORE + j * CHUNK, 16)
            own = ids[pl.ds(start, CHUNK), :]
            here = gl_s[b, at, :]
            left = (block - 1 - j * CHUNK - lax.broadcasted_iota(jnp.int32, (CHUNK, LANES), 0)).astype(F32)
            state = q[at, lanes] + jnp.where(own == last, jnp.exp(-rate * left) * mine, 0.0)
            total += jnp.sum((car[at, lanes] * state).reshape(CHUNK // 8, 8, LANES), axis=0)
            base = (bias - tail) * here + state
            after = ids_s[start] == ids_s[start + CHUNK - 1 + FIR - 1]
            before = ids_s[start + CHUNK - 1] == ids_s[start - FIR + 1]

            def finish(grad):
                gc_s[0, b, at, :] = grad * x1[at, lanes]
                gc_s[1, b, at, :] = gmix[at, lanes] * long[at, lanes]
                gc_s[2, b, at, :] = grad * v[at, lanes]

            @pl.when(after)
            def _():
                grad = base
                for k in range(FIR):
                    grad += vblk[16 + k : 17 + k, lanes] * gl_s[b, pl.ds(j * CHUNK + k, CHUNK), :]
                finish(grad)

            @pl.when(jnp.logical_not(after))
            def _():
                grad = base
                for k in range(FIR):
                    term = vblk[16 + k : 17 + k, lanes] * gl_s[b, pl.ds(j * CHUNK + k, CHUNK), :]
                    grad += jnp.where(own == ids[pl.ds(start + k, CHUNK), :], term, 0.0)
                finish(grad)

            @pl.when(before)
            def _():
                for k in range(FIR):
                    term = here * u_s[b, pl.ds(start - k, CHUNK), :]
                    taps_s[b, k] += jnp.sum(term.reshape(CHUNK // 8, 8, LANES), axis=0)

            @pl.when(jnp.logical_not(before))
            def _():
                for k in range(FIR):
                    term = here * u_s[b, pl.ds(start - k, CHUNK), :]
                    term = jnp.where(own == ids[pl.ds(start - k, CHUNK), :], term, 0.0)
                    taps_s[b, k] += jnp.sum(term.reshape(CHUNK // 8, 8, LANES), axis=0)

            return total

        total = lax.fori_loop(0, block // CHUNK, chunk, zero)
        sums_o[41:42, lanes] = jnp.sum(total, axis=0, keepdims=True)
        for k in range(FIR):
            sums_o[k : k + 1, lanes] = jnp.sum(taps_s[b, k], axis=0, keepdims=True)

        start = BEFORE + block
        own = ids[pl.ds(start, 8), :]
        end_id = ids_s[BEFORE + block + AFTER].astype(F32)
        left = (block - 1 - lax.broadcasted_iota(jnp.int32, (8, LANES), 0)).astype(F32)
        state = halo[48:56, lanes] + jnp.where(own == end_id, jnp.exp(-rate * left) * following, 0.0)
        grad = (bias - tail) * gl_s[b, block : block + 8, :] + state
        for k in range(FIR):
            term = vblk[16 + k : 17 + k, lanes] * gl_s[b, block + k : block + k + 8, :]
            grad += jnp.where(own == ids[pl.ds(start + k, 8), :], term, 0.0)
        gc_s[0, b, block : block + 8, :] = grad * halo[56:64, lanes]
        gc_s[1, b, block : block + 8, :] = halo[72:80, lanes]
        gc_s[2, b, block : block + 8, :] = grad * halo[64:72, lanes]

        def short(j, totals):
            at = pl.ds(pl.multiple_of(j * 32, 32), 32)
            start = pl.multiple_of(BEFORE + j * 32, 16)
            own = ids[pl.ds(start, 32), :]
            same = [own == ids[pl.ds(start - k, 32), :] for k in (1, 2)]
            later = [own == ids[pl.ds(start + k, 32), :] for k in (1, 2)]
            result = []
            for s in range(3):
                here = gc_s[s, b, at, :]
                value = vblk[6 + s : 7 + s, lanes] * here
                for k in (1, 2):
                    tap = vblk[6 + 3 * k + s : 7 + 3 * k + s, lanes]
                    value += jnp.where(later[k - 1], tap * gc_s[s, b, pl.ds(j * 32 + k, 32), :], 0.0)
                gp_s[s, at, lanes] = value.astype(BF16)
                for k in range(3):
                    term = here * proj_s[s, b, pl.ds(start - k, 32), :]
                    if k:
                        term = jnp.where(same[k - 1], term, 0.0)
                    result.append(totals[3 * s + k] + jnp.sum(term.reshape(4, 8, LANES), axis=0))
            return tuple(result)

        totals = lax.fori_loop(0, block // 32, short, (zero,) * 9)
        for s in range(3):
            for k in range(3):
                sums_o[32 + 3 * k + s : 33 + 3 * k + s, lanes] = jnp.sum(totals[3 * s + k], axis=0, keepdims=True)
        sums_o[42:SUMS, lanes] = jnp.zeros((SUMS - 42, LANES), F32)

    for s in range(3):
        part = gp_s[s]
        gw_o[s] = contract(n1[...], part, ((0,), (0,))).astype(BF16)
        gn1_s[...] += contract(part, win[s], ((1,), (1,)))

    @pl.when(step == steps - 1)
    def _():
        def back(j, total):
            at = pl.ds(pl.multiple_of(j * 32, 32), 32)
            normal, inverse = row_stats(tok[pl.ds(pl.multiple_of(BEFORE + j * 32, 16), 32), :].astype(F32))
            grad = gn1_s[at, :]
            total += jnp.sum(grad * normal, axis=0, keepdims=True)
            scaled = grad * vec[0:1, :]
            cross = jnp.mean(scaled * normal, axis=1, keepdims=True)
            gtok_o[at, :] = gmid[at, :] + inverse * (
                scaled - jnp.mean(scaled, axis=1, keepdims=True) - normal * cross)
            return total

        gain_o[...] = lax.fori_loop(0, block // 32, back, jnp.zeros_like(gain_o))


def back(ids_s, glong, q, halo, joined, gmix, long, car, x1, v, u, proj, vec, ids, n1, win, tok, gmid):
    block, full = glong.shape
    rows, steps = BEFORE + block, full // BLOCK
    lane_blocks = BLOCK // LANES
    whole = lambda *shape: pl.BlockSpec(shape, lambda i: (0,) * len(shape))
    by_channel = lambda count: pl.BlockSpec((count, BLOCK), lambda i: (0, i))
    stacked = lambda count: pl.BlockSpec((3, count, BLOCK), lambda i: (0, 0, i))
    return pl.pallas_call(
        functools.partial(back_kernel, block, steps),
        name="back",
        grid=(steps,),
        out_shape=(
            jax.ShapeDtypeStruct((3, full, full), BF16),
            jax.ShapeDtypeStruct((block, full), F32),
            jax.ShapeDtypeStruct((SUMS, full), F32),
            jax.ShapeDtypeStruct((1, full), F32),
        ),
        in_specs=[
            pl.BlockSpec(memory_space=pltpu.SMEM),
            by_channel(block), by_channel(block), by_channel(80), by_channel(2),
            by_channel(block), by_channel(block), by_channel(block), by_channel(block), by_channel(block),
            by_channel(rows), stacked(rows), whole(*vec.shape), by_channel(vec.shape[0]), whole(*ids.shape),
            whole(block, full), stacked(full), whole(*tok.shape), whole(block, full),
        ],
        out_specs=(stacked(full), whole(block, full), by_channel(SUMS), whole(1, full)),
        scratch_shapes=[
            pltpu.VMEM((lane_blocks, block + 48, LANES), F32),
            pltpu.VMEM((lane_blocks, rows, LANES), F32),
            pltpu.VMEM((3, lane_blocks, rows, LANES), F32),
            pltpu.VMEM((3, lane_blocks, block + 8, LANES), F32),
            pltpu.VMEM((3, block, BLOCK), BF16),
            pltpu.VMEM((block, full), F32),
            pltpu.VMEM((lane_blocks, FIR, 8, LANES), F32),
        ],
        compiler_params=pltpu.CompilerParams(vmem_limit_bytes=VMEM_LIMIT),
    )(ids_s, glong, q, halo, joined, gmix, long, car, x1, v, u, proj, vec, vec, ids, n1, win, tok, gmid)


def reduce_kernel(sizes, g_in, g_out, small, out, gtok,
                  total_o, small_o, out_full, gtok_full,
                  held, first, arrived, small_s, small_r, local_sem, send_sem, recv_sem, block_send, block_recv):
    n, width, block = sizes
    bits = n.bit_length() - 1
    s, c = lax.axis_index("seq"), lax.axis_index("ch")
    half = held.shape[2] // 2
    partner = (s, 1 - c)
    peers = []
    for bit in range(bits):
        flipped = s + (1 - 2 * ((s // (1 << bit)) % 2)) * (1 << bit)
        peers.append((flipped, c))
    barrier = pltpu.get_barrier_semaphore()
    for peer in [partner] + peers:
        pl.semaphore_signal(barrier, inc=1, device_id=peer, device_id_type=MESH)
    pl.semaphore_wait(barrier, 1 + bits)

    def columns(which, size):
        return pl.ds(pl.multiple_of(which * size, size), size)

    def remote(src, dst, k, target):
        return pltpu.make_async_remote_copy(
            src_ref=src, dst_ref=dst, send_sem=send_sem.at[k], recv_sem=recv_sem.at[k],
            device_id=target, device_id_type=MESH)

    def segments(which):
        parts, start = [], 0
        for stream in range(3):
            parts.append((g_in.at[stream, :, :, columns(which, width)], pl.ds(start, width)))
            start += width
        parts.append((g_out.at[:, :, columns(which, width)], pl.ds(start, width)))
        return parts

    started = []
    for k, (src, at) in enumerate(segments(1 - c)):
        copy = remote(src, first.at[:, :, at], k, partner)
        copy.start()
        started.append(copy)
    copies = [remote(small, small_r.at[0], 6, partner)]
    copies[0].start()
    own_rows = columns(c, block)
    tails = []
    for k, (src, dst) in enumerate(((out, out_full), (gtok, gtok_full))):
        copy = remote(src.at[:, columns(1 - c, width)], dst.at[own_rows, :], 7 + k, partner)
        copy.start()
        tails.append(copy)
    locals_ = []
    for k, (src, at) in enumerate(segments(c)):
        copy = pltpu.make_async_copy(src, held.at[:, :, at], local_sem.at[k])
        copy.start()
        locals_.append(copy)
    for k, (src, dst) in enumerate(((out, out_full), (gtok, gtok_full))):
        copy = pltpu.make_async_copy(src.at[:, columns(c, width)], dst.at[own_rows, :], local_sem.at[6 + k])
        copy.start()
        locals_.append(copy)
    copies[0].wait()
    small_s[0] = small[...] + small_r[0]
    for copy in locals_ + started:
        copy.wait()

    def add_first(b, _):
        held[b] = (held[b].astype(F32) + first[b].astype(F32)).astype(BF16)
        return 0

    lax.fori_loop(0, n, add_first, 0)

    orders = [list(range(bits)), [1, 0] + list(range(2, bits))]
    slot_of, count = [], 0
    for k in range(bits):
        slot_of.append(count)
        count += n >> (k + 1)

    def places(part, k, mine):
        order = orders[part]
        bit, open_bits = order[k], order[k + 1 :]
        fixed = 0
        for done in order[:k]:
            fixed += ((s // (1 << done)) % 2) * (1 << done)
        own = (s // (1 << bit)) % 2
        fixed += (own if mine else 1 - own) * (1 << bit)
        return [fixed + sum(((e >> i) & 1) << b for i, b in enumerate(open_bits)) for e in range(1 << len(open_bits))]

    def block_copy(part, k, e, place):
        slot = slot_of[k] + e
        return pltpu.make_async_remote_copy(
            src_ref=held.at[place, :, pl.ds(part * half, half)], dst_ref=arrived.at[part, slot],
            send_sem=block_send.at[part, slot], recv_sem=block_recv.at[part, slot],
            device_id=peers[orders[part][k]], device_id_type=MESH)

    sent = []
    for k in range(bits):
        for part in range(2):
            if k:
                for e, place in enumerate(places(part, k - 1, True)):
                    block_copy(part, k - 1, e, place).wait_recv()
                    mine = held.at[place, :, pl.ds(part * half, half)]
                    mine[...] = (mine[...].astype(F32) + arrived[part, slot_of[k - 1] + e].astype(F32)).astype(BF16)
            for e, place in enumerate(places(part, k, False)):
                copy = block_copy(part, k, e, place)
                copy.start()
                sent.append(copy)
        if k:
            copies[k].wait()
            small_s[k] = small_s[k - 1] + small_r[k]
        copy = remote(small_s.at[k], small_r.at[k + 1], 9 + k, peers[k])
        copy.start()
        copies.append(copy)
    copies[bits].wait()
    small_o[...] = small_s[bits - 1] + small_r[bits]
    for part in range(2):
        place = places(part, bits - 1, True)[0]
        block_copy(part, bits - 1, 0, place).wait_recv()
        at = pl.ds(part * half, half)
        total_o[:, at] = held[place, :, at].astype(F32) + arrived[part, slot_of[bits - 1]].astype(F32)
    for copy in sent:
        copy.wait_send()
    for copy in tails:
        copy.wait()


def reduce(n, g_in, g_out, small, out, gtok):
    full, block = out.shape[1], out.shape[0]
    width = full // 2
    rows = full // n
    columns = 4 * width
    bits = n.bit_length() - 1
    anywhere = pl.BlockSpec(memory_space=pl.ANY)
    vmem = pl.BlockSpec(memory_space=pltpu.VMEM)
    return pl.pallas_call(
        functools.partial(reduce_kernel, (n, width, block)),
        name="reduce",
        out_shape=(
            jax.ShapeDtypeStruct((rows, columns), F32),
            jax.ShapeDtypeStruct(small.shape, F32),
            jax.ShapeDtypeStruct((2 * block, width), F32),
            jax.ShapeDtypeStruct((2 * block, width), F32),
        ),
        in_specs=[anywhere] * 2 + [vmem] + [anywhere] * 2,
        out_specs=(vmem, vmem, vmem, vmem),
        scratch_shapes=[
            pltpu.VMEM((n, rows, columns), BF16),
            pltpu.VMEM((n, rows, columns), BF16),
            pltpu.VMEM((2, n - 1, rows, columns // 2), BF16),
            pltpu.VMEM((bits,) + small.shape, F32),
            pltpu.VMEM((bits + 1,) + small.shape, F32),
            pltpu.SemaphoreType.DMA((8,)),
            pltpu.SemaphoreType.DMA((9 + bits,)),
            pltpu.SemaphoreType.DMA((9 + bits,)),
            pltpu.SemaphoreType.DMA((2, n - 1)),
            pltpu.SemaphoreType.DMA((2, n - 1)),
        ],
        compiler_params=pltpu.CompilerParams(collective_id=3, has_side_effects=True, vmem_limit_bytes=VMEM_LIMIT),
    )(g_in.reshape(3, n, rows, full), g_out.reshape(n, rows, full), small, out, gtok)


def reduce_plain(n, g_in, g_out, g_up, g_dn, small, out, gtok):
    full = out.shape[1]
    width, hidden = full // 2, g_up.shape[1] // 2
    parts = []
    for stream in range(3):
        parts.append((g_in[stream], width))
    parts += [(g_out, width), (g_up, hidden), (g_dn, hidden)]
    halves = [
        jnp.concatenate([part[:, k * size : (k + 1) * size] for part, size in parts], axis=1).astype(F32)
        for k in range(2)
    ]
    both = lax.psum_scatter(jnp.stack(halves), "ch", scatter_dimension=0, tiled=False)
    total = lax.psum_scatter(both, "seq", scatter_dimension=0, tiled=True)
    swap = lambda whole: lax.all_to_all(whole, "ch", split_axis=1, concat_axis=0, tiled=True)
    return total, lax.psum(small, ("seq", "ch")), swap(out), swap(gtok)


def on_device(tokens, seg_ids, norm1_gain, in_weight, short_weight, filt_w1, filt_b1, filt_w2, filt_w3,
              long_bias, tail_gain, tail_rate, out_weight, norm2_gain, up_weight, down_weight, grad_out):
    rows, width = tokens.shape
    full, block = 2 * width, rows // 2
    n = lax.axis_size("seq")
    devices = 2 * n
    me = 2 * lax.axis_index("seq") + lax.axis_index("ch")
    row_start = me * block
    total_rows = seg_ids.shape[0]
    length = min(SEQ_LEN, total_rows)

    keys = seg_ids + (jnp.arange(total_rows, dtype=jnp.int32) // length) * 65536
    padded = jnp.concatenate([jnp.full((BEFORE,), -1, jnp.int32), keys, jnp.full((block + AFTER,), -2, jnp.int32)])
    near = lax.dynamic_slice_in_dim(padded, row_start, BEFORE + 2 * block)
    window = near[: BEFORE + block + AFTER]
    ids_s = jnp.concatenate([window, jnp.full((8,), 1, jnp.int32) * near[BEFORE + 2 * block - 1]])
    ids = jnp.broadcast_to(window.astype(F32)[:, None], (window.shape[0], LANES))

    channel_start = lax.axis_index("ch") * width
    pos_table = position_table(FIR, (filt_w1.shape[0] - 1) // 2)
    pre_one = jnp.dot(pos_table, filt_w1, precision=HIGHEST) + filt_b1
    hidden_one = jnp.sin(pre_one)
    pre_two = jnp.dot(hidden_one, filt_w2, precision=HIGHEST)
    hidden_two = jnp.sin(pre_two)
    channel = channel_start.astype(F32) + jnp.arange(width, dtype=F32)
    window_of = lambda channels: jnp.exp(
        -(0.5 + 3.0 * channels / full)[None, :] * jnp.arange(FIR, dtype=F32)[:, None] / FIR)
    taps = jnp.dot(hidden_two, filt_w3, precision=HIGHEST) * window_of(channel)
    norm_tail = jnp.sqrt(-jnp.expm1(-2.0 * tail_rate))
    rows_of = [norm1_gain, norm2_gain, long_bias, tail_gain, tail_rate, norm_tail]
    rows_of += [short_weight[j, s] for j in range(3) for s in range(3)]
    row_index = jnp.arange(HEAD)[:, None]
    head = jnp.zeros((HEAD, width), F32)
    for k, row in enumerate(rows_of):
        head = jnp.where(row_index == k, row[None, :], head)

    tok, g, win, wout, wup, wdn, vec = exchange(
        n, tokens, grad_out, jnp.transpose(in_weight, (1, 0, 2)), out_weight, up_weight, down_weight, head, taps, filt_w3)
    rate, gain, nu = vec[4], vec[3], vec[5]

    n1, proj, v, x0, x1, u, base, car, end = mixer(ids_s, tok, win, vec, ids)

    summed = n == 16 and full % (16 * 16) == 0
    firsts, lasts = keys[::block], keys[block - 1 :: block]
    reach = min(DOC_MOST // block, devices - 1)
    order = jnp.arange(reach)
    source = jnp.clip(me - 1 - order, 0, devices - 1)
    valid = (me - 1 - order >= 0) & (lasts[source] == lasts[jnp.clip(me - 1, 0, devices - 1)])
    weights = jnp.where(valid[:, None], jnp.exp(-rate[None, :] * (block * order.astype(F32))[:, None]), 0.0)
    (enter,) = push(n, end, weights[None], False, 1)

    out, long, car, gmid, gmix, gw_out, gw_up, gw_dn, gain_two = ffn(summed, tok, x0, base, car, ids, enter, g, vec, wout, wup, wdn)

    glong, q, first, halo, sums = gate(gmix, x0, x1, v, long, car, u, vec, ids)
    reach = min(DOC_MOST // block + 1, devices - 1)
    order = jnp.arange(reach)
    source = jnp.clip(me + 1 + order, 0, devices - 1)
    weights = []
    for later in range(2):
        valid = (me + 1 + order < devices) & (order >= later) & (
            firsts[source] == lasts[jnp.clip(me + later, 0, devices - 1)])
        distance = (block * (order - later) + 1).astype(F32)
        weights.append(jnp.where(valid[:, None], jnp.exp(-rate[None, :] * jnp.maximum(distance, 0.0)[:, None]), 0.0))
    joined, halo = push(n, first, jnp.stack(weights), True, 2, halo)

    gw_in, gtok, sums_two, gain_one = back(
        ids_s, glong, q, halo, joined, gmix, long, car, x1, v, u, proj, vec, ids, n1, win, tok, gmid)

    small = jnp.concatenate([sums_two[:42], sums, gain_one, gain_two, jnp.zeros((2, full), F32)])
    hidden = up_weight.shape[1]
    if summed:
        total, small, out, gtok = reduce(n, gw_in, gw_out, small, out, gtok)
    else:
        total, small, out, gtok = reduce_plain(n, gw_in, gw_out, gw_up, gw_dn, small, out, gtok)
        gw_up, gw_dn = total[:, 4 * width : 4 * width + hidden], total[:, 4 * width + hidden :]

    taps_grad, short_grad = small[:FIR], small[FIR : FIR + 9].reshape(3, 3, full)
    carried_q, bias_grad, long_car = small[41], small[42], small[43]
    factor = jnp.exp(-rate)
    rate_grad = gain * long_car * factor * factor / nu - carried_q
    raw_grad = taps_grad * window_of(jnp.arange(full, dtype=F32))
    w3_grad = jnp.dot(hidden_two.T, raw_grad, precision=HIGHEST)
    pre_two_grad = jnp.dot(raw_grad, vec[48:].T, precision=HIGHEST) * jnp.cos(pre_two)
    w2_grad = jnp.dot(hidden_one.T, pre_two_grad, precision=HIGHEST)
    pre_one_grad = jnp.dot(pre_two_grad, filt_w2.T, precision=HIGHEST) * jnp.cos(pre_one)
    w1_grad = jnp.dot(pos_table.T, pre_one_grad, precision=HIGHEST)
    in_grad = jnp.stack([total[:, k * width : (k + 1) * width] for k in range(3)], axis=1)
    return (
        out,
        gtok,
        small[44],
        in_grad,
        short_grad,
        w1_grad,
        jnp.sum(pre_one_grad, axis=0),
        w2_grad,
        w3_grad,
        bias_grad,
        nu * long_car,
        rate_grad,
        total[:, 3 * width : 4 * width].T,
        small[45],
        gw_up,
        gw_dn.T,
    )


def solution(mesh):
    placed = (
        P("seq", "ch"),
        P(),
        P("ch"),
        P(None, None, "ch"),
        P(None, None, "ch"),
        P(),
        P(),
        P(),
        P(None, "ch"),
        P("ch"),
        P("ch"),
        P("ch"),
        P("ch", None),
        P("ch"),
        P(None, "ch"),
        P("ch", None),
        P("seq", "ch"),
    )
    return jax.shard_map(
        on_device,
        mesh=mesh,
        in_specs=placed,
        out_specs=(
            P("seq", "ch"),
            P("seq", "ch"),
            P(),
            P("seq", None, "ch"),
            P(),
            P(),
            P(),
            P(),
            P(),
            P(),
            P(),
            P(),
            P("ch", "seq"),
            P(),
            P("seq", "ch"),
            P("ch", "seq"),
        ),
        check_vma=False,
    )
```

```python
import functools

import jax
import jax.numpy as jnp
from jax import lax
from jax.experimental import pallas as pl
from jax.experimental.pallas import tpu as pltpu
from jax.sharding import PartitionSpec as P

FIR = 32
SEQ_LEN = 16384
DOC_MOST = 8192
EPSILON = 1e-05
FREQUENCY = 0.4
HIGHEST = lax.Precision.HIGHEST
MESH = pl.DeviceIdType.MESH
F32, BF16 = jnp.float32, jnp.bfloat16

BEFORE = 48
AFTER = 80
LANES = 128
BLOCK = 256
CHUNK = 64
SUMS = 48
HEAD = 16
VMEM_LIMIT = 56 << 20
ROOT_TWO_OVER_PI = 0.7978845608028654


def position_table(filter_len, band_count):
    places = jnp.arange(filter_len, dtype=F32)
    harmonics = jnp.arange(1, band_count + 1, dtype=F32)
    angles = FREQUENCY * places[:, None] * harmonics[None, :]
    return jnp.concatenate([places[:, None] / filter_len, jnp.cos(angles), jnp.sin(angles)], axis=1)


def of(ref, start, size):
    return pl.ds(pl.multiple_of(start, size), size)


def exchange_kernel(sizes, tokens, gout, w_in, w_out, w_up, w_down, gains, head, taps,
                    tok_o, g_o, in_o, out_o, up_o, down_o, gains_o, vec_o, local_sem, send_sem, recv_sem):
    n, rows, width, hidden = sizes
    block = rows // 2
    s, c = lax.axis_index("seq"), lax.axis_index("ch")
    barrier = pltpu.get_barrier_semaphore()
    pl.semaphore_signal(barrier, inc=1, device_id=(s, 1 - c), device_id_type=MESH)

    @pl.when((c == 0) & (s > 0))
    def _():
        for k in range(2):
            pl.semaphore_signal(barrier, inc=1, device_id=(s - 1, k), device_id_type=MESH)

    @pl.when(s < n - 1)
    def _():
        pl.semaphore_wait(barrier, 2)

    @pl.when(s == n - 1)
    def _():
        pl.semaphore_wait(barrier, 1)

    cols = pl.ds(pl.multiple_of(c * width, width), width)
    hid = pl.ds(pl.multiple_of(c * hidden, hidden), hidden)
    pairs = [
        (gains, gains_o.at[:, cols]),
        (w_up, up_o.at[:, hid]),
        (w_down, down_o.at[hid, :]),
    ]
    for i in range(width // LANES):
        source = pl.ds(i * LANES, LANES)
        paired = pl.ds(pl.multiple_of((2 * i + c) * LANES, LANES), LANES)
        pairs += [
            (w_in.at[:, :, source], in_o.at[:, :, paired]),
            (w_out.at[source, :], out_o.at[paired, :]),
            (head.at[:, source], vec_o.at[pl.ds(0, HEAD), paired]),
            (taps.at[:, source], vec_o.at[pl.ds(HEAD, FIR), paired]),
        ]

    def remote(src, dst, k, target):
        return pltpu.make_async_remote_copy(
            src_ref=src, dst_ref=dst, send_sem=send_sem.at[k], recv_sem=recv_sem.at[k],
            device_id=target, device_id_type=MESH)

    partner = (s, 1 - c)
    left, right = pl.ds(0, width), pl.ds(width, width)
    first, second = pl.ds(0, block), pl.ds(block, block)
    early = pl.ds(block - BEFORE, block + BEFORE)
    tail = pl.ds(rows - BEFORE, BEFORE)

    @pl.when(c == 0)
    def _():
        remote(tokens.at[early, :], tok_o.at[:, left], 0, partner).start()
        remote(gout.at[second, :], g_o.at[:, left], 1, partner).start()
        pltpu.make_async_copy(tokens.at[first, :], tok_o.at[pl.ds(BEFORE, block), left], local_sem.at[0]).start()
        pltpu.make_async_copy(gout.at[first, :], g_o.at[:, left], local_sem.at[1]).start()

        @pl.when(s < n - 1)
        def _():
            remote(tokens.at[tail, :], tok_o.at[pl.ds(0, BEFORE), left], 2, (s + 1, 0)).start()

    @pl.when(c == 1)
    def _():
        remote(tokens.at[first, :], tok_o.at[pl.ds(BEFORE, block), right], 0, partner).start()
        remote(gout.at[first, :], g_o.at[:, right], 1, partner).start()
        pltpu.make_async_copy(tokens.at[early, :], tok_o.at[:, right], local_sem.at[0]).start()
        pltpu.make_async_copy(gout.at[second, :], g_o.at[:, right], local_sem.at[1]).start()

        @pl.when(s < n - 1)
        def _():
            remote(tokens.at[tail, :], tok_o.at[pl.ds(0, BEFORE), right], 3, (s + 1, 0)).start()

    for k, (src, dst) in enumerate(pairs):
        remote(src, dst, 4 + k, partner).start()
        pltpu.make_async_copy(src, dst, local_sem.at[2 + k]).start()

    for k, (src, dst) in enumerate(pairs):
        pltpu.make_async_copy(src, dst, local_sem.at[2 + k]).wait()
        remote(src, dst, 4 + k, partner).wait()

    @pl.when(c == 0)
    def _():
        remote(tokens.at[early, :], tok_o.at[:, left], 0, partner).wait_send()
        remote(gout.at[second, :], g_o.at[:, left], 1, partner).wait_send()
        remote(tokens.at[first, :], tok_o.at[pl.ds(BEFORE, block), right], 0, partner).wait_recv()
        remote(gout.at[first, :], g_o.at[:, right], 1, partner).wait_recv()
        pltpu.make_async_copy(tokens.at[first, :], tok_o.at[pl.ds(BEFORE, block), left], local_sem.at[0]).wait()
        pltpu.make_async_copy(gout.at[first, :], g_o.at[:, left], local_sem.at[1]).wait()

        @pl.when(s < n - 1)
        def _():
            remote(tokens.at[tail, :], tok_o.at[pl.ds(0, BEFORE), left], 2, (s + 1, 0)).wait_send()

        @pl.when(s > 0)
        def _():
            remote(tokens.at[tail, :], tok_o.at[pl.ds(0, BEFORE), left], 2, partner).wait_recv()
            remote(tokens.at[tail, :], tok_o.at[pl.ds(0, BEFORE), right], 3, partner).wait_recv()

    @pl.when(c == 1)
    def _():
        remote(tokens.at[first, :], tok_o.at[pl.ds(BEFORE, block), right], 0, partner).wait_send()
        remote(gout.at[first, :], g_o.at[:, right], 1, partner).wait_send()
        remote(tokens.at[early, :], tok_o.at[:, left], 0, partner).wait_recv()
        remote(gout.at[second, :], g_o.at[:, left], 1, partner).wait_recv()
        pltpu.make_async_copy(tokens.at[early, :], tok_o.at[:, right], local_sem.at[0]).wait()
        pltpu.make_async_copy(gout.at[second, :], g_o.at[:, right], local_sem.at[1]).wait()

        @pl.when(s < n - 1)
        def _():
            remote(tokens.at[tail, :], tok_o.at[pl.ds(0, BEFORE), right], 3, (s + 1, 0)).wait_send()


def exchange(n, tokens, gout, w_in, w_out, w_up, w_down, *vec):
    rows, width = tokens.shape
    hidden = w_up.shape[1]
    full, block = 2 * width, rows // 2
    pieces = 3 + 4 * (width // LANES)
    anywhere = pl.BlockSpec(memory_space=pl.ANY)
    return pl.pallas_call(
        functools.partial(exchange_kernel, (n, rows, width, hidden)),
        name="exchange",
        out_shape=(
            jax.ShapeDtypeStruct((BEFORE + block, full), BF16),
            jax.ShapeDtypeStruct((block, full), BF16),
            jax.ShapeDtypeStruct((3, full, full), BF16),
            jax.ShapeDtypeStruct((full, full), BF16),
            jax.ShapeDtypeStruct((full, 2 * hidden), BF16),
            jax.ShapeDtypeStruct((2 * hidden, full), BF16),
            jax.ShapeDtypeStruct((vec[0].shape[0], full), F32),
            jax.ShapeDtypeStruct((HEAD + FIR, full), F32),
        ),
        in_specs=[anywhere] * 9,
        out_specs=[pl.BlockSpec(memory_space=pltpu.VMEM)] * 8,
        scratch_shapes=[pltpu.SemaphoreType.DMA((2 + pieces,))] + [pltpu.SemaphoreType.DMA((4 + pieces,))] * 2,
        compiler_params=pltpu.CompilerParams(collective_id=0, has_side_effects=True, vmem_limit_bytes=VMEM_LIMIT),
    )(tokens, gout, w_in, w_out, w_up, w_down, *vec)


def row_stats(values):
    center = jnp.mean(values, axis=1, keepdims=True)
    shifted = values - center
    inverse = lax.rsqrt(jnp.mean(shifted * shifted, axis=1, keepdims=True) + EPSILON)
    return shifted * inverse, inverse


def mixer_kernel(block, ids_s, tok, win, gains, vblk, ids, n1_o, proj_o, x0_o, u_o, long_o, car_o, end_o, heads_o,
                 n1_s, proj_s, state_s):
    rows = BEFORE + block
    lane_blocks = BLOCK // LANES

    @pl.when(pl.program_id(0) == 0)
    def _():
        gain = gains[0:1, :]

        def normed(j, _):
            at = pl.ds(pl.multiple_of(j * 16, 16), 16)
            values = jnp.where(ids[at, 0:1] >= 0.0, tok[at, :].astype(F32), 0.0)
            n1_s[at, :] = (row_stats(values)[0] * gain).astype(BF16)
            return 0

        lax.fori_loop(0, rows // 16, normed, 0)
        n1_o[...] = n1_s[pl.ds(BEFORE, block), :]

    for s in range(3):
        part = jnp.dot(n1_s[...], win[s], preferred_element_type=F32).astype(BF16)
        for b in range(lane_blocks):
            proj_o[s, b] = part[:, b * LANES : (b + 1) * LANES]
            proj_s[s, b] = part[:, b * LANES : (b + 1) * LANES].astype(F32)

    def convolved(start, size):
        own = ids[pl.ds(start, size), :]
        same = [None] + [own == ids[pl.ds(start - j, size), :] for j in (1, 2)]
        results = []
        for b in range(lane_blocks):
            lanes = slice(b * LANES, (b + 1) * LANES)
            streams = []
            for s in range(3):
                value = vblk[6 + s : 7 + s, lanes] * proj_s[s, b, pl.ds(start, size), :]
                for j in (1, 2):
                    tap = vblk[6 + 3 * j + s : 7 + 3 * j + s, lanes]
                    value += jnp.where(same[j], tap * proj_s[s, b, pl.ds(start - j, size), :], 0.0)
                streams.append(value)
            u_o[b, pl.ds(start, size), :] = (streams[0] * streams[2]).astype(BF16).astype(F32)
            results.append(streams)
        return results

    convolved(16, 32)
    for b, streams in enumerate(convolved(BEFORE, 8)):
        heads_o[0:8, b * LANES : (b + 1) * LANES] = streams[2]
        heads_o[8:16, b * LANES : (b + 1) * LANES] = streams[0]
    for b in range(lane_blocks):
        u_o[b, 0:16, :] = jnp.zeros((16, LANES), F32)

    def conv_chunk(j, _):
        start = pl.multiple_of(BEFORE + j * 32, 16)
        for b, streams in enumerate(convolved(start, 32)):
            x0_o[b, pl.ds(pl.multiple_of(j * 32, 32), 32), :] = streams[1]
        return 0

    lax.fori_loop(0, block // 32, conv_chunk, 0)

    row_id = lax.broadcasted_iota(jnp.int32, (8, LANES), 0)
    rates = [vblk[4:5, b * LANES : (b + 1) * LANES] for b in range(lane_blocks)]
    powers = [jnp.exp(-rate * (row_id + 1).astype(F32)) for rate in rates]
    lams = [[jnp.exp(-rate * float(step)) for step in (1, 2, 4)] for rate in rates]
    for b in range(lane_blocks):
        state_s[b, 0:8, :] = jnp.zeros((8, LANES), F32)

    def scan_group(g, carry):
        start = pl.multiple_of(BEFORE + g * 8, 8)
        own = ids[pl.ds(start, 8), :]
        masks = [(own == ids[pl.ds(start - step, 8), :]) & (row_id >= step) for step in (1, 2, 4)]
        joined = own == jnp.broadcast_to(ids[pl.ds(start - 1, 1), :], (8, LANES))
        result = []
        for b in range(lane_blocks):
            value = u_o[b, pl.ds(start, 8), :]
            for mask, lam, step in zip(masks, lams[b], (1, 2, 4)):
                value += jnp.where(mask, lam * pltpu.roll(value, step, 0), 0.0)
            value += jnp.where(joined, powers[b] * carry[b], 0.0)
            state_s[b, pl.ds(pl.multiple_of(8 + g * 8, 8), 8), :] = value
            result.append(jnp.broadcast_to(value[7:8, :], (8, LANES)))
        return tuple(result)

    zero = jnp.zeros((8, LANES), F32)
    final = lax.fori_loop(0, block // 8, scan_group, (zero,) * lane_blocks, unroll=4)
    for b in range(lane_blocks):
        end_o[:, b * LANES : (b + 1) * LANES] = final[b][0:1, :]

    for b in range(lane_blocks):
        lanes = slice(b * LANES, (b + 1) * LANES)
        bias, gain, lam = vblk[2:3, lanes], vblk[3:4, lanes], lams[b][0]
        nu = vblk[5:6, lanes]

        def long_chunk(j, _):
            start = pl.multiple_of(BEFORE + j * CHUNK, 16)
            to = pl.ds(pl.multiple_of(j * CHUNK, CHUNK), CHUNK)
            own = ids[pl.ds(start, CHUNK), :]
            here = u_o[b, pl.ds(start, CHUNK), :]
            previous = state_s[b, pl.ds(7 + j * CHUNK, CHUNK), :]
            carried = jnp.where(own == ids[pl.ds(start - 1, CHUNK), :], lam * previous, 0.0)
            car_o[b, to, :] = carried
            base = bias * here + (gain * nu) * carried
            whole = ids_s[start + CHUNK - 1] == ids_s[start - FIR + 1]

            @pl.when(whole)
            def _():
                total = base
                for k in range(FIR):
                    total += vblk[16 + k : 17 + k, lanes] * u_o[b, pl.ds(start - k, CHUNK), :]
                long_o[b, to, :] = total

            @pl.when(jnp.logical_not(whole))
            def _():
                total = base
                for k in range(FIR):
                    term = vblk[16 + k : 17 + k, lanes] * u_o[b, pl.ds(start - k, CHUNK), :]
                    total += jnp.where(own == ids[pl.ds(start - k, CHUNK), :], term, 0.0)
                long_o[b, to, :] = total

            return 0

        lax.fori_loop(0, block // CHUNK, long_chunk, 0)


def mixer(ids_s, tok, win, gains, vec, ids):
    rows, full = tok.shape
    block = rows - BEFORE
    lane_blocks, lanes = BLOCK // LANES, full // LANES
    whole = lambda *shape: pl.BlockSpec(shape, lambda i: (0,) * len(shape))
    by_channel = lambda count: pl.BlockSpec((count, BLOCK), lambda i: (0, i))
    stacked = lambda count: pl.BlockSpec((lane_blocks, count, LANES), lambda i: (i, 0, 0))
    return pl.pallas_call(
        functools.partial(mixer_kernel, block),
        name="mixer",
        grid=(full // BLOCK,),
        out_shape=(
            jax.ShapeDtypeStruct((block, full), BF16),
            jax.ShapeDtypeStruct((3, lanes, rows, LANES), BF16),
            jax.ShapeDtypeStruct((lanes, block, LANES), F32),
            jax.ShapeDtypeStruct((lanes, rows, LANES), F32),
            jax.ShapeDtypeStruct((lanes, block, LANES), F32),
            jax.ShapeDtypeStruct((lanes, block, LANES), F32),
            jax.ShapeDtypeStruct((1, full), F32),
            jax.ShapeDtypeStruct((16, full), F32),
        ),
        in_specs=[
            pl.BlockSpec(memory_space=pltpu.SMEM),
            whole(rows, full),
            pl.BlockSpec((3, full, BLOCK), lambda i: (0, 0, i)),
            whole(*gains.shape),
            by_channel(vec.shape[0]),
            whole(*ids.shape),
        ],
        out_specs=(
            whole(block, full),
            pl.BlockSpec((3, lane_blocks, rows, LANES), lambda i: (0, i, 0, 0)),
            stacked(block),
            stacked(rows),
            stacked(block),
            stacked(block),
            by_channel(1),
            by_channel(16),
        ),
        scratch_shapes=[
            pltpu.VMEM((rows, full), BF16),
            pltpu.VMEM((3, lane_blocks, rows, LANES), F32),
            pltpu.VMEM((lane_blocks, 8 + block, LANES), F32),
        ],
        compiler_params=pltpu.CompilerParams(vmem_limit_bytes=VMEM_LIMIT),
    )(ids_s, tok, win, gains, vec, ids)


def device_of(index):
    return (index // 2, index % 2)


class Pushing:
    def __init__(self, n, reach, backward, source, slots, send_sem, recv_sem):
        self.total, self.reach = 2 * n, reach
        self.me = 2 * lax.axis_index("seq") + lax.axis_index("ch")
        self.ahead = -1 if backward else 1
        self.place = self.total - 1 - self.me if backward else self.me
        self.source, self.slots, self.send_sem, self.recv_sem = source, slots, send_sem, recv_sem

    def greet(self, barrier):
        for k in range(self.reach):

            @pl.when(self.place - 1 - k >= 0)
            def _():
                pl.semaphore_signal(
                    barrier, inc=1, device_id=device_of(self.me - self.ahead * (1 + k)), device_id_type=MESH)

    def await_greetings(self, barrier, others):
        following = self.total - 1 - self.place
        for count in range(0, self.reach + 1):
            if count + others:

                @pl.when((following >= count) if count == self.reach else (following == count))
                def _():
                    pl.semaphore_wait(barrier, count + others)

    def copy(self, k):
        return pltpu.make_async_remote_copy(
            src_ref=self.source, dst_ref=self.slots.at[k], send_sem=self.send_sem.at[k], recv_sem=self.recv_sem.at[k],
            device_id=device_of(self.me + self.ahead * (1 + k)), device_id_type=MESH)

    def start(self):
        for k in range(self.reach):

            @pl.when(self.place + 1 + k < self.total)
            def _():
                self.copy(k).start()

    def take(self, use):
        for k in range(self.reach):

            @pl.when(self.place - 1 - k >= 0)
            def _():
                self.copy(k).wait_recv()
                use(k, self.slots[k])

            @pl.when(self.place + 1 + k < self.total)
            def _():
                self.copy(k).wait_send()


def push_kernel(n, reach, block, marks, end, vec, enter_o, slots, send_sem, recv_sem):
    pushing = Pushing(n, reach, False, end, slots, send_sem, recv_sem)
    barrier = pltpu.get_barrier_semaphore()
    pushing.greet(barrier)
    pushing.await_greetings(barrier, 0)
    pushing.start()
    enter_o[...] = jnp.zeros_like(enter_o)
    rate = vec[4:5, :]
    last = marks[2 * n + jnp.maximum(pushing.me - 1, 0)]

    def use(k, state):
        same = jnp.where(marks[2 * n + pushing.me - 1 - k] == last, 1.0, 0.0)
        enter_o[...] += same * jnp.exp(-rate * float(block * k)) * state

    pushing.take(use)


def push(n, block, marks, end, vec):
    full = end.shape[1]
    reach = min(DOC_MOST // block, 2 * n - 1)
    vmem = pl.BlockSpec(memory_space=pltpu.VMEM)
    return pl.pallas_call(
        functools.partial(push_kernel, n, reach, block),
        name="push",
        out_shape=jax.ShapeDtypeStruct((1, full), F32),
        in_specs=[pl.BlockSpec(memory_space=pltpu.SMEM), vmem, vmem],
        out_specs=vmem,
        scratch_shapes=[
            pltpu.VMEM((reach, 1, full), F32), pltpu.SemaphoreType.DMA((reach,)), pltpu.SemaphoreType.DMA((reach,))],
        compiler_params=pltpu.CompilerParams(collective_id=1, has_side_effects=True),
    )(marks, end, vec)


TILE = 512
PART = TILE // 2
STAGES = 5


class Summing:
    def __init__(self, slots, rows, staged, first, second, third, fourth, fifth, send_sem, recv_sem):
        self.slots, self.rows, self.staged = slots, rows, staged
        self.first, self.second, self.third, self.fourth, self.fifth = first, second, third, fourth, fifth
        self.send_sem, self.recv_sem = send_sem, recv_sem
        self.s, self.c = lax.axis_index("seq"), lax.axis_index("ch")
        self.bits = [(self.s // (1 << b)) % 2 for b in range(4)]
        self.peers = [(self.s + (1 - 2 * bit) * (1 << b), self.c) for b, bit in enumerate(self.bits)]
        self.partner = (self.s, 1 - self.c)
        self.order = ((0, 1, 2, 3), (1, 0, 2, 3))

    @staticmethod
    def scratch(tiles, slots, rows):
        return [
            pltpu.VMEM((2, 2, 2, 2, 2, 2, rows, TILE), BF16),
            pltpu.VMEM((slots, 2, 2, 2, 2, rows, TILE), BF16),
            pltpu.VMEM((slots, 2, 2, 2, 2, rows, PART), BF16),
            pltpu.VMEM((slots, 2, 2, 2, rows, PART), BF16),
            pltpu.VMEM((slots, 2, 2, rows, PART), BF16),
            pltpu.VMEM((slots, 2, rows, PART), BF16),
            pltpu.SemaphoreType.DMA((tiles, 1 + 2 * 4)),
            pltpu.SemaphoreType.DMA((tiles, 1 + 2 * 4)),
        ]

    def greet(self, barrier):
        for peer in [self.partner] + self.peers:
            pl.semaphore_signal(barrier, inc=1, device_id=peer, device_id_type=MESH)

    def remote(self, src, dst, tile, k, target):
        return pltpu.make_async_remote_copy(
            src_ref=src, dst_ref=dst, send_sem=self.send_sem.at[tile, k], recv_sem=self.recv_sem.at[tile, k],
            device_id=target, device_id_type=MESH)

    def copies(self, tile, stage):
        slot = tile % self.slots
        if stage == 0:
            return [self.remote(self.staged.at[tile % 2, 1], self.first.at[slot], tile, 0, self.partner)]
        result = []
        for part in range(2):
            bit = self.order[part][stage - 1]
            away = 1 - self.bits[bit]
            at = pl.ds(part * PART, PART)
            if stage == 1:
                src = self.first.at[slot, :, :, :, away, :, at] if part == 0 else self.first.at[slot, :, :, away, :, :, at]
                dst = self.second.at[slot, part]
            elif stage == 2:
                src, dst = self.second.at[slot, part, :, :, away], self.third.at[slot, part]
            elif stage == 3:
                src, dst = self.third.at[slot, part, :, away], self.fourth.at[slot, part]
            else:
                src, dst = self.fourth.at[slot, part, away], self.fifth.at[slot, part]
            result.append(self.remote(src, dst, tile, 1 + 2 * (stage - 1) + part, self.peers[bit]))
        return result

    def start(self, tile, stage):
        for copy in self.copies(tile, stage):
            copy.start()

    def advance(self, tile, stage, total):
        for copy in self.copies(tile, stage):
            copy.wait()
        x, y, low, high = self.bits
        slot = tile % self.slots
        if stage == 0:
            def add(i, _):
                for h in range(2):
                    for j in range(2):
                        for k in range(2):
                            self.first[slot, h, i, j, k] += self.staged[tile % 2, 0, h, i, j, k]
                return 0
            lax.fori_loop(0, 2, add, 0)
        elif stage == 1:
            def add(i, _):
                for h in range(2):
                    for k in range(2):
                        self.second[slot, 0, h, i, k] += self.first[slot, h, i, k, x, :, 0:PART]
                        self.second[slot, 1, h, i, k] += self.first[slot, h, i, y, k, :, PART:TILE]
                return 0
            lax.fori_loop(0, 2, add, 0)
        elif stage == 2:
            for i in range(2):
                for k in range(2):
                    self.third[slot, 0, i, k] += self.second[slot, 0, i, k, y]
                    self.third[slot, 1, i, k] += self.second[slot, 1, i, k, x]
        elif stage == 3:
            for part in range(2):
                for i in range(2):
                    self.fourth[slot, part, i] += self.third[slot, part, i, low]
        else:
            for part in range(2):
                mine = self.fourth[slot, part, high].astype(F32)
                total(tile, part, mine + self.fifth[slot, part].astype(F32))
            return
        self.start(tile, stage + 1)


class Joining:
    def __init__(self, sums, held, arrived, send_sem, recv_sem):
        self.held, self.arrived, self.send_sem, self.recv_sem = held, arrived, send_sem, recv_sem
        self.targets = [sums.partner] + sums.peers

    @staticmethod
    def scratch(*shape):
        return [pltpu.VMEM((STAGES,) + shape, F32), pltpu.VMEM((STAGES,) + shape, F32),
                pltpu.SemaphoreType.DMA((STAGES,)), pltpu.SemaphoreType.DMA((STAGES,))]

    def copy(self, stage):
        return pltpu.make_async_remote_copy(
            src_ref=self.held.at[stage], dst_ref=self.arrived.at[stage], send_sem=self.send_sem.at[stage],
            recv_sem=self.recv_sem.at[stage], device_id=self.targets[stage], device_id_type=MESH)

    def start(self, stage):
        self.copy(stage).start()

    def advance(self, stage, result):
        self.copy(stage).wait()
        total = self.held[stage] + self.arrived[stage]
        if stage == STAGES - 1:
            result[...] = total
        else:
            self.held[stage + 1] = total
            self.start(stage + 1)


def contract(left, right, dims):
    return lax.dot_general(left, right, (dims, ((), ())), preferred_element_type=F32)


def contract(left, right, dims):
    return lax.dot_general(left, right, (dims, ((), ())), preferred_element_type=F32)


TILES = 6
EPILOGUE, GATE, TAPS, BACK = TILES, TILES + 1, TILES + 2, TILES + 3
HALO = 80


def backward_kernel(n, block, reach, summed, marks, tok, ids, enter, g, gains, vec, wout, x0, base, car, u, n1, heads,
                    wup_a, wup_b, wdn_a, wdn_b, win, proj, *refs):
    full = g.shape[1]
    width, lane_blocks = full // 2, full // LANES
    steps = full // BLOCK
    last_back = BACK + steps - 1
    outs, refs = refs[:6], refs[6:]
    if summed:
        part_a, part_b, small_a, small_b, out_full, gtok_full = outs
    else:
        grads_o, small_a, small_b, out_o, gtok_o, _ = outs
    (mixed_s, middle_s, n2_s, gn_s, gout_s, out_s, gmid_s, long_s, car_s, glong_s, q_s, gc_s, gp_s, proj_s,
     dist_s, rest_s, taps_s, first_s, slots_s, joined_s, halo_s, halo_r, head_s,
     push_send, push_recv, halo_sem, *buffers) = refs
    step = pl.program_id(0)
    groups = block // 32
    barrier = pltpu.get_barrier_semaphore()
    pushing = Pushing(n, reach, True, first_s, slots_s, push_send, push_recv)
    c = lax.axis_index("ch")
    lanes_of = lambda b: pl.ds(pl.multiple_of(b * LANES, LANES), LANES)
    if summed:
        sums = Summing(TILES, full // 16, *buffers[:8])
        joins = [(Joining(sums, *buffers[8:12]), small_a, TAPS), (Joining(sums, *buffers[12:16]), small_b, last_back)]
        local_sem, exchange_send, exchange_recv = buffers[16:]

        def shares(k, src, dst):
            at = pl.ds(pl.multiple_of(c * block, block), block)
            of_core = lambda which: src.at[:, pl.ds(pl.multiple_of(which * width, width), width)]
            return (
                pltpu.make_async_copy(of_core(c), dst.at[at, :], local_sem.at[k]),
                pltpu.make_async_remote_copy(
                    src_ref=of_core(1 - c), dst_ref=dst.at[at, :], send_sem=exchange_send.at[k],
                    recv_sem=exchange_recv.at[k], device_id=sums.partner, device_id_type=MESH),
            )

    halo_copy = pltpu.make_async_remote_copy(
        src_ref=halo_s, dst_ref=halo_r, send_sem=halo_sem.at[0], recv_sem=halo_sem.at[1],
        device_id=device_of(pushing.me - 1), device_id_type=MESH)

    @pl.when(step == 0)
    def _():
        pushing.greet(barrier)
        if summed:
            sums.greet(barrier)

        last = ids[pl.ds(BEFORE - 1, 1), :]
        for b in range(lane_blocks):
            lanes = slice(b * LANES, (b + 1) * LANES)
            rate, tail = vec[4:5, lanes], vec[3:4, lanes] * vec[5:6, lanes]
            state = enter[0:1, lanes]

            def mix(j, _):
                at = pl.ds(pl.multiple_of(j * 32, 32), 32)
                passed = (lax.broadcasted_iota(jnp.int32, (32, LANES), 0) + (j * 32 + 1)).astype(F32)
                same = ids[pl.ds(pl.multiple_of(BEFORE + j * 32, 16), 32), :] == last
                entered = jnp.where(same, jnp.exp(-rate * passed) * state, 0.0)
                car_s[b, at, :] = car[b, at, :] + entered
                long = base[b, at, :] + tail * entered
                long_s[b, at, :] = long
                mixed_s[at, lanes] = (long * x0[b, at, :]).astype(BF16)
                return 0

            lax.fori_loop(0, groups, mix, 0)
        middle_s[...] = jnp.dot(mixed_s[...], wout[...], preferred_element_type=F32)

        def norm(j, _):
            at = pl.ds(pl.multiple_of(j * 32, 32), 32)
            start = pl.multiple_of(BEFORE + j * 32, 16)
            values = middle_s[at, :] + tok[pl.ds(start, 32), :].astype(F32)
            middle_s[at, :] = values
            out_s[at, :] = values
            n2_s[at, :] = (row_stats(values)[0] * gains[1:2, :]).astype(BF16)
            gn_s[at, :] = jnp.zeros_like(values)
            own = ids[pl.ds(start, 32), :]
            before = after = jnp.zeros((32, LANES), F32)
            for k in range(1, FIR):
                before += jnp.where(own == ids[pl.ds(start - k, 32), :], 1.0, 0.0)
                after += jnp.where(own == ids[pl.ds(start + k, 32), :], 1.0, 0.0)
            dist_s[at, :] = before
            rest_s[at, :] = after
            return 0

        lax.fori_loop(0, groups, norm, 0)
        pushing.await_greetings(barrier, 5 if summed else 0)

    if summed:

        def total(tile, part, value):
            (part_a, part_b)[part][:, pl.ds(pl.multiple_of(tile * PART, PART), PART)] = value

        for stage in range(STAGES - 1, -1, -1):
            since = step - 1 - stage

            @pl.when(((since >= 0) & (since < TILES)) | ((since >= BACK) & (since <= last_back)))
            def _():
                sums.advance(since - (BACK - TILES) * (since // BACK), stage, total)

            for join, result, begun in joins:

                @pl.when(since == begun)
                def _():
                    join.advance(stage, result)

    def put(tile, start, grad):
        size = grad[0].shape[1]
        at = pl.ds(start, size)
        for half in range(2):
            if summed:
                whose = (half + c) % 2
                for q in range(16):
                    sums.staged[tile % 2, whose, q // 8, q // 4 % 2, q // 2 % 2, q % 2, :, at] = (
                        grad[half][q * sums.rows : (q + 1) * sums.rows])
            else:
                grads_o[0, half, :, at] = grad[half]

    @pl.when(step < TILES)
    def _():
        for half, (wup, wdn) in enumerate(((wup_a, wdn_a), (wup_b, wdn_b))):
            n2, rows = n2_s[...], g[...]
            up = jnp.dot(n2, wup[...], preferred_element_type=F32)
            pulled = contract(rows, wdn[...], ((1,), (1,)))
            square = up * up
            inner = ROOT_TWO_OVER_PI * up * (1.0 + 0.044715 * square)
            bent = jnp.tanh(inner)
            part = 0.5 * (1.0 + bent)
            active = (up * part).astype(BF16)
            slope = part + (0.5 * ROOT_TWO_OVER_PI) * up * (1.0 - bent * bent) * (1.0 + 0.134145 * square)
            g_up = (pulled * slope).astype(BF16)
            out_s[...] += jnp.dot(active, wdn[...], preferred_element_type=F32)
            gn_s[...] += contract(g_up, wup[...], ((1,), (1,)))
            pair = (contract(n2, g_up, ((0,), (0,))).astype(BF16), contract(rows, active, ((0,), (0,))).astype(BF16))
            for k in range(2):
                at = pl.ds(k * PART, PART)
                if summed:
                    whose = (half + c) % 2
                    for q in range(16):
                        sums.staged[step % 2, whose, q // 8, q // 4 % 2, q // 2 % 2, q % 2, :, at] = (
                            pair[k][q * sums.rows : (q + 1) * sums.rows])
                else:
                    grads_o[0, half, :, at] = pair[k]
        if summed:
            sums.start(step, 0)

    @pl.when(step == EPILOGUE)
    def _():
        if summed:
            for copy in shares(0, out_s, out_full):
                copy.start()
        else:
            out_o[...] = out_s[...]

        def back(j, total):
            at = pl.ds(pl.multiple_of(j * 32, 32), 32)
            normal, inverse = row_stats(middle_s[at, :])
            grad = gn_s[at, :]
            total += jnp.sum(grad * normal, axis=0, keepdims=True)
            scaled = grad * gains[1:2, :]
            cross = jnp.mean(scaled * normal, axis=1, keepdims=True)
            result = g[at, :].astype(F32) + inverse * (
                scaled - jnp.mean(scaled, axis=1, keepdims=True) - normal * cross)
            gmid_s[at, :] = result
            gout_s[at, :] = result.astype(BF16)
            gn_s[at, :] = jnp.zeros_like(grad)
            return total

        gain_two = lax.fori_loop(0, groups, back, jnp.zeros((1, full), F32))
        head_s[...] = jnp.zeros_like(head_s)
        head_s[0:1, :] = gain_two
        for i in range(steps):
            gmix = contract(gout_s[...], wout[i * BLOCK : (i + 1) * BLOCK, :], ((1,), (1,)))
            for k in range(BLOCK // LANES):
                b = i * (BLOCK // LANES) + k
                part = gmix[:, k * LANES : (k + 1) * LANES]
                glong_s[b, 0:block, :] = part * x0[b]
                long_s[b] = part * long_s[b]

    row_id = lax.broadcasted_iota(jnp.int32, (8, LANES), 0)
    zero = jnp.zeros((8, LANES), F32)

    @pl.when(step == GATE)
    def _():
        rates = [vec[4:5, b * LANES : (b + 1) * LANES] for b in range(lane_blocks)]
        tails = [vec[3:4, b * LANES : (b + 1) * LANES] * vec[5:6, b * LANES : (b + 1) * LANES] for b in range(lane_blocks)]
        lams = [[jnp.exp(-rate * float(k)) for k in (1, 2, 4)] for rate in rates]
        powers = [jnp.exp(-rate * (8 - row_id).astype(F32)) for rate in rates]

        def scan_group(i, carry):
            at = block // 8 - 1 - i
            to = pl.ds(pl.multiple_of(at * 8, 8), 8)
            start = pl.multiple_of(BEFORE + at * 8, 8)
            own = ids[pl.ds(start, 8), :]
            masks = [(own == ids[pl.ds(start + k, 8), :]) & (row_id < 8 - k) for k in (1, 2, 4)]
            joined = own == jnp.broadcast_to(ids[pl.ds(start + 8, 1), :], (8, LANES))
            states, biases, carries = [], [], []
            for b in range(lane_blocks):
                grad = glong_s[b, to, :]
                value = grad * tails[b]
                for mask, lam, k in zip(masks, lams[b], (1, 2, 4)):
                    value += jnp.where(mask, lam * pltpu.roll(value, 8 - k, 0), 0.0)
                value += jnp.where(joined, powers[b] * carry[0][b], 0.0)
                q_s[b, to, :] = value
                states.append(jnp.broadcast_to(value[0:1, :], (8, LANES)))
                biases.append(carry[1][b] + grad * u[b, pl.ds(start, 8), :])
                carries.append(carry[2][b] + grad * car_s[b, to, :])
            return tuple(states), tuple(biases), tuple(carries)

        many = (zero,) * lane_blocks
        states, biases, carries = lax.fori_loop(0, block // 8, scan_group, (many, many, many), unroll=2)
        for b in range(lane_blocks):
            lanes = slice(b * LANES, (b + 1) * LANES)
            first_s[:, lanes] = states[b][0:1, :]
            head_s[1:2, lanes] = jnp.sum(biases[b], axis=0, keepdims=True)
            head_s[2:3, lanes] = jnp.sum(carries[b], axis=0, keepdims=True)
            halo_s[0:48, lanes] = glong_s[b, 0:48, :]
            halo_s[48:56, lanes] = q_s[b, 0:8, :]
            halo_s[72:80, lanes] = long_s[b, 0:8, :]
        halo_s[56:72, :] = heads[...]
        pushing.start()

        @pl.when(pushing.me > 0)
        def _():
            halo_copy.start()

    @pl.when(step == TAPS)
    def _():
        taps_s[...] = jnp.zeros_like(taps_s)

        def pairs(p, _):
            def chunk(j, _):
                at = pl.ds(pl.multiple_of(j * 32, 32), 32)
                start = BEFORE + j * 32
                near = dist_s[at, :]
                here = [glong_s[2 * p + k, at, :] for k in range(2)]
                for tap in range(FIR):
                    same = near >= float(tap)
                    for k in range(2):
                        term = jnp.where(same, here[k] * u[2 * p + k, pl.ds(start - tap, 32), :], 0.0)
                        taps_s[2 * p + k, tap] += jnp.sum(term.reshape(4, 8, LANES), axis=0)
                return 0

            lax.fori_loop(0, groups, chunk, 0)
            return 0

        lax.fori_loop(0, lane_blocks // 2, pairs, 0)
        result = joins[0][0].held.at[0] if summed else small_a
        for b in range(lane_blocks):
            lanes = slice(b * LANES, (b + 1) * LANES)
            result[0:FIR, lanes] = jnp.sum(taps_s[b], axis=1)
        result[FIR : FIR + 8, :] = head_s[...]
        if summed:
            joins[0][0].start(0)

    @pl.when(step == BACK)
    def _():
        joined_s[...] = jnp.zeros_like(joined_s)
        rate = vec[4:5, :]
        following = 2 * n + jnp.minimum(pushing.me + 1, 2 * n - 1)
        lasts = (marks[2 * n + pushing.me], marks[following])

        def use(k, state):
            first = marks[pushing.me + 1 + k]
            for row in range(2):
                if k >= row:
                    same = jnp.where(first == lasts[row], 1.0, 0.0)
                    joined_s[row : row + 1, :] += same * jnp.exp(-rate * float(block * (k - row) + 1)) * state

        pushing.take(use)

        @pl.when(pushing.me > 0)
        def _():
            halo_copy.wait_send()

        @pl.when(pushing.me < 2 * n - 1)
        def _():
            halo_copy.wait_recv()

        for b in range(lane_blocks):
            glong_s[b, block : block + 48, :] = halo_r[0:48, b * LANES : (b + 1) * LANES]

    @pl.when((step >= BACK) & (step <= last_back))
    def _():
        i = step - BACK
        two = range(2)
        lanes = [lanes_of(2 * i + k) for k in two]
        rates = [vec[4:5, lanes[k]] for k in two]
        scales = [vec[2:3, lanes[k]] - vec[3:4, lanes[k]] * vec[5:6, lanes[k]] for k in two]
        mine = [joined_s[0:1, lanes[k]] for k in two]
        for k in two:
            for s in range(3):
                proj_s[s, k] = proj[s, k].astype(F32)
        last = ids[pl.ds(BEFORE + block - 1, 1), :]

        def conv_at(s, k, start, size, same):
            value = vec[6 + s : 7 + s, lanes[k]] * proj_s[s, k, pl.ds(start, size), :]
            for j in (1, 2):
                tap = vec[6 + 3 * j + s : 7 + 3 * j + s, lanes[k]]
                value += jnp.where(same[j - 1], tap * proj_s[s, k, pl.ds(start - j, size), :], 0.0)
            return value

        def chunk(j, totals):
            at = pl.ds(pl.multiple_of(j * 32, 32), 32)
            start = pl.multiple_of(BEFORE + j * 32, 16)
            own = ids[pl.ds(start, 32), :]
            left = (block - 1 - j * 32 - lax.broadcasted_iota(jnp.int32, (32, LANES), 0)).astype(F32)
            after = rest_s[at, :]
            near = dist_s[at, :]
            grads, result = [], []
            for k in two:
                b = 2 * i + k
                state = q_s[b, at, :] + jnp.where(own == last, jnp.exp(-rates[k] * left) * mine[k], 0.0)
                result.append(totals[k] + jnp.sum((car_s[b, at, :] * state).reshape(4, 8, LANES), axis=0))
                grads.append(scales[k] * glong_s[b, at, :] + state)
            for tap in range(FIR):
                same = after >= float(tap)
                for k in two:
                    term = vec[16 + tap : 17 + tap, lanes[k]] * glong_s[2 * i + k, pl.ds(j * 32 + tap, 32), :]
                    grads[k] += jnp.where(same, term, 0.0)
            same = [near >= 1.0, near >= 2.0]
            for k in two:
                gc_s[0, k, at, :] = grads[k] * conv_at(2, k, start, 32, same)
                gc_s[1, k, at, :] = long_s[2 * i + k, at, :]
                gc_s[2, k, at, :] = grads[k] * conv_at(0, k, start, 32, same)
            return tuple(result)

        crossed = lax.fori_loop(0, groups, chunk, (zero, zero))

        start = BEFORE + block
        own = ids[pl.ds(start, 8), :]
        end_id = marks[2 * n + jnp.minimum(pushing.me + 1, 2 * n - 1)].astype(F32)
        left = (block - 1 - row_id).astype(F32)
        for k in two:
            b = 2 * i + k
            entered = jnp.exp(-rates[k] * left) * joined_s[1:2, lanes[k]]
            grad = halo_r[48:56, lanes[k]] + jnp.where(own == end_id, entered, 0.0)
            grad += scales[k] * glong_s[b, block : block + 8, :]
            for tap in range(FIR):
                term = vec[16 + tap : 17 + tap, lanes[k]] * glong_s[b, block + tap : block + tap + 8, :]
                grad += jnp.where(own == ids[pl.ds(start + tap, 8), :], term, 0.0)
            gc_s[0, k, block : block + 8, :] = grad * halo_r[56:64, lanes[k]]
            gc_s[1, k, block : block + 8, :] = halo_r[72:80, lanes[k]]
            gc_s[2, k, block : block + 8, :] = grad * halo_r[64:72, lanes[k]]

        small = joins[1][0].held.at[0] if summed else small_b
        for k in two:

            def short(j, totals):
                at = pl.ds(pl.multiple_of(j * 32, 32), 32)
                start = pl.multiple_of(BEFORE + j * 32, 16)
                same = [dist_s[at, :] >= float(d) for d in (1, 2)]
                later = [rest_s[at, :] >= float(d) for d in (1, 2)]
                result = []
                for s in range(3):
                    here = gc_s[s, k, at, :]
                    value = vec[6 + s : 7 + s, lanes[k]] * here
                    for d in (1, 2):
                        tap = vec[6 + 3 * d + s : 7 + 3 * d + s, lanes[k]]
                        value += jnp.where(later[d - 1], tap * gc_s[s, k, pl.ds(j * 32 + d, 32), :], 0.0)
                    gp_s[s, at, k * LANES : (k + 1) * LANES] = value.astype(BF16)
                    for d in range(3):
                        term = here * proj_s[s, k, pl.ds(start - d, 32), :]
                        if d:
                            term = jnp.where(same[d - 1], term, 0.0)
                        result.append(totals[3 * s + d] + jnp.sum(term.reshape(4, 8, LANES), axis=0))
                return tuple(result)

            totals = lax.fori_loop(0, groups, short, (zero,) * 9)
            rows = [None] * 9
            for s in range(3):
                for d in range(3):
                    rows[3 * d + s] = jnp.sum(totals[3 * s + d], axis=0, keepdims=True)
            rows.append(jnp.sum(crossed[k], axis=0, keepdims=True))
            for row, value in enumerate(rows):
                small[row : row + 1, lanes[k]] = value

        tile = TILES + i
        pieces = []
        for s in range(3):
            part = gp_s[s]
            pieces.append(contract(n1[...], part, ((0,), (0,))).astype(BF16))
            gn_s[...] += contract(part, win[s], ((1,), (1,)))
        at = pl.ds(pl.multiple_of(i * BLOCK, BLOCK), BLOCK)
        pieces.append(contract(gout_s[...], mixed_s[:, at], ((0,), (0,))).astype(BF16))
        for s, piece in enumerate(pieces):
            put(tile, s * LANES, [piece[:, half * LANES : (half + 1) * LANES] for half in range(2)])
        if summed:
            sums.start(tile, 0)

    @pl.when(step == last_back)
    def _():
        def back(j, total):
            at = pl.ds(pl.multiple_of(j * 32, 32), 32)
            normal, inverse = row_stats(tok[pl.ds(pl.multiple_of(BEFORE + j * 32, 16), 32), :].astype(F32))
            grad = gn_s[at, :]
            total += jnp.sum(grad * normal, axis=0, keepdims=True)
            scaled = grad * gains[0:1, :]
            cross = jnp.mean(scaled * normal, axis=1, keepdims=True)
            middle_s[at, :] = gmid_s[at, :] + inverse * (
                scaled - jnp.mean(scaled, axis=1, keepdims=True) - normal * cross)
            return total

        gain_one = lax.fori_loop(0, groups, back, jnp.zeros((1, full), F32))
        small = joins[1][0].held.at[0] if summed else small_b
        small[10:11, :] = gain_one
        small[11:16, :] = jnp.zeros((5, full), F32)
        if summed:
            joins[1][0].start(0)
            for copy in shares(1, middle_s, gtok_full):
                copy.start()
        else:
            gtok_o[...] = middle_s[...]

    if summed:

        @pl.when(step == last_back + STAGES)
        def _():
            for k, (src, dst) in enumerate(((out_s, out_full), (middle_s, gtok_full))):
                for copy in shares(k, src, dst):
                    copy.wait()


def backward(n, summed, marks, tok, ids, enter, g, gains, vec, wout, x0, base, car, u, n1, heads, wup, wdn, win, proj):
    block, full = g.shape
    rows, lane_blocks = BEFORE + block, full // LANES
    steps = full // BLOCK
    tiles = TILES + steps
    reach = min(DOC_MOST // block + 1, 2 * n - 1)
    whole = lambda *shape: pl.BlockSpec(shape, lambda i: (0,) * len(shape), pipeline_mode=pl.Buffered(1))
    tile = lambda i, half: jnp.minimum(i, TILES - 1) + half * TILES
    back = lambda i: jnp.clip(i - BACK, 0, steps - 1)
    wide = lambda dtype: pltpu.VMEM((block, full), dtype)
    stacked = lambda count, dtype=F32: pltpu.VMEM((lane_blocks, count, LANES), dtype)
    shape = jax.ShapeDtypeStruct
    if summed:
        out_shape = [shape((full // 16, tiles * PART), F32)] * 2 + [shape((FIR + 8, full), F32), shape((16, full), F32)]
        out_shape += [shape((2 * block, full // 2), F32)] * 2
        out_specs = [whole(full // 16, tiles * PART)] * 2 + [whole(FIR + 8, full), whole(16, full)]
        out_specs += [pl.BlockSpec(memory_space=pl.ANY)] * 2
        extra = Summing.scratch(tiles, TILES, full // 16) + Joining.scratch(FIR + 8, full) + Joining.scratch(16, full)
        extra += [pltpu.SemaphoreType.DMA((2,))] * 3
    else:
        out_shape = [shape((tiles, 2, full, TILE), BF16), shape((FIR + 8, full), F32), shape((16, full), F32)]
        out_shape += [shape((block, full), F32)] * 2 + [shape((8, LANES), F32)]
        place = lambda i: jnp.minimum(i, TILES - 1) + jnp.clip(i - BACK + 1, 0, steps)
        out_specs = [pl.BlockSpec((1, 2, full, TILE), lambda i: (place(i), 0, 0, 0)), whole(FIR + 8, full), whole(16, full)]
        out_specs += [whole(block, full)] * 2 + [whole(8, LANES)]
        extra = []
    return pl.pallas_call(
        functools.partial(backward_kernel, n, block, reach, summed),
        name="backward",
        grid=(BACK + steps + (STAGES if summed else 0),),
        out_shape=out_shape,
        in_specs=[
            pl.BlockSpec(memory_space=pltpu.SMEM),
            whole(*tok.shape), whole(*ids.shape), whole(*enter.shape), whole(*g.shape), whole(*gains.shape),
            whole(*vec.shape), whole(*wout.shape), whole(*x0.shape), whole(*base.shape), whole(*car.shape),
            whole(*u.shape), whole(*n1.shape), whole(*heads.shape),
            pl.BlockSpec((full, PART), lambda i: (0, tile(i, 0))),
            pl.BlockSpec((full, PART), lambda i: (0, tile(i, 1))),
            pl.BlockSpec((PART, full), lambda i: (tile(i, 0), 0)),
            pl.BlockSpec((PART, full), lambda i: (tile(i, 1), 0)),
            pl.BlockSpec((3, full, BLOCK), lambda i: (0, 0, back(i))),
            pl.BlockSpec((3, BLOCK // LANES, rows, LANES), lambda i: (0, back(i), 0, 0)),
        ],
        out_specs=out_specs,
        scratch_shapes=[
            wide(BF16), wide(F32), wide(BF16), wide(F32), wide(BF16), wide(F32), wide(F32),
            stacked(block), stacked(block), stacked(block + 48), stacked(block),
            pltpu.VMEM((3, BLOCK // LANES, block + 8, LANES), F32),
            pltpu.VMEM((3, block, BLOCK), BF16),
            pltpu.VMEM((3, BLOCK // LANES, rows, LANES), F32),
            pltpu.VMEM((block, LANES), F32),
            pltpu.VMEM((block, LANES), F32),
            pltpu.VMEM((lane_blocks, FIR, 8, LANES), F32),
            pltpu.VMEM((1, full), F32),
            pltpu.VMEM((reach, 1, full), F32),
            pltpu.VMEM((2, full), F32),
            pltpu.VMEM((HALO, full), F32),
            pltpu.VMEM((HALO, full), F32),
            pltpu.VMEM((8, full), F32),
            pltpu.SemaphoreType.DMA((reach,)),
            pltpu.SemaphoreType.DMA((reach,)),
            pltpu.SemaphoreType.DMA((2,)),
            *extra,
        ],
        compiler_params=pltpu.CompilerParams(collective_id=2, has_side_effects=True, vmem_limit_bytes=60 << 20),
    )(marks, tok, ids, enter, g, gains, vec, wout, x0, base, car, u, n1, heads, wup, wup, wdn, wdn, win, proj)


def reduce_plain(n, grads, small_a, small_b, out, gtok):
    both = lax.psum_scatter(grads.astype(F32), "ch", scatter_dimension=1, tiled=False)
    total = lax.psum_scatter(both, "seq", scatter_dimension=1, tiled=True)
    total = jnp.transpose(total, (1, 0, 2))
    parts = [total[:, :, k * PART : (k + 1) * PART].reshape(total.shape[0], -1) for k in range(2)]
    swap = lambda whole: lax.all_to_all(whole, "ch", split_axis=1, concat_axis=0, tiled=True)
    small_a, small_b = lax.psum((small_a, small_b), ("seq", "ch"))
    return *parts, small_a, small_b, swap(out), swap(gtok)


def on_device(tokens, seg_ids, norm1_gain, in_weight, short_weight, filt_w1, filt_b1, filt_w2, filt_w3,
              long_bias, tail_gain, tail_rate, out_weight, norm2_gain, up_weight, down_weight, grad_out):
    rows, width = tokens.shape
    full, block = 2 * width, rows // 2
    n = lax.axis_size("seq")
    devices = 2 * n
    me = 2 * lax.axis_index("seq") + lax.axis_index("ch")
    row_start = me * block
    total_rows = seg_ids.shape[0]
    length = min(SEQ_LEN, total_rows)

    keys = seg_ids + (jnp.arange(total_rows, dtype=jnp.int32) // length) * 65536
    padded = jnp.concatenate([jnp.full((BEFORE,), -1, jnp.int32), keys, jnp.full((block + AFTER,), -2, jnp.int32)])
    near = lax.dynamic_slice_in_dim(padded, row_start, BEFORE + block + AFTER)
    window, ids_s = near, near
    ids = jnp.broadcast_to(window.astype(F32)[:, None], (window.shape[0], LANES))

    channel_start = lax.axis_index("ch") * width
    pos_table = position_table(FIR, (filt_w1.shape[0] - 1) // 2)
    pre_one = jnp.dot(pos_table, filt_w1, precision=HIGHEST) + filt_b1
    hidden_one = jnp.sin(pre_one)
    pre_two = jnp.dot(hidden_one, filt_w2, precision=HIGHEST)
    hidden_two = jnp.sin(pre_two)
    channel = channel_start.astype(F32) + jnp.arange(width, dtype=F32)
    window_of = lambda channels: jnp.exp(
        -(0.5 + 3.0 * channels / full)[None, :] * jnp.arange(FIR, dtype=F32)[:, None] / FIR)
    taps = jnp.dot(hidden_two, filt_w3, precision=HIGHEST) * window_of(channel)
    norm_tail = jnp.sqrt(-jnp.expm1(-2.0 * tail_rate))
    def rows_in(count, parts):
        index = jnp.arange(count)[:, None]
        rows = jnp.zeros((count, width), F32)
        for k, part in enumerate(parts):
            rows = jnp.where(index == k, part[None, :], rows)
        return rows

    gains = jnp.concatenate([rows_in(8, [norm1_gain, norm2_gain]), filt_w3])
    zeros = jnp.zeros((width,), F32)
    head = rows_in(HEAD, [zeros, zeros, long_bias, tail_gain, tail_rate, norm_tail] + [
        short_weight[j, s] for j in range(3) for s in range(3)])

    tok, g, win, wout, wup, wdn, gains, vec = exchange(
        n, tokens, grad_out, jnp.transpose(in_weight, (1, 0, 2)), out_weight, up_weight, down_weight, gains, head, taps)

    n1, proj, x0, u, base, car, end, heads = mixer(ids_s, tok, win, gains, vec, ids)
    marks = jnp.concatenate([keys[::block], keys[block - 1 :: block]])
    enter = push(n, block, marks, end, vec)

    summed = n == 16
    results = backward(n, summed, marks, tok, ids, enter, g, gains[:8], vec, wout, x0, base, car, u, n1, heads, wup, wdn, win, proj)
    if not summed:
        results = reduce_plain(n, *results[:5])
    part_a, part_b, small_a, small_b, out, gtok = results

    def natural(paired):
        count = paired.shape[0]
        return jnp.transpose(paired.reshape(count, -1, 2, LANES), (0, 2, 1, 3)).reshape(count, full)

    small_a, gain_two = natural(small_a), small_a[FIR]
    small_b, gain_one = natural(small_b), small_b[10]
    taps_grad, bias_grad, long_car = small_a[:FIR], small_a[FIR + 1], small_a[FIR + 2]
    short_grad, carried_q = small_b[:9].reshape(3, 3, full), small_b[9]
    vec = natural(vec[:HEAD])
    gain, rate, nu = vec[3], vec[4], vec[5]
    factor = jnp.exp(-rate)
    rate_grad = gain * long_car * factor * factor / nu - carried_q
    raw_grad = taps_grad * window_of(jnp.arange(full, dtype=F32))
    w3_grad = jnp.dot(hidden_two.T, raw_grad, precision=HIGHEST)
    pre_two_grad = jnp.dot(raw_grad, gains[8:].T, precision=HIGHEST) * jnp.cos(pre_two)
    w2_grad = jnp.dot(hidden_one.T, pre_two_grad, precision=HIGHEST)
    pre_one_grad = jnp.dot(pre_two_grad, filt_w2.T, precision=HIGHEST) * jnp.cos(pre_one)
    w1_grad = jnp.dot(pos_table.T, pre_one_grad, precision=HIGHEST)
    hidden = up_weight.shape[1]
    rows_out = part_a.shape[0]
    mixer_grads = jnp.stack([part[:, hidden:].reshape(rows_out, -1, 2, LANES) for part in (part_a, part_b)], axis=2)
    mixer_grads = mixer_grads.reshape(rows_out, -1, 4, LANES)
    mixer_grads = jnp.transpose(mixer_grads, (0, 2, 1, 3)).reshape(rows_out, 4, width)
    return (
        out,
        gtok,
        gain_one,
        mixer_grads[:, :3],
        short_grad,
        w1_grad,
        jnp.sum(pre_one_grad, axis=0),
        w2_grad,
        w3_grad,
        bias_grad,
        nu * long_car,
        rate_grad,
        mixer_grads[:, 3].T,
        gain_two,
        part_a[:, :hidden],
        part_b[:, :hidden].T,
    )


def solution(mesh):
    placed = (
        P("seq", "ch"),
        P(),
        P("ch"),
        P(None, None, "ch"),
        P(None, None, "ch"),
        P(),
        P(),
        P(),
        P(None, "ch"),
        P("ch"),
        P("ch"),
        P("ch"),
        P("ch", None),
        P("ch"),
        P(None, "ch"),
        P("ch", None),
        P("seq", "ch"),
    )
    return jax.shard_map(
        on_device,
        mesh=mesh,
        in_specs=placed,
        out_specs=(
            P("seq", "ch"),
            P("seq", "ch"),
            P(),
            P("seq", None, "ch"),
            P(),
            P(),
            P(),
            P(),
            P(),
            P(),
            P(),
            P(),
            P("ch", "seq"),
            P(),
            P("seq", "ch"),
            P("ch", "seq"),
        ),
        check_vma=False,
    )
```

```python
import functools

import jax
import jax.numpy as jnp
from jax import lax
from jax.experimental import pallas as pl
from jax.experimental.pallas import tpu as pltpu
from jax.sharding import PartitionSpec as P

FIR = 32
SEQ_LEN = 16384
DOC_MOST = 8192
EPSILON = 1e-05
FREQUENCY = 0.4
HIGHEST = lax.Precision.HIGHEST
MESH = pl.DeviceIdType.MESH
F32, BF16 = jnp.float32, jnp.bfloat16

BEFORE = 48
AFTER = 80
LANES = 128
BLOCK = 256
CHUNK = 64
SUMS = 48
HEAD = 16
VMEM_LIMIT = 56 << 20
ROOT_TWO_OVER_PI = 0.7978845608028654


def position_table(filter_len, band_count):
    places = jnp.arange(filter_len, dtype=F32)
    harmonics = jnp.arange(1, band_count + 1, dtype=F32)
    angles = FREQUENCY * places[:, None] * harmonics[None, :]
    return jnp.concatenate([places[:, None] / filter_len, jnp.cos(angles), jnp.sin(angles)], axis=1)


def of(ref, start, size):
    return pl.ds(pl.multiple_of(start, size), size)


def device_of(index):
    return (index // 2, index % 2)


class Pushing:
    def __init__(self, n, reach, backward, source, slots, send_sem, recv_sem):
        self.total, self.reach = 2 * n, reach
        self.me = 2 * lax.axis_index("seq") + lax.axis_index("ch")
        self.ahead = -1 if backward else 1
        self.place = self.total - 1 - self.me if backward else self.me
        self.source, self.slots, self.send_sem, self.recv_sem = source, slots, send_sem, recv_sem

    def greet(self, barrier):
        for k in range(self.reach):

            @pl.when(self.place - 1 - k >= 0)
            def _():
                pl.semaphore_signal(
                    barrier, inc=1, device_id=device_of(self.me - self.ahead * (1 + k)), device_id_type=MESH)

    def await_greetings(self, barrier, others):
        following = self.total - 1 - self.place
        for count in range(0, self.reach + 1):
            if count + others:

                @pl.when((following >= count) if count == self.reach else (following == count))
                def _():
                    pl.semaphore_wait(barrier, count + others)

    def copy(self, k):
        return pltpu.make_async_remote_copy(
            src_ref=self.source, dst_ref=self.slots.at[k], send_sem=self.send_sem.at[k], recv_sem=self.recv_sem.at[k],
            device_id=device_of(self.me + self.ahead * (1 + k)), device_id_type=MESH)

    def start(self):
        for k in range(self.reach):

            @pl.when(self.place + 1 + k < self.total)
            def _():
                self.copy(k).start()

    def take(self, use):
        for k in range(self.reach):

            @pl.when(self.place - 1 - k >= 0)
            def _():
                self.copy(k).wait_recv()
                use(k, self.slots[k])

            @pl.when(self.place + 1 + k < self.total)
            def _():
                self.copy(k).wait_send()


def row_stats(values):
    center = jnp.mean(values, axis=1, keepdims=True)
    shifted = values - center
    inverse = lax.rsqrt(jnp.mean(shifted * shifted, axis=1, keepdims=True) + EPSILON)
    return shifted * inverse, inverse


def forward_kernel(n, rows, reach, marks, tokens, gout, w_in, w_out, w_up, w_down, gains, head, taps, ids,
                   tok_o, g_o, in_o, out_o, up_o, down_o, gains_o, vec_o,
                   n1_o, proj_o, x0_o, u_o, heads_o, long_o, car_o, dist_o, rest_o, enter_o,
                   tok_v, g_v, in_v, out_v, gains_v, vec_v, n1_s, proj_s, u_s, state_s, end_s, slots_s,
                   local_sem, store_sem, send_sem, recv_sem, push_send, push_recv):
    block, full = rows // 2, in_v.shape[1]
    width = full // 2
    steps = full // BLOCK
    two = range(BLOCK // LANES)
    step = pl.program_id(0)
    s, c = lax.axis_index("seq"), lax.axis_index("ch")
    barrier = pltpu.get_barrier_semaphore()
    pushing = Pushing(n, reach, False, end_s, slots_s, push_send, push_recv)
    partner = (s, 1 - c)
    cols = pl.ds(pl.multiple_of(c * width, width), width)
    early = [(gains, gains_v.at[:, cols])]
    late = []
    for i in range(width // LANES):
        source = pl.ds(i * LANES, LANES)
        paired = pl.ds(pl.multiple_of((2 * i + c) * LANES, LANES), LANES)
        early += [
            (head.at[:, source], vec_v.at[pl.ds(0, HEAD), paired]),
            (taps.at[:, source], vec_v.at[pl.ds(HEAD, FIR), paired]),
            (w_in.at[:, :, source], in_v.at[:, :, paired]),
        ]
        late.append((w_out.at[source, :], out_v.at[paired, :]))

    def remote(src, dst, k, target=partner):
        return pltpu.make_async_remote_copy(
            src_ref=src, dst_ref=dst, send_sem=send_sem.at[k], recv_sem=recv_sem.at[k],
            device_id=target, device_id_type=MESH)

    halves = [(early[k], k) for k in range(len(early))] + [(late[k], len(early) + k) for k in range(len(late))]
    count = len(halves)
    far = [remote(w_up, up_o, count), remote(w_down, down_o, count + 1)]
    at_tokens = count + 2

    left, right = pl.ds(0, width), pl.ds(width, width)
    first, second = pl.ds(0, block), pl.ds(block, block)
    ahead, tail = pl.ds(block - BEFORE, block + BEFORE), pl.ds(rows - BEFORE, BEFORE)
    main = pl.ds(BEFORE, block)
    keeps = [
        [(tokens.at[first, :], tok_v.at[main, left]), (gout.at[first, :], g_v.at[:, left])],
        [(tokens.at[ahead, :], tok_v.at[:, right]), (gout.at[second, :], g_v.at[:, right])],
    ]
    sends = [
        [(tokens.at[ahead, :], tok_v.at[:, left]), (gout.at[second, :], g_v.at[:, left])],
        [(tokens.at[first, :], tok_v.at[main, right]), (gout.at[first, :], g_v.at[:, right])],
    ]

    def edge(which, target):
        return remote(
            tokens.at[tail, :], tok_v.at[pl.ds(0, BEFORE), (left, right)[which]], at_tokens + 2 + which, target)

    def for_core(action):
        for which in range(2):

            @pl.when(c == which)
            def _():
                action(which)

    stores = [(tok_v, tok_o), (gains_v, gains_o), (vec_v, vec_o), (in_v, in_o), (g_v, g_o), (out_v, out_o)]

    def store(k):
        return pltpu.make_async_copy(*stores[k], store_sem.at[k])

    @pl.when(step == 0)
    def _():
        pushing.greet(barrier)
        pl.semaphore_signal(barrier, inc=1, device_id=partner, device_id_type=MESH)

        @pl.when((c == 0) & (s > 0))
        def _():
            for k in range(2):
                pl.semaphore_signal(barrier, inc=1, device_id=(s - 1, k), device_id_type=MESH)

        def begin_own(which):
            for k, (src, dst) in enumerate(keeps[which]):
                pltpu.make_async_copy(src, dst, local_sem.at[at_tokens + k]).start()

        for_core(begin_own)
        for (src, dst), k in halves:
            pltpu.make_async_copy(src, dst, local_sem.at[k]).start()

        @pl.when(s < n - 1)
        def _():
            pushing.await_greetings(barrier, 2)

        @pl.when(s == n - 1)
        def _():
            pushing.await_greetings(barrier, 1)

        def begin(which):
            remote(*sends[which][0], at_tokens).start()

            @pl.when(s < n - 1)
            def _():
                edge(which, (s + 1, 0)).start()

        for_core(begin)
        for (src, dst), k in halves[: len(early)]:
            remote(src, dst, k).start()
        for_core(lambda which: remote(*sends[which][1], at_tokens + 1).start())
        for (src, dst), k in halves[len(early) :]:
            remote(src, dst, k).start()
        for copy in far:
            copy.start()

        def distances(j, _):
            at = pl.ds(pl.multiple_of(j * 32, 32), 32)
            start = pl.multiple_of(BEFORE + j * 32, 16)
            own = ids[pl.ds(start, 32), :]
            before = after = jnp.zeros((32, LANES), F32)
            for k in range(1, FIR):
                before += jnp.where(own == ids[pl.ds(start - k, 32), :], 1.0, 0.0)
                after += jnp.where(own == ids[pl.ds(start + k, 32), :], 1.0, 0.0)
            dist_o[at, :] = before
            rest_o[at, :] = after
            return 0

        lax.fori_loop(0, block // 32, distances, 0)

        def take_tokens(which):
            remote(*sends[which][0], at_tokens).wait_send()
            remote(*sends[1 - which][0], at_tokens).wait_recv()
            pltpu.make_async_copy(*keeps[which][0], local_sem.at[at_tokens]).wait()

            @pl.when(s < n - 1)
            def _():
                edge(which, (s + 1, 0)).wait_send()

            if which == 0:

                @pl.when(s > 0)
                def _():
                    for k in range(2):
                        edge(k, partner).wait_recv()

        for_core(take_tokens)
        for (src, dst), k in halves[:1]:
            pltpu.make_async_copy(src, dst, local_sem.at[k]).wait()
            remote(src, dst, k).wait()
        store(0).start()
        store(1).start()

        def normed(j, _):
            at = pl.ds(pl.multiple_of(j * 80, 16), 80)
            values = jnp.where(ids[at, 0:1] >= 0.0, tok_v[at, :].astype(F32), 0.0)
            n1_s[at, :] = (row_stats(values)[0] * gains_v[0:1, :]).astype(BF16)
            return 0

        lax.fori_loop(0, (BEFORE + block) // 80, normed, 0)
        n1_o[...] = n1_s[pl.ds(BEFORE, block), :]
        for (src, dst), k in halves[1 : len(early)]:
            pltpu.make_async_copy(src, dst, local_sem.at[k]).wait()
            remote(src, dst, k).wait()
        store(2).start()
        store(3).start()

    @pl.when(step < steps)
    def _():
        lanes = [pl.ds(pl.multiple_of((2 * step + b) * LANES, LANES), LANES) for b in two]
        wide = pl.ds(pl.multiple_of(step * BLOCK, BLOCK), BLOCK)
        for t in range(3):
            part = jnp.dot(n1_s[...], in_v[t, :, wide], preferred_element_type=F32).astype(BF16)
            for b in two:
                proj_o[t, b] = part[:, b * LANES : (b + 1) * LANES]
                proj_s[t, b] = part[:, b * LANES : (b + 1) * LANES].astype(F32)

        def convolved(start, size):
            own = ids[pl.ds(start, size), :]
            same = [None] + [own == ids[pl.ds(start - j, size), :] for j in (1, 2)]
            results = []
            for b in two:
                streams = []
                for t in range(3):
                    value = vec_v[6 + t : 7 + t, lanes[b]] * proj_s[t, b, pl.ds(start, size), :]
                    for j in (1, 2):
                        tap = vec_v[6 + 3 * j + t : 7 + 3 * j + t, lanes[b]]
                        value += jnp.where(same[j], tap * proj_s[t, b, pl.ds(start - j, size), :], 0.0)
                    streams.append(value)
                gated = (streams[0] * streams[2]).astype(BF16).astype(F32)
                u_s[2 * step + b, pl.ds(start, size), :] = gated
                u_o[b, pl.ds(start, size), :] = gated
                results.append(streams)
            return results

        convolved(16, 32)
        for b, streams in enumerate(convolved(BEFORE, 8)):
            heads_o[0:8, b * LANES : (b + 1) * LANES] = streams[2]
            heads_o[8:16, b * LANES : (b + 1) * LANES] = streams[0]
            u_o[b, 0:16, :] = jnp.zeros((16, LANES), F32)
            u_s[2 * step + b, 0:16, :] = jnp.zeros((16, LANES), F32)

        def conv_chunk(j, _):
            start = pl.multiple_of(BEFORE + j * 32, 16)
            for b, streams in enumerate(convolved(start, 32)):
                x0_o[b, pl.ds(pl.multiple_of(j * 32, 32), 32), :] = streams[1]
            return 0

        lax.fori_loop(0, block // 32, conv_chunk, 0)

        row_id = lax.broadcasted_iota(jnp.int32, (8, LANES), 0)
        rates = [vec_v[4:5, lanes[b]] for b in two]
        powers = [jnp.exp(-rate * (row_id + 1).astype(F32)) for rate in rates]
        lams = [[jnp.exp(-rate * float(k)) for k in (1, 2, 4)] for rate in rates]
        for b in two:
            state_s[2 * step + b, 0:8, :] = jnp.zeros((8, LANES), F32)

        def scan_group(g, carry):
            start = pl.multiple_of(BEFORE + g * 8, 8)
            own = ids[pl.ds(start, 8), :]
            masks = [(own == ids[pl.ds(start - k, 8), :]) & (row_id >= k) for k in (1, 2, 4)]
            joined = own == jnp.broadcast_to(ids[pl.ds(start - 1, 1), :], (8, LANES))
            result = []
            for b in two:
                value = u_s[2 * step + b, pl.ds(start, 8), :]
                for mask, lam, k in zip(masks, lams[b], (1, 2, 4)):
                    value += jnp.where(mask, lam * pltpu.roll(value, k, 0), 0.0)
                value += jnp.where(joined, powers[b] * carry[b], 0.0)
                state_s[2 * step + b, pl.ds(pl.multiple_of(8 + g * 8, 8), 8), :] = value
                result.append(jnp.broadcast_to(value[7:8, :], (8, LANES)))
            return tuple(result)

        zero = jnp.zeros((8, LANES), F32)
        final = lax.fori_loop(0, block // 8, scan_group, (zero,) * len(two), unroll=4)
        for b in two:
            end_s[:, lanes[b]] = final[b][0:1, :]

    @pl.when(step == steps - 1)
    def _():
        pushing.start()

    @pl.when(step >= steps)
    def _():
        i = step - steps
        lanes = [pl.ds(pl.multiple_of((2 * i + b) * LANES, LANES), LANES) for b in two]
        lam = [jnp.exp(-vec_v[4:5, lanes[b]]) for b in two]
        tails = [vec_v[3:4, lanes[b]] * vec_v[5:6, lanes[b]] for b in two]

        def long_chunk(j, _):
            at = pl.ds(pl.multiple_of(j * 32, 32), 32)
            start = pl.multiple_of(BEFORE + j * 32, 16)
            near = dist_o[at, :]
            totals = []
            for b in two:
                previous = state_s[2 * i + b, pl.ds(7 + j * 32, 32), :]
                carried = jnp.where(near >= 1.0, lam[b] * previous, 0.0)
                car_o[b, at, :] = carried
                here = u_s[2 * i + b, pl.ds(start, 32), :]
                totals.append((vec_v[2:3, lanes[b]] + vec_v[16:17, lanes[b]]) * here + tails[b] * carried)
            for k in range(1, FIR):
                same = near >= float(k)
                for b in two:
                    term = vec_v[16 + k : 17 + k, lanes[b]] * u_s[2 * i + b, pl.ds(start - k, 32), :]
                    totals[b] += jnp.where(same, term, 0.0)
            for b in two:
                long_o[b, at, :] = totals[b]
            return 0

        lax.fori_loop(0, block // 32, long_chunk, 0)

    @pl.when(step == steps)
    def _():
        def take_rows(which):
            remote(*sends[which][1], at_tokens + 1).wait_send()
            remote(*sends[1 - which][1], at_tokens + 1).wait_recv()
            pltpu.make_async_copy(*keeps[which][1], local_sem.at[at_tokens + 1]).wait()

        for_core(take_rows)
        for (src, dst), k in halves[len(early) :]:
            pltpu.make_async_copy(src, dst, local_sem.at[k]).wait()
            remote(src, dst, k).wait()
        store(4).start()
        store(5).start()

    @pl.when(step == 2 * steps - 1)
    def _():
        enter_o[...] = jnp.zeros_like(enter_o)
        rate = vec_v[4:5, :]
        last = marks[2 * n + jnp.maximum(pushing.me - 1, 0)]

        def use(k, state):
            same = jnp.where(marks[2 * n + pushing.me - 1 - k] == last, 1.0, 0.0)
            enter_o[...] += same * jnp.exp(-rate * float(block * k)) * state

        pushing.take(use)
        for copy in far:
            copy.wait()
        for k in range(len(stores)):
            store(k).wait()


def forward(n, marks, tokens, gout, w_in, w_out, w_up, w_down, gains, head, taps, ids):
    rows, width = tokens.shape
    hidden = w_up.shape[1]
    full, block = 2 * width, rows // 2
    window = BEFORE + block
    steps, lane_blocks = full // BLOCK, full // LANES
    reach = min(DOC_MOST // block, 2 * n - 1)
    anywhere = pl.BlockSpec(memory_space=pl.ANY)
    whole = lambda *shape: pl.BlockSpec(shape, lambda i: (0,) * len(shape), pipeline_mode=pl.Buffered(1))
    soon, later = lambda i: jnp.minimum(i, steps - 1), lambda i: jnp.maximum(i - steps, 0)
    stacked = lambda count, place: pl.BlockSpec((BLOCK // LANES, count, LANES), lambda i: (place(i), 0, 0))
    shape = jax.ShapeDtypeStruct
    vmem = pltpu.VMEM
    far = 1 + 4 * (width // LANES) + 2 + 4
    dma = pltpu.SemaphoreType.DMA
    landing = [
        ((window, full), BF16), ((block, full), BF16), ((3, full, full), BF16), ((full, full), BF16),
        ((gains.shape[0], full), F32), ((HEAD + FIR, full), F32),
    ]
    return pl.pallas_call(
        functools.partial(forward_kernel, n, rows, reach),
        name="forward",
        grid=(2 * steps,),
        out_shape=(
            *[shape(*part) for part in landing[:4]],
            shape((full, hidden), BF16),
            shape((hidden, full), BF16),
            *[shape(*part) for part in landing[4:]],
            shape((block, full), BF16),
            shape((3, lane_blocks, window, LANES), BF16),
            shape((lane_blocks, block, LANES), F32),
            shape((lane_blocks, window, LANES), F32),
            shape((16, full), F32),
            shape((lane_blocks, block, LANES), F32),
            shape((lane_blocks, block, LANES), F32),
            shape((block, LANES), F32),
            shape((block, LANES), F32),
            shape((1, full), F32),
        ),
        in_specs=[pl.BlockSpec(memory_space=pltpu.SMEM)] + [anywhere] * 9 + [whole(*ids.shape)],
        out_specs=(
            *[anywhere] * 8,
            whole(block, full),
            pl.BlockSpec((3, BLOCK // LANES, window, LANES), lambda i: (0, soon(i), 0, 0)),
            stacked(block, soon),
            stacked(window, soon),
            pl.BlockSpec((16, BLOCK), lambda i: (0, soon(i))),
            stacked(block, later),
            stacked(block, later),
            whole(block, LANES),
            whole(block, LANES),
            whole(1, full),
        ),
        scratch_shapes=[
            *[vmem(*part) for part in landing],
            vmem((window, full), BF16),
            vmem((3, BLOCK // LANES, window, LANES), F32),
            vmem((lane_blocks, window, LANES), F32),
            vmem((lane_blocks, 8 + block, LANES), F32),
            vmem((1, full), F32),
            vmem((reach, 1, full), F32),
            dma((far,)), dma((6,)), dma((far,)), dma((far,)), dma((reach,)), dma((reach,)),
        ],
        compiler_params=pltpu.CompilerParams(collective_id=0, has_side_effects=True, vmem_limit_bytes=VMEM_LIMIT),
    )(marks, tokens, gout, w_in, w_out, w_up, w_down, gains, head, taps, ids)


TILE = 512
PART = TILE // 2
STAGES = 5


class Summing:
    def __init__(self, slots, rows, staged, first, second, third, fourth, fifth, send_sem, recv_sem):
        self.slots, self.rows, self.staged = slots, rows, staged
        self.first, self.second, self.third, self.fourth, self.fifth = first, second, third, fourth, fifth
        self.send_sem, self.recv_sem = send_sem, recv_sem
        self.s, self.c = lax.axis_index("seq"), lax.axis_index("ch")
        self.bits = [(self.s // (1 << b)) % 2 for b in range(4)]
        self.peers = [(self.s + (1 - 2 * bit) * (1 << b), self.c) for b, bit in enumerate(self.bits)]
        self.partner = (self.s, 1 - self.c)
        self.order = ((0, 1, 2, 3), (1, 0, 2, 3))

    @staticmethod
    def scratch(tiles, slots, rows):
        return [
            pltpu.VMEM((2, 2, 2, 2, 2, 2, rows, TILE), BF16),
            pltpu.VMEM((slots, 2, 2, 2, 2, rows, TILE), BF16),
            pltpu.VMEM((slots, 2, 2, 2, 2, rows, PART), BF16),
            pltpu.VMEM((slots, 2, 2, 2, rows, PART), BF16),
            pltpu.VMEM((slots, 2, 2, rows, PART), BF16),
            pltpu.VMEM((slots, 2, rows, PART), BF16),
            pltpu.SemaphoreType.DMA((tiles, 1 + 2 * 4)),
            pltpu.SemaphoreType.DMA((tiles, 1 + 2 * 4)),
        ]

    def greet(self, barrier):
        for peer in [self.partner] + self.peers:
            pl.semaphore_signal(barrier, inc=1, device_id=peer, device_id_type=MESH)

    def remote(self, src, dst, tile, k, target):
        return pltpu.make_async_remote_copy(
            src_ref=src, dst_ref=dst, send_sem=self.send_sem.at[tile, k], recv_sem=self.recv_sem.at[tile, k],
            device_id=target, device_id_type=MESH)

    def copies(self, tile, stage):
        slot = tile % self.slots
        if stage == 0:
            return [self.remote(self.staged.at[tile % 2, 1], self.first.at[slot], tile, 0, self.partner)]
        result = []
        for part in range(2):
            bit = self.order[part][stage - 1]
            away = 1 - self.bits[bit]
            at = pl.ds(part * PART, PART)
            if stage == 1:
                src = self.first.at[slot, :, :, :, away, :, at] if part == 0 else self.first.at[slot, :, :, away, :, :, at]
                dst = self.second.at[slot, part]
            elif stage == 2:
                src, dst = self.second.at[slot, part, :, :, away], self.third.at[slot, part]
            elif stage == 3:
                src, dst = self.third.at[slot, part, :, away], self.fourth.at[slot, part]
            else:
                src, dst = self.fourth.at[slot, part, away], self.fifth.at[slot, part]
            result.append(self.remote(src, dst, tile, 1 + 2 * (stage - 1) + part, self.peers[bit]))
        return result

    def start(self, tile, stage):
        for copy in self.copies(tile, stage):
            copy.start()

    def advance(self, tile, stage, total):
        for copy in self.copies(tile, stage):
            copy.wait()
        x, y, low, high = self.bits
        slot = tile % self.slots
        if stage == 0:
            def add(i, _):
                for h in range(2):
                    for j in range(2):
                        for k in range(2):
                            self.first[slot, h, i, j, k] += self.staged[tile % 2, 0, h, i, j, k]
                return 0
            lax.fori_loop(0, 2, add, 0)
        elif stage == 1:
            def add(i, _):
                for h in range(2):
                    for k in range(2):
                        self.second[slot, 0, h, i, k] += self.first[slot, h, i, k, x, :, 0:PART]
                        self.second[slot, 1, h, i, k] += self.first[slot, h, i, y, k, :, PART:TILE]
                return 0
            lax.fori_loop(0, 2, add, 0)
        elif stage == 2:
            for i in range(2):
                for k in range(2):
                    self.third[slot, 0, i, k] += self.second[slot, 0, i, k, y]
                    self.third[slot, 1, i, k] += self.second[slot, 1, i, k, x]
        elif stage == 3:
            for part in range(2):
                for i in range(2):
                    self.fourth[slot, part, i] += self.third[slot, part, i, low]
        else:
            for part in range(2):
                mine = self.fourth[slot, part, high].astype(F32)
                total(tile, part, mine + self.fifth[slot, part].astype(F32))
            return
        self.start(tile, stage + 1)


class Joining:
    def __init__(self, sums, held, arrived, send_sem, recv_sem):
        self.held, self.arrived, self.send_sem, self.recv_sem = held, arrived, send_sem, recv_sem
        self.targets = [sums.partner] + sums.peers

    @staticmethod
    def scratch(*shape):
        return [pltpu.VMEM((STAGES,) + shape, F32), pltpu.VMEM((STAGES,) + shape, F32),
                pltpu.SemaphoreType.DMA((STAGES,)), pltpu.SemaphoreType.DMA((STAGES,))]

    def copy(self, stage):
        return pltpu.make_async_remote_copy(
            src_ref=self.held.at[stage], dst_ref=self.arrived.at[stage], send_sem=self.send_sem.at[stage],
            recv_sem=self.recv_sem.at[stage], device_id=self.targets[stage], device_id_type=MESH)

    def start(self, stage):
        self.copy(stage).start()

    def advance(self, stage, result):
        self.copy(stage).wait()
        total = self.held[stage] + self.arrived[stage]
        if stage == STAGES - 1:
            result[...] = total
        else:
            self.held[stage + 1] = total
            self.start(stage + 1)


def contract(left, right, dims):
    return lax.dot_general(left, right, (dims, ((), ())), preferred_element_type=F32)


def contract(left, right, dims):
    return lax.dot_general(left, right, (dims, ((), ())), preferred_element_type=F32)


TILES = 6
EPILOGUE, GATE, TAPS, BACK = TILES, TILES + 1, TILES + 2, TILES + 3
LAGS = (1, 3, 5, 6, 7)
HALO = 80


def backward_kernel(n, block, reach, summed, marks, tok, ids, dist_s, rest_s, enter, g, gains, vec, wout, x0, base, car, u, n1, heads,
                    wup_a, wup_b, wdn_a, wdn_b, win, proj, *refs):
    full = g.shape[1]
    width, lane_blocks = full // 2, full // LANES
    steps = full // BLOCK
    last_back = BACK + steps - 1
    outs, refs = refs[:6], refs[6:]
    if summed:
        part_a, part_b, small_a, small_b, out_full, gtok_full = outs
    else:
        grads_o, small_a, small_b, out_o, gtok_o, _ = outs
    (mixed_s, middle_s, n2_s, gn_s, gout_s, out_s, gmid_s, long_s, car_s, glong_s, q_s, gc_s, gp_s, proj_s,
     taps_s, first_s, slots_s, joined_s, halo_s, halo_r, head_s,
     push_send, push_recv, halo_sem, *buffers) = refs
    step = pl.program_id(0)
    groups = block // 32
    barrier = pltpu.get_barrier_semaphore()
    pushing = Pushing(n, reach, True, first_s, slots_s, push_send, push_recv)
    c = lax.axis_index("ch")
    lanes_of = lambda b: pl.ds(pl.multiple_of(b * LANES, LANES), LANES)
    if summed:
        sums = Summing(TILES, full // 16, *buffers[:8])
        joins = [(Joining(sums, *buffers[8:12]), small_a, TAPS), (Joining(sums, *buffers[12:16]), small_b, last_back)]
        local_sem, exchange_send, exchange_recv = buffers[16:]

        def shares(k, src, dst):
            at = pl.ds(pl.multiple_of(c * block, block), block)
            of_core = lambda which: src.at[:, pl.ds(pl.multiple_of(which * width, width), width)]
            return (
                pltpu.make_async_copy(of_core(c), dst.at[at, :], local_sem.at[k]),
                pltpu.make_async_remote_copy(
                    src_ref=of_core(1 - c), dst_ref=dst.at[at, :], send_sem=exchange_send.at[k],
                    recv_sem=exchange_recv.at[k], device_id=sums.partner, device_id_type=MESH),
            )

    halo_copy = pltpu.make_async_remote_copy(
        src_ref=halo_s, dst_ref=halo_r, send_sem=halo_sem.at[0], recv_sem=halo_sem.at[1],
        device_id=device_of(pushing.me - 1), device_id_type=MESH)

    @pl.when(step == 0)
    def _():
        pushing.greet(barrier)
        if summed:
            sums.greet(barrier)

        last = ids[pl.ds(BEFORE - 1, 1), :]
        for b in range(lane_blocks):
            lanes = slice(b * LANES, (b + 1) * LANES)
            rate, tail = vec[4:5, lanes], vec[3:4, lanes] * vec[5:6, lanes]
            state = enter[0:1, lanes]

            def mix(j, _):
                at = pl.ds(pl.multiple_of(j * 32, 32), 32)
                passed = (lax.broadcasted_iota(jnp.int32, (32, LANES), 0) + (j * 32 + 1)).astype(F32)
                same = ids[pl.ds(pl.multiple_of(BEFORE + j * 32, 16), 32), :] == last
                entered = jnp.where(same, jnp.exp(-rate * passed) * state, 0.0)
                car_s[b, at, :] = car[b, at, :] + entered
                long = base[b, at, :] + tail * entered
                long_s[b, at, :] = long
                mixed_s[at, lanes] = (long * x0[b, at, :]).astype(BF16)
                return 0

            lax.fori_loop(0, groups, mix, 0)
        middle_s[...] = jnp.dot(mixed_s[...], wout[...], preferred_element_type=F32)

        def norm(j, _):
            at = pl.ds(pl.multiple_of(j * 32, 32), 32)
            start = pl.multiple_of(BEFORE + j * 32, 16)
            values = middle_s[at, :] + tok[pl.ds(start, 32), :].astype(F32)
            middle_s[at, :] = values
            out_s[at, :] = values
            n2_s[at, :] = (row_stats(values)[0] * gains[1:2, :]).astype(BF16)
            gn_s[at, :] = jnp.zeros_like(values)
            return 0

        lax.fori_loop(0, groups, norm, 0)
        pushing.await_greetings(barrier, 5 if summed else 0)

    if summed:

        def total(tile, part, value):
            (part_a, part_b)[part][:, pl.ds(pl.multiple_of(tile * PART, PART), PART)] = value

        for stage in range(STAGES - 1, -1, -1):
            since, early = step - 1 - stage, step - LAGS[stage]
            is_late = step // (BACK + 1 + stage)

            @pl.when(((early >= 0) & (early < TILES)) | ((since >= BACK) & (since <= last_back)))
            def _():
                sums.advance(early + (since - (BACK - TILES) - early) * is_late, stage, total)

            for join, result, begun in joins:

                @pl.when(since == begun)
                def _():
                    join.advance(stage, result)

    def put(tile, start, grad):
        size = grad[0].shape[1]
        at = pl.ds(start, size)
        for half in range(2):
            if summed:
                whose = (half + c) % 2
                for q in range(16):
                    sums.staged[tile % 2, whose, q // 8, q // 4 % 2, q // 2 % 2, q % 2, :, at] = (
                        grad[half][q * sums.rows : (q + 1) * sums.rows])
            else:
                grads_o[0, half, :, at] = grad[half]

    @pl.when(step < TILES)
    def _():
        for half, (wup, wdn) in enumerate(((wup_a, wdn_a), (wup_b, wdn_b))):
            n2, rows = n2_s[...], g[...]
            up = jnp.dot(n2, wup[...], preferred_element_type=F32)
            pulled = contract(rows, wdn[...], ((1,), (1,)))
            square = up * up
            inner = ROOT_TWO_OVER_PI * up * (1.0 + 0.044715 * square)
            bent = jnp.tanh(inner)
            part = 0.5 * (1.0 + bent)
            active = (up * part).astype(BF16)
            slope = part + (0.5 * ROOT_TWO_OVER_PI) * up * (1.0 - bent * bent) * (1.0 + 0.134145 * square)
            g_up = (pulled * slope).astype(BF16)
            out_s[...] += jnp.dot(active, wdn[...], preferred_element_type=F32)
            gn_s[...] += contract(g_up, wup[...], ((1,), (1,)))
            pair = (contract(n2, g_up, ((0,), (0,))).astype(BF16), contract(rows, active, ((0,), (0,))).astype(BF16))
            for k in range(2):
                at = pl.ds(k * PART, PART)
                if summed:
                    for q in range(16):
                        sums.staged[step % 2, half, q // 8, q // 4 % 2, q // 2 % 2, q % 2, :, at] = (
                            pair[k][q * sums.rows : (q + 1) * sums.rows])
                else:
                    grads_o[0, (half + c) % 2, :, at] = pair[k]
        if summed:
            sums.start(step, 0)

    @pl.when(step == EPILOGUE)
    def _():
        if summed:
            for copy in shares(0, out_s, out_full):
                copy.start()
        else:
            out_o[...] = out_s[...]

        def back(j, total):
            at = pl.ds(pl.multiple_of(j * 32, 32), 32)
            normal, inverse = row_stats(middle_s[at, :])
            grad = gn_s[at, :]
            total += jnp.sum(grad * normal, axis=0, keepdims=True)
            scaled = grad * gains[1:2, :]
            cross = jnp.mean(scaled * normal, axis=1, keepdims=True)
            result = g[at, :].astype(F32) + inverse * (
                scaled - jnp.mean(scaled, axis=1, keepdims=True) - normal * cross)
            gmid_s[at, :] = result
            gout_s[at, :] = result.astype(BF16)
            gn_s[at, :] = jnp.zeros_like(grad)
            return total

        gain_two = lax.fori_loop(0, groups, back, jnp.zeros((1, full), F32))
        head_s[...] = jnp.zeros_like(head_s)
        head_s[0:1, :] = gain_two
        for i in range(steps):
            gmix = contract(gout_s[...], wout[i * BLOCK : (i + 1) * BLOCK, :], ((1,), (1,)))
            for k in range(BLOCK // LANES):
                b = i * (BLOCK // LANES) + k
                part = gmix[:, k * LANES : (k + 1) * LANES]
                glong_s[b, 0:block, :] = part * x0[b]
                long_s[b] = part * long_s[b]

    row_id = lax.broadcasted_iota(jnp.int32, (8, LANES), 0)
    zero = jnp.zeros((8, LANES), F32)

    @pl.when(step == GATE)
    def _():
        rates = [vec[4:5, b * LANES : (b + 1) * LANES] for b in range(lane_blocks)]
        tails = [vec[3:4, b * LANES : (b + 1) * LANES] * vec[5:6, b * LANES : (b + 1) * LANES] for b in range(lane_blocks)]
        lams = [[jnp.exp(-rate * float(k)) for k in (1, 2, 4)] for rate in rates]
        powers = [jnp.exp(-rate * (8 - row_id).astype(F32)) for rate in rates]

        def scan_group(i, carry):
            at = block // 8 - 1 - i
            to = pl.ds(pl.multiple_of(at * 8, 8), 8)
            start = pl.multiple_of(BEFORE + at * 8, 8)
            own = ids[pl.ds(start, 8), :]
            masks = [(own == ids[pl.ds(start + k, 8), :]) & (row_id < 8 - k) for k in (1, 2, 4)]
            joined = own == jnp.broadcast_to(ids[pl.ds(start + 8, 1), :], (8, LANES))
            states, biases, carries = [], [], []
            for b in range(lane_blocks):
                grad = glong_s[b, to, :]
                value = grad * tails[b]
                for mask, lam, k in zip(masks, lams[b], (1, 2, 4)):
                    value += jnp.where(mask, lam * pltpu.roll(value, 8 - k, 0), 0.0)
                value += jnp.where(joined, powers[b] * carry[0][b], 0.0)
                q_s[b, to, :] = value
                states.append(jnp.broadcast_to(value[0:1, :], (8, LANES)))
                biases.append(carry[1][b] + grad * u[b, pl.ds(start, 8), :])
                carries.append(carry[2][b] + grad * car_s[b, to, :])
            return tuple(states), tuple(biases), tuple(carries)

        many = (zero,) * lane_blocks
        states, biases, carries = lax.fori_loop(0, block // 8, scan_group, (many, many, many), unroll=2)
        for b in range(lane_blocks):
            lanes = slice(b * LANES, (b + 1) * LANES)
            first_s[:, lanes] = states[b][0:1, :]
            head_s[1:2, lanes] = jnp.sum(biases[b], axis=0, keepdims=True)
            head_s[2:3, lanes] = jnp.sum(carries[b], axis=0, keepdims=True)
            halo_s[0:48, lanes] = glong_s[b, 0:48, :]
            halo_s[48:56, lanes] = q_s[b, 0:8, :]
            halo_s[72:80, lanes] = long_s[b, 0:8, :]
        halo_s[56:72, :] = heads[...]
        pushing.start()

        @pl.when(pushing.me > 0)
        def _():
            halo_copy.start()

    @pl.when(step == TAPS)
    def _():
        taps_s[...] = jnp.zeros_like(taps_s)

        def pairs(p, _):
            def chunk(j, _):
                at = pl.ds(pl.multiple_of(j * 32, 32), 32)
                start = BEFORE + j * 32
                near = dist_s[at, :]
                here = [glong_s[2 * p + k, at, :] for k in range(2)]
                for tap in range(FIR):
                    same = near >= float(tap)
                    for k in range(2):
                        term = jnp.where(same, here[k] * u[2 * p + k, pl.ds(start - tap, 32), :], 0.0)
                        taps_s[2 * p + k, tap] += jnp.sum(term.reshape(4, 8, LANES), axis=0)
                return 0

            lax.fori_loop(0, groups, chunk, 0)
            return 0

        lax.fori_loop(0, lane_blocks // 2, pairs, 0)
        result = joins[0][0].held.at[0] if summed else small_a
        for b in range(lane_blocks):
            lanes = slice(b * LANES, (b + 1) * LANES)
            result[0:FIR, lanes] = jnp.sum(taps_s[b], axis=1)
        result[FIR : FIR + 8, :] = head_s[...]
        if summed:
            joins[0][0].start(0)

    @pl.when(step == BACK)
    def _():
        joined_s[...] = jnp.zeros_like(joined_s)
        rate = vec[4:5, :]
        following = 2 * n + jnp.minimum(pushing.me + 1, 2 * n - 1)
        lasts = (marks[2 * n + pushing.me], marks[following])

        def use(k, state):
            first = marks[pushing.me + 1 + k]
            for row in range(2):
                if k >= row:
                    same = jnp.where(first == lasts[row], 1.0, 0.0)
                    joined_s[row : row + 1, :] += same * jnp.exp(-rate * float(block * (k - row) + 1)) * state

        pushing.take(use)

        @pl.when(pushing.me > 0)
        def _():
            halo_copy.wait_send()

        @pl.when(pushing.me < 2 * n - 1)
        def _():
            halo_copy.wait_recv()

        for b in range(lane_blocks):
            glong_s[b, block : block + 48, :] = halo_r[0:48, b * LANES : (b + 1) * LANES]

    @pl.when((step >= BACK) & (step <= last_back))
    def _():
        i = step - BACK
        two = range(2)
        lanes = [lanes_of(2 * i + k) for k in two]
        rates = [vec[4:5, lanes[k]] for k in two]
        scales = [vec[2:3, lanes[k]] - vec[3:4, lanes[k]] * vec[5:6, lanes[k]] for k in two]
        mine = [joined_s[0:1, lanes[k]] for k in two]
        for k in two:
            for s in range(3):
                proj_s[s, k] = proj[s, k].astype(F32)
        last = ids[pl.ds(BEFORE + block - 1, 1), :]

        def conv_at(s, k, start, size, same):
            value = vec[6 + s : 7 + s, lanes[k]] * proj_s[s, k, pl.ds(start, size), :]
            for j in (1, 2):
                tap = vec[6 + 3 * j + s : 7 + 3 * j + s, lanes[k]]
                value += jnp.where(same[j - 1], tap * proj_s[s, k, pl.ds(start - j, size), :], 0.0)
            return value

        def chunk(j, totals):
            at = pl.ds(pl.multiple_of(j * 32, 32), 32)
            start = pl.multiple_of(BEFORE + j * 32, 16)
            own = ids[pl.ds(start, 32), :]
            left = (block - 1 - j * 32 - lax.broadcasted_iota(jnp.int32, (32, LANES), 0)).astype(F32)
            after = rest_s[at, :]
            near = dist_s[at, :]
            grads, result = [], []
            for k in two:
                b = 2 * i + k
                state = q_s[b, at, :] + jnp.where(own == last, jnp.exp(-rates[k] * left) * mine[k], 0.0)
                result.append(totals[k] + jnp.sum((car_s[b, at, :] * state).reshape(4, 8, LANES), axis=0))
                grads.append(scales[k] * glong_s[b, at, :] + state)
            for tap in range(FIR):
                same = after >= float(tap)
                for k in two:
                    term = vec[16 + tap : 17 + tap, lanes[k]] * glong_s[2 * i + k, pl.ds(j * 32 + tap, 32), :]
                    grads[k] += jnp.where(same, term, 0.0)
            same = [near >= 1.0, near >= 2.0]
            for k in two:
                gc_s[0, k, at, :] = grads[k] * conv_at(2, k, start, 32, same)
                gc_s[1, k, at, :] = long_s[2 * i + k, at, :]
                gc_s[2, k, at, :] = grads[k] * conv_at(0, k, start, 32, same)
            return tuple(result)

        crossed = lax.fori_loop(0, groups, chunk, (zero, zero))

        start = BEFORE + block
        own = ids[pl.ds(start, 8), :]
        end_id = marks[2 * n + jnp.minimum(pushing.me + 1, 2 * n - 1)].astype(F32)
        left = (block - 1 - row_id).astype(F32)
        for k in two:
            b = 2 * i + k
            entered = jnp.exp(-rates[k] * left) * joined_s[1:2, lanes[k]]
            grad = halo_r[48:56, lanes[k]] + jnp.where(own == end_id, entered, 0.0)
            grad += scales[k] * glong_s[b, block : block + 8, :]
            for tap in range(FIR):
                term = vec[16 + tap : 17 + tap, lanes[k]] * glong_s[b, block + tap : block + tap + 8, :]
                grad += jnp.where(own == ids[pl.ds(start + tap, 8), :], term, 0.0)
            gc_s[0, k, block : block + 8, :] = grad * halo_r[56:64, lanes[k]]
            gc_s[1, k, block : block + 8, :] = halo_r[72:80, lanes[k]]
            gc_s[2, k, block : block + 8, :] = grad * halo_r[64:72, lanes[k]]

        small = joins[1][0].held.at[0] if summed else small_b
        for k in two:

            def short(j, totals):
                at = pl.ds(pl.multiple_of(j * 32, 32), 32)
                start = pl.multiple_of(BEFORE + j * 32, 16)
                same = [dist_s[at, :] >= float(d) for d in (1, 2)]
                later = [rest_s[at, :] >= float(d) for d in (1, 2)]
                result = []
                for s in range(3):
                    here = gc_s[s, k, at, :]
                    value = vec[6 + s : 7 + s, lanes[k]] * here
                    for d in (1, 2):
                        tap = vec[6 + 3 * d + s : 7 + 3 * d + s, lanes[k]]
                        value += jnp.where(later[d - 1], tap * gc_s[s, k, pl.ds(j * 32 + d, 32), :], 0.0)
                    gp_s[s, at, k * LANES : (k + 1) * LANES] = value.astype(BF16)
                    for d in range(3):
                        term = here * proj_s[s, k, pl.ds(start - d, 32), :]
                        if d:
                            term = jnp.where(same[d - 1], term, 0.0)
                        result.append(totals[3 * s + d] + jnp.sum(term.reshape(4, 8, LANES), axis=0))
                return tuple(result)

            totals = lax.fori_loop(0, groups, short, (zero,) * 9)
            rows = [None] * 9
            for s in range(3):
                for d in range(3):
                    rows[3 * d + s] = jnp.sum(totals[3 * s + d], axis=0, keepdims=True)
            rows.append(jnp.sum(crossed[k], axis=0, keepdims=True))
            for row, value in enumerate(rows):
                small[row : row + 1, lanes[k]] = value

        tile = TILES + i
        pieces = [contract(n1[...], gp_s[s], ((0,), (0,))).astype(BF16) for s in range(3)]
        at = pl.ds(pl.multiple_of(i * BLOCK, BLOCK), BLOCK)
        pieces.append(contract(gout_s[...], mixed_s[:, at], ((0,), (0,))).astype(BF16))
        for s, piece in enumerate(pieces):
            put(tile, s * LANES, [piece[:, half * LANES : (half + 1) * LANES] for half in range(2)])
        if summed:
            sums.start(tile, 0)
        for s in range(3):
            gn_s[...] += contract(gp_s[s], win[s], ((1,), (1,)))

    @pl.when(step == last_back)
    def _():
        def back(j, total):
            at = pl.ds(pl.multiple_of(j * 32, 32), 32)
            normal, inverse = row_stats(tok[pl.ds(pl.multiple_of(BEFORE + j * 32, 16), 32), :].astype(F32))
            grad = gn_s[at, :]
            total += jnp.sum(grad * normal, axis=0, keepdims=True)
            scaled = grad * gains[0:1, :]
            cross = jnp.mean(scaled * normal, axis=1, keepdims=True)
            middle_s[at, :] = gmid_s[at, :] + inverse * (
                scaled - jnp.mean(scaled, axis=1, keepdims=True) - normal * cross)
            return total

        gain_one = lax.fori_loop(0, groups, back, jnp.zeros((1, full), F32))
        small = joins[1][0].held.at[0] if summed else small_b
        small[10:11, :] = gain_one
        small[11:16, :] = jnp.zeros((5, full), F32)
        if summed:
            joins[1][0].start(0)
            for copy in shares(1, middle_s, gtok_full):
                copy.start()
        else:
            gtok_o[...] = middle_s[...]

    if summed:

        @pl.when(step == last_back + STAGES)
        def _():
            for k, (src, dst) in enumerate(((out_s, out_full), (middle_s, gtok_full))):
                for copy in shares(k, src, dst):
                    copy.wait()


def backward(n, summed, marks, tok, ids, dist, rest, enter, g, gains, vec, wout, x0, base, car, u, n1, heads, ups, downs,
             win, proj):
    block, full = g.shape
    rows, lane_blocks = BEFORE + block, full // LANES
    steps = full // BLOCK
    tiles = TILES + steps
    reach = min(DOC_MOST // block + 1, 2 * n - 1)
    whole = lambda *shape: pl.BlockSpec(shape, lambda i: (0,) * len(shape), pipeline_mode=pl.Buffered(1))
    tile = lambda i: jnp.minimum(i, TILES - 1)
    back = lambda i: jnp.clip(i - BACK, 0, steps - 1)
    wide = lambda dtype: pltpu.VMEM((block, full), dtype)
    stacked = lambda count, dtype=F32: pltpu.VMEM((lane_blocks, count, LANES), dtype)
    shape = jax.ShapeDtypeStruct
    if summed:
        out_shape = [shape((full // 16, tiles * PART), F32)] * 2 + [shape((FIR + 8, full), F32), shape((16, full), F32)]
        out_shape += [shape((2 * block, full // 2), F32)] * 2
        out_specs = [whole(full // 16, tiles * PART)] * 2 + [whole(FIR + 8, full), whole(16, full)]
        out_specs += [pl.BlockSpec(memory_space=pl.ANY)] * 2
        extra = Summing.scratch(tiles, TILES, full // 16) + Joining.scratch(FIR + 8, full) + Joining.scratch(16, full)
        extra += [pltpu.SemaphoreType.DMA((2,))] * 3
    else:
        out_shape = [shape((tiles, 2, full, TILE), BF16), shape((FIR + 8, full), F32), shape((16, full), F32)]
        out_shape += [shape((block, full), F32)] * 2 + [shape((8, LANES), F32)]
        place = lambda i: jnp.minimum(i, TILES - 1) + jnp.clip(i - BACK + 1, 0, steps)
        out_specs = [pl.BlockSpec((1, 2, full, TILE), lambda i: (place(i), 0, 0, 0)), whole(FIR + 8, full), whole(16, full)]
        out_specs += [whole(block, full)] * 2 + [whole(8, LANES)]
        extra = []
    return pl.pallas_call(
        functools.partial(backward_kernel, n, block, reach, summed),
        name="backward",
        grid=(BACK + steps + (STAGES if summed else 0),),
        out_shape=out_shape,
        in_specs=[
            pl.BlockSpec(memory_space=pltpu.SMEM),
            whole(*tok.shape), whole(*ids.shape), whole(*dist.shape), whole(*rest.shape), whole(*enter.shape), whole(*g.shape), whole(*gains.shape),
            whole(*vec.shape), whole(*wout.shape), whole(*x0.shape), whole(*base.shape), whole(*car.shape),
            whole(*u.shape), whole(*n1.shape), whole(*heads.shape),
            *[pl.BlockSpec((full, PART), lambda i: (0, tile(i)))] * 2,
            *[pl.BlockSpec((PART, full), lambda i: (tile(i), 0))] * 2,
            pl.BlockSpec((3, full, BLOCK), lambda i: (0, 0, back(i))),
            pl.BlockSpec((3, BLOCK // LANES, rows, LANES), lambda i: (0, back(i), 0, 0)),
        ],
        out_specs=out_specs,
        scratch_shapes=[
            wide(BF16), wide(F32), wide(BF16), wide(F32), wide(BF16), wide(F32), wide(F32),
            stacked(block), stacked(block), stacked(block + 48), stacked(block),
            pltpu.VMEM((3, BLOCK // LANES, block + 8, LANES), F32),
            pltpu.VMEM((3, block, BLOCK), BF16),
            pltpu.VMEM((3, BLOCK // LANES, rows, LANES), F32),
            pltpu.VMEM((lane_blocks, FIR, 8, LANES), F32),
            pltpu.VMEM((1, full), F32),
            pltpu.VMEM((reach, 1, full), F32),
            pltpu.VMEM((2, full), F32),
            pltpu.VMEM((HALO, full), F32),
            pltpu.VMEM((HALO, full), F32),
            pltpu.VMEM((8, full), F32),
            pltpu.SemaphoreType.DMA((reach,)),
            pltpu.SemaphoreType.DMA((reach,)),
            pltpu.SemaphoreType.DMA((2,)),
            *extra,
        ],
        compiler_params=pltpu.CompilerParams(collective_id=2, has_side_effects=True, vmem_limit_bytes=60 << 20),
    )(marks, tok, ids, dist, rest, enter, g, gains, vec, wout, x0, base, car, u, n1, heads, *ups, *downs, win, proj)


def reduce_plain(n, grads, small_a, small_b, out, gtok):
    both = lax.psum_scatter(grads.astype(F32), "ch", scatter_dimension=1, tiled=False)
    total = lax.psum_scatter(both, "seq", scatter_dimension=1, tiled=True)
    total = jnp.transpose(total, (1, 0, 2))
    parts = [total[:, :, k * PART : (k + 1) * PART].reshape(total.shape[0], -1) for k in range(2)]
    swap = lambda whole: lax.all_to_all(whole, "ch", split_axis=1, concat_axis=0, tiled=True)
    small_a, small_b = lax.psum((small_a, small_b), ("seq", "ch"))
    return *parts, small_a, small_b, swap(out), swap(gtok)


def on_device(tokens, seg_ids, norm1_gain, in_weight, short_weight, filt_w1, filt_b1, filt_w2, filt_w3,
              long_bias, tail_gain, tail_rate, out_weight, norm2_gain, up_weight, down_weight, grad_out):
    rows, width = tokens.shape
    full, block = 2 * width, rows // 2
    n = lax.axis_size("seq")
    devices = 2 * n
    me = 2 * lax.axis_index("seq") + lax.axis_index("ch")
    row_start = me * block
    total_rows = seg_ids.shape[0]
    length = min(SEQ_LEN, total_rows)

    keys = seg_ids + (jnp.arange(total_rows, dtype=jnp.int32) // length) * 65536
    padded = jnp.concatenate([jnp.full((BEFORE,), -1, jnp.int32), keys, jnp.full((block + AFTER,), -2, jnp.int32)])
    near = lax.dynamic_slice_in_dim(padded, row_start, BEFORE + block + AFTER)
    window = near
    ids = jnp.broadcast_to(window.astype(F32)[:, None], (window.shape[0], LANES))

    channel_start = lax.axis_index("ch") * width
    pos_table = position_table(FIR, (filt_w1.shape[0] - 1) // 2)
    pre_one = jnp.dot(pos_table, filt_w1, precision=HIGHEST) + filt_b1
    hidden_one = jnp.sin(pre_one)
    pre_two = jnp.dot(hidden_one, filt_w2, precision=HIGHEST)
    hidden_two = jnp.sin(pre_two)
    channel = channel_start.astype(F32) + jnp.arange(width, dtype=F32)
    window_of = lambda channels: jnp.exp(
        -(0.5 + 3.0 * channels / full)[None, :] * jnp.arange(FIR, dtype=F32)[:, None] / FIR)
    taps = jnp.dot(hidden_two, filt_w3, precision=HIGHEST) * window_of(channel)
    norm_tail = jnp.sqrt(-jnp.expm1(-2.0 * tail_rate))
    def rows_in(count, parts):
        index = jnp.arange(count)[:, None]
        rows = jnp.zeros((count, width), F32)
        for k, part in enumerate(parts):
            rows = jnp.where(index == k, part[None, :], rows)
        return rows

    gains = jnp.concatenate([rows_in(8, [norm1_gain, norm2_gain]), filt_w3])
    zeros = jnp.zeros((width,), F32)
    head = rows_in(HEAD, [zeros, zeros, long_bias, tail_gain, tail_rate, norm_tail] + [
        short_weight[j, s] for j in range(3) for s in range(3)])

    marks = jnp.concatenate([keys[::block], keys[block - 1 :: block]])
    (tok, g, win, wout, up_other, down_other, gains, vec, n1, proj, x0, u, heads, base, car, dist, rest, enter) = forward(
        n, marks, tokens, grad_out, jnp.transpose(in_weight, (1, 0, 2)), out_weight, up_weight, down_weight,
        gains, head, taps, ids)

    summed = n == 16
    results = backward(
        n, summed, marks, tok, ids, dist, rest, enter, g, gains[:8], vec, wout, x0, base, car, u, n1, heads,
        (up_weight, up_other), (down_weight, down_other), win, proj)
    if not summed:
        results = reduce_plain(n, *results[:5])
    part_a, part_b, small_a, small_b, out, gtok = results

    def natural(paired):
        count = paired.shape[0]
        return jnp.transpose(paired.reshape(count, -1, 2, LANES), (0, 2, 1, 3)).reshape(count, full)

    small_a, gain_two = natural(small_a), small_a[FIR]
    small_b, gain_one = natural(small_b), small_b[10]
    taps_grad, bias_grad, long_car = small_a[:FIR], small_a[FIR + 1], small_a[FIR + 2]
    short_grad, carried_q = small_b[:9].reshape(3, 3, full), small_b[9]
    vec = natural(vec[:HEAD])
    gain, rate, nu = vec[3], vec[4], vec[5]
    factor = jnp.exp(-rate)
    rate_grad = gain * long_car * factor * factor / nu - carried_q
    raw_grad = taps_grad * window_of(jnp.arange(full, dtype=F32))
    w3_grad = jnp.dot(hidden_two.T, raw_grad, precision=HIGHEST)
    pre_two_grad = jnp.dot(raw_grad, gains[8:].T, precision=HIGHEST) * jnp.cos(pre_two)
    w2_grad = jnp.dot(hidden_one.T, pre_two_grad, precision=HIGHEST)
    pre_one_grad = jnp.dot(pre_two_grad, filt_w2.T, precision=HIGHEST) * jnp.cos(pre_one)
    w1_grad = jnp.dot(pos_table.T, pre_one_grad, precision=HIGHEST)
    hidden = up_weight.shape[1]
    rows_out = part_a.shape[0]
    mixer_grads = jnp.stack([part[:, hidden:].reshape(rows_out, -1, 2, LANES) for part in (part_a, part_b)], axis=2)
    mixer_grads = mixer_grads.reshape(rows_out, -1, 4, LANES)
    mixer_grads = jnp.transpose(mixer_grads, (0, 2, 1, 3)).reshape(rows_out, 4, width)
    return (
        out,
        gtok,
        gain_one,
        mixer_grads[:, :3],
        short_grad,
        w1_grad,
        jnp.sum(pre_one_grad, axis=0),
        w2_grad,
        w3_grad,
        bias_grad,
        nu * long_car,
        rate_grad,
        mixer_grads[:, 3].T,
        gain_two,
        part_a[:, :hidden],
        part_b[:, :hidden].T,
    )


def solution(mesh):
    placed = (
        P("seq", "ch"),
        P(),
        P("ch"),
        P(None, None, "ch"),
        P(None, None, "ch"),
        P(),
        P(),
        P(),
        P(None, "ch"),
        P("ch"),
        P("ch"),
        P("ch"),
        P("ch", None),
        P("ch"),
        P(None, "ch"),
        P("ch", None),
        P("seq", "ch"),
    )
    return jax.shard_map(
        on_device,
        mesh=mesh,
        in_specs=placed,
        out_specs=(
            P("seq", "ch"),
            P("seq", "ch"),
            P(),
            P("seq", None, "ch"),
            P(),
            P(),
            P(),
            P(),
            P(),
            P(),
            P(),
            P(),
            P("ch", "seq"),
            P(),
            P("seq", "ch"),
            P("ch", "seq"),
        ),
        check_vma=False,
    )
```

```python
import functools

import jax
import jax.numpy as jnp
from jax import lax
from jax.experimental import pallas as pl
from jax.experimental.pallas import tpu as pltpu
from jax.sharding import PartitionSpec as P

FIR = 32
SEQ_LEN = 16384
DOC_MOST = 8192
EPSILON = 1e-05
FREQUENCY = 0.4
HIGHEST = lax.Precision.HIGHEST
MESH = pl.DeviceIdType.MESH
F32, BF16 = jnp.float32, jnp.bfloat16

BEFORE = 48
AFTER = 80
LANES = 128
BLOCK = 256
CHUNK = 64
SUMS = 48
HEAD = 16
VMEM_LIMIT = 56 << 20
ROOT_TWO_OVER_PI = 0.7978845608028654


def position_table(filter_len, band_count):
    places = jnp.arange(filter_len, dtype=F32)
    harmonics = jnp.arange(1, band_count + 1, dtype=F32)
    angles = FREQUENCY * places[:, None] * harmonics[None, :]
    return jnp.concatenate([places[:, None] / filter_len, jnp.cos(angles), jnp.sin(angles)], axis=1)


def of(ref, start, size):
    return pl.ds(pl.multiple_of(start, size), size)


def filter_layers(table, w1, b1, w2):
    pre_one = jnp.dot(table, w1, precision=HIGHEST, preferred_element_type=F32) + b1
    hidden_one = jnp.sin(pre_one)
    pre_two = jnp.dot(hidden_one, w2, precision=HIGHEST, preferred_element_type=F32)
    return pre_one, hidden_one, pre_two, jnp.sin(pre_two)


def filter_window(start, count, full):
    channel = (start + lax.broadcasted_iota(jnp.int32, (FIR, count), 1)).astype(F32)
    place = lax.broadcasted_iota(jnp.int32, (FIR, count), 0).astype(F32)
    return jnp.exp(-(0.5 + 3.0 * channel / full) * place / FIR)


def device_of(index):
    return (index // 2, index % 2)


class Pushing:
    def __init__(self, n, reach, backward, source, slots, send_sem, recv_sem):
        self.total, self.reach = 2 * n, reach
        self.me = 2 * lax.axis_index("seq") + lax.axis_index("ch")
        self.ahead = -1 if backward else 1
        self.place = self.total - 1 - self.me if backward else self.me
        self.source, self.slots, self.send_sem, self.recv_sem = source, slots, send_sem, recv_sem

    def greet(self, barrier):
        for k in range(self.reach):

            @pl.when(self.place - 1 - k >= 0)
            def _():
                pl.semaphore_signal(
                    barrier, inc=1, device_id=device_of(self.me - self.ahead * (1 + k)), device_id_type=MESH)

    def await_greetings(self, barrier, others):
        following = self.total - 1 - self.place
        for count in range(0, self.reach + 1):
            if count + others:

                @pl.when((following >= count) if count == self.reach else (following == count))
                def _():
                    pl.semaphore_wait(barrier, count + others)

    def copy(self, k):
        return pltpu.make_async_remote_copy(
            src_ref=self.source, dst_ref=self.slots.at[k], send_sem=self.send_sem.at[k], recv_sem=self.recv_sem.at[k],
            device_id=device_of(self.me + self.ahead * (1 + k)), device_id_type=MESH)

    def start(self):
        for k in range(self.reach):

            @pl.when(self.place + 1 + k < self.total)
            def _():
                self.copy(k).start()

    def take(self, use):
        for k in range(self.reach):

            @pl.when(self.place - 1 - k >= 0)
            def _():
                self.copy(k).wait_recv()
                use(k, self.slots[k])

            @pl.when(self.place + 1 + k < self.total)
            def _():
                self.copy(k).wait_send()


def row_stats(values):
    center = jnp.mean(values, axis=1, keepdims=True)
    shifted = values - center
    inverse = lax.rsqrt(jnp.mean(shifted * shifted, axis=1, keepdims=True) + EPSILON)
    return shifted * inverse, inverse


def forward_kernel(n, rows, reach, marks, tokens, gout, w_in, w_out, w_up, w_down, filt_w3, table, filt_w1, filt_b1, filt_w2,
                   norms_a, norms_b, biases, tails, decays, nus, shorts, ids,
                   tok_o, g_o, in_o, out_o, up_o, down_o, gains_o, vec_o,
                   n1_o, proj_o, x0_o, u_o, heads_o, long_o, car_o, dist_o, rest_o, enter_o,
                   tok_v, g_v, in_v, out_v, gains_v, vec_v, gains, head, n1_s, proj_s, u_s, state_s, end_s, slots_s,
                   local_sem, store_sem, send_sem, recv_sem, push_send, push_recv):
    block, full = rows // 2, in_v.shape[1]
    width = full // 2
    steps = full // BLOCK
    two = range(BLOCK // LANES)
    step = pl.program_id(0)
    s, c = lax.axis_index("seq"), lax.axis_index("ch")
    barrier = pltpu.get_barrier_semaphore()
    pushing = Pushing(n, reach, False, end_s, slots_s, push_send, push_recv)
    partner = (s, 1 - c)
    cols = pl.ds(pl.multiple_of(c * width, width), width)
    early = [(gains, gains_v.at[pl.ds(0, 8), cols]), (filt_w3, gains_v.at[pl.ds(8, filt_w3.shape[0]), cols])]
    late = []
    for i in range(width // LANES):
        source = pl.ds(i * LANES, LANES)
        paired = pl.ds(pl.multiple_of((2 * i + c) * LANES, LANES), LANES)
        early += [
            (head.at[:, source], vec_v.at[pl.ds(0, HEAD), paired]),
            (w_in.at[:, :, source], in_v.at[:, :, paired]),
        ]
        late.append((w_out.at[source, :], out_v.at[paired, :]))

    def remote(src, dst, k, target=partner):
        return pltpu.make_async_remote_copy(
            src_ref=src, dst_ref=dst, send_sem=send_sem.at[k], recv_sem=recv_sem.at[k],
            device_id=target, device_id_type=MESH)

    halves = [(early[k], k) for k in range(len(early))] + [(late[k], len(early) + k) for k in range(len(late))]
    count = len(halves)
    far = [remote(w_up, up_o, count), remote(w_down, down_o, count + 1)]
    at_tokens = count + 2

    left, right = pl.ds(0, width), pl.ds(width, width)
    first, second = pl.ds(0, block), pl.ds(block, block)
    ahead, tail = pl.ds(block - BEFORE, block + BEFORE), pl.ds(rows - BEFORE, BEFORE)
    main = pl.ds(BEFORE, block)
    keeps = [
        [(tokens.at[first, :], tok_v.at[main, left]), (gout.at[first, :], g_v.at[:, left])],
        [(tokens.at[ahead, :], tok_v.at[:, right]), (gout.at[second, :], g_v.at[:, right])],
    ]
    sends = [
        [(tokens.at[ahead, :], tok_v.at[:, left]), (gout.at[second, :], g_v.at[:, left])],
        [(tokens.at[first, :], tok_v.at[main, right]), (gout.at[first, :], g_v.at[:, right])],
    ]

    def edge(which, target):
        return remote(
            tokens.at[tail, :], tok_v.at[pl.ds(0, BEFORE), (left, right)[which]], at_tokens + 2 + which, target)

    def for_core(action):
        for which in range(2):

            @pl.when(c == which)
            def _():
                action(which)

    stores = [(tok_v, tok_o), (gains_v, gains_o), (vec_v, vec_o), (in_v, in_o), (g_v, g_o), (out_v, out_o)]

    def store(k):
        return pltpu.make_async_copy(*stores[k], store_sem.at[k])

    @pl.when(step == 0)
    def _():
        pushing.greet(barrier)
        pl.semaphore_signal(barrier, inc=1, device_id=partner, device_id_type=MESH)

        @pl.when((c == 0) & (s > 0))
        def _():
            for k in range(2):
                pl.semaphore_signal(barrier, inc=1, device_id=(s - 1, k), device_id_type=MESH)

        gains[...] = jnp.zeros_like(gains)
        head[...] = jnp.zeros_like(head)
        for ref, row, value in ((gains, 0, norms_a), (gains, 1, norms_b), (head, 2, biases), (head, 3, tails),
                                (head, 4, decays), (head, 5, nus)):
            ref[row : row + 1, :] = value[...].reshape(1, width)
        for j in range(3):
            for t in range(3):
                head[6 + 3 * j + t : 7 + 3 * j + t, :] = shorts[j, t : t + 1, :]

        def begin_own(which):
            for k, (src, dst) in enumerate(keeps[which]):
                pltpu.make_async_copy(src, dst, local_sem.at[at_tokens + k]).start()

        for_core(begin_own)
        for (src, dst), k in halves:
            pltpu.make_async_copy(src, dst, local_sem.at[k]).start()

        @pl.when(s < n - 1)
        def _():
            pushing.await_greetings(barrier, 2)

        @pl.when(s == n - 1)
        def _():
            pushing.await_greetings(barrier, 1)

        def begin(which):
            remote(*sends[which][0], at_tokens).start()

            @pl.when(s < n - 1)
            def _():
                edge(which, (s + 1, 0)).start()

        for_core(begin)
        for (src, dst), k in halves[: len(early)]:
            remote(src, dst, k).start()
        for_core(lambda which: remote(*sends[which][1], at_tokens + 1).start())
        for (src, dst), k in halves[len(early) :]:
            remote(src, dst, k).start()
        for copy in far:
            copy.start()

        def distances(j, _):
            at = pl.ds(pl.multiple_of(j * 32, 32), 32)
            start = pl.multiple_of(BEFORE + j * 32, 16)
            own = ids[pl.ds(start, 32), :]
            before = after = jnp.zeros((32, LANES), F32)
            for k in range(1, FIR):
                before += jnp.where(own == ids[pl.ds(start - k, 32), :], 1.0, 0.0)
                after += jnp.where(own == ids[pl.ds(start + k, 32), :], 1.0, 0.0)
            dist_o[at, :] = before
            rest_o[at, :] = after
            return 0

        lax.fori_loop(0, block // 32, distances, 0)

        def take_tokens(which):
            remote(*sends[which][0], at_tokens).wait_send()
            remote(*sends[1 - which][0], at_tokens).wait_recv()
            pltpu.make_async_copy(*keeps[which][0], local_sem.at[at_tokens]).wait()

            @pl.when(s < n - 1)
            def _():
                edge(which, (s + 1, 0)).wait_send()

            if which == 0:

                @pl.when(s > 0)
                def _():
                    for k in range(2):
                        edge(k, partner).wait_recv()

        for_core(take_tokens)
        hidden_two = filter_layers(table[...], filt_w1[...], filt_b1[...], filt_w2[...])[3]
        for (src, dst), k in halves[:2]:
            pltpu.make_async_copy(src, dst, local_sem.at[k]).wait()
            remote(src, dst, k).wait()
        store(0).start()
        store(1).start()

        def normed(j, _):
            at = pl.ds(pl.multiple_of(j * 80, 16), 80)
            values = jnp.where(ids[at, 0:1] >= 0.0, tok_v[at, :].astype(F32), 0.0)
            n1_s[at, :] = (row_stats(values)[0] * gains_v[0:1, :]).astype(BF16)
            return 0

        lax.fori_loop(0, (BEFORE + block) // 80, normed, 0)
        n1_o[...] = n1_s[pl.ds(BEFORE, block), :]
        for (src, dst), k in halves[2 : len(early)]:
            pltpu.make_async_copy(src, dst, local_sem.at[k]).wait()
            remote(src, dst, k).wait()
        taps = jnp.dot(hidden_two, gains_v[8:, :], precision=HIGHEST, preferred_element_type=F32)
        taps *= filter_window(0, full, full)
        for i in range(width // LANES):
            for half in range(2):
                source = half * width + i * LANES
                vec_v[HEAD : HEAD + FIR, (2 * i + half) * LANES : (2 * i + half + 1) * LANES] = (
                    taps[:, source : source + LANES])
        store(2).start()
        store(3).start()

    @pl.when(step < steps)
    def _():
        lanes = [pl.ds(pl.multiple_of((2 * step + b) * LANES, LANES), LANES) for b in two]
        wide = pl.ds(pl.multiple_of(step * BLOCK, BLOCK), BLOCK)
        for t in range(3):
            part = jnp.dot(n1_s[...], in_v[t, :, wide], preferred_element_type=F32).astype(BF16)
            for b in two:
                proj_o[t, b] = part[:, b * LANES : (b + 1) * LANES]
                proj_s[t, b] = part[:, b * LANES : (b + 1) * LANES].astype(F32)

        def convolved(start, size):
            own = ids[pl.ds(start, size), :]
            same = [None] + [own == ids[pl.ds(start - j, size), :] for j in (1, 2)]
            results = []
            for b in two:
                streams = []
                for t in range(3):
                    value = vec_v[6 + t : 7 + t, lanes[b]] * proj_s[t, b, pl.ds(start, size), :]
                    for j in (1, 2):
                        tap = vec_v[6 + 3 * j + t : 7 + 3 * j + t, lanes[b]]
                        value += jnp.where(same[j], tap * proj_s[t, b, pl.ds(start - j, size), :], 0.0)
                    streams.append(value)
                gated = (streams[0] * streams[2]).astype(BF16).astype(F32)
                u_s[2 * step + b, pl.ds(start, size), :] = gated
                u_o[b, pl.ds(start, size), :] = gated
                results.append(streams)
            return results

        convolved(16, 32)
        for b, streams in enumerate(convolved(BEFORE, 8)):
            heads_o[0:8, b * LANES : (b + 1) * LANES] = streams[2]
            heads_o[8:16, b * LANES : (b + 1) * LANES] = streams[0]
            u_o[b, 0:16, :] = jnp.zeros((16, LANES), F32)
            u_s[2 * step + b, 0:16, :] = jnp.zeros((16, LANES), F32)

        def conv_chunk(j, _):
            start = pl.multiple_of(BEFORE + j * 32, 16)
            for b, streams in enumerate(convolved(start, 32)):
                x0_o[b, pl.ds(pl.multiple_of(j * 32, 32), 32), :] = streams[1]
            return 0

        lax.fori_loop(0, block // 32, conv_chunk, 0)

        row_id = lax.broadcasted_iota(jnp.int32, (8, LANES), 0)
        rates = [vec_v[4:5, lanes[b]] for b in two]
        powers = [jnp.exp(-rate * (row_id + 1).astype(F32)) for rate in rates]
        lams = [[jnp.exp(-rate * float(k)) for k in (1, 2, 4)] for rate in rates]
        for b in two:
            state_s[2 * step + b, 0:8, :] = jnp.zeros((8, LANES), F32)

        def scan_group(g, carry):
            start = pl.multiple_of(BEFORE + g * 8, 8)
            own = ids[pl.ds(start, 8), :]
            masks = [(own == ids[pl.ds(start - k, 8), :]) & (row_id >= k) for k in (1, 2, 4)]
            joined = own == jnp.broadcast_to(ids[pl.ds(start - 1, 1), :], (8, LANES))
            result = []
            for b in two:
                value = u_s[2 * step + b, pl.ds(start, 8), :]
                for mask, lam, k in zip(masks, lams[b], (1, 2, 4)):
                    value += jnp.where(mask, lam * pltpu.roll(value, k, 0), 0.0)
                value += jnp.where(joined, powers[b] * carry[b], 0.0)
                state_s[2 * step + b, pl.ds(pl.multiple_of(8 + g * 8, 8), 8), :] = value
                result.append(jnp.broadcast_to(value[7:8, :], (8, LANES)))
            return tuple(result)

        zero = jnp.zeros((8, LANES), F32)
        final = lax.fori_loop(0, block // 8, scan_group, (zero,) * len(two), unroll=4)
        for b in two:
            end_s[:, lanes[b]] = final[b][0:1, :]

    @pl.when(step == steps - 1)
    def _():
        pushing.start()

    @pl.when(step >= steps)
    def _():
        i = step - steps
        lanes = [pl.ds(pl.multiple_of((2 * i + b) * LANES, LANES), LANES) for b in two]
        lam = [jnp.exp(-vec_v[4:5, lanes[b]]) for b in two]
        tails = [vec_v[3:4, lanes[b]] * vec_v[5:6, lanes[b]] for b in two]

        def long_chunk(j, _):
            at = pl.ds(pl.multiple_of(j * 32, 32), 32)
            start = pl.multiple_of(BEFORE + j * 32, 16)
            near = dist_o[at, :]
            totals = []
            for b in two:
                previous = state_s[2 * i + b, pl.ds(7 + j * 32, 32), :]
                carried = jnp.where(near >= 1.0, lam[b] * previous, 0.0)
                car_o[b, at, :] = carried
                here = u_s[2 * i + b, pl.ds(start, 32), :]
                totals.append((vec_v[2:3, lanes[b]] + vec_v[16:17, lanes[b]]) * here + tails[b] * carried)
            for k in range(1, FIR):
                same = near >= float(k)
                for b in two:
                    term = vec_v[16 + k : 17 + k, lanes[b]] * u_s[2 * i + b, pl.ds(start - k, 32), :]
                    totals[b] += jnp.where(same, term, 0.0)
            for b in two:
                long_o[b, at, :] = totals[b]
            return 0

        lax.fori_loop(0, block // 32, long_chunk, 0)

    @pl.when(step == steps)
    def _():
        def take_rows(which):
            remote(*sends[which][1], at_tokens + 1).wait_send()
            remote(*sends[1 - which][1], at_tokens + 1).wait_recv()
            pltpu.make_async_copy(*keeps[which][1], local_sem.at[at_tokens + 1]).wait()

        for_core(take_rows)
        for (src, dst), k in halves[len(early) :]:
            pltpu.make_async_copy(src, dst, local_sem.at[k]).wait()
            remote(src, dst, k).wait()
        store(4).start()
        store(5).start()

    @pl.when(step == 2 * steps - 1)
    def _():
        enter_o[...] = jnp.zeros_like(enter_o)
        rate = vec_v[4:5, :]
        last = marks[2 * n + jnp.maximum(pushing.me - 1, 0)]

        def use(k, state):
            same = jnp.where(marks[2 * n + pushing.me - 1 - k] == last, 1.0, 0.0)
            enter_o[...] += same * jnp.exp(-rate * float(block * k)) * state

        pushing.take(use)
        for copy in far:
            copy.wait()
        for k in range(len(stores)):
            store(k).wait()


def forward(n, marks, tokens, gout, w_in, w_out, w_up, w_down, filt_w3, table, filt_w1, filt_b1, filt_w2, vectors, ids):
    rows, width = tokens.shape
    hidden = w_up.shape[1]
    full, block = 2 * width, rows // 2
    window = BEFORE + block
    steps, lane_blocks = full // BLOCK, full // LANES
    reach = min(DOC_MOST // block, 2 * n - 1)
    anywhere = pl.BlockSpec(memory_space=pl.ANY)
    whole = lambda *shape: pl.BlockSpec(shape, lambda i: (0,) * len(shape), pipeline_mode=pl.Buffered(1))
    soon, later = lambda i: jnp.minimum(i, steps - 1), lambda i: jnp.maximum(i - steps, 0)
    stacked = lambda count, place: pl.BlockSpec((BLOCK // LANES, count, LANES), lambda i: (place(i), 0, 0))
    shape = jax.ShapeDtypeStruct
    vmem = pltpu.VMEM
    far = 2 + 3 * (width // LANES) + 2 + 4
    dma = pltpu.SemaphoreType.DMA
    landing = [
        ((window, full), BF16), ((block, full), BF16), ((3, full, full), BF16), ((full, full), BF16),
        ((8 + filt_w3.shape[0], full), F32), ((HEAD + FIR, full), F32),
    ]
    return pl.pallas_call(
        functools.partial(forward_kernel, n, rows, reach),
        name="forward",
        grid=(2 * steps,),
        out_shape=(
            *[shape(*part) for part in landing[:4]],
            shape((full, hidden), BF16),
            shape((hidden, full), BF16),
            *[shape(*part) for part in landing[4:]],
            shape((block, full), BF16),
            shape((3, lane_blocks, window, LANES), BF16),
            shape((lane_blocks, block, LANES), F32),
            shape((lane_blocks, window, LANES), F32),
            shape((16, full), F32),
            shape((lane_blocks, block, LANES), F32),
            shape((lane_blocks, block, LANES), F32),
            shape((block, LANES), F32),
            shape((block, LANES), F32),
            shape((1, full), F32),
        ),
        in_specs=[pl.BlockSpec(memory_space=pltpu.SMEM)] + [anywhere] * 7 + [
            whole(*part.shape) for part in (table, filt_w1, filt_b1, filt_w2, *vectors, ids)],
        out_specs=(
            *[anywhere] * 8,
            whole(block, full),
            pl.BlockSpec((3, BLOCK // LANES, window, LANES), lambda i: (0, soon(i), 0, 0)),
            stacked(block, soon),
            stacked(window, soon),
            pl.BlockSpec((16, BLOCK), lambda i: (0, soon(i))),
            stacked(block, later),
            stacked(block, later),
            whole(block, LANES),
            whole(block, LANES),
            whole(1, full),
        ),
        scratch_shapes=[
            *[vmem(*part) for part in landing],
            vmem((8, width), F32),
            vmem((HEAD, width), F32),
            vmem((window, full), BF16),
            vmem((3, BLOCK // LANES, window, LANES), F32),
            vmem((lane_blocks, window, LANES), F32),
            vmem((lane_blocks, 8 + block, LANES), F32),
            vmem((1, full), F32),
            vmem((reach, 1, full), F32),
            dma((far,)), dma((6,)), dma((far,)), dma((far,)), dma((reach,)), dma((reach,)),
        ],
        compiler_params=pltpu.CompilerParams(collective_id=0, has_side_effects=True, vmem_limit_bytes=VMEM_LIMIT),
    )(marks, tokens, gout, w_in, w_out, w_up, w_down, filt_w3, table, filt_w1, filt_b1, filt_w2, *vectors, ids)


TILE = 512
PART = TILE // 2
STAGES = 5


class Summing:
    def __init__(self, slots, rows, staged, first, second, third, fourth, fifth, send_sem, recv_sem):
        self.slots, self.rows, self.staged = slots, rows, staged
        self.first, self.second, self.third, self.fourth, self.fifth = first, second, third, fourth, fifth
        self.send_sem, self.recv_sem = send_sem, recv_sem
        self.s, self.c = lax.axis_index("seq"), lax.axis_index("ch")
        self.bits = [(self.s // (1 << b)) % 2 for b in range(4)]
        self.peers = [(self.s + (1 - 2 * bit) * (1 << b), self.c) for b, bit in enumerate(self.bits)]
        self.partner = (self.s, 1 - self.c)
        self.order = ((0, 1, 2, 3), (1, 0, 2, 3))

    @staticmethod
    def scratch(tiles, slots, rows):
        return [
            pltpu.VMEM((2, 2, 2, 2, 2, 2, rows, TILE), BF16),
            pltpu.VMEM((slots, 2, 2, 2, 2, rows, TILE), BF16),
            pltpu.VMEM((slots, 2, 2, 2, 2, rows, PART), BF16),
            pltpu.VMEM((slots, 2, 2, 2, rows, PART), BF16),
            pltpu.VMEM((slots, 2, 2, rows, PART), BF16),
            pltpu.VMEM((slots, 2, rows, PART), BF16),
            pltpu.SemaphoreType.DMA((tiles, 1 + 2 * 4)),
            pltpu.SemaphoreType.DMA((tiles, 1 + 2 * 4)),
        ]

    def greet(self, barrier):
        for peer in [self.partner] + self.peers:
            pl.semaphore_signal(barrier, inc=1, device_id=peer, device_id_type=MESH)

    def remote(self, src, dst, tile, k, target):
        return pltpu.make_async_remote_copy(
            src_ref=src, dst_ref=dst, send_sem=self.send_sem.at[tile, k], recv_sem=self.recv_sem.at[tile, k],
            device_id=target, device_id_type=MESH)

    def copies(self, tile, stage):
        slot = tile % self.slots
        if stage == 0:
            return [self.remote(self.staged.at[tile % 2, 1], self.first.at[slot], tile, 0, self.partner)]
        result = []
        for part in range(2):
            bit = self.order[part][stage - 1]
            away = 1 - self.bits[bit]
            at = pl.ds(part * PART, PART)
            if stage == 1:
                src = self.first.at[slot, :, :, :, away, :, at] if part == 0 else self.first.at[slot, :, :, away, :, :, at]
                dst = self.second.at[slot, part]
            elif stage == 2:
                src, dst = self.second.at[slot, part, :, :, away], self.third.at[slot, part]
            elif stage == 3:
                src, dst = self.third.at[slot, part, :, away], self.fourth.at[slot, part]
            else:
                src, dst = self.fourth.at[slot, part, away], self.fifth.at[slot, part]
            result.append(self.remote(src, dst, tile, 1 + 2 * (stage - 1) + part, self.peers[bit]))
        return result

    def start(self, tile, stage):
        for copy in self.copies(tile, stage):
            copy.start()

    def advance(self, tile, stage, total):
        for copy in self.copies(tile, stage):
            copy.wait()
        x, y, low, high = self.bits
        slot = tile % self.slots
        if stage == 0:
            def add(i, _):
                for h in range(2):
                    for j in range(2):
                        for k in range(2):
                            self.first[slot, h, i, j, k] += self.staged[tile % 2, 0, h, i, j, k]
                return 0
            lax.fori_loop(0, 2, add, 0)
        elif stage == 1:
            def add(i, _):
                for h in range(2):
                    for k in range(2):
                        self.second[slot, 0, h, i, k] += self.first[slot, h, i, k, x, :, 0:PART]
                        self.second[slot, 1, h, i, k] += self.first[slot, h, i, y, k, :, PART:TILE]
                return 0
            lax.fori_loop(0, 2, add, 0)
        elif stage == 2:
            for i in range(2):
                for k in range(2):
                    self.third[slot, 0, i, k] += self.second[slot, 0, i, k, y]
                    self.third[slot, 1, i, k] += self.second[slot, 1, i, k, x]
        elif stage == 3:
            for part in range(2):
                for i in range(2):
                    self.fourth[slot, part, i] += self.third[slot, part, i, low]
        else:
            for part in range(2):
                mine = self.fourth[slot, part, high].astype(F32)
                total(tile, part, mine + self.fifth[slot, part].astype(F32))
            return
        self.start(tile, stage + 1)


class Joining:
    def __init__(self, sums, held, arrived, send_sem, recv_sem):
        self.held, self.arrived, self.send_sem, self.recv_sem = held, arrived, send_sem, recv_sem
        self.targets = [sums.partner] + sums.peers

    @staticmethod
    def scratch(*shape):
        return [pltpu.VMEM((STAGES,) + shape, F32), pltpu.VMEM((STAGES,) + shape, F32),
                pltpu.SemaphoreType.DMA((STAGES,)), pltpu.SemaphoreType.DMA((STAGES,))]

    def copy(self, stage):
        return pltpu.make_async_remote_copy(
            src_ref=self.held.at[stage], dst_ref=self.arrived.at[stage], send_sem=self.send_sem.at[stage],
            recv_sem=self.recv_sem.at[stage], device_id=self.targets[stage], device_id_type=MESH)

    def start(self, stage):
        self.copy(stage).start()

    def advance(self, stage, result):
        self.copy(stage).wait()
        total = self.held[stage] + self.arrived[stage]
        if stage == STAGES - 1:
            result[...] = total
        else:
            self.held[stage + 1] = total
            self.start(stage + 1)


def contract(left, right, dims):
    return lax.dot_general(left, right, (dims, ((), ())), preferred_element_type=F32)


def contract(left, right, dims):
    return lax.dot_general(left, right, (dims, ((), ())), preferred_element_type=F32)


TILES = 6
EPILOGUE, GATE, TAPS, BACK = TILES, TILES + 1, TILES + 2, TILES + 3
LAGS = (1, 3, 5, 6, 7)
HALO = 80


def backward_kernel(n, block, reach, summed, marks, tok, ids, dist_s, rest_s, enter, g, gains, vec, wout, x0, base, car, u, n1, heads,
                    wup_a, wup_b, wdn_a, wdn_b, win, proj, *refs):
    full = g.shape[1]
    width, lane_blocks = full // 2, full // LANES
    steps = full // BLOCK
    last_back = BACK + steps - 1
    outs, refs = refs[:6], refs[6:]
    if summed:
        part_a, part_b, small_a, small_b, out_full, gtok_full = outs
    else:
        grads_o, small_a, small_b, out_o, gtok_o, _ = outs
    (mixed_s, middle_s, n2_s, gn_s, gout_s, out_s, gmid_s, long_s, car_s, glong_s, q_s, gc_s, gp_s, proj_s,
     taps_s, first_s, slots_s, joined_s, halo_s, halo_r, head_s,
     push_send, push_recv, halo_sem, *buffers) = refs
    step = pl.program_id(0)
    groups = block // 32
    barrier = pltpu.get_barrier_semaphore()
    pushing = Pushing(n, reach, True, first_s, slots_s, push_send, push_recv)
    c = lax.axis_index("ch")
    lanes_of = lambda b: pl.ds(pl.multiple_of(b * LANES, LANES), LANES)
    if summed:
        sums = Summing(TILES, full // 16, *buffers[:8])
        joins = [(Joining(sums, *buffers[8:12]), small_a, TAPS), (Joining(sums, *buffers[12:16]), small_b, last_back)]
        local_sem, exchange_send, exchange_recv = buffers[16:]

        def shares(k, src, dst):
            at = pl.ds(pl.multiple_of(c * block, block), block)
            of_core = lambda which: src.at[:, pl.ds(pl.multiple_of(which * width, width), width)]
            return (
                pltpu.make_async_copy(of_core(c), dst.at[at, :], local_sem.at[k]),
                pltpu.make_async_remote_copy(
                    src_ref=of_core(1 - c), dst_ref=dst.at[at, :], send_sem=exchange_send.at[k],
                    recv_sem=exchange_recv.at[k], device_id=sums.partner, device_id_type=MESH),
            )

    halo_copy = pltpu.make_async_remote_copy(
        src_ref=halo_s, dst_ref=halo_r, send_sem=halo_sem.at[0], recv_sem=halo_sem.at[1],
        device_id=device_of(pushing.me - 1), device_id_type=MESH)

    @pl.when(step == 0)
    def _():
        pushing.greet(barrier)
        if summed:
            sums.greet(barrier)

        last = ids[pl.ds(BEFORE - 1, 1), :]
        for b in range(lane_blocks):
            lanes = slice(b * LANES, (b + 1) * LANES)
            rate, tail = vec[4:5, lanes], vec[3:4, lanes] * vec[5:6, lanes]
            state = enter[0:1, lanes]

            def mix(j, _):
                at = pl.ds(pl.multiple_of(j * 32, 32), 32)
                passed = (lax.broadcasted_iota(jnp.int32, (32, LANES), 0) + (j * 32 + 1)).astype(F32)
                same = ids[pl.ds(pl.multiple_of(BEFORE + j * 32, 16), 32), :] == last
                entered = jnp.where(same, jnp.exp(-rate * passed) * state, 0.0)
                car_s[b, at, :] = car[b, at, :] + entered
                long = base[b, at, :] + tail * entered
                long_s[b, at, :] = long
                mixed_s[at, lanes] = (long * x0[b, at, :]).astype(BF16)
                return 0

            lax.fori_loop(0, groups, mix, 0)
        middle_s[...] = jnp.dot(mixed_s[...], wout[...], preferred_element_type=F32)

        def norm(j, _):
            at = pl.ds(pl.multiple_of(j * 32, 32), 32)
            start = pl.multiple_of(BEFORE + j * 32, 16)
            values = middle_s[at, :] + tok[pl.ds(start, 32), :].astype(F32)
            middle_s[at, :] = values
            out_s[at, :] = values
            n2_s[at, :] = (row_stats(values)[0] * gains[1:2, :]).astype(BF16)
            gn_s[at, :] = jnp.zeros_like(values)
            return 0

        lax.fori_loop(0, groups, norm, 0)
        pushing.await_greetings(barrier, 5 if summed else 0)

    if summed:

        def total(tile, part, value):
            (part_a, part_b)[part][:, pl.ds(pl.multiple_of(tile * PART, PART), PART)] = value

        for stage in range(STAGES - 1, -1, -1):
            since, early = step - 1 - stage, step - LAGS[stage]
            is_late = step // (BACK + 1 + stage)

            @pl.when(((early >= 0) & (early < TILES)) | ((since >= BACK) & (since <= last_back)))
            def _():
                sums.advance(early + (since - (BACK - TILES) - early) * is_late, stage, total)

            for join, result, begun in joins:

                @pl.when(since == begun)
                def _():
                    join.advance(stage, result)

    def put(tile, start, grad):
        size = grad[0].shape[1]
        at = pl.ds(start, size)
        for half in range(2):
            if summed:
                whose = (half + c) % 2
                for q in range(16):
                    sums.staged[tile % 2, whose, q // 8, q // 4 % 2, q // 2 % 2, q % 2, :, at] = (
                        grad[half][q * sums.rows : (q + 1) * sums.rows])
            else:
                grads_o[0, half, :, at] = grad[half]

    @pl.when(step < TILES)
    def _():
        for half, (wup, wdn) in enumerate(((wup_a, wdn_a), (wup_b, wdn_b))):
            n2, rows = n2_s[...], g[...]
            up = jnp.dot(n2, wup[...], preferred_element_type=F32)
            pulled = contract(rows, wdn[...], ((1,), (1,)))
            square = up * up
            inner = ROOT_TWO_OVER_PI * up * (1.0 + 0.044715 * square)
            bent = jnp.tanh(inner)
            part = 0.5 * (1.0 + bent)
            active = (up * part).astype(BF16)
            slope = part + (0.5 * ROOT_TWO_OVER_PI) * up * (1.0 - bent * bent) * (1.0 + 0.134145 * square)
            g_up = (pulled * slope).astype(BF16)
            out_s[...] += jnp.dot(active, wdn[...], preferred_element_type=F32)
            gn_s[...] += contract(g_up, wup[...], ((1,), (1,)))
            pair = (contract(n2, g_up, ((0,), (0,))).astype(BF16), contract(rows, active, ((0,), (0,))).astype(BF16))
            for k in range(2):
                at = pl.ds(k * PART, PART)
                if summed:
                    for q in range(16):
                        sums.staged[step % 2, half, q // 8, q // 4 % 2, q // 2 % 2, q % 2, :, at] = (
                            pair[k][q * sums.rows : (q + 1) * sums.rows])
                else:
                    grads_o[0, (half + c) % 2, :, at] = pair[k]
        if summed:
            sums.start(step, 0)

    @pl.when(step == EPILOGUE)
    def _():
        if summed:
            for copy in shares(0, out_s, out_full):
                copy.start()
        else:
            out_o[...] = out_s[...]

        def back(j, total):
            at = pl.ds(pl.multiple_of(j * 32, 32), 32)
            normal, inverse = row_stats(middle_s[at, :])
            grad = gn_s[at, :]
            total += jnp.sum(grad * normal, axis=0, keepdims=True)
            scaled = grad * gains[1:2, :]
            cross = jnp.mean(scaled * normal, axis=1, keepdims=True)
            result = g[at, :].astype(F32) + inverse * (
                scaled - jnp.mean(scaled, axis=1, keepdims=True) - normal * cross)
            gmid_s[at, :] = result
            gout_s[at, :] = result.astype(BF16)
            gn_s[at, :] = jnp.zeros_like(grad)
            return total

        gain_two = lax.fori_loop(0, groups, back, jnp.zeros((1, full), F32))
        head_s[...] = jnp.zeros_like(head_s)
        head_s[0:1, :] = gain_two
        for i in range(steps):
            gmix = contract(gout_s[...], wout[i * BLOCK : (i + 1) * BLOCK, :], ((1,), (1,)))
            for k in range(BLOCK // LANES):
                b = i * (BLOCK // LANES) + k
                part = gmix[:, k * LANES : (k + 1) * LANES]
                glong_s[b, 0:block, :] = part * x0[b]
                long_s[b] = part * long_s[b]

    row_id = lax.broadcasted_iota(jnp.int32, (8, LANES), 0)
    zero = jnp.zeros((8, LANES), F32)

    @pl.when(step == GATE)
    def _():
        rates = [vec[4:5, b * LANES : (b + 1) * LANES] for b in range(lane_blocks)]
        tails = [vec[3:4, b * LANES : (b + 1) * LANES] * vec[5:6, b * LANES : (b + 1) * LANES] for b in range(lane_blocks)]
        lams = [[jnp.exp(-rate * float(k)) for k in (1, 2, 4)] for rate in rates]
        powers = [jnp.exp(-rate * (8 - row_id).astype(F32)) for rate in rates]

        def scan_group(i, carry):
            at = block // 8 - 1 - i
            to = pl.ds(pl.multiple_of(at * 8, 8), 8)
            start = pl.multiple_of(BEFORE + at * 8, 8)
            own = ids[pl.ds(start, 8), :]
            masks = [(own == ids[pl.ds(start + k, 8), :]) & (row_id < 8 - k) for k in (1, 2, 4)]
            joined = own == jnp.broadcast_to(ids[pl.ds(start + 8, 1), :], (8, LANES))
            states, biases, carries = [], [], []
            for b in range(lane_blocks):
                grad = glong_s[b, to, :]
                value = grad * tails[b]
                for mask, lam, k in zip(masks, lams[b], (1, 2, 4)):
                    value += jnp.where(mask, lam * pltpu.roll(value, 8 - k, 0), 0.0)
                value += jnp.where(joined, powers[b] * carry[0][b], 0.0)
                q_s[b, to, :] = value
                states.append(jnp.broadcast_to(value[0:1, :], (8, LANES)))
                biases.append(carry[1][b] + grad * u[b, pl.ds(start, 8), :])
                carries.append(carry[2][b] + grad * car_s[b, to, :])
            return tuple(states), tuple(biases), tuple(carries)

        many = (zero,) * lane_blocks
        states, biases, carries = lax.fori_loop(0, block // 8, scan_group, (many, many, many), unroll=2)
        for b in range(lane_blocks):
            lanes = slice(b * LANES, (b + 1) * LANES)
            first_s[:, lanes] = states[b][0:1, :]
            head_s[1:2, lanes] = jnp.sum(biases[b], axis=0, keepdims=True)
            head_s[2:3, lanes] = jnp.sum(carries[b], axis=0, keepdims=True)
            halo_s[0:48, lanes] = glong_s[b, 0:48, :]
            halo_s[48:56, lanes] = q_s[b, 0:8, :]
            halo_s[72:80, lanes] = long_s[b, 0:8, :]
        halo_s[56:72, :] = heads[...]
        pushing.start()

        @pl.when(pushing.me > 0)
        def _():
            halo_copy.start()

    @pl.when(step == TAPS)
    def _():
        taps_s[...] = jnp.zeros_like(taps_s)

        def pairs(p, _):
            def chunk(j, _):
                at = pl.ds(pl.multiple_of(j * 32, 32), 32)
                start = BEFORE + j * 32
                near = dist_s[at, :]
                here = [glong_s[2 * p + k, at, :] for k in range(2)]
                for tap in range(FIR):
                    same = near >= float(tap)
                    for k in range(2):
                        term = jnp.where(same, here[k] * u[2 * p + k, pl.ds(start - tap, 32), :], 0.0)
                        taps_s[2 * p + k, tap] += jnp.sum(term.reshape(4, 8, LANES), axis=0)
                return 0

            lax.fori_loop(0, groups, chunk, 0)
            return 0

        lax.fori_loop(0, lane_blocks // 2, pairs, 0)
        result = joins[0][0].held.at[0] if summed else small_a
        for b in range(lane_blocks):
            lanes = slice(b * LANES, (b + 1) * LANES)
            result[0:FIR, lanes] = jnp.sum(taps_s[b], axis=1)
        result[FIR : FIR + 8, :] = head_s[...]
        if summed:
            joins[0][0].start(0)

    @pl.when(step == BACK)
    def _():
        joined_s[...] = jnp.zeros_like(joined_s)
        rate = vec[4:5, :]
        following = 2 * n + jnp.minimum(pushing.me + 1, 2 * n - 1)
        lasts = (marks[2 * n + pushing.me], marks[following])

        def use(k, state):
            first = marks[pushing.me + 1 + k]
            for row in range(2):
                if k >= row:
                    same = jnp.where(first == lasts[row], 1.0, 0.0)
                    joined_s[row : row + 1, :] += same * jnp.exp(-rate * float(block * (k - row) + 1)) * state

        pushing.take(use)

        @pl.when(pushing.me > 0)
        def _():
            halo_copy.wait_send()

        @pl.when(pushing.me < 2 * n - 1)
        def _():
            halo_copy.wait_recv()

        for b in range(lane_blocks):
            glong_s[b, block : block + 48, :] = halo_r[0:48, b * LANES : (b + 1) * LANES]

    @pl.when((step >= BACK) & (step <= last_back))
    def _():
        i = step - BACK
        two = range(2)
        lanes = [lanes_of(2 * i + k) for k in two]
        rates = [vec[4:5, lanes[k]] for k in two]
        scales = [vec[2:3, lanes[k]] - vec[3:4, lanes[k]] * vec[5:6, lanes[k]] for k in two]
        mine = [joined_s[0:1, lanes[k]] for k in two]
        for k in two:
            for s in range(3):
                proj_s[s, k] = proj[s, k].astype(F32)
        last = ids[pl.ds(BEFORE + block - 1, 1), :]

        def conv_at(s, k, start, size, same):
            value = vec[6 + s : 7 + s, lanes[k]] * proj_s[s, k, pl.ds(start, size), :]
            for j in (1, 2):
                tap = vec[6 + 3 * j + s : 7 + 3 * j + s, lanes[k]]
                value += jnp.where(same[j - 1], tap * proj_s[s, k, pl.ds(start - j, size), :], 0.0)
            return value

        def chunk(j, totals):
            at = pl.ds(pl.multiple_of(j * 32, 32), 32)
            start = pl.multiple_of(BEFORE + j * 32, 16)
            own = ids[pl.ds(start, 32), :]
            left = (block - 1 - j * 32 - lax.broadcasted_iota(jnp.int32, (32, LANES), 0)).astype(F32)
            after = rest_s[at, :]
            near = dist_s[at, :]
            grads, result = [], []
            for k in two:
                b = 2 * i + k
                state = q_s[b, at, :] + jnp.where(own == last, jnp.exp(-rates[k] * left) * mine[k], 0.0)
                result.append(totals[k] + jnp.sum((car_s[b, at, :] * state).reshape(4, 8, LANES), axis=0))
                grads.append(scales[k] * glong_s[b, at, :] + state)
            for tap in range(FIR):
                same = after >= float(tap)
                for k in two:
                    term = vec[16 + tap : 17 + tap, lanes[k]] * glong_s[2 * i + k, pl.ds(j * 32 + tap, 32), :]
                    grads[k] += jnp.where(same, term, 0.0)
            same = [near >= 1.0, near >= 2.0]
            for k in two:
                gc_s[0, k, at, :] = grads[k] * conv_at(2, k, start, 32, same)
                gc_s[1, k, at, :] = long_s[2 * i + k, at, :]
                gc_s[2, k, at, :] = grads[k] * conv_at(0, k, start, 32, same)
            return tuple(result)

        crossed = lax.fori_loop(0, groups, chunk, (zero, zero))

        start = BEFORE + block
        own = ids[pl.ds(start, 8), :]
        end_id = marks[2 * n + jnp.minimum(pushing.me + 1, 2 * n - 1)].astype(F32)
        left = (block - 1 - row_id).astype(F32)
        for k in two:
            b = 2 * i + k
            entered = jnp.exp(-rates[k] * left) * joined_s[1:2, lanes[k]]
            grad = halo_r[48:56, lanes[k]] + jnp.where(own == end_id, entered, 0.0)
            grad += scales[k] * glong_s[b, block : block + 8, :]
            for tap in range(FIR):
                term = vec[16 + tap : 17 + tap, lanes[k]] * glong_s[b, block + tap : block + tap + 8, :]
                grad += jnp.where(own == ids[pl.ds(start + tap, 8), :], term, 0.0)
            gc_s[0, k, block : block + 8, :] = grad * halo_r[56:64, lanes[k]]
            gc_s[1, k, block : block + 8, :] = halo_r[72:80, lanes[k]]
            gc_s[2, k, block : block + 8, :] = grad * halo_r[64:72, lanes[k]]

        small = joins[1][0].held.at[0] if summed else small_b
        for k in two:

            def short(j, totals):
                at = pl.ds(pl.multiple_of(j * 32, 32), 32)
                start = pl.multiple_of(BEFORE + j * 32, 16)
                same = [dist_s[at, :] >= float(d) for d in (1, 2)]
                later = [rest_s[at, :] >= float(d) for d in (1, 2)]
                result = []
                for s in range(3):
                    here = gc_s[s, k, at, :]
                    value = vec[6 + s : 7 + s, lanes[k]] * here
                    for d in (1, 2):
                        tap = vec[6 + 3 * d + s : 7 + 3 * d + s, lanes[k]]
                        value += jnp.where(later[d - 1], tap * gc_s[s, k, pl.ds(j * 32 + d, 32), :], 0.0)
                    gp_s[s, at, k * LANES : (k + 1) * LANES] = value.astype(BF16)
                    for d in range(3):
                        term = here * proj_s[s, k, pl.ds(start - d, 32), :]
                        if d:
                            term = jnp.where(same[d - 1], term, 0.0)
                        result.append(totals[3 * s + d] + jnp.sum(term.reshape(4, 8, LANES), axis=0))
                return tuple(result)

            totals = lax.fori_loop(0, groups, short, (zero,) * 9)
            rows = [None] * 9
            for s in range(3):
                for d in range(3):
                    rows[3 * d + s] = jnp.sum(totals[3 * s + d], axis=0, keepdims=True)
            rows.append(jnp.sum(crossed[k], axis=0, keepdims=True))
            for row, value in enumerate(rows):
                small[row : row + 1, lanes[k]] = value

        tile = TILES + i
        pieces = [contract(n1[...], gp_s[s], ((0,), (0,))).astype(BF16) for s in range(3)]
        at = pl.ds(pl.multiple_of(i * BLOCK, BLOCK), BLOCK)
        pieces.append(contract(gout_s[...], mixed_s[:, at], ((0,), (0,))).astype(BF16))
        for s, piece in enumerate(pieces):
            put(tile, s * LANES, [piece[:, half * LANES : (half + 1) * LANES] for half in range(2)])
        if summed:
            sums.start(tile, 0)
        for s in range(3):
            gn_s[...] += contract(gp_s[s], win[s], ((1,), (1,)))

    @pl.when(step == last_back)
    def _():
        def back(j, total):
            at = pl.ds(pl.multiple_of(j * 32, 32), 32)
            normal, inverse = row_stats(tok[pl.ds(pl.multiple_of(BEFORE + j * 32, 16), 32), :].astype(F32))
            grad = gn_s[at, :]
            total += jnp.sum(grad * normal, axis=0, keepdims=True)
            scaled = grad * gains[0:1, :]
            cross = jnp.mean(scaled * normal, axis=1, keepdims=True)
            middle_s[at, :] = gmid_s[at, :] + inverse * (
                scaled - jnp.mean(scaled, axis=1, keepdims=True) - normal * cross)
            return total

        gain_one = lax.fori_loop(0, groups, back, jnp.zeros((1, full), F32))
        small = joins[1][0].held.at[0] if summed else small_b
        small[10:11, :] = gain_one
        small[11:16, :] = jnp.zeros((5, full), F32)
        if summed:
            joins[1][0].start(0)
            for copy in shares(1, middle_s, gtok_full):
                copy.start()
        else:
            gtok_o[...] = middle_s[...]

    if summed:

        @pl.when(step == last_back + STAGES)
        def _():
            for k, (src, dst) in enumerate(((out_s, out_full), (middle_s, gtok_full))):
                for copy in shares(k, src, dst):
                    copy.wait()


def backward(n, summed, marks, tok, ids, dist, rest, enter, g, gains, vec, wout, x0, base, car, u, n1, heads, ups, downs,
             win, proj):
    block, full = g.shape
    rows, lane_blocks = BEFORE + block, full // LANES
    steps = full // BLOCK
    tiles = TILES + steps
    reach = min(DOC_MOST // block + 1, 2 * n - 1)
    whole = lambda *shape: pl.BlockSpec(shape, lambda i: (0,) * len(shape), pipeline_mode=pl.Buffered(1))
    tile = lambda i: jnp.minimum(i, TILES - 1)
    back = lambda i: jnp.clip(i - BACK, 0, steps - 1)
    wide = lambda dtype: pltpu.VMEM((block, full), dtype)
    stacked = lambda count, dtype=F32: pltpu.VMEM((lane_blocks, count, LANES), dtype)
    shape = jax.ShapeDtypeStruct
    if summed:
        out_shape = [shape((full // 16, tiles * PART), F32)] * 2 + [shape((FIR + 8, full), F32), shape((16, full), F32)]
        out_shape += [shape((2 * block, full // 2), F32)] * 2
        out_specs = [whole(full // 16, tiles * PART)] * 2 + [whole(FIR + 8, full), whole(16, full)]
        out_specs += [pl.BlockSpec(memory_space=pl.ANY)] * 2
        extra = Summing.scratch(tiles, TILES, full // 16) + Joining.scratch(FIR + 8, full) + Joining.scratch(16, full)
        extra += [pltpu.SemaphoreType.DMA((2,))] * 3
    else:
        out_shape = [shape((tiles, 2, full, TILE), BF16), shape((FIR + 8, full), F32), shape((16, full), F32)]
        out_shape += [shape((block, full), F32)] * 2 + [shape((8, LANES), F32)]
        place = lambda i: jnp.minimum(i, TILES - 1) + jnp.clip(i - BACK + 1, 0, steps)
        out_specs = [pl.BlockSpec((1, 2, full, TILE), lambda i: (place(i), 0, 0, 0)), whole(FIR + 8, full), whole(16, full)]
        out_specs += [whole(block, full)] * 2 + [whole(8, LANES)]
        extra = []
    return pl.pallas_call(
        functools.partial(backward_kernel, n, block, reach, summed),
        name="backward",
        grid=(BACK + steps + (STAGES if summed else 0),),
        out_shape=out_shape,
        in_specs=[
            pl.BlockSpec(memory_space=pltpu.SMEM),
            whole(*tok.shape), whole(*ids.shape), whole(*dist.shape), whole(*rest.shape), whole(*enter.shape), whole(*g.shape), whole(*gains.shape),
            whole(*vec.shape), whole(*wout.shape), whole(*x0.shape), whole(*base.shape), whole(*car.shape),
            whole(*u.shape), whole(*n1.shape), whole(*heads.shape),
            *[pl.BlockSpec((full, PART), lambda i: (0, tile(i)))] * 2,
            *[pl.BlockSpec((PART, full), lambda i: (tile(i), 0))] * 2,
            pl.BlockSpec((3, full, BLOCK), lambda i: (0, 0, back(i))),
            pl.BlockSpec((3, BLOCK // LANES, rows, LANES), lambda i: (0, back(i), 0, 0)),
        ],
        out_specs=out_specs,
        scratch_shapes=[
            wide(BF16), wide(F32), wide(BF16), wide(F32), wide(BF16), wide(F32), wide(F32),
            stacked(block), stacked(block), stacked(block + 48), stacked(block),
            pltpu.VMEM((3, BLOCK // LANES, block + 8, LANES), F32),
            pltpu.VMEM((3, block, BLOCK), BF16),
            pltpu.VMEM((3, BLOCK // LANES, rows, LANES), F32),
            pltpu.VMEM((lane_blocks, FIR, 8, LANES), F32),
            pltpu.VMEM((1, full), F32),
            pltpu.VMEM((reach, 1, full), F32),
            pltpu.VMEM((2, full), F32),
            pltpu.VMEM((HALO, full), F32),
            pltpu.VMEM((HALO, full), F32),
            pltpu.VMEM((8, full), F32),
            pltpu.SemaphoreType.DMA((reach,)),
            pltpu.SemaphoreType.DMA((reach,)),
            pltpu.SemaphoreType.DMA((2,)),
            *extra,
        ],
        compiler_params=pltpu.CompilerParams(collective_id=2, has_side_effects=True, vmem_limit_bytes=60 << 20),
    )(marks, tok, ids, dist, rest, enter, g, gains, vec, wout, x0, base, car, u, n1, heads, *ups, *downs, win, proj)


def reduce_plain(n, grads, small_a, small_b, out, gtok):
    both = lax.psum_scatter(grads.astype(F32), "ch", scatter_dimension=1, tiled=False)
    total = lax.psum_scatter(both, "seq", scatter_dimension=1, tiled=True)
    total = jnp.transpose(total, (1, 0, 2))
    parts = [total[:, :, k * PART : (k + 1) * PART].reshape(total.shape[0], -1) for k in range(2)]
    swap = lambda whole: lax.all_to_all(whole, "ch", split_axis=1, concat_axis=0, tiled=True)
    small_a, small_b = lax.psum((small_a, small_b), ("seq", "ch"))
    return *parts, small_a, small_b, swap(out), swap(gtok)


def finish_kernel(part_a, part_b, small_a, small_b, gains, vec, table, w1, b1, w2, out, gtok,
                  out_o, gtok_o, gain_one_o, in_o, short_o, w1_o, b1_o, w2_o, w3_o, bias_o, tgain_o, trate_o,
                  outw_o, gain_two_o, up_o, down_o, out_v, gtok_v, sem):
    full = gains.shape[1]
    width, hidden = full // 2, up_o.shape[1]
    loads = [pltpu.make_async_copy(src, dst, sem.at[k]) for k, (src, dst) in enumerate(((out, out_v), (gtok, gtok_v)))]
    saves = [pltpu.make_async_copy(src, dst, sem.at[2 + k]) for k, (src, dst) in enumerate(((out_v, out_o), (gtok_v, gtok_o)))]
    for copy in loads:
        copy.start()

    def natural(rows):
        blocks = [rows[:, b * LANES : (b + 1) * LANES] for b in range(full // LANES)]
        return jnp.concatenate(blocks[0::2] + blocks[1::2], axis=1)

    raw = natural(small_a[0:FIR, :]) * filter_window(0, full, full)
    pre_one, hidden_one, pre_two, hidden_two = filter_layers(table[...], w1[...], b1[...], w2[...])

    def exact(left, right, dims):
        return lax.dot_general(left, right, (dims, ((), ())), precision=HIGHEST, preferred_element_type=F32)

    w3_o[...] = exact(hidden_two, raw, ((0,), (0,)))
    pre_two_grad = exact(raw, gains[8:, :], ((1,), (1,))) * jnp.cos(pre_two)
    w2_o[...] = exact(hidden_one, pre_two_grad, ((0,), (0,)))
    pre_one_grad = exact(pre_two_grad, w2[...], ((1,), (1,))) * jnp.cos(pre_one)
    w1_o[...] = exact(table[...], pre_one_grad, ((0,), (0,)))
    b1_o[...] = jnp.sum(pre_one_grad, axis=0, keepdims=True).reshape(b1_o.shape)

    for copy, following in zip(loads, saves):
        copy.wait()
        following.start()

    gain_one_o[...] = small_b[10:11, :].reshape(full)
    gain_two_o[...] = small_a[FIR : FIR + 1, :].reshape(full)
    bias_o[...] = natural(small_a[FIR + 1 : FIR + 2, :]).reshape(full)
    long_car, rate, nu = small_a[FIR + 2 : FIR + 3, :], vec[4:5, :], vec[5:6, :]
    factor = jnp.exp(-rate)
    tgain_o[...] = natural(nu * long_car).reshape(full)
    trate_o[...] = natural(vec[3:4, :] * long_car * factor * factor / nu - small_b[9:10, :]).reshape(full)
    short = natural(small_b[0:9, :])
    for j in range(3):
        for s in range(3):
            short_o[j, s : s + 1, :] = short[3 * j + s : 3 * j + s + 1, :]
    up_o[...] = part_a[:, 0:hidden]
    down_o[...] = part_b[:, 0:hidden]
    for i in range(width // LANES):
        at, lanes = hidden + i * PART, slice(i * LANES, (i + 1) * LANES)
        for s, (ref, start) in enumerate(((part_a, at), (part_a, at + LANES), (part_b, at))):
            in_o[s, :, lanes] = ref[:, start : start + LANES]
        outw_o[:, lanes] = part_b[:, at + LANES : at + 2 * LANES]
    for copy in saves:
        copy.wait()


def finish(part_a, part_b, small_a, small_b, gains, vec, table, w1, b1, w2, out, gtok):
    full, rows = gains.shape[1], part_a.shape[0]
    width, hidden = full // 2, part_a.shape[1] - full // 2 // LANES * PART
    shape = jax.ShapeDtypeStruct
    vmem, anywhere = pl.BlockSpec(memory_space=pltpu.VMEM), pl.BlockSpec(memory_space=pl.ANY)
    vector = shape((full,), F32)
    return pl.pallas_call(
        finish_kernel,
        name="finish",
        out_shape=(
            shape(out.shape, F32), shape(gtok.shape, F32), vector, shape((3, rows, width), F32), shape((3, 3, full), F32),
            shape(w1.shape, F32), shape((b1.shape[1],), F32), shape(w2.shape, F32), shape((w2.shape[0], full), F32),
            vector, vector, vector, shape((rows, width), F32), vector, shape((rows, hidden), F32), shape((rows, hidden), F32),
        ),
        in_specs=[vmem] * 10 + [anywhere] * 2,
        out_specs=(anywhere, anywhere) + (vmem,) * 14,
        scratch_shapes=[pltpu.VMEM(out.shape, F32), pltpu.VMEM(gtok.shape, F32), pltpu.SemaphoreType.DMA((4,))],
        compiler_params=pltpu.CompilerParams(vmem_limit_bytes=VMEM_LIMIT),
    )(part_a, part_b, small_a, small_b, gains, vec, table, w1, b1, w2, out, gtok)


def on_device(tokens, seg_ids, norm1_gain, in_weight, short_weight, filt_w1, filt_b1, filt_w2, filt_w3,
              long_bias, tail_gain, tail_rate, out_weight, norm2_gain, up_weight, down_weight, grad_out):
    rows, width = tokens.shape
    full, block = 2 * width, rows // 2
    n = lax.axis_size("seq")
    devices = 2 * n
    me = 2 * lax.axis_index("seq") + lax.axis_index("ch")
    row_start = me * block
    total_rows = seg_ids.shape[0]
    length = min(SEQ_LEN, total_rows)

    keys = seg_ids + (jnp.arange(total_rows, dtype=jnp.int32) // length) * 65536
    padded = jnp.concatenate([jnp.full((BEFORE,), -1, jnp.int32), keys, jnp.full((block + AFTER,), -2, jnp.int32)])
    near = lax.dynamic_slice_in_dim(padded, row_start, BEFORE + block + AFTER)
    window = near
    ids = jnp.broadcast_to(window.astype(F32)[:, None], (window.shape[0], LANES))

    table = position_table(FIR, (filt_w1.shape[0] - 1) // 2)
    norm_tail = jnp.sqrt(-jnp.expm1(-2.0 * tail_rate))
    vectors = (norm1_gain, norm2_gain, long_bias, tail_gain, tail_rate, norm_tail, short_weight)
    filt_b1 = filt_b1[None, :]
    marks = jnp.concatenate([keys[::block], keys[block - 1 :: block]])
    (tok, g, win, wout, up_other, down_other, gains, vec, n1, proj, x0, u, heads, base, car, dist, rest, enter) = forward(
        n, marks, tokens, grad_out, jnp.transpose(in_weight, (1, 0, 2)), out_weight, up_weight, down_weight,
        filt_w3, table, filt_w1, filt_b1, filt_w2, vectors, ids)

    summed = n == 16
    results = backward(
        n, summed, marks, tok, ids, dist, rest, enter, g, gains, vec, wout, x0, base, car, u, n1, heads,
        (up_weight, up_other), (down_weight, down_other), win, proj)
    if not summed:
        results = reduce_plain(n, *results[:5])
    part_a, part_b, small_a, small_b, out, gtok = results

    (out, gtok, gain_one, in_grad, short_grad, w1_grad, b1_grad, w2_grad, w3_grad, bias_grad, tail_gain_grad, rate_grad,
     out_grad, gain_two, up_grad, down_grad) = finish(
        part_a, part_b, small_a, small_b, gains, vec, table, filt_w1, filt_b1, filt_w2, out, gtok)
    return (
        out, gtok, gain_one, jnp.transpose(in_grad, (1, 0, 2)), short_grad, w1_grad, b1_grad, w2_grad, w3_grad, bias_grad,
        tail_gain_grad, rate_grad, out_grad.T, gain_two, up_grad, down_grad.T,
    )


def solution(mesh):
    placed = (
        P("seq", "ch"),
        P(),
        P("ch"),
        P(None, None, "ch"),
        P(None, None, "ch"),
        P(),
        P(),
        P(),
        P(None, "ch"),
        P("ch"),
        P("ch"),
        P("ch"),
        P("ch", None),
        P("ch"),
        P(None, "ch"),
        P("ch", None),
        P("seq", "ch"),
    )
    return jax.shard_map(
        on_device,
        mesh=mesh,
        in_specs=placed,
        out_specs=(
            P("seq", "ch"),
            P("seq", "ch"),
            P(),
            P("seq", None, "ch"),
            P(),
            P(),
            P(),
            P(),
            P(),
            P(),
            P(),
            P(),
            P("ch", "seq"),
            P(),
            P("seq", "ch"),
            P("ch", "seq"),
        ),
        check_vma=False,
    )
```

```python
import functools

import jax
import jax.numpy as jnp
from jax import lax
from jax.experimental import pallas as pl
from jax.experimental.pallas import tpu as pltpu
from jax.sharding import PartitionSpec as P

FIR = 32
SEQ_LEN = 16384
DOC_MOST = 8192
EPSILON = 1e-05
FREQUENCY = 0.4
HIGHEST = lax.Precision.HIGHEST
MESH = pl.DeviceIdType.MESH
F32, BF16 = jnp.float32, jnp.bfloat16

BEFORE = 48
AFTER = 80
LANES = 128
BLOCK = 256
CHUNK = 64
SUMS = 48
HEAD = 16
VMEM_LIMIT = 56 << 20
ROOT_TWO_OVER_PI = 0.7978845608028654


def position_table(filter_len, band_count):
    places = jnp.arange(filter_len, dtype=F32)
    harmonics = jnp.arange(1, band_count + 1, dtype=F32)
    angles = FREQUENCY * places[:, None] * harmonics[None, :]
    return jnp.concatenate([places[:, None] / filter_len, jnp.cos(angles), jnp.sin(angles)], axis=1)


def of(ref, start, size):
    return pl.ds(pl.multiple_of(start, size), size)


def filter_layers(table, w1, b1, w2):
    pre_one = jnp.dot(table, w1, precision=HIGHEST, preferred_element_type=F32) + b1
    hidden_one = jnp.sin(pre_one)
    pre_two = jnp.dot(hidden_one, w2, precision=HIGHEST, preferred_element_type=F32)
    return pre_one, hidden_one, pre_two, jnp.sin(pre_two)


def filter_window(start, count, full):
    channel = (start + lax.broadcasted_iota(jnp.int32, (FIR, count), 1)).astype(F32)
    place = lax.broadcasted_iota(jnp.int32, (FIR, count), 0).astype(F32)
    return jnp.exp(-(0.5 + 3.0 * channel / full) * place / FIR)


def device_of(index):
    return (index // 2, index % 2)


class Pushing:
    def __init__(self, n, reach, backward, source, slots, send_sem, recv_sem):
        self.total, self.reach = 2 * n, reach
        self.me = 2 * lax.axis_index("seq") + lax.axis_index("ch")
        self.ahead = -1 if backward else 1
        self.place = self.total - 1 - self.me if backward else self.me
        self.source, self.slots, self.send_sem, self.recv_sem = source, slots, send_sem, recv_sem

    def greet(self, barrier):
        for k in range(self.reach):

            @pl.when(self.place - 1 - k >= 0)
            def _():
                pl.semaphore_signal(
                    barrier, inc=1, device_id=device_of(self.me - self.ahead * (1 + k)), device_id_type=MESH)

    def await_greetings(self, barrier, others):
        following = self.total - 1 - self.place
        for count in range(0, self.reach + 1):
            if count + others:

                @pl.when((following >= count) if count == self.reach else (following == count))
                def _():
                    pl.semaphore_wait(barrier, count + others)

    def copy(self, k):
        return pltpu.make_async_remote_copy(
            src_ref=self.source, dst_ref=self.slots.at[k], send_sem=self.send_sem.at[k], recv_sem=self.recv_sem.at[k],
            device_id=device_of(self.me + self.ahead * (1 + k)), device_id_type=MESH)

    def start(self):
        for k in range(self.reach):

            @pl.when(self.place + 1 + k < self.total)
            def _():
                self.copy(k).start()

    def take(self, use):
        for k in range(self.reach):

            @pl.when(self.place - 1 - k >= 0)
            def _():
                self.copy(k).wait_recv()
                use(k, self.slots[k])

            @pl.when(self.place + 1 + k < self.total)
            def _():
                self.copy(k).wait_send()


def row_stats(values):
    center = jnp.mean(values, axis=1, keepdims=True)
    shifted = values - center
    inverse = lax.rsqrt(jnp.mean(shifted * shifted, axis=1, keepdims=True) + EPSILON)
    return shifted * inverse, inverse


def forward_kernel(n, rows, reach, marks, tokens, gout, w_in, w_out, w_up, w_down, filt_w3, table, filt_w1, filt_b1, filt_w2,
                   norms_a, norms_b, biases, tails, decays, nus, shorts, ids,
                   tok_o, g_o, in_o, out_o, up_o, down_o, gains_o, vec_o,
                   n1_o, proj_o, x0_o, u_o, heads_o, long_o, car_o, dist_o, rest_o, enter_o,
                   tok_v, g_v, in_v, out_v, gains_v, vec_v, gains, head, n1_s, proj_s, u_s, state_s, end_s, slots_s,
                   local_sem, store_sem, send_sem, recv_sem, push_send, push_recv):
    block, full = rows // 2, in_v.shape[1]
    width = full // 2
    steps = full // BLOCK
    two = range(BLOCK // LANES)
    step = pl.program_id(0)
    s, c = lax.axis_index("seq"), lax.axis_index("ch")
    barrier = pltpu.get_barrier_semaphore()
    pushing = Pushing(n, reach, False, end_s, slots_s, push_send, push_recv)
    partner = (s, 1 - c)
    cols = pl.ds(pl.multiple_of(c * width, width), width)
    early = [(gains, gains_v.at[pl.ds(0, 8), cols]), (filt_w3, gains_v.at[pl.ds(8, filt_w3.shape[0]), cols])]
    late = []
    for i in range(width // LANES):
        source = pl.ds(i * LANES, LANES)
        paired = pl.ds(pl.multiple_of((2 * i + c) * LANES, LANES), LANES)
        early += [
            (head.at[:, source], vec_v.at[pl.ds(0, HEAD), paired]),
            (w_in.at[:, :, source], in_v.at[:, :, paired]),
        ]
        late.append((w_out.at[source, :], out_v.at[paired, :]))

    def remote(src, dst, k, target=partner):
        return pltpu.make_async_remote_copy(
            src_ref=src, dst_ref=dst, send_sem=send_sem.at[k], recv_sem=recv_sem.at[k],
            device_id=target, device_id_type=MESH)

    halves = [(early[k], k) for k in range(len(early))] + [(late[k], len(early) + k) for k in range(len(late))]
    count = len(halves)
    far = [remote(w_up, up_o, count), remote(w_down, down_o, count + 1)]
    at_tokens = count + 2

    left, right = pl.ds(0, width), pl.ds(width, width)
    first, second = pl.ds(0, block), pl.ds(block, block)
    ahead, tail = pl.ds(block - BEFORE, block + BEFORE), pl.ds(rows - BEFORE, BEFORE)
    main = pl.ds(BEFORE, block)
    keeps = [
        [(tokens.at[first, :], tok_v.at[main, left]), (gout.at[first, :], g_v.at[:, left])],
        [(tokens.at[ahead, :], tok_v.at[:, right]), (gout.at[second, :], g_v.at[:, right])],
    ]
    sends = [
        [(tokens.at[ahead, :], tok_v.at[:, left]), (gout.at[second, :], g_v.at[:, left])],
        [(tokens.at[first, :], tok_v.at[main, right]), (gout.at[first, :], g_v.at[:, right])],
    ]

    def edge(which, target):
        return remote(
            tokens.at[tail, :], tok_v.at[pl.ds(0, BEFORE), (left, right)[which]], at_tokens + 2 + which, target)

    def for_core(action):
        for which in range(2):

            @pl.when(c == which)
            def _():
                action(which)

    stores = [(tok_v, tok_o), (gains_v, gains_o), (vec_v, vec_o), (in_v, in_o), (g_v, g_o), (out_v, out_o)]

    def store(k):
        return pltpu.make_async_copy(*stores[k], store_sem.at[k])

    @pl.when(step == 0)
    def _():
        pushing.greet(barrier)
        pl.semaphore_signal(barrier, inc=1, device_id=partner, device_id_type=MESH)

        @pl.when((c == 0) & (s > 0))
        def _():
            for k in range(2):
                pl.semaphore_signal(barrier, inc=1, device_id=(s - 1, k), device_id_type=MESH)

        gains[...] = jnp.zeros_like(gains)
        head[...] = jnp.zeros_like(head)
        for ref, row, value in ((gains, 0, norms_a), (gains, 1, norms_b), (head, 2, biases), (head, 3, tails),
                                (head, 4, decays), (head, 5, nus)):
            ref[row : row + 1, :] = value[...].reshape(1, width)
        for j in range(3):
            for t in range(3):
                head[6 + 3 * j + t : 7 + 3 * j + t, :] = shorts[j, t : t + 1, :]

        def begin_own(which):
            for k, (src, dst) in enumerate(keeps[which]):
                pltpu.make_async_copy(src, dst, local_sem.at[at_tokens + k]).start()

        for_core(begin_own)
        for (src, dst), k in halves:
            pltpu.make_async_copy(src, dst, local_sem.at[k]).start()

        @pl.when(s < n - 1)
        def _():
            pushing.await_greetings(barrier, 2)

        @pl.when(s == n - 1)
        def _():
            pushing.await_greetings(barrier, 1)

        def begin(which):
            remote(*sends[which][0], at_tokens).start()

            @pl.when(s < n - 1)
            def _():
                edge(which, (s + 1, 0)).start()

        for_core(begin)
        for (src, dst), k in halves[: len(early)]:
            remote(src, dst, k).start()
        for_core(lambda which: remote(*sends[which][1], at_tokens + 1).start())
        for (src, dst), k in halves[len(early) :]:
            remote(src, dst, k).start()
        for copy in far:
            copy.start()

        def distances(j, _):
            at = pl.ds(pl.multiple_of(j * 32, 32), 32)
            start = pl.multiple_of(BEFORE + j * 32, 16)
            own = ids[pl.ds(start, 32), :]
            before = after = jnp.zeros((32, LANES), F32)
            for k in range(1, FIR):
                before += jnp.where(own == ids[pl.ds(start - k, 32), :], 1.0, 0.0)
                after += jnp.where(own == ids[pl.ds(start + k, 32), :], 1.0, 0.0)
            dist_o[at, :] = before
            rest_o[at, :] = after
            return 0

        lax.fori_loop(0, block // 32, distances, 0)

        def take_tokens(which):
            remote(*sends[which][0], at_tokens).wait_send()
            remote(*sends[1 - which][0], at_tokens).wait_recv()
            pltpu.make_async_copy(*keeps[which][0], local_sem.at[at_tokens]).wait()

            @pl.when(s < n - 1)
            def _():
                edge(which, (s + 1, 0)).wait_send()

            if which == 0:

                @pl.when(s > 0)
                def _():
                    for k in range(2):
                        edge(k, partner).wait_recv()

        for_core(take_tokens)
        hidden_two = filter_layers(table[...], filt_w1[...], filt_b1[...], filt_w2[...])[3]
        for (src, dst), k in halves[:2]:
            pltpu.make_async_copy(src, dst, local_sem.at[k]).wait()
            remote(src, dst, k).wait()
        store(0).start()
        store(1).start()

        def normed(j, _):
            at = pl.ds(pl.multiple_of(j * 80, 16), 80)
            values = jnp.where(ids[at, 0:1] >= 0.0, tok_v[at, :].astype(F32), 0.0)
            n1_s[at, :] = (row_stats(values)[0] * gains_v[0:1, :]).astype(BF16)
            return 0

        lax.fori_loop(0, (BEFORE + block) // 80, normed, 0)
        n1_o[...] = n1_s[pl.ds(BEFORE, block), :]
        for (src, dst), k in halves[2 : len(early)]:
            pltpu.make_async_copy(src, dst, local_sem.at[k]).wait()
            remote(src, dst, k).wait()
        taps = jnp.dot(hidden_two, gains_v[8:, :], precision=HIGHEST, preferred_element_type=F32)
        taps *= filter_window(0, full, full)
        for i in range(width // LANES):
            for half in range(2):
                source = half * width + i * LANES
                vec_v[HEAD : HEAD + FIR, (2 * i + half) * LANES : (2 * i + half + 1) * LANES] = (
                    taps[:, source : source + LANES])
        store(2).start()
        store(3).start()

    @pl.when(step < steps)
    def _():
        lanes = [pl.ds(pl.multiple_of((2 * step + b) * LANES, LANES), LANES) for b in two]
        wide = pl.ds(pl.multiple_of(step * BLOCK, BLOCK), BLOCK)
        for t in range(3):
            part = jnp.dot(n1_s[...], in_v[t, :, wide], preferred_element_type=F32).astype(BF16)
            for b in two:
                proj_o[t, b] = part[:, b * LANES : (b + 1) * LANES]
                proj_s[t, b] = part[:, b * LANES : (b + 1) * LANES].astype(F32)

        def convolved(start, size):
            own = ids[pl.ds(start, size), :]
            same = [None] + [own == ids[pl.ds(start - j, size), :] for j in (1, 2)]
            results = []
            for b in two:
                streams = []
                for t in range(3):
                    value = vec_v[6 + t : 7 + t, lanes[b]] * proj_s[t, b, pl.ds(start, size), :]
                    for j in (1, 2):
                        tap = vec_v[6 + 3 * j + t : 7 + 3 * j + t, lanes[b]]
                        value += jnp.where(same[j], tap * proj_s[t, b, pl.ds(start - j, size), :], 0.0)
                    streams.append(value)
                gated = (streams[0] * streams[2]).astype(BF16).astype(F32)
                u_s[2 * step + b, pl.ds(start, size), :] = gated
                u_o[b, pl.ds(start, size), :] = gated
                results.append(streams)
            return results

        convolved(16, 32)
        for b, streams in enumerate(convolved(BEFORE, 8)):
            heads_o[0:8, b * LANES : (b + 1) * LANES] = streams[2]
            heads_o[8:16, b * LANES : (b + 1) * LANES] = streams[0]
            u_o[b, 0:16, :] = jnp.zeros((16, LANES), F32)
            u_s[2 * step + b, 0:16, :] = jnp.zeros((16, LANES), F32)

        def conv_chunk(j, _):
            start = pl.multiple_of(BEFORE + j * 32, 16)
            for b, streams in enumerate(convolved(start, 32)):
                x0_o[b, pl.ds(pl.multiple_of(j * 32, 32), 32), :] = streams[1]
            return 0

        lax.fori_loop(0, block // 32, conv_chunk, 0)

        row_id = lax.broadcasted_iota(jnp.int32, (8, LANES), 0)
        rates = [vec_v[4:5, lanes[b]] for b in two]
        powers = [jnp.exp(-rate * (row_id + 1).astype(F32)) for rate in rates]
        lams = [[jnp.exp(-rate * float(k)) for k in (1, 2, 4)] for rate in rates]
        for b in two:
            state_s[2 * step + b, 0:8, :] = jnp.zeros((8, LANES), F32)

        def scan_group(g, carry):
            start = pl.multiple_of(BEFORE + g * 8, 8)
            own = ids[pl.ds(start, 8), :]
            masks = [(own == ids[pl.ds(start - k, 8), :]) & (row_id >= k) for k in (1, 2, 4)]
            joined = own == jnp.broadcast_to(ids[pl.ds(start - 1, 1), :], (8, LANES))
            result = []
            for b in two:
                value = u_s[2 * step + b, pl.ds(start, 8), :]
                for mask, lam, k in zip(masks, lams[b], (1, 2, 4)):
                    value += jnp.where(mask, lam * pltpu.roll(value, k, 0), 0.0)
                value += jnp.where(joined, powers[b] * carry[b], 0.0)
                state_s[2 * step + b, pl.ds(pl.multiple_of(8 + g * 8, 8), 8), :] = value
                result.append(jnp.broadcast_to(value[7:8, :], (8, LANES)))
            return tuple(result)

        zero = jnp.zeros((8, LANES), F32)
        final = lax.fori_loop(0, block // 8, scan_group, (zero,) * len(two), unroll=4)
        for b in two:
            end_s[:, lanes[b]] = final[b][0:1, :]

    @pl.when(step == steps - 1)
    def _():
        pushing.start()

    @pl.when(step >= steps)
    def _():
        i = step - steps
        lanes = [pl.ds(pl.multiple_of((2 * i + b) * LANES, LANES), LANES) for b in two]
        lam = [jnp.exp(-vec_v[4:5, lanes[b]]) for b in two]
        tails = [vec_v[3:4, lanes[b]] * vec_v[5:6, lanes[b]] for b in two]

        def long_chunk(j, _):
            at = pl.ds(pl.multiple_of(j * 32, 32), 32)
            start = pl.multiple_of(BEFORE + j * 32, 16)
            near = dist_o[at, :]
            totals = []
            for b in two:
                previous = state_s[2 * i + b, pl.ds(7 + j * 32, 32), :]
                carried = jnp.where(near >= 1.0, lam[b] * previous, 0.0)
                car_o[b, at, :] = carried
                here = u_s[2 * i + b, pl.ds(start, 32), :]
                totals.append((vec_v[2:3, lanes[b]] + vec_v[16:17, lanes[b]]) * here + tails[b] * carried)
            for k in range(1, FIR):
                same = near >= float(k)
                for b in two:
                    term = vec_v[16 + k : 17 + k, lanes[b]] * u_s[2 * i + b, pl.ds(start - k, 32), :]
                    totals[b] += jnp.where(same, term, 0.0)
            for b in two:
                long_o[b, at, :] = totals[b]
            return 0

        lax.fori_loop(0, block // 32, long_chunk, 0)

    @pl.when(step == steps)
    def _():
        def take_rows(which):
            remote(*sends[which][1], at_tokens + 1).wait_send()
            remote(*sends[1 - which][1], at_tokens + 1).wait_recv()
            pltpu.make_async_copy(*keeps[which][1], local_sem.at[at_tokens + 1]).wait()

        for_core(take_rows)
        for (src, dst), k in halves[len(early) :]:
            pltpu.make_async_copy(src, dst, local_sem.at[k]).wait()
            remote(src, dst, k).wait()
        store(4).start()
        store(5).start()

    @pl.when(step == 2 * steps - 1)
    def _():
        enter_o[...] = jnp.zeros_like(enter_o)
        rate = vec_v[4:5, :]
        last = marks[2 * n + jnp.maximum(pushing.me - 1, 0)]

        def use(k, state):
            same = jnp.where(marks[2 * n + pushing.me - 1 - k] == last, 1.0, 0.0)
            enter_o[...] += same * jnp.exp(-rate * float(block * k)) * state

        pushing.take(use)
        for copy in far:
            copy.wait()
        for k in range(len(stores)):
            store(k).wait()


def forward(n, marks, tokens, gout, w_in, w_out, w_up, w_down, filt_w3, table, filt_w1, filt_b1, filt_w2, vectors, ids):
    rows, width = tokens.shape
    hidden = w_up.shape[1]
    full, block = 2 * width, rows // 2
    window = BEFORE + block
    steps, lane_blocks = full // BLOCK, full // LANES
    reach = min(DOC_MOST // block, 2 * n - 1)
    anywhere = pl.BlockSpec(memory_space=pl.ANY)
    whole = lambda *shape: pl.BlockSpec(shape, lambda i: (0,) * len(shape), pipeline_mode=pl.Buffered(1))
    soon, later = lambda i: jnp.minimum(i, steps - 1), lambda i: jnp.maximum(i - steps, 0)
    stacked = lambda count, place: pl.BlockSpec((BLOCK // LANES, count, LANES), lambda i: (place(i), 0, 0))
    shape = jax.ShapeDtypeStruct
    vmem = pltpu.VMEM
    far = 2 + 3 * (width // LANES) + 2 + 4
    dma = pltpu.SemaphoreType.DMA
    landing = [
        ((window, full), BF16), ((block, full), BF16), ((3, full, full), BF16), ((full, full), BF16),
        ((8 + filt_w3.shape[0], full), F32), ((HEAD + FIR, full), F32),
    ]
    return pl.pallas_call(
        functools.partial(forward_kernel, n, rows, reach),
        name="forward",
        grid=(2 * steps,),
        out_shape=(
            *[shape(*part) for part in landing[:4]],
            shape((full, hidden), BF16),
            shape((hidden, full), BF16),
            *[shape(*part) for part in landing[4:]],
            shape((block, full), BF16),
            shape((3, lane_blocks, window, LANES), BF16),
            shape((lane_blocks, block, LANES), F32),
            shape((lane_blocks, window, LANES), F32),
            shape((16, full), F32),
            shape((lane_blocks, block, LANES), F32),
            shape((lane_blocks, block, LANES), F32),
            shape((block, LANES), F32),
            shape((block, LANES), F32),
            shape((1, full), F32),
        ),
        in_specs=[pl.BlockSpec(memory_space=pltpu.SMEM)] + [anywhere] * 7 + [
            whole(*part.shape) for part in (table, filt_w1, filt_b1, filt_w2, *vectors, ids)],
        out_specs=(
            *[anywhere] * 8,
            whole(block, full),
            pl.BlockSpec((3, BLOCK // LANES, window, LANES), lambda i: (0, soon(i), 0, 0)),
            stacked(block, soon),
            stacked(window, soon),
            pl.BlockSpec((16, BLOCK), lambda i: (0, soon(i))),
            stacked(block, later),
            stacked(block, later),
            whole(block, LANES),
            whole(block, LANES),
            whole(1, full),
        ),
        scratch_shapes=[
            *[vmem(*part) for part in landing],
            vmem((8, width), F32),
            vmem((HEAD, width), F32),
            vmem((window, full), BF16),
            vmem((3, BLOCK // LANES, window, LANES), F32),
            vmem((lane_blocks, window, LANES), F32),
            vmem((lane_blocks, 8 + block, LANES), F32),
            vmem((1, full), F32),
            vmem((reach, 1, full), F32),
            dma((far,)), dma((6,)), dma((far,)), dma((far,)), dma((reach,)), dma((reach,)),
        ],
        compiler_params=pltpu.CompilerParams(collective_id=0, has_side_effects=True, vmem_limit_bytes=VMEM_LIMIT),
    )(marks, tokens, gout, w_in, w_out, w_up, w_down, filt_w3, table, filt_w1, filt_b1, filt_w2, *vectors, ids)


TILE = 512
PART = TILE // 2
STAGES = 5
FEED_ORDERS = ((0, 1, 2, 3), (0, 2, 3, 1), (1, 0, 2, 3), (1, 2, 3, 0))
MIX_ORDERS = ((0, 1, 2, 3), (1, 0, 2, 3), (2, 0, 1, 3))


class Summing:
    def __init__(self, slots, rows, staged, first, second, third, fourth, fifth, send_sem, recv_sem):
        self.slots, self.rows, self.staged = slots, rows, staged
        self.held = (first, second, third, fourth, fifth)
        self.send_sem, self.recv_sem = send_sem, recv_sem
        self.s, self.c = lax.axis_index("seq"), lax.axis_index("ch")
        self.bits = [(self.s // (1 << b)) % 2 for b in range(4)]
        self.peers = [(self.s + (1 - 2 * bit) * (1 << b), self.c) for b, bit in enumerate(self.bits)]
        self.partner = (self.s, 1 - self.c)

    @staticmethod
    def scratch(tiles, slots, rows):
        parts = len(FEED_ORDERS)
        return [
            pltpu.VMEM((2, 2, parts, 2, 2, 2, 2, rows, LANES), BF16),
            pltpu.VMEM((slots, parts, 2, 2, 2, 2, rows, LANES), BF16),
            pltpu.VMEM((slots, parts, 2, 2, 2, rows, LANES), BF16),
            pltpu.VMEM((slots, parts, 2, 2, rows, LANES), BF16),
            pltpu.VMEM((slots, parts, 2, rows, LANES), BF16),
            pltpu.VMEM((slots, parts, rows, LANES), BF16),
            pltpu.SemaphoreType.DMA((tiles, 1 + 4 * parts)),
            pltpu.SemaphoreType.DMA((tiles, 1 + 4 * parts)),
        ]

    def greet(self, barrier):
        for peer in [self.partner] + self.peers:
            pl.semaphore_signal(barrier, inc=1, device_id=peer, device_id_type=MESH)

    def remote(self, src, dst, tile, k, target):
        return pltpu.make_async_remote_copy(
            src_ref=src, dst_ref=dst, send_sem=self.send_sem.at[tile, k], recv_sem=self.recv_sem.at[tile, k],
            device_id=target, device_id_type=MESH)

    def stage_in(self, tile, whose, part, order, grad):
        for q in range(16):
            at = [(q >> bit) & 1 for bit in order]
            self.staged[(tile % 2, whose, part, *at)] = grad[q * self.rows : (q + 1) * self.rows]

    def copies(self, tile, stage, orders):
        slot = tile % self.slots
        if stage == 0:
            parts = pl.ds(0, len(orders))
            return [self.remote(self.staged.at[tile % 2, 1, parts], self.held[0].at[slot, parts], tile, 0, self.partner)]
        result = []
        for part, order in enumerate(orders):
            bit = order[stage - 1]
            src, dst = self.held[stage - 1].at[slot, part, 1 - self.bits[bit]], self.held[stage].at[slot, part]
            result.append(self.remote(src, dst, tile, 1 + 4 * (stage - 1) + part, self.peers[bit]))
        return result

    def start(self, tile, stage, orders):
        for copy in self.copies(tile, stage, orders):
            copy.start()

    def advance(self, tile, stage, orders, total):
        for copy in self.copies(tile, stage, orders):
            copy.wait()
        slot = tile % self.slots
        if stage == 0:

            def add(part, _):
                for q in range(16):
                    at = (q >> 3, q >> 2 & 1, q >> 1 & 1, q & 1)
                    self.held[0][(slot, part, *at)] += self.staged[(tile % 2, 0, part, *at)]
                return 0

            lax.fori_loop(0, len(orders), add, 0)
        else:
            for part, order in enumerate(orders):
                mine = self.bits[order[stage - 1]]
                for e in range(1 << (4 - stage)):
                    inner = [(e >> (3 - stage - k)) & 1 for k in range(4 - stage)]
                    source = self.held[stage - 1][(slot, part, mine, *inner)]
                    if stage == STAGES - 1:
                        total(tile, part, source.astype(F32) + self.held[stage][slot, part].astype(F32))
                    else:
                        self.held[stage][(slot, part, *inner)] += source
        if stage < STAGES - 1:
            self.start(tile, stage + 1, orders)


class Joining:
    def __init__(self, sums, held, arrived, send_sem, recv_sem):
        self.held, self.arrived, self.send_sem, self.recv_sem = held, arrived, send_sem, recv_sem
        self.targets = [sums.partner] + sums.peers

    @staticmethod
    def scratch(*shape):
        return [pltpu.VMEM((STAGES,) + shape, F32), pltpu.VMEM((STAGES,) + shape, F32),
                pltpu.SemaphoreType.DMA((STAGES,)), pltpu.SemaphoreType.DMA((STAGES,))]

    def copy(self, stage):
        return pltpu.make_async_remote_copy(
            src_ref=self.held.at[stage], dst_ref=self.arrived.at[stage], send_sem=self.send_sem.at[stage],
            recv_sem=self.recv_sem.at[stage], device_id=self.targets[stage], device_id_type=MESH)

    def start(self, stage):
        self.copy(stage).start()

    def advance(self, stage, result):
        self.copy(stage).wait()
        total = self.held[stage] + self.arrived[stage]
        if stage == STAGES - 1:
            result(total)
        else:
            self.held[stage + 1] = total
            self.start(stage + 1)


def contract(left, right, dims):
    return lax.dot_general(left, right, (dims, ((), ())), preferred_element_type=F32)


def contract(left, right, dims):
    return lax.dot_general(left, right, (dims, ((), ())), preferred_element_type=F32)


TILES = 6
EPILOGUE, GATE, TAPS, BACK = TILES, TILES + 1, TILES + 2, TILES + 3
LAGS = (1, 3, 5, 6, 7)
HALO = 80


def backward_kernel(n, block, reach, summed, marks, tok, ids, dist_s, rest_s, enter, g, gains, vec, wout, x0, base, car, u, n1, heads,
                    wup_a, wup_b, wdn_a, wdn_b, win, proj, *refs):
    full = g.shape[1]
    width, lane_blocks = full // 2, full // LANES
    steps = full // BLOCK
    last_back = BACK + steps - 1
    (grads_o, small_a, small_b, out_o, gtok_o), refs = refs[:5], refs[5:]
    (mixed_s, middle_s, n2_s, gn_s, gout_s, out_s, gmid_s, long_s, car_s, glong_s, q_s, gc_s, gp_s, proj_s,
     taps_s, first_s, slots_s, joined_s, halo_s, halo_r, head_s,
     push_send, push_recv, halo_sem, *buffers) = refs
    step = pl.program_id(0)
    groups = block // 32
    barrier = pltpu.get_barrier_semaphore()
    pushing = Pushing(n, reach, True, first_s, slots_s, push_send, push_recv)
    c = lax.axis_index("ch")
    lanes_of = lambda b: pl.ds(pl.multiple_of(b * LANES, LANES), LANES)
    if summed:
        sums = Summing(TILES, full // 16, *buffers[:8])
        held_b = buffers[12]
        joins = [(Joining(sums, *buffers[8:12]), lambda value: small_a.__setitem__(Ellipsis, value), TAPS)]
        for k in range(steps):
            at = slice(k * BLOCK, (k + 1) * BLOCK)
            joins.append((Joining(sums, *[ref.at[k] for ref in buffers[12:16]]),
                          lambda value, at=at: small_b.__setitem__((slice(None), at), value), BACK + k))
        local_sem, exchange_send, exchange_recv = buffers[16:]

        def shares(k, src, dst):
            at = pl.ds(pl.multiple_of(c * block, block), block)
            of_core = lambda which: src.at[:, pl.ds(pl.multiple_of(which * width, width), width)]
            return (
                pltpu.make_async_copy(of_core(c), dst.at[at, :], local_sem.at[k]),
                pltpu.make_async_remote_copy(
                    src_ref=of_core(1 - c), dst_ref=dst.at[at, :], send_sem=exchange_send.at[k],
                    recv_sem=exchange_recv.at[k], device_id=sums.partner, device_id_type=MESH),
            )

    halo_copy = pltpu.make_async_remote_copy(
        src_ref=halo_s, dst_ref=halo_r, send_sem=halo_sem.at[0], recv_sem=halo_sem.at[1],
        device_id=device_of(pushing.me - 1), device_id_type=MESH)

    @pl.when(step == 0)
    def _():
        pushing.greet(barrier)
        if summed:
            sums.greet(barrier)

        last = ids[pl.ds(BEFORE - 1, 1), :]
        for b in range(lane_blocks):
            lanes = slice(b * LANES, (b + 1) * LANES)
            rate, tail = vec[4:5, lanes], vec[3:4, lanes] * vec[5:6, lanes]
            state = enter[0:1, lanes]

            def mix(j, _):
                at = pl.ds(pl.multiple_of(j * 32, 32), 32)
                passed = (lax.broadcasted_iota(jnp.int32, (32, LANES), 0) + (j * 32 + 1)).astype(F32)
                same = ids[pl.ds(pl.multiple_of(BEFORE + j * 32, 16), 32), :] == last
                entered = jnp.where(same, jnp.exp(-rate * passed) * state, 0.0)
                car_s[b, at, :] = car[b, at, :] + entered
                long = base[b, at, :] + tail * entered
                long_s[b, at, :] = long
                mixed_s[at, lanes] = (long * x0[b, at, :]).astype(BF16)
                return 0

            lax.fori_loop(0, groups, mix, 0)
        middle_s[...] = jnp.dot(mixed_s[...], wout[...], preferred_element_type=F32)

        def norm(j, _):
            at = pl.ds(pl.multiple_of(j * 32, 32), 32)
            start = pl.multiple_of(BEFORE + j * 32, 16)
            values = middle_s[at, :] + tok[pl.ds(start, 32), :].astype(F32)
            middle_s[at, :] = values
            out_s[at, :] = values
            n2_s[at, :] = (row_stats(values)[0] * gains[1:2, :]).astype(BF16)
            gn_s[at, :] = jnp.zeros_like(values)
            return 0

        lax.fori_loop(0, groups, norm, 0)
        pushing.await_greetings(barrier, 5 if summed else 0)

    def put(tile, part, grad):
        for half in range(2):
            if summed:
                sums.stage_in(tile, (half + c) % 2, part, MIX_ORDERS[part], grad[half])
            else:
                grads_o[0, half, :, part * LANES : (part + 1) * LANES] = grad[half]

    def note(row, i, lanes, value):
        if summed:
            held_b[i, 0, row : row + 1, lanes] = value
        else:
            at = pl.ds(pl.multiple_of(i * BLOCK + lanes.start, LANES), lanes.stop - lanes.start)
            small_b[row : row + 1, at] = value

    def feed(half, wup, wdn):
        n2, rows = n2_s[...], g[...]
        up = jnp.dot(n2, wup[...], preferred_element_type=F32)
        pulled = contract(rows, wdn[...], ((1,), (1,)))
        square = up * up
        inner = ROOT_TWO_OVER_PI * up * (1.0 + 0.044715 * square)
        bent = jnp.tanh(inner)
        part = 0.5 * (1.0 + bent)
        active = (up * part).astype(BF16)
        slope = part + (0.5 * ROOT_TWO_OVER_PI) * up * (1.0 - bent * bent) * (1.0 + 0.134145 * square)
        g_up = (pulled * slope).astype(BF16)
        out_s[...] += jnp.dot(active, wdn[...], preferred_element_type=F32)
        gn_s[...] += contract(g_up, wup[...], ((1,), (1,)))
        pair = (contract(n2, g_up, ((0,), (0,))).astype(BF16), contract(rows, active, ((0,), (0,))).astype(BF16))
        for k in range(2):
            if summed:
                for j in range(2):
                    columns = pair[k][:, j * LANES : (j + 1) * LANES]
                    sums.stage_in(step, half, 2 * k + j, FEED_ORDERS[2 * k + j], columns)
            else:
                grads_o[0, (half + c) % 2, :, k * PART : (k + 1) * PART] = pair[k]

    row_id = lax.broadcasted_iota(jnp.int32, (8, LANES), 0)
    zero = jnp.zeros((8, LANES), F32)

    @pl.when(step < TILES)
    def _():
        feed(0, wup_a, wdn_a)

    @pl.when(step == EPILOGUE)
    def _():
        if summed:
            for copy in shares(0, out_s, out_o):
                copy.start()
        else:
            out_o[...] = out_s[...]

        def back(j, total):
            at = pl.ds(pl.multiple_of(j * 32, 32), 32)
            normal, inverse = row_stats(middle_s[at, :])
            grad = gn_s[at, :]
            total += jnp.sum(grad * normal, axis=0, keepdims=True)
            scaled = grad * gains[1:2, :]
            cross = jnp.mean(scaled * normal, axis=1, keepdims=True)
            result = g[at, :].astype(F32) + inverse * (
                scaled - jnp.mean(scaled, axis=1, keepdims=True) - normal * cross)
            gmid_s[at, :] = result
            gout_s[at, :] = result.astype(BF16)
            gn_s[at, :] = jnp.zeros_like(grad)
            return total

        gain_two = lax.fori_loop(0, groups, back, jnp.zeros((1, full), F32))
        head_s[...] = jnp.zeros_like(head_s)
        head_s[0:1, :] = gain_two
        for i in range(steps):
            gmix = contract(gout_s[...], wout[i * BLOCK : (i + 1) * BLOCK, :], ((1,), (1,)))
            for k in range(BLOCK // LANES):
                b = i * (BLOCK // LANES) + k
                part = gmix[:, k * LANES : (k + 1) * LANES]
                glong_s[b, 0:block, :] = part * x0[b]
                long_s[b] = part * long_s[b]

    @pl.when(step == BACK)
    def _():
        for i in range(steps):
            for row in range(10, 16):
                note(row, i, slice(0, BLOCK), jnp.zeros((1, BLOCK), F32))
        joined_s[...] = jnp.zeros_like(joined_s)
        rate = vec[4:5, :]
        following = 2 * n + jnp.minimum(pushing.me + 1, 2 * n - 1)
        lasts = (marks[2 * n + pushing.me], marks[following])

        def use(k, state):
            first = marks[pushing.me + 1 + k]
            for row in range(2):
                if k >= row:
                    same = jnp.where(first == lasts[row], 1.0, 0.0)
                    joined_s[row : row + 1, :] += same * jnp.exp(-rate * float(block * (k - row) + 1)) * state

        pushing.take(use)

        @pl.when(pushing.me > 0)
        def _():
            halo_copy.wait_send()

        @pl.when(pushing.me < 2 * n - 1)
        def _():
            halo_copy.wait_recv()

        for b in range(lane_blocks):
            glong_s[b, block : block + 48, :] = halo_r[0:48, b * LANES : (b + 1) * LANES]

    @pl.when((step >= BACK) & (step <= last_back))
    def _():
        i = step - BACK
        two = range(2)
        lanes = [lanes_of(2 * i + k) for k in two]
        rates = [vec[4:5, lanes[k]] for k in two]
        scales = [vec[2:3, lanes[k]] - vec[3:4, lanes[k]] * vec[5:6, lanes[k]] for k in two]
        mine = [joined_s[0:1, lanes[k]] for k in two]
        for k in two:
            for s in range(3):
                proj_s[s, k] = proj[s, k].astype(F32)
        last = ids[pl.ds(BEFORE + block - 1, 1), :]

        def conv_at(s, k, start, size, same):
            value = vec[6 + s : 7 + s, lanes[k]] * proj_s[s, k, pl.ds(start, size), :]
            for j in (1, 2):
                tap = vec[6 + 3 * j + s : 7 + 3 * j + s, lanes[k]]
                value += jnp.where(same[j - 1], tap * proj_s[s, k, pl.ds(start - j, size), :], 0.0)
            return value

        def chunk(j, totals):
            at = pl.ds(pl.multiple_of(j * 32, 32), 32)
            start = pl.multiple_of(BEFORE + j * 32, 16)
            own = ids[pl.ds(start, 32), :]
            left = (block - 1 - j * 32 - lax.broadcasted_iota(jnp.int32, (32, LANES), 0)).astype(F32)
            after = rest_s[at, :]
            near = dist_s[at, :]
            grads, result = [], []
            for k in two:
                b = 2 * i + k
                state = q_s[b, at, :] + jnp.where(own == last, jnp.exp(-rates[k] * left) * mine[k], 0.0)
                result.append(totals[k] + jnp.sum((car_s[b, at, :] * state).reshape(4, 8, LANES), axis=0))
                grads.append(scales[k] * glong_s[b, at, :] + state)
            for tap in range(FIR):
                same = after >= float(tap)
                for k in two:
                    term = vec[16 + tap : 17 + tap, lanes[k]] * glong_s[2 * i + k, pl.ds(j * 32 + tap, 32), :]
                    grads[k] += jnp.where(same, term, 0.0)
            same = [near >= 1.0, near >= 2.0]
            for k in two:
                gc_s[0, k, at, :] = grads[k] * conv_at(2, k, start, 32, same)
                gc_s[1, k, at, :] = long_s[2 * i + k, at, :]
                gc_s[2, k, at, :] = grads[k] * conv_at(0, k, start, 32, same)
            return tuple(result)

        crossed = lax.fori_loop(0, groups, chunk, (zero, zero))
        for k in two:
            note(9, i, slice(k * LANES, (k + 1) * LANES), jnp.sum(crossed[k], axis=0, keepdims=True))

    if summed:

        def fed(tile, part, value):
            grads_o[:, pl.ds(pl.multiple_of(tile * TILE + part * LANES, LANES), LANES)] = value

        def mixed(tile, part, value):
            at = TILES * TILE + (tile - TILES) * len(MIX_ORDERS) * LANES + part * LANES
            grads_o[:, pl.ds(pl.multiple_of(at, LANES), LANES)] = value

        for stage in range(STAGES - 1, -1, -1):
            since, early = step - 1 - stage, step - LAGS[stage]

            @pl.when((early >= 0) & (early < TILES))
            def _():
                sums.advance(early, stage, FEED_ORDERS, fed)

            @pl.when((since == GATE) | ((since >= BACK) & (since <= last_back)))
            def _():
                sums.advance(since - 1 - since // BACK, stage, MIX_ORDERS, mixed)

            for join, result, begun in joins:

                @pl.when(since == begun)
                def _():
                    join.advance(stage, result)

    @pl.when(step < TILES)
    def _():
        feed(1, wup_b, wdn_b)
        if summed:
            sums.start(step, 0, FEED_ORDERS)

    @pl.when(step == GATE)
    def _():
        for i in range(steps):
            piece = contract(gout_s[...], mixed_s[:, i * BLOCK : (i + 1) * BLOCK], ((0,), (0,))).astype(BF16)
            put(TILES, i, [piece[:, half * LANES : (half + 1) * LANES] for half in range(2)])
        if summed:
            sums.start(TILES, 0, MIX_ORDERS)

    @pl.when(step == GATE)
    def _():
        rates = [vec[4:5, b * LANES : (b + 1) * LANES] for b in range(lane_blocks)]
        tails = [vec[3:4, b * LANES : (b + 1) * LANES] * vec[5:6, b * LANES : (b + 1) * LANES] for b in range(lane_blocks)]
        lams = [[jnp.exp(-rate * float(k)) for k in (1, 2, 4)] for rate in rates]
        powers = [jnp.exp(-rate * (8 - row_id).astype(F32)) for rate in rates]

        def scan_group(i, carry):
            at = block // 8 - 1 - i
            to = pl.ds(pl.multiple_of(at * 8, 8), 8)
            start = pl.multiple_of(BEFORE + at * 8, 8)
            own = ids[pl.ds(start, 8), :]
            masks = [(own == ids[pl.ds(start + k, 8), :]) & (row_id < 8 - k) for k in (1, 2, 4)]
            joined = own == jnp.broadcast_to(ids[pl.ds(start + 8, 1), :], (8, LANES))
            states, biases, carries = [], [], []
            for b in range(lane_blocks):
                grad = glong_s[b, to, :]
                value = grad * tails[b]
                for mask, lam, k in zip(masks, lams[b], (1, 2, 4)):
                    value += jnp.where(mask, lam * pltpu.roll(value, 8 - k, 0), 0.0)
                value += jnp.where(joined, powers[b] * carry[0][b], 0.0)
                q_s[b, to, :] = value
                states.append(jnp.broadcast_to(value[0:1, :], (8, LANES)))
                biases.append(carry[1][b] + grad * u[b, pl.ds(start, 8), :])
                carries.append(carry[2][b] + grad * car_s[b, to, :])
            return tuple(states), tuple(biases), tuple(carries)

        many = (zero,) * lane_blocks
        states, biases, carries = lax.fori_loop(0, block // 8, scan_group, (many, many, many), unroll=2)
        for b in range(lane_blocks):
            lanes = slice(b * LANES, (b + 1) * LANES)
            first_s[:, lanes] = states[b][0:1, :]
            head_s[1:2, lanes] = jnp.sum(biases[b], axis=0, keepdims=True)
            head_s[2:3, lanes] = jnp.sum(carries[b], axis=0, keepdims=True)
            halo_s[0:48, lanes] = glong_s[b, 0:48, :]
            halo_s[48:56, lanes] = q_s[b, 0:8, :]
            halo_s[72:80, lanes] = long_s[b, 0:8, :]
        halo_s[56:72, :] = heads[...]
        pushing.start()

        @pl.when(pushing.me > 0)
        def _():
            halo_copy.start()

    @pl.when(step == TAPS)
    def _():
        taps_s[...] = jnp.zeros_like(taps_s)

        def pairs(p, _):
            def chunk(j, _):
                at = pl.ds(pl.multiple_of(j * 32, 32), 32)
                start = BEFORE + j * 32
                near = dist_s[at, :]
                here = [glong_s[2 * p + k, at, :] for k in range(2)]
                for tap in range(FIR):
                    same = near >= float(tap)
                    for k in range(2):
                        term = jnp.where(same, here[k] * u[2 * p + k, pl.ds(start - tap, 32), :], 0.0)
                        taps_s[2 * p + k, tap] += jnp.sum(term.reshape(4, 8, LANES), axis=0)
                return 0

            lax.fori_loop(0, groups, chunk, 0)
            return 0

        lax.fori_loop(0, lane_blocks // 2, pairs, 0)
        result = joins[0][0].held.at[0] if summed else small_a
        for b in range(lane_blocks):
            lanes = slice(b * LANES, (b + 1) * LANES)
            result[0:FIR, lanes] = jnp.sum(taps_s[b], axis=1)
        result[FIR : FIR + 8, :] = head_s[...]
        if summed:
            joins[0][0].start(0)

    @pl.when((step >= BACK) & (step <= last_back))
    def _():
        i = step - BACK
        two = range(2)
        lanes = [lanes_of(2 * i + k) for k in two]
        rates = [vec[4:5, lanes[k]] for k in two]
        scales = [vec[2:3, lanes[k]] - vec[3:4, lanes[k]] * vec[5:6, lanes[k]] for k in two]
        start = BEFORE + block
        own = ids[pl.ds(start, 8), :]
        end_id = marks[2 * n + jnp.minimum(pushing.me + 1, 2 * n - 1)].astype(F32)
        left = (block - 1 - row_id).astype(F32)
        for k in two:
            b = 2 * i + k
            entered = jnp.exp(-rates[k] * left) * joined_s[1:2, lanes[k]]
            grad = halo_r[48:56, lanes[k]] + jnp.where(own == end_id, entered, 0.0)
            grad += scales[k] * glong_s[b, block : block + 8, :]
            for tap in range(FIR):
                term = vec[16 + tap : 17 + tap, lanes[k]] * glong_s[b, block + tap : block + tap + 8, :]
                grad += jnp.where(own == ids[pl.ds(start + tap, 8), :], term, 0.0)
            gc_s[0, k, block : block + 8, :] = grad * halo_r[56:64, lanes[k]]
            gc_s[1, k, block : block + 8, :] = halo_r[72:80, lanes[k]]
            gc_s[2, k, block : block + 8, :] = grad * halo_r[64:72, lanes[k]]

        for k in two:

            def short(j, totals):
                at = pl.ds(pl.multiple_of(j * 32, 32), 32)
                start = pl.multiple_of(BEFORE + j * 32, 16)
                same = [dist_s[at, :] >= float(d) for d in (1, 2)]
                later = [rest_s[at, :] >= float(d) for d in (1, 2)]
                result = []
                for s in range(3):
                    here = gc_s[s, k, at, :]
                    value = vec[6 + s : 7 + s, lanes[k]] * here
                    for d in (1, 2):
                        tap = vec[6 + 3 * d + s : 7 + 3 * d + s, lanes[k]]
                        value += jnp.where(later[d - 1], tap * gc_s[s, k, pl.ds(j * 32 + d, 32), :], 0.0)
                    gp_s[s, at, k * LANES : (k + 1) * LANES] = value.astype(BF16)
                    for d in range(3):
                        term = here * proj_s[s, k, pl.ds(start - d, 32), :]
                        if d:
                            term = jnp.where(same[d - 1], term, 0.0)
                        result.append(totals[3 * s + d] + jnp.sum(term.reshape(4, 8, LANES), axis=0))
                return tuple(result)

            totals = lax.fori_loop(0, groups, short, (zero,) * 9)
            rows = [None] * 9
            for s in range(3):
                for d in range(3):
                    rows[3 * d + s] = jnp.sum(totals[3 * s + d], axis=0, keepdims=True)
            for row, value in enumerate(rows):
                note(row, i, slice(k * LANES, (k + 1) * LANES), value)

        tile = TILES + 1 + i
        pieces = [contract(n1[...], gp_s[s], ((0,), (0,))).astype(BF16) for s in range(3)]
        for s, piece in enumerate(pieces):
            put(tile, s, [piece[:, half * LANES : (half + 1) * LANES] for half in range(2)])
        if summed:
            sums.start(tile, 0, MIX_ORDERS)
        for s in range(3):
            gn_s[...] += contract(gp_s[s], win[s], ((1,), (1,)))

    @pl.when(step == last_back)
    def _():
        def back(j, total):
            at = pl.ds(pl.multiple_of(j * 32, 32), 32)
            normal, inverse = row_stats(tok[pl.ds(pl.multiple_of(BEFORE + j * 32, 16), 32), :].astype(F32))
            grad = gn_s[at, :]
            total += jnp.sum(grad * normal, axis=0, keepdims=True)
            scaled = grad * gains[0:1, :]
            cross = jnp.mean(scaled * normal, axis=1, keepdims=True)
            middle_s[at, :] = gmid_s[at, :] + inverse * (
                scaled - jnp.mean(scaled, axis=1, keepdims=True) - normal * cross)
            return total

        gain_one = lax.fori_loop(0, groups, back, jnp.zeros((1, full), F32))
        for k in range(steps):
            note(10 + k, steps - 1, slice(0, BLOCK), gain_one[:, k * BLOCK : (k + 1) * BLOCK])
        if summed:
            for copy in shares(1, middle_s, gtok_o):
                copy.start()
        else:
            gtok_o[...] = middle_s[...]

    if summed:
        for join, _, begun in joins[1:]:

            @pl.when(step == begun)
            def _():
                join.start(0)

        @pl.when(step == last_back + STAGES)
        def _():
            for k, (src, dst) in enumerate(((out_s, out_o), (middle_s, gtok_o))):
                for copy in shares(k, src, dst):
                    copy.wait()


def backward(n, summed, marks, tok, ids, dist, rest, enter, g, gains, vec, wout, x0, base, car, u, n1, heads, ups, downs,
             win, proj):
    block, full = g.shape
    rows, lane_blocks = BEFORE + block, full // LANES
    steps = full // BLOCK
    tiles = TILES + 1 + steps
    reach = min(DOC_MOST // block + 1, 2 * n - 1)
    whole = lambda *shape: pl.BlockSpec(shape, lambda i: (0,) * len(shape), pipeline_mode=pl.Buffered(1))
    tile = lambda i: jnp.minimum(i, TILES - 1)
    back = lambda i: jnp.clip(i - BACK, 0, steps - 1)
    wide = lambda dtype: pltpu.VMEM((block, full), dtype)
    stacked = lambda count, dtype=F32: pltpu.VMEM((lane_blocks, count, LANES), dtype)
    shape = jax.ShapeDtypeStruct
    if summed:
        columns = TILES * TILE + (1 + steps) * len(MIX_ORDERS) * LANES
        out_shape = [shape((full // 16, columns), F32), shape((FIR + 8, full), F32), shape((16, full), F32)]
        out_shape += [shape((2 * block, full // 2), F32)] * 2
        out_specs = [whole(full // 16, columns), whole(FIR + 8, full), whole(16, full)]
        out_specs += [pl.BlockSpec(memory_space=pl.ANY)] * 2
        extra = Summing.scratch(tiles, TILES, full // 16) + Joining.scratch(FIR + 8, full)
        extra += [pltpu.VMEM((steps, STAGES, 16, BLOCK), F32)] * 2 + [pltpu.SemaphoreType.DMA((steps, STAGES))] * 2
        extra += [pltpu.SemaphoreType.DMA((2,))] * 3
    else:
        out_shape = [shape((tiles, 2, full, TILE), BF16), shape((FIR + 8, full), F32), shape((16, full), F32)]
        out_shape += [shape((block, full), F32)] * 2
        place = lambda i: jnp.minimum(i, TILES - 1) + jnp.clip(i - GATE + 1, 0, 1) + jnp.clip(i - BACK + 1, 0, steps)
        out_specs = [pl.BlockSpec((1, 2, full, TILE), lambda i: (place(i), 0, 0, 0)), whole(FIR + 8, full), whole(16, full)]
        out_specs += [whole(block, full)] * 2
        extra = []
    return pl.pallas_call(
        functools.partial(backward_kernel, n, block, reach, summed),
        name="backward",
        grid=(BACK + steps + (STAGES if summed else 0),),
        out_shape=out_shape,
        in_specs=[
            pl.BlockSpec(memory_space=pltpu.SMEM),
            whole(*tok.shape), whole(*ids.shape), whole(*dist.shape), whole(*rest.shape), whole(*enter.shape), whole(*g.shape), whole(*gains.shape),
            whole(*vec.shape), whole(*wout.shape), whole(*x0.shape), whole(*base.shape), whole(*car.shape),
            whole(*u.shape), whole(*n1.shape), whole(*heads.shape),
            *[pl.BlockSpec((full, PART), lambda i: (0, tile(i)))] * 2,
            *[pl.BlockSpec((PART, full), lambda i: (tile(i), 0))] * 2,
            pl.BlockSpec((3, full, BLOCK), lambda i: (0, 0, back(i))),
            pl.BlockSpec((3, BLOCK // LANES, rows, LANES), lambda i: (0, back(i), 0, 0)),
        ],
        out_specs=out_specs,
        scratch_shapes=[
            wide(BF16), wide(F32), wide(BF16), wide(F32), wide(BF16), wide(F32), wide(F32),
            stacked(block), stacked(block), stacked(block + 48), stacked(block),
            pltpu.VMEM((3, BLOCK // LANES, block + 8, LANES), F32),
            pltpu.VMEM((3, block, BLOCK), BF16),
            pltpu.VMEM((3, BLOCK // LANES, rows, LANES), F32),
            pltpu.VMEM((lane_blocks, FIR, 8, LANES), F32),
            pltpu.VMEM((1, full), F32),
            pltpu.VMEM((reach, 1, full), F32),
            pltpu.VMEM((2, full), F32),
            pltpu.VMEM((HALO, full), F32),
            pltpu.VMEM((HALO, full), F32),
            pltpu.VMEM((8, full), F32),
            pltpu.SemaphoreType.DMA((reach,)),
            pltpu.SemaphoreType.DMA((reach,)),
            pltpu.SemaphoreType.DMA((2,)),
            *extra,
        ],
        compiler_params=pltpu.CompilerParams(collective_id=2, has_side_effects=True, vmem_limit_bytes=60 << 20),
    )(marks, tok, ids, dist, rest, enter, g, gains, vec, wout, x0, base, car, u, n1, heads, *ups, *downs, win, proj)


def reduce_plain(n, grads, small_a, small_b, out, gtok):
    both = lax.psum_scatter(grads.astype(F32), "ch", scatter_dimension=1, tiled=False)
    total = lax.psum_scatter(both, "seq", scatter_dimension=1, tiled=True)
    total = jnp.transpose(total, (1, 0, 2))
    used = len(MIX_ORDERS) * LANES
    total = jnp.concatenate([total[:, :TILES].reshape(total.shape[0], -1), total[:, TILES:, :used].reshape(total.shape[0], -1)], axis=1)
    swap = lambda whole: lax.all_to_all(whole, "ch", split_axis=1, concat_axis=0, tiled=True)
    small_a, small_b = lax.psum((small_a, small_b), ("seq", "ch"))
    return total, small_a, small_b, swap(out), swap(gtok)


def finish_kernel(total, small_a, small_b, gains, vec, table, w1, b1, w2, out, gtok,
                  out_o, gtok_o, gain_one_o, in_o, short_o, w1_o, b1_o, w2_o, w3_o, bias_o, tgain_o, trate_o,
                  outw_o, gain_two_o, up_o, down_o, out_v, gtok_v, sem):
    full = gains.shape[1]
    width, hidden = full // 2, up_o.shape[1]
    loads = [pltpu.make_async_copy(src, dst, sem.at[k]) for k, (src, dst) in enumerate(((out, out_v), (gtok, gtok_v)))]
    saves = [pltpu.make_async_copy(src, dst, sem.at[2 + k]) for k, (src, dst) in enumerate(((out_v, out_o), (gtok_v, gtok_o)))]
    for copy in loads:
        copy.start()

    def natural(rows):
        blocks = [rows[:, b * LANES : (b + 1) * LANES] for b in range(full // LANES)]
        return jnp.concatenate(blocks[0::2] + blocks[1::2], axis=1)

    raw = natural(small_a[0:FIR, :]) * filter_window(0, full, full)
    pre_one, hidden_one, pre_two, hidden_two = filter_layers(table[...], w1[...], b1[...], w2[...])

    def exact(left, right, dims):
        return lax.dot_general(left, right, (dims, ((), ())), precision=HIGHEST, preferred_element_type=F32)

    w3_o[...] = exact(hidden_two, raw, ((0,), (0,)))
    pre_two_grad = exact(raw, gains[8:, :], ((1,), (1,))) * jnp.cos(pre_two)
    w2_o[...] = exact(hidden_one, pre_two_grad, ((0,), (0,)))
    pre_one_grad = exact(pre_two_grad, w2[...], ((1,), (1,))) * jnp.cos(pre_one)
    w1_o[...] = exact(table[...], pre_one_grad, ((0,), (0,)))
    b1_o[...] = jnp.sum(pre_one_grad, axis=0, keepdims=True).reshape(b1_o.shape)

    for copy, following in zip(loads, saves):
        copy.wait()
        following.start()

    last = [small_b[10 + k : 11 + k, full - BLOCK : full] for k in range(full // BLOCK)]
    gain_one_o[...] = jnp.concatenate(last, axis=1).reshape(full)
    gain_two_o[...] = small_a[FIR : FIR + 1, :].reshape(full)
    bias_o[...] = natural(small_a[FIR + 1 : FIR + 2, :]).reshape(full)
    long_car, rate, nu = small_a[FIR + 2 : FIR + 3, :], vec[4:5, :], vec[5:6, :]
    factor = jnp.exp(-rate)
    tgain_o[...] = natural(nu * long_car).reshape(full)
    trate_o[...] = natural(vec[3:4, :] * long_car * factor * factor / nu - small_b[9:10, :]).reshape(full)
    short = natural(small_b[0:9, :])
    for j in range(3):
        for s in range(3):
            short_o[j, s : s + 1, :] = short[3 * j + s : 3 * j + s + 1, :]
    for k in range(TILES):
        up_o[:, k * PART : (k + 1) * PART] = total[:, k * TILE : k * TILE + PART]
        down_o[:, k * PART : (k + 1) * PART] = total[:, k * TILE + PART : (k + 1) * TILE]
    outw_o[...] = total[:, TILES * TILE : TILES * TILE + width]
    for i in range(width // LANES):
        for s in range(3):
            at = TILES * TILE + (1 + i) * len(MIX_ORDERS) * LANES + s * LANES
            in_o[s, :, i * LANES : (i + 1) * LANES] = total[:, at : at + LANES]
    for copy in saves:
        copy.wait()


def finish(total, small_a, small_b, gains, vec, table, w1, b1, w2, out, gtok):
    full, rows = gains.shape[1], total.shape[0]
    width, hidden = full // 2, TILES * PART
    shape = jax.ShapeDtypeStruct
    vmem, anywhere = pl.BlockSpec(memory_space=pltpu.VMEM), pl.BlockSpec(memory_space=pl.ANY)
    vector = shape((full,), F32)
    return pl.pallas_call(
        finish_kernel,
        name="finish",
        out_shape=(
            shape(out.shape, F32), shape(gtok.shape, F32), vector, shape((3, rows, width), F32), shape((3, 3, full), F32),
            shape(w1.shape, F32), shape((b1.shape[1],), F32), shape(w2.shape, F32), shape((w2.shape[0], full), F32),
            vector, vector, vector, shape((rows, width), F32), vector, shape((rows, hidden), F32), shape((rows, hidden), F32),
        ),
        in_specs=[vmem] * 9 + [anywhere] * 2,
        out_specs=(anywhere, anywhere) + (vmem,) * 14,
        scratch_shapes=[pltpu.VMEM(out.shape, F32), pltpu.VMEM(gtok.shape, F32), pltpu.SemaphoreType.DMA((4,))],
        compiler_params=pltpu.CompilerParams(vmem_limit_bytes=VMEM_LIMIT),
    )(total, small_a, small_b, gains, vec, table, w1, b1, w2, out, gtok)


def on_device(tokens, seg_ids, norm1_gain, in_weight, short_weight, filt_w1, filt_b1, filt_w2, filt_w3,
              long_bias, tail_gain, tail_rate, out_weight, norm2_gain, up_weight, down_weight, grad_out):
    rows, width = tokens.shape
    full, block = 2 * width, rows // 2
    n = lax.axis_size("seq")
    devices = 2 * n
    me = 2 * lax.axis_index("seq") + lax.axis_index("ch")
    row_start = me * block
    total_rows = seg_ids.shape[0]
    length = min(SEQ_LEN, total_rows)

    keys = seg_ids + (jnp.arange(total_rows, dtype=jnp.int32) // length) * 65536
    padded = jnp.concatenate([jnp.full((BEFORE,), -1, jnp.int32), keys, jnp.full((block + AFTER,), -2, jnp.int32)])
    near = lax.dynamic_slice_in_dim(padded, row_start, BEFORE + block + AFTER)
    window = near
    ids = jnp.broadcast_to(window.astype(F32)[:, None], (window.shape[0], LANES))

    table = position_table(FIR, (filt_w1.shape[0] - 1) // 2)
    norm_tail = jnp.sqrt(-jnp.expm1(-2.0 * tail_rate))
    vectors = (norm1_gain, norm2_gain, long_bias, tail_gain, tail_rate, norm_tail, short_weight)
    filt_b1 = filt_b1[None, :]
    marks = jnp.concatenate([keys[::block], keys[block - 1 :: block]])
    (tok, g, win, wout, up_other, down_other, gains, vec, n1, proj, x0, u, heads, base, car, dist, rest, enter) = forward(
        n, marks, tokens, grad_out, jnp.transpose(in_weight, (1, 0, 2)), out_weight, up_weight, down_weight,
        filt_w3, table, filt_w1, filt_b1, filt_w2, vectors, ids)

    summed = n == 16
    results = backward(
        n, summed, marks, tok, ids, dist, rest, enter, g, gains, vec, wout, x0, base, car, u, n1, heads,
        (up_weight, up_other), (down_weight, down_other), win, proj)
    if not summed:
        results = reduce_plain(n, *results)
    total, small_a, small_b, out, gtok = results

    (out, gtok, gain_one, in_grad, short_grad, w1_grad, b1_grad, w2_grad, w3_grad, bias_grad, tail_gain_grad, rate_grad,
     out_grad, gain_two, up_grad, down_grad) = finish(
        total, small_a, small_b, gains, vec, table, filt_w1, filt_b1, filt_w2, out, gtok)
    return (
        out, gtok, gain_one, jnp.transpose(in_grad, (1, 0, 2)), short_grad, w1_grad, b1_grad, w2_grad, w3_grad, bias_grad,
        tail_gain_grad, rate_grad, out_grad.T, gain_two, up_grad, down_grad.T,
    )


def solution(mesh):
    placed = (
        P("seq", "ch"),
        P(),
        P("ch"),
        P(None, None, "ch"),
        P(None, None, "ch"),
        P(),
        P(),
        P(),
        P(None, "ch"),
        P("ch"),
        P("ch"),
        P("ch"),
        P("ch", None),
        P("ch"),
        P(None, "ch"),
        P("ch", None),
        P("seq", "ch"),
    )
    return jax.shard_map(
        on_device,
        mesh=mesh,
        in_specs=placed,
        out_specs=(
            P("seq", "ch"),
            P("seq", "ch"),
            P(),
            P("seq", None, "ch"),
            P(),
            P(),
            P(),
            P(),
            P(),
            P(),
            P(),
            P(),
            P("ch", "seq"),
            P(),
            P("seq", "ch"),
            P("ch", "seq"),
        ),
        check_vma=False,
    )
```

```python
import functools

import jax
import jax.numpy as jnp
import numpy as np
from jax import lax
from jax.experimental import pallas as pl
from jax.experimental.pallas import tpu as pltpu
from jax.sharding import PartitionSpec as P

FIR = 32
SEQ_LEN = 16384
DOC_MOST = 8192
EPSILON = 1e-05
FREQUENCY = 0.4
HIGHEST = lax.Precision.HIGHEST
MESH = pl.DeviceIdType.MESH
F32, BF16 = jnp.float32, jnp.bfloat16

BEFORE = 48
AFTER = 80
LANES = 128
BLOCK = 256
CHUNK = 64
SUMS = 48
HEAD = 16
VMEM_LIMIT = 56 << 20
ROOT_TWO_OVER_PI = 0.7978845608028654


def position_table(filter_len, band_count):
    places = np.arange(filter_len, dtype=np.float32)
    harmonics = np.arange(1, band_count + 1, dtype=np.float32)
    angles = (np.float32(FREQUENCY) * places[:, None] * harmonics[None, :]).astype(np.float64)
    table = np.concatenate([places[:, None] / filter_len, np.cos(angles), np.sin(angles)], axis=1)
    return jnp.asarray(table.astype(np.float32))


def filter_layers(table, w1, b1, w2):
    pre_one = jnp.dot(table, w1, precision=HIGHEST, preferred_element_type=F32) + b1
    hidden_one = jnp.sin(pre_one)
    pre_two = jnp.dot(hidden_one, w2, precision=HIGHEST, preferred_element_type=F32)
    return pre_one, hidden_one, pre_two, jnp.sin(pre_two)


def filter_window(start, count, full):
    channel = (start + lax.broadcasted_iota(jnp.int32, (FIR, count), 1)).astype(F32)
    place = lax.broadcasted_iota(jnp.int32, (FIR, count), 0).astype(F32)
    return jnp.exp(-(0.5 + 3.0 * channel / full) * place / FIR)


def device_of(index):
    return (index // 2, index % 2)


class Pushing:
    def __init__(self, n, reach, backward, source, slots, send_sem, recv_sem):
        self.total, self.reach = 2 * n, reach
        self.me = 2 * lax.axis_index("seq") + lax.axis_index("ch")
        self.ahead = -1 if backward else 1
        self.place = self.total - 1 - self.me if backward else self.me
        self.source, self.slots, self.send_sem, self.recv_sem = source, slots, send_sem, recv_sem

    def greet(self, barrier):
        for k in range(self.reach):

            @pl.when(self.place - 1 - k >= 0)
            def _():
                pl.semaphore_signal(
                    barrier, inc=1, device_id=device_of(self.me - self.ahead * (1 + k)), device_id_type=MESH)

    def await_greetings(self, barrier, others):
        following = self.total - 1 - self.place
        for count in range(0, self.reach + 1):
            if count + others:

                @pl.when((following >= count) if count == self.reach else (following == count))
                def _():
                    pl.semaphore_wait(barrier, count + others)

    def copy(self, k):
        return pltpu.make_async_remote_copy(
            src_ref=self.source, dst_ref=self.slots.at[k], send_sem=self.send_sem.at[k], recv_sem=self.recv_sem.at[k],
            device_id=device_of(self.me + self.ahead * (1 + k)), device_id_type=MESH)

    def start(self):
        for k in range(self.reach):

            @pl.when(self.place + 1 + k < self.total)
            def _():
                self.copy(k).start()

    def take(self, use):
        for k in range(self.reach):

            @pl.when(self.place - 1 - k >= 0)
            def _():
                self.copy(k).wait_recv()
                use(k, self.slots[k])

            @pl.when(self.place + 1 + k < self.total)
            def _():
                self.copy(k).wait_send()


def row_stats(values):
    center = jnp.mean(values, axis=1, keepdims=True)
    shifted = values - center
    inverse = lax.rsqrt(jnp.mean(shifted * shifted, axis=1, keepdims=True) + EPSILON)
    return shifted * inverse, inverse


def forward_kernel(n, rows, reach, marks, tokens, gout, w_in, w_out, w_up, w_down, filt_w3, table, filt_w1, filt_b1, filt_w2,
                   norms_a, norms_b, biases, tails, decays, nus, shorts, ids,
                   tok_o, g_o, in_o, out_o, up_o, down_o, gains_o, vec_o,
                   n1_o, proj_o, x0_o, u_o, heads_o, long_o, car_o, dist_o, rest_o, enter_o,
                   tok_v, g_v, in_v, out_v, gains_v, vec_v, gains, head, n1_s, proj_s, u_s, state_s, end_s, slots_s,
                   local_sem, store_sem, send_sem, recv_sem, push_send, push_recv):
    block, full = rows // 2, in_v.shape[1]
    width = full // 2
    steps = full // BLOCK
    two = range(BLOCK // LANES)
    step = pl.program_id(0)
    s, c = lax.axis_index("seq"), lax.axis_index("ch")
    barrier = pltpu.get_barrier_semaphore()
    pushing = Pushing(n, reach, False, end_s, slots_s, push_send, push_recv)
    partner = (s, 1 - c)
    cols = pl.ds(pl.multiple_of(c * width, width), width)
    early = [(gains, gains_v.at[pl.ds(0, 8), cols]), (filt_w3, gains_v.at[pl.ds(8, filt_w3.shape[0]), cols])]
    late = []
    for i in range(width // LANES):
        source = pl.ds(i * LANES, LANES)
        paired = pl.ds(pl.multiple_of((2 * i + c) * LANES, LANES), LANES)
        early += [
            (head.at[:, source], vec_v.at[pl.ds(0, HEAD), paired]),
            (w_in.at[:, :, source], in_v.at[:, :, paired]),
        ]
        late.append((w_out.at[source, :], out_v.at[paired, :]))

    def remote(src, dst, k, target=partner):
        return pltpu.make_async_remote_copy(
            src_ref=src, dst_ref=dst, send_sem=send_sem.at[k], recv_sem=recv_sem.at[k],
            device_id=target, device_id_type=MESH)

    halves = [(early[k], k) for k in range(len(early))] + [(late[k], len(early) + k) for k in range(len(late))]
    count = len(halves)
    far = [remote(w_up, up_o, count), remote(w_down, down_o, count + 1)]
    at_tokens = count + 2

    left, right = pl.ds(0, width), pl.ds(width, width)
    first, second = pl.ds(0, block), pl.ds(block, block)
    ahead, tail = pl.ds(block - BEFORE, block + BEFORE), pl.ds(rows - BEFORE, BEFORE)
    main = pl.ds(BEFORE, block)
    keeps = [
        [(tokens.at[first, :], tok_v.at[main, left]), (gout.at[first, :], g_v.at[:, left])],
        [(tokens.at[ahead, :], tok_v.at[:, right]), (gout.at[second, :], g_v.at[:, right])],
    ]
    sends = [
        [(tokens.at[ahead, :], tok_v.at[:, left]), (gout.at[second, :], g_v.at[:, left])],
        [(tokens.at[first, :], tok_v.at[main, right]), (gout.at[first, :], g_v.at[:, right])],
    ]

    def edge(which, target):
        return remote(
            tokens.at[tail, :], tok_v.at[pl.ds(0, BEFORE), (left, right)[which]], at_tokens + 2 + which, target)

    def for_core(action):
        for which in range(2):

            @pl.when(c == which)
            def _():
                action(which)

    stores = [(tok_v, tok_o), (gains_v, gains_o), (vec_v, vec_o), (in_v, in_o), (g_v, g_o), (out_v, out_o)]

    def store(k):
        return pltpu.make_async_copy(*stores[k], store_sem.at[k])

    @pl.when(step == 0)
    def _():
        pushing.greet(barrier)
        pl.semaphore_signal(barrier, inc=1, device_id=partner, device_id_type=MESH)

        @pl.when((c == 0) & (s > 0))
        def _():
            for k in range(2):
                pl.semaphore_signal(barrier, inc=1, device_id=(s - 1, k), device_id_type=MESH)

        gains[...] = jnp.zeros_like(gains)
        head[...] = jnp.zeros_like(head)
        for ref, row, value in ((gains, 0, norms_a), (gains, 1, norms_b), (head, 2, biases), (head, 3, tails),
                                (head, 4, decays), (head, 5, nus)):
            ref[row : row + 1, :] = value[...].reshape(1, width)
        for j in range(3):
            for t in range(3):
                head[6 + 3 * j + t : 7 + 3 * j + t, :] = shorts[j, t : t + 1, :]

        def begin_own(which):
            for k, (src, dst) in enumerate(keeps[which]):
                pltpu.make_async_copy(src, dst, local_sem.at[at_tokens + k]).start()

        for_core(begin_own)
        for (src, dst), k in halves:
            pltpu.make_async_copy(src, dst, local_sem.at[k]).start()

        @pl.when(s < n - 1)
        def _():
            pushing.await_greetings(barrier, 2)

        @pl.when(s == n - 1)
        def _():
            pushing.await_greetings(barrier, 1)

        def begin(which):
            remote(*sends[which][0], at_tokens).start()

            @pl.when(s < n - 1)
            def _():
                edge(which, (s + 1, 0)).start()

        for_core(begin)
        for (src, dst), k in halves[: len(early)]:
            remote(src, dst, k).start()
        for_core(lambda which: remote(*sends[which][1], at_tokens + 1).start())
        for (src, dst), k in halves[len(early) :]:
            remote(src, dst, k).start()
        for copy in far:
            copy.start()

        def distances(j, _):
            at = pl.ds(pl.multiple_of(j * 32, 32), 32)
            start = pl.multiple_of(BEFORE + j * 32, 16)
            own = ids[pl.ds(start, 32), :]
            before = after = jnp.zeros((32, LANES), F32)
            for k in range(1, FIR):
                before += jnp.where(own == ids[pl.ds(start - k, 32), :], 1.0, 0.0)
                after += jnp.where(own == ids[pl.ds(start + k, 32), :], 1.0, 0.0)
            dist_o[at, :] = before
            rest_o[at, :] = after
            return 0

        lax.fori_loop(0, block // 32, distances, 0)

        def take_tokens(which):
            remote(*sends[which][0], at_tokens).wait_send()
            remote(*sends[1 - which][0], at_tokens).wait_recv()
            pltpu.make_async_copy(*keeps[which][0], local_sem.at[at_tokens]).wait()

            @pl.when(s < n - 1)
            def _():
                edge(which, (s + 1, 0)).wait_send()

            if which == 0:

                @pl.when(s > 0)
                def _():
                    for k in range(2):
                        edge(k, partner).wait_recv()

        for_core(take_tokens)
        hidden_two = filter_layers(table[...], filt_w1[...], filt_b1[...], filt_w2[...])[3]
        for (src, dst), k in halves[:2]:
            pltpu.make_async_copy(src, dst, local_sem.at[k]).wait()
            remote(src, dst, k).wait()
        store(0).start()
        store(1).start()

        def normed(j, _):
            at = pl.ds(pl.multiple_of(j * 80, 16), 80)
            values = jnp.where(ids[at, 0:1] >= 0.0, tok_v[at, :].astype(F32), 0.0)
            n1_s[at, :] = (row_stats(values)[0] * gains_v[0:1, :]).astype(BF16)
            return 0

        lax.fori_loop(0, (BEFORE + block) // 80, normed, 0)
        n1_o[...] = n1_s[pl.ds(BEFORE, block), :]
        for (src, dst), k in halves[2 : len(early)]:
            pltpu.make_async_copy(src, dst, local_sem.at[k]).wait()
            remote(src, dst, k).wait()
        taps = jnp.dot(hidden_two, gains_v[8:, :], precision=HIGHEST, preferred_element_type=F32)
        taps *= filter_window(0, full, full)
        for i in range(width // LANES):
            for half in range(2):
                source = half * width + i * LANES
                vec_v[HEAD : HEAD + FIR, (2 * i + half) * LANES : (2 * i + half + 1) * LANES] = (
                    taps[:, source : source + LANES])
        store(2).start()
        store(3).start()

    @pl.when(step < steps)
    def _():
        lanes = [pl.ds(pl.multiple_of((2 * step + b) * LANES, LANES), LANES) for b in two]
        wide = pl.ds(pl.multiple_of(step * BLOCK, BLOCK), BLOCK)
        for t in range(3):
            part = jnp.dot(n1_s[...], in_v[t, :, wide], preferred_element_type=F32).astype(BF16)
            for b in two:
                proj_o[t, b] = part[:, b * LANES : (b + 1) * LANES]
                proj_s[t, b] = part[:, b * LANES : (b + 1) * LANES].astype(F32)

        def convolved(start, size):
            own = ids[pl.ds(start, size), :]
            same = [None] + [own == ids[pl.ds(start - j, size), :] for j in (1, 2)]
            results = []
            for b in two:
                streams = []
                for t in range(3):
                    value = vec_v[6 + t : 7 + t, lanes[b]] * proj_s[t, b, pl.ds(start, size), :]
                    for j in (1, 2):
                        tap = vec_v[6 + 3 * j + t : 7 + 3 * j + t, lanes[b]]
                        value += jnp.where(same[j], tap * proj_s[t, b, pl.ds(start - j, size), :], 0.0)
                    streams.append(value)
                gated = (streams[0] * streams[2]).astype(BF16).astype(F32)
                u_s[2 * step + b, pl.ds(start, size), :] = gated
                u_o[b, pl.ds(start, size), :] = gated
                results.append(streams)
            return results

        convolved(16, 32)
        for b, streams in enumerate(convolved(BEFORE, 8)):
            heads_o[0:8, b * LANES : (b + 1) * LANES] = streams[2]
            heads_o[8:16, b * LANES : (b + 1) * LANES] = streams[0]
            u_o[b, 0:16, :] = jnp.zeros((16, LANES), F32)
            u_s[2 * step + b, 0:16, :] = jnp.zeros((16, LANES), F32)

        def conv_chunk(j, _):
            start = pl.multiple_of(BEFORE + j * 32, 16)
            for b, streams in enumerate(convolved(start, 32)):
                x0_o[b, pl.ds(pl.multiple_of(j * 32, 32), 32), :] = streams[1]
            return 0

        lax.fori_loop(0, block // 32, conv_chunk, 0)

        row_id = lax.broadcasted_iota(jnp.int32, (8, LANES), 0)
        rates = [vec_v[4:5, lanes[b]] for b in two]
        powers = [jnp.exp(-rate * (row_id + 1).astype(F32)) for rate in rates]
        lams = [[jnp.exp(-rate * float(k)) for k in (1, 2, 4)] for rate in rates]
        for b in two:
            state_s[2 * step + b, 0:8, :] = jnp.zeros((8, LANES), F32)

        def scan_group(g, carry):
            start = pl.multiple_of(BEFORE + g * 8, 8)
            own = ids[pl.ds(start, 8), :]
            masks = [(own == ids[pl.ds(start - k, 8), :]) & (row_id >= k) for k in (1, 2, 4)]
            joined = own == jnp.broadcast_to(ids[pl.ds(start - 1, 1), :], (8, LANES))
            result = []
            for b in two:
                value = u_s[2 * step + b, pl.ds(start, 8), :]
                for mask, lam, k in zip(masks, lams[b], (1, 2, 4)):
                    value += jnp.where(mask, lam * pltpu.roll(value, k, 0), 0.0)
                value += jnp.where(joined, powers[b] * carry[b], 0.0)
                state_s[2 * step + b, pl.ds(pl.multiple_of(8 + g * 8, 8), 8), :] = value
                result.append(jnp.broadcast_to(value[7:8, :], (8, LANES)))
            return tuple(result)

        zero = jnp.zeros((8, LANES), F32)
        final = lax.fori_loop(0, block // 8, scan_group, (zero,) * len(two), unroll=4)
        for b in two:
            end_s[:, lanes[b]] = final[b][0:1, :]

    @pl.when(step == steps - 1)
    def _():
        pushing.start()

    @pl.when(step >= steps)
    def _():
        i = step - steps
        lanes = [pl.ds(pl.multiple_of((2 * i + b) * LANES, LANES), LANES) for b in two]
        lam = [jnp.exp(-vec_v[4:5, lanes[b]]) for b in two]
        tails = [vec_v[3:4, lanes[b]] * vec_v[5:6, lanes[b]] for b in two]

        def long_chunk(j, _):
            at = pl.ds(pl.multiple_of(j * 32, 32), 32)
            start = pl.multiple_of(BEFORE + j * 32, 16)
            near = dist_o[at, :]
            totals = []
            for b in two:
                previous = state_s[2 * i + b, pl.ds(7 + j * 32, 32), :]
                carried = jnp.where(near >= 1.0, lam[b] * previous, 0.0)
                car_o[b, at, :] = carried
                here = u_s[2 * i + b, pl.ds(start, 32), :]
                totals.append((vec_v[2:3, lanes[b]] + vec_v[16:17, lanes[b]]) * here + tails[b] * carried)
            for k in range(1, FIR):
                same = near >= float(k)
                for b in two:
                    term = vec_v[16 + k : 17 + k, lanes[b]] * u_s[2 * i + b, pl.ds(start - k, 32), :]
                    totals[b] += jnp.where(same, term, 0.0)
            for b in two:
                long_o[b, at, :] = totals[b]
            return 0

        lax.fori_loop(0, block // 32, long_chunk, 0)

    @pl.when(step == steps)
    def _():
        def take_rows(which):
            remote(*sends[which][1], at_tokens + 1).wait_send()
            remote(*sends[1 - which][1], at_tokens + 1).wait_recv()
            pltpu.make_async_copy(*keeps[which][1], local_sem.at[at_tokens + 1]).wait()

        for_core(take_rows)
        for (src, dst), k in halves[len(early) :]:
            pltpu.make_async_copy(src, dst, local_sem.at[k]).wait()
            remote(src, dst, k).wait()
        store(4).start()
        store(5).start()

    @pl.when(step == 2 * steps - 1)
    def _():
        enter_o[...] = jnp.zeros_like(enter_o)
        rate = vec_v[4:5, :]
        last = marks[2 * n + jnp.maximum(pushing.me - 1, 0)]

        def use(k, state):
            same = jnp.where(marks[2 * n + pushing.me - 1 - k] == last, 1.0, 0.0)
            enter_o[...] += same * jnp.exp(-rate * float(block * k)) * state

        pushing.take(use)
        for copy in far:
            copy.wait()
        for k in range(len(stores)):
            store(k).wait()


def forward(n, marks, tokens, gout, w_in, w_out, w_up, w_down, filt_w3, table, filt_w1, filt_b1, filt_w2, vectors, ids):
    rows, width = tokens.shape
    hidden = w_up.shape[1]
    full, block = 2 * width, rows // 2
    window = BEFORE + block
    steps, lane_blocks = full // BLOCK, full // LANES
    reach = min(DOC_MOST // block, 2 * n - 1)
    anywhere = pl.BlockSpec(memory_space=pl.ANY)
    whole = lambda *shape: pl.BlockSpec(shape, lambda i: (0,) * len(shape), pipeline_mode=pl.Buffered(1))
    soon, later = lambda i: jnp.minimum(i, steps - 1), lambda i: jnp.maximum(i - steps, 0)
    stacked = lambda count, place: pl.BlockSpec((BLOCK // LANES, count, LANES), lambda i: (place(i), 0, 0))
    shape = jax.ShapeDtypeStruct
    vmem = pltpu.VMEM
    far = 2 + 3 * (width // LANES) + 2 + 4
    dma = pltpu.SemaphoreType.DMA
    landing = [
        ((window, full), BF16), ((block, full), BF16), ((3, full, full), BF16), ((full, full), BF16),
        ((8 + filt_w3.shape[0], full), F32), ((HEAD + FIR, full), F32),
    ]
    return pl.pallas_call(
        functools.partial(forward_kernel, n, rows, reach),
        name="forward",
        grid=(2 * steps,),
        out_shape=(
            *[shape(*part) for part in landing[:4]],
            shape((full, hidden), BF16),
            shape((hidden, full), BF16),
            *[shape(*part) for part in landing[4:]],
            shape((block, full), BF16),
            shape((3, lane_blocks, window, LANES), BF16),
            shape((lane_blocks, block, LANES), F32),
            shape((lane_blocks, window, LANES), F32),
            shape((16, full), F32),
            shape((lane_blocks, block, LANES), F32),
            shape((lane_blocks, block, LANES), F32),
            shape((block, LANES), F32),
            shape((block, LANES), F32),
            shape((1, full), F32),
        ),
        in_specs=[pl.BlockSpec(memory_space=pltpu.SMEM)] + [anywhere] * 7 + [
            whole(*part.shape) for part in (table, filt_w1, filt_b1, filt_w2, *vectors, ids)],
        out_specs=(
            *[anywhere] * 8,
            whole(block, full),
            pl.BlockSpec((3, BLOCK // LANES, window, LANES), lambda i: (0, soon(i), 0, 0)),
            stacked(block, soon),
            stacked(window, soon),
            pl.BlockSpec((16, BLOCK), lambda i: (0, soon(i))),
            stacked(block, later),
            stacked(block, later),
            whole(block, LANES),
            whole(block, LANES),
            whole(1, full),
        ),
        scratch_shapes=[
            *[vmem(*part) for part in landing],
            vmem((8, width), F32),
            vmem((HEAD, width), F32),
            vmem((window, full), BF16),
            vmem((3, BLOCK // LANES, window, LANES), F32),
            vmem((lane_blocks, window, LANES), F32),
            vmem((lane_blocks, 8 + block, LANES), F32),
            vmem((1, full), F32),
            vmem((reach, 1, full), F32),
            dma((far,)), dma((6,)), dma((far,)), dma((far,)), dma((reach,)), dma((reach,)),
        ],
        compiler_params=pltpu.CompilerParams(collective_id=0, has_side_effects=True, vmem_limit_bytes=VMEM_LIMIT),
    )(marks, tokens, gout, w_in, w_out, w_up, w_down, filt_w3, table, filt_w1, filt_b1, filt_w2, *vectors, ids)


TILE = 512
PART = TILE // 2
STAGES = 5
FEED_ORDERS = ((0, 1, 2, 3), (0, 2, 3, 1), (1, 0, 2, 3), (1, 2, 3, 0))
MIX_ORDERS = ((0, 1, 2, 3), (1, 0, 2, 3), (2, 0, 1, 3))


class Summing:
    def __init__(self, slots, rows, staged, first, second, third, fourth, fifth, send_sem, recv_sem):
        self.slots, self.rows, self.staged = slots, rows, staged
        self.held = (first, second, third, fourth, fifth)
        self.send_sem, self.recv_sem = send_sem, recv_sem
        self.s, self.c = lax.axis_index("seq"), lax.axis_index("ch")
        self.bits = [(self.s // (1 << b)) % 2 for b in range(4)]
        self.peers = [(self.s + (1 - 2 * bit) * (1 << b), self.c) for b, bit in enumerate(self.bits)]
        self.partner = (self.s, 1 - self.c)

    @staticmethod
    def scratch(tiles, slots, rows):
        parts = len(FEED_ORDERS)
        return [
            pltpu.VMEM((2, 2, parts, 2, 2, 2, 2, rows, LANES), BF16),
            pltpu.VMEM((slots, parts, 2, 2, 2, 2, rows, LANES), BF16),
            pltpu.VMEM((slots, parts, 2, 2, 2, rows, LANES), BF16),
            pltpu.VMEM((slots, parts, 2, 2, rows, LANES), BF16),
            pltpu.VMEM((slots, parts, 2, rows, LANES), BF16),
            pltpu.VMEM((slots, parts, rows, LANES), BF16),
            pltpu.SemaphoreType.DMA((tiles, 1 + 4 * parts)),
            pltpu.SemaphoreType.DMA((tiles, 1 + 4 * parts)),
        ]

    def greet(self, barrier):
        for peer in [self.partner] + self.peers:
            pl.semaphore_signal(barrier, inc=1, device_id=peer, device_id_type=MESH)

    def remote(self, src, dst, tile, k, target):
        return pltpu.make_async_remote_copy(
            src_ref=src, dst_ref=dst, send_sem=self.send_sem.at[tile, k], recv_sem=self.recv_sem.at[tile, k],
            device_id=target, device_id_type=MESH)

    def stage_in(self, tile, whose, part, order, grad):
        for q in range(16):
            at = [(q >> bit) & 1 for bit in order]
            self.staged[(tile % 2, whose, part, *at)] = grad[q * self.rows : (q + 1) * self.rows]

    def copies(self, tile, stage, orders):
        slot = tile % self.slots
        if stage == 0:
            parts = pl.ds(0, len(orders))
            return [self.remote(self.staged.at[tile % 2, 1, parts], self.held[0].at[slot, parts], tile, 0, self.partner)]
        result = []
        for part, order in enumerate(orders):
            bit = order[stage - 1]
            src, dst = self.held[stage - 1].at[slot, part, 1 - self.bits[bit]], self.held[stage].at[slot, part]
            result.append(self.remote(src, dst, tile, 1 + 4 * (stage - 1) + part, self.peers[bit]))
        return result

    def start(self, tile, stage, orders):
        for copy in self.copies(tile, stage, orders):
            copy.start()

    def advance(self, tile, stage, orders, total):
        slot = tile % self.slots
        arriving = self.copies(tile, stage, orders)
        following = self.copies(tile, stage + 1, orders) if stage < STAGES - 1 else []
        if stage == 0:
            arriving[0].wait()
        for part, order in enumerate(orders):
            if stage == 0:

                def add(i, _):
                    for q in range(8):
                        at = (q >> 2 & 1, q >> 1 & 1, q & 1)
                        self.held[0][(slot, part, i, *at)] += self.staged[(tile % 2, 0, part, i, *at)]
                    return 0

                lax.fori_loop(0, 2, add, 0)
            else:
                arriving[part].wait()
                mine = self.bits[order[stage - 1]]
                for e in range(1 << (4 - stage)):
                    inner = [(e >> (3 - stage - k)) & 1 for k in range(4 - stage)]
                    source = self.held[stage - 1][(slot, part, mine, *inner)]
                    if stage == STAGES - 1:
                        total(tile, part, source.astype(F32) + self.held[stage][slot, part].astype(F32))
                    else:
                        self.held[stage][(slot, part, *inner)] += source
            if following:
                following[part].start()


class Joining:
    def __init__(self, sums, held, arrived, send_sem, recv_sem):
        self.held, self.arrived, self.send_sem, self.recv_sem = held, arrived, send_sem, recv_sem
        self.targets = [sums.partner] + sums.peers

    @staticmethod
    def scratch(*shape):
        return [pltpu.VMEM((STAGES,) + shape, F32), pltpu.VMEM((STAGES,) + shape, F32),
                pltpu.SemaphoreType.DMA((STAGES,)), pltpu.SemaphoreType.DMA((STAGES,))]

    def copy(self, stage):
        return pltpu.make_async_remote_copy(
            src_ref=self.held.at[stage], dst_ref=self.arrived.at[stage], send_sem=self.send_sem.at[stage],
            recv_sem=self.recv_sem.at[stage], device_id=self.targets[stage], device_id_type=MESH)

    def start(self, stage):
        self.copy(stage).start()

    def advance(self, stage, result):
        self.copy(stage).wait()
        total = self.held[stage] + self.arrived[stage]
        if stage == STAGES - 1:
            result(total)
        else:
            self.held[stage + 1] = total
            self.start(stage + 1)


def contract(left, right, dims):
    return lax.dot_general(left, right, (dims, ((), ())), preferred_element_type=F32)


def contract(left, right, dims):
    return lax.dot_general(left, right, (dims, ((), ())), preferred_element_type=F32)


TILES = 6
EPILOGUE, GATE, TAPS, BACK = TILES, TILES + 1, TILES + 2, TILES + 3
TURN_OF_BACK = TILES + 1
LAGS = (1, 3, 5, 6, 7)
HALO = 80


def when(condition):
    if isinstance(condition, bool):
        return lambda body: body() if condition else None
    return pl.when(condition)


def lanes_at(start):
    return pl.ds(start if isinstance(start, int) else pl.multiple_of(start, LANES), LANES)


def backward_kernel(n, block, reach, summed, marks, tok, ids, dist_s, rest_s, enter, g, gains, vec, wout, x0, base, car, u, n1, heads,
                    wup_a, wup_b, wdn_a, wdn_b, win, proj, *refs):
    full = g.shape[1]
    width, lane_blocks = full // 2, full // LANES
    steps = full // BLOCK
    last_back = BACK + steps - 1
    (grads_o, small_a, small_b, out_o, gtok_o), refs = refs[:5], refs[5:]
    (mixed_s, middle_s, n2_s, gn_s, gout_s, out_s, gmid_s, long_s, car_s, glong_s, q_s, gc_s, gp_s, proj_s,
     taps_s, first_s, slots_s, joined_s, halo_s, halo_r, head_s,
     push_send, push_recv, halo_sem, *buffers) = refs
    turn = pl.program_id(0)
    step = turn + (BACK - TURN_OF_BACK) * (turn // TURN_OF_BACK)
    groups = block // 32
    barrier = pltpu.get_barrier_semaphore()
    pushing = Pushing(n, reach, True, first_s, slots_s, push_send, push_recv)
    c = lax.axis_index("ch")
    lanes_of = lambda b: pl.ds(pl.multiple_of(b * LANES, LANES), LANES)
    if summed:
        sums = Summing(TILES, full // 16, *buffers[:8])
        held_b = buffers[12]
        joins = [(Joining(sums, *buffers[8:12]), lambda value: small_a.__setitem__(Ellipsis, value), TAPS)]
        for k in range(steps):
            at = slice(k * BLOCK, (k + 1) * BLOCK)
            joins.append((Joining(sums, *[ref.at[k] for ref in buffers[12:16]]),
                          lambda value, at=at: small_b.__setitem__((slice(None), at), value), BACK + k))
        local_sem, exchange_send, exchange_recv = buffers[16:]

        def shares(k, src, dst):
            at = pl.ds(pl.multiple_of(c * block, block), block)
            of_core = lambda which: src.at[:, pl.ds(pl.multiple_of(which * width, width), width)]
            return (
                pltpu.make_async_copy(of_core(c), dst.at[at, :], local_sem.at[k]),
                pltpu.make_async_remote_copy(
                    src_ref=of_core(1 - c), dst_ref=dst.at[at, :], send_sem=exchange_send.at[k],
                    recv_sem=exchange_recv.at[k], device_id=sums.partner, device_id_type=MESH),
            )

    halo_copy = pltpu.make_async_remote_copy(
        src_ref=halo_s, dst_ref=halo_r, send_sem=halo_sem.at[0], recv_sem=halo_sem.at[1],
        device_id=device_of(pushing.me - 1), device_id_type=MESH)

    @pl.when(step == 0)
    def _():
        pushing.greet(barrier)
        if summed:
            sums.greet(barrier)

        last = ids[pl.ds(BEFORE - 1, 1), :]
        for b in range(lane_blocks):
            lanes = slice(b * LANES, (b + 1) * LANES)
            rate, tail = vec[4:5, lanes], vec[3:4, lanes] * vec[5:6, lanes]
            state = enter[0:1, lanes]

            def mix(j, _):
                at = pl.ds(pl.multiple_of(j * 32, 32), 32)
                passed = (lax.broadcasted_iota(jnp.int32, (32, LANES), 0) + (j * 32 + 1)).astype(F32)
                same = ids[pl.ds(pl.multiple_of(BEFORE + j * 32, 16), 32), :] == last
                entered = jnp.where(same, jnp.exp(-rate * passed) * state, 0.0)
                car_s[b, at, :] = car[b, at, :] + entered
                long = base[b, at, :] + tail * entered
                long_s[b, at, :] = long
                mixed_s[at, lanes] = (long * x0[b, at, :]).astype(BF16)
                return 0

            lax.fori_loop(0, groups, mix, 0)
        middle_s[...] = jnp.dot(mixed_s[...], wout[...], preferred_element_type=F32)

        def norm(j, _):
            at = pl.ds(pl.multiple_of(j * 32, 32), 32)
            start = pl.multiple_of(BEFORE + j * 32, 16)
            values = middle_s[at, :] + tok[pl.ds(start, 32), :].astype(F32)
            middle_s[at, :] = values
            out_s[at, :] = values
            n2_s[at, :] = (row_stats(values)[0] * gains[1:2, :]).astype(BF16)
            gn_s[at, :] = jnp.zeros_like(values)
            return 0

        lax.fori_loop(0, groups, norm, 0)
        pushing.await_greetings(barrier, 5 if summed else 0)

    def put(tile, part, grad):
        for half in range(2):
            if summed:
                sums.stage_in(tile, (half + c) % 2, part, MIX_ORDERS[part], grad[half])
            else:
                grads_o[0, half, :, part * LANES : (part + 1) * LANES] = grad[half]

    def note(row, i, lanes, value):
        if summed:
            held_b[i, 0, row : row + 1, lanes] = value
        else:
            at = pl.ds(pl.multiple_of(i * BLOCK + lanes.start, LANES), lanes.stop - lanes.start)
            small_b[row : row + 1, at] = value

    def feed(half, wup, wdn):
        n2, rows = n2_s[...], g[...]
        up = jnp.dot(n2, wup[...], preferred_element_type=F32)
        pulled = contract(rows, wdn[...], ((1,), (1,)))
        square = up * up
        inner = ROOT_TWO_OVER_PI * up * (1.0 + 0.044715 * square)
        bent = jnp.tanh(inner)
        part = 0.5 * (1.0 + bent)
        active = (up * part).astype(BF16)
        slope = part + (0.5 * ROOT_TWO_OVER_PI) * up * (1.0 - bent * bent) * (1.0 + 0.134145 * square)
        g_up = (pulled * slope).astype(BF16)
        out_s[...] += jnp.dot(active, wdn[...], preferred_element_type=F32)
        gn_s[...] += contract(g_up, wup[...], ((1,), (1,)))
        pair = (contract(n2, g_up, ((0,), (0,))).astype(BF16), contract(rows, active, ((0,), (0,))).astype(BF16))
        for k in range(2):
            if summed:
                for j in range(2):
                    columns = pair[k][:, j * LANES : (j + 1) * LANES]
                    sums.stage_in(step, half, 2 * k + j, FEED_ORDERS[2 * k + j], columns)
            else:
                grads_o[0, (half + c) % 2, :, k * PART : (k + 1) * PART] = pair[k]

    row_id = lax.broadcasted_iota(jnp.int32, (8, LANES), 0)
    zero = jnp.zeros((8, LANES), F32)

    @pl.when(step < TILES)
    def _():
        feed(0, wup_a, wdn_a)

    @pl.when(step == EPILOGUE)
    def _():
        if summed:
            for copy in shares(0, out_s, out_o):
                copy.start()
        else:
            out_o[...] = out_s[...]

        def back(j, total):
            at = pl.ds(pl.multiple_of(j * 32, 32), 32)
            normal, inverse = row_stats(middle_s[at, :])
            grad = gn_s[at, :]
            total += jnp.sum(grad * normal, axis=0, keepdims=True)
            scaled = grad * gains[1:2, :]
            cross = jnp.mean(scaled * normal, axis=1, keepdims=True)
            result = g[at, :].astype(F32) + inverse * (
                scaled - jnp.mean(scaled, axis=1, keepdims=True) - normal * cross)
            gmid_s[at, :] = result
            gout_s[at, :] = result.astype(BF16)
            gn_s[at, :] = jnp.zeros_like(grad)
            return total

        gain_two = lax.fori_loop(0, groups, back, jnp.zeros((1, full), F32))
        head_s[...] = jnp.zeros_like(head_s)
        head_s[0:1, :] = gain_two
        for i in range(steps):
            gmix = contract(gout_s[...], wout[i * BLOCK : (i + 1) * BLOCK, :], ((1,), (1,)))
            for k in range(BLOCK // LANES):
                b = i * (BLOCK // LANES) + k
                part = gmix[:, k * LANES : (k + 1) * LANES]
                glong_s[b, 0:block, :] = part * x0[b]
                long_s[b] = part * long_s[b]

    @pl.when(step == BACK)
    def _():
        for i in range(steps):
            for row in range(10, 16):
                note(row, i, slice(0, BLOCK), jnp.zeros((1, BLOCK), F32))
        joined_s[...] = jnp.zeros_like(joined_s)
        rate = vec[4:5, :]
        following = 2 * n + jnp.minimum(pushing.me + 1, 2 * n - 1)
        lasts = (marks[2 * n + pushing.me], marks[following])

        def use(k, state):
            first = marks[pushing.me + 1 + k]
            for row in range(2):
                if k >= row:
                    same = jnp.where(first == lasts[row], 1.0, 0.0)
                    joined_s[row : row + 1, :] += same * jnp.exp(-rate * float(block * (k - row) + 1)) * state

        pushing.take(use)

        @pl.when(pushing.me > 0)
        def _():
            halo_copy.wait_send()

        @pl.when(pushing.me < 2 * n - 1)
        def _():
            halo_copy.wait_recv()

        for b in range(lane_blocks):
            glong_s[b, block : block + 48, :] = halo_r[0:48, b * LANES : (b + 1) * LANES]

    @pl.when((step >= BACK) & (step <= last_back))
    def _():
        i = step - BACK
        two = range(2)
        lanes = [lanes_of(2 * i + k) for k in two]
        rates = [vec[4:5, lanes[k]] for k in two]
        scales = [vec[2:3, lanes[k]] - vec[3:4, lanes[k]] * vec[5:6, lanes[k]] for k in two]
        mine = [joined_s[0:1, lanes[k]] for k in two]
        for k in two:
            for s in range(3):
                proj_s[s, k] = proj[s, k].astype(F32)
        last = ids[pl.ds(BEFORE + block - 1, 1), :]

        def conv_at(s, k, start, size, same):
            value = vec[6 + s : 7 + s, lanes[k]] * proj_s[s, k, pl.ds(start, size), :]
            for j in (1, 2):
                tap = vec[6 + 3 * j + s : 7 + 3 * j + s, lanes[k]]
                value += jnp.where(same[j - 1], tap * proj_s[s, k, pl.ds(start - j, size), :], 0.0)
            return value

        def chunk(j, totals):
            at = pl.ds(pl.multiple_of(j * 32, 32), 32)
            start = pl.multiple_of(BEFORE + j * 32, 16)
            own = ids[pl.ds(start, 32), :]
            left = (block - 1 - j * 32 - lax.broadcasted_iota(jnp.int32, (32, LANES), 0)).astype(F32)
            after = rest_s[at, :]
            near = dist_s[at, :]
            grads, result = [], []
            for k in two:
                b = 2 * i + k
                state = q_s[b, at, :] + jnp.where(own == last, jnp.exp(-rates[k] * left) * mine[k], 0.0)
                result.append(totals[k] + jnp.sum((car_s[b, at, :] * state).reshape(4, 8, LANES), axis=0))
                grads.append(scales[k] * glong_s[b, at, :] + state)
            for tap in range(FIR):
                same = after >= float(tap)
                for k in two:
                    term = vec[16 + tap : 17 + tap, lanes[k]] * glong_s[2 * i + k, pl.ds(j * 32 + tap, 32), :]
                    grads[k] += jnp.where(same, term, 0.0)
            same = [near >= 1.0, near >= 2.0]
            for k in two:
                gc_s[0, k, at, :] = grads[k] * conv_at(2, k, start, 32, same)
                gc_s[1, k, at, :] = long_s[2 * i + k, at, :]
                gc_s[2, k, at, :] = grads[k] * conv_at(0, k, start, 32, same)
            return tuple(result)

        crossed = lax.fori_loop(0, groups, chunk, (zero, zero))
        for k in two:
            note(9, i, slice(k * LANES, (k + 1) * LANES), jnp.sum(crossed[k], axis=0, keepdims=True))

    def fed(tile, part, value):
        grads_o[:, lanes_at(tile * TILE + part * LANES)] = value

    def mixed(tile, part, value):
        grads_o[:, lanes_at(TILES * TILE + (tile - TILES) * len(MIX_ORDERS) * LANES + part * LANES)] = value

    def advance(step):
        if not summed:
            return
        for stage in range(STAGES - 1, -1, -1):
            for join, result, begun in joins:

                @when(step - 1 - stage == begun)
                def _():
                    join.advance(stage, result)

        for stage in range(STAGES - 1, -1, -1):
            since, early = step - 1 - stage, step - LAGS[stage]

            @when((early >= 0) & (early < TILES))
            def _():
                sums.advance(early, stage, FEED_ORDERS, fed)

            @when((since == GATE) | ((since >= BACK) & (since <= last_back)))
            def _():
                sums.advance(since - 1 - since // BACK, stage, MIX_ORDERS, mixed)

    advance(step)

    @pl.when(step < TILES)
    def _():
        feed(1, wup_b, wdn_b)
        if summed:
            sums.start(step, 0, FEED_ORDERS)

    @pl.when(step == EPILOGUE)
    def _():
        for i in range(steps):
            piece = contract(gout_s[...], mixed_s[:, i * BLOCK : (i + 1) * BLOCK], ((0,), (0,))).astype(BF16)
            put(TILES, i, [piece[:, half * LANES : (half + 1) * LANES] for half in range(2)])
        if summed:
            sums.start(TILES, 0, MIX_ORDERS)
        advance(GATE)

    @pl.when(step == EPILOGUE)
    def _():
        rates = [vec[4:5, b * LANES : (b + 1) * LANES] for b in range(lane_blocks)]
        tails = [vec[3:4, b * LANES : (b + 1) * LANES] * vec[5:6, b * LANES : (b + 1) * LANES] for b in range(lane_blocks)]
        lams = [[jnp.exp(-rate * float(k)) for k in (1, 2, 4)] for rate in rates]
        powers = [jnp.exp(-rate * (8 - row_id).astype(F32)) for rate in rates]

        def scan_group(i, carry):
            at = block // 8 - 1 - i
            to = pl.ds(pl.multiple_of(at * 8, 8), 8)
            start = pl.multiple_of(BEFORE + at * 8, 8)
            own = ids[pl.ds(start, 8), :]
            masks = [(own == ids[pl.ds(start + k, 8), :]) & (row_id < 8 - k) for k in (1, 2, 4)]
            joined = own == jnp.broadcast_to(ids[pl.ds(start + 8, 1), :], (8, LANES))
            states, biases, carries = [], [], []
            for b in range(lane_blocks):
                grad = glong_s[b, to, :]
                value = grad * tails[b]
                for mask, lam, k in zip(masks, lams[b], (1, 2, 4)):
                    value += jnp.where(mask, lam * pltpu.roll(value, 8 - k, 0), 0.0)
                value += jnp.where(joined, powers[b] * carry[0][b], 0.0)
                q_s[b, to, :] = value
                states.append(jnp.broadcast_to(value[0:1, :], (8, LANES)))
                biases.append(carry[1][b] + grad * u[b, pl.ds(start, 8), :])
                carries.append(carry[2][b] + grad * car_s[b, to, :])
            return tuple(states), tuple(biases), tuple(carries)

        many = (zero,) * lane_blocks
        states, biases, carries = lax.fori_loop(0, block // 8, scan_group, (many, many, many), unroll=2)
        for b in range(lane_blocks):
            lanes = slice(b * LANES, (b + 1) * LANES)
            first_s[:, lanes] = states[b][0:1, :]
            head_s[1:2, lanes] = jnp.sum(biases[b], axis=0, keepdims=True)
            head_s[2:3, lanes] = jnp.sum(carries[b], axis=0, keepdims=True)
            halo_s[0:48, lanes] = glong_s[b, 0:48, :]
            halo_s[48:56, lanes] = q_s[b, 0:8, :]
            halo_s[72:80, lanes] = long_s[b, 0:8, :]
        halo_s[56:72, :] = heads[...]
        pushing.start()

        @pl.when(pushing.me > 0)
        def _():
            halo_copy.start()
        advance(TAPS)

    @pl.when(step == EPILOGUE)
    def _():
        taps_s[...] = jnp.zeros_like(taps_s)

        def pairs(p, _):
            def chunk(j, _):
                at = pl.ds(pl.multiple_of(j * 32, 32), 32)
                start = BEFORE + j * 32
                near = dist_s[at, :]
                here = [glong_s[2 * p + k, at, :] for k in range(2)]
                for tap in range(FIR):
                    same = near >= float(tap)
                    for k in range(2):
                        term = jnp.where(same, here[k] * u[2 * p + k, pl.ds(start - tap, 32), :], 0.0)
                        taps_s[2 * p + k, tap] += jnp.sum(term.reshape(4, 8, LANES), axis=0)
                return 0

            lax.fori_loop(0, groups, chunk, 0)
            return 0

        lax.fori_loop(0, lane_blocks // 2, pairs, 0)
        result = joins[0][0].held.at[0] if summed else small_a
        for b in range(lane_blocks):
            lanes = slice(b * LANES, (b + 1) * LANES)
            result[0:FIR, lanes] = jnp.sum(taps_s[b], axis=1)
        result[FIR : FIR + 8, :] = head_s[...]
        if summed:
            joins[0][0].start(0)

    @pl.when((step >= BACK) & (step <= last_back))
    def _():
        i = step - BACK
        two = range(2)
        lanes = [lanes_of(2 * i + k) for k in two]
        rates = [vec[4:5, lanes[k]] for k in two]
        scales = [vec[2:3, lanes[k]] - vec[3:4, lanes[k]] * vec[5:6, lanes[k]] for k in two]
        start = BEFORE + block
        own = ids[pl.ds(start, 8), :]
        end_id = marks[2 * n + jnp.minimum(pushing.me + 1, 2 * n - 1)].astype(F32)
        left = (block - 1 - row_id).astype(F32)
        for k in two:
            b = 2 * i + k
            entered = jnp.exp(-rates[k] * left) * joined_s[1:2, lanes[k]]
            grad = halo_r[48:56, lanes[k]] + jnp.where(own == end_id, entered, 0.0)
            grad += scales[k] * glong_s[b, block : block + 8, :]
            for tap in range(FIR):
                term = vec[16 + tap : 17 + tap, lanes[k]] * glong_s[b, block + tap : block + tap + 8, :]
                grad += jnp.where(own == ids[pl.ds(start + tap, 8), :], term, 0.0)
            gc_s[0, k, block : block + 8, :] = grad * halo_r[56:64, lanes[k]]
            gc_s[1, k, block : block + 8, :] = halo_r[72:80, lanes[k]]
            gc_s[2, k, block : block + 8, :] = grad * halo_r[64:72, lanes[k]]

        for k in two:

            def short(j, totals):
                at = pl.ds(pl.multiple_of(j * 32, 32), 32)
                start = pl.multiple_of(BEFORE + j * 32, 16)
                same = [dist_s[at, :] >= float(d) for d in (1, 2)]
                later = [rest_s[at, :] >= float(d) for d in (1, 2)]
                result = []
                for s in range(3):
                    here = gc_s[s, k, at, :]
                    value = vec[6 + s : 7 + s, lanes[k]] * here
                    for d in (1, 2):
                        tap = vec[6 + 3 * d + s : 7 + 3 * d + s, lanes[k]]
                        value += jnp.where(later[d - 1], tap * gc_s[s, k, pl.ds(j * 32 + d, 32), :], 0.0)
                    gp_s[s, at, k * LANES : (k + 1) * LANES] = value.astype(BF16)
                    for d in range(3):
                        term = here * proj_s[s, k, pl.ds(start - d, 32), :]
                        if d:
                            term = jnp.where(same[d - 1], term, 0.0)
                        result.append(totals[3 * s + d] + jnp.sum(term.reshape(4, 8, LANES), axis=0))
                return tuple(result)

            totals = lax.fori_loop(0, groups, short, (zero,) * 9)
            rows = [None] * 9
            for s in range(3):
                for d in range(3):
                    rows[3 * d + s] = jnp.sum(totals[3 * s + d], axis=0, keepdims=True)
            for row, value in enumerate(rows):
                note(row, i, slice(k * LANES, (k + 1) * LANES), value)

        tile = TILES + 1 + i
        pieces = [contract(n1[...], gp_s[s], ((0,), (0,))).astype(BF16) for s in range(3)]
        for s, piece in enumerate(pieces):
            put(tile, s, [piece[:, half * LANES : (half + 1) * LANES] for half in range(2)])
        if summed:
            sums.start(tile, 0, MIX_ORDERS)
        for s in range(3):
            gn_s[...] += contract(gp_s[s], win[s], ((1,), (1,)))

    @pl.when(step == last_back)
    def _():
        def back(j, total):
            at = pl.ds(pl.multiple_of(j * 32, 32), 32)
            normal, inverse = row_stats(tok[pl.ds(pl.multiple_of(BEFORE + j * 32, 16), 32), :].astype(F32))
            grad = gn_s[at, :]
            total += jnp.sum(grad * normal, axis=0, keepdims=True)
            scaled = grad * gains[0:1, :]
            cross = jnp.mean(scaled * normal, axis=1, keepdims=True)
            middle_s[at, :] = gmid_s[at, :] + inverse * (
                scaled - jnp.mean(scaled, axis=1, keepdims=True) - normal * cross)
            return total

        gain_one = lax.fori_loop(0, groups, back, jnp.zeros((1, full), F32))
        for k in range(steps):
            note(10 + k, steps - 1, slice(0, BLOCK), gain_one[:, k * BLOCK : (k + 1) * BLOCK])
        if summed:
            for copy in shares(1, middle_s, gtok_o):
                copy.start()
        else:
            gtok_o[...] = middle_s[...]

    if summed:
        for join, _, begun in joins[1:]:

            @pl.when(step == begun)
            def _():
                join.start(0)

        @pl.when(step == last_back + 1)
        def _():
            for drain in range(2, STAGES + 1):
                advance(last_back + drain)
            for k, (src, dst) in enumerate(((out_s, out_o), (middle_s, gtok_o))):
                for copy in shares(k, src, dst):
                    copy.wait()


def backward(n, summed, marks, tok, ids, dist, rest, enter, g, gains, vec, wout, x0, base, car, u, n1, heads, ups, downs,
             win, proj):
    block, full = g.shape
    rows, lane_blocks = BEFORE + block, full // LANES
    steps = full // BLOCK
    tiles = TILES + 1 + steps
    reach = min(DOC_MOST // block + 1, 2 * n - 1)
    whole = lambda *shape: pl.BlockSpec(shape, lambda i: (0,) * len(shape), pipeline_mode=pl.Buffered(1))
    tile = lambda i: jnp.minimum(i, TILES - 1)
    back = lambda i: jnp.clip(i - TURN_OF_BACK, 0, steps - 1)
    wide = lambda dtype: pltpu.VMEM((block, full), dtype)
    stacked = lambda count, dtype=F32: pltpu.VMEM((lane_blocks, count, LANES), dtype)
    shape = jax.ShapeDtypeStruct
    if summed:
        columns = TILES * TILE + (1 + steps) * len(MIX_ORDERS) * LANES
        out_shape = [shape((full // 16, columns), F32), shape((FIR + 8, full), F32), shape((16, full), F32)]
        out_shape += [shape((2 * block, full // 2), F32)] * 2
        out_specs = [whole(full // 16, columns), whole(FIR + 8, full), whole(16, full)]
        out_specs += [pl.BlockSpec(memory_space=pl.ANY)] * 2
        extra = Summing.scratch(tiles, TILES, full // 16) + Joining.scratch(FIR + 8, full)
        extra += [pltpu.VMEM((steps, STAGES, 16, BLOCK), F32)] * 2 + [pltpu.SemaphoreType.DMA((steps, STAGES))] * 2
        extra += [pltpu.SemaphoreType.DMA((2,))] * 3
    else:
        out_shape = [shape((tiles, 2, full, TILE), BF16), shape((FIR + 8, full), F32), shape((16, full), F32)]
        out_shape += [shape((block, full), F32)] * 2
        place = lambda i: jnp.minimum(i, TILES - 1) + jnp.clip(i - EPILOGUE + 1, 0, 1) + jnp.clip(i - TURN_OF_BACK + 1, 0, steps)
        out_specs = [pl.BlockSpec((1, 2, full, TILE), lambda i: (place(i), 0, 0, 0)), whole(FIR + 8, full), whole(16, full)]
        out_specs += [whole(block, full)] * 2
        extra = []
    return pl.pallas_call(
        functools.partial(backward_kernel, n, block, reach, summed),
        name="backward",
        grid=(TURN_OF_BACK + steps + (1 if summed else 0),),
        out_shape=out_shape,
        in_specs=[
            pl.BlockSpec(memory_space=pltpu.SMEM),
            whole(*tok.shape), whole(*ids.shape), whole(*dist.shape), whole(*rest.shape), whole(*enter.shape), whole(*g.shape), whole(*gains.shape),
            whole(*vec.shape), whole(*wout.shape), whole(*x0.shape), whole(*base.shape), whole(*car.shape),
            whole(*u.shape), whole(*n1.shape), whole(*heads.shape),
            *[pl.BlockSpec((full, PART), lambda i: (0, tile(i)))] * 2,
            *[pl.BlockSpec((PART, full), lambda i: (tile(i), 0))] * 2,
            pl.BlockSpec((3, full, BLOCK), lambda i: (0, 0, back(i))),
            pl.BlockSpec((3, BLOCK // LANES, rows, LANES), lambda i: (0, back(i), 0, 0)),
        ],
        out_specs=out_specs,
        scratch_shapes=[
            wide(BF16), wide(F32), wide(BF16), wide(F32), wide(BF16), wide(F32), wide(F32),
            stacked(block), stacked(block), stacked(block + 48), stacked(block),
            pltpu.VMEM((3, BLOCK // LANES, block + 8, LANES), F32),
            pltpu.VMEM((3, block, BLOCK), BF16),
            pltpu.VMEM((3, BLOCK // LANES, rows, LANES), F32),
            pltpu.VMEM((lane_blocks, FIR, 8, LANES), F32),
            pltpu.VMEM((1, full), F32),
            pltpu.VMEM((reach, 1, full), F32),
            pltpu.VMEM((2, full), F32),
            pltpu.VMEM((HALO, full), F32),
            pltpu.VMEM((HALO, full), F32),
            pltpu.VMEM((8, full), F32),
            pltpu.SemaphoreType.DMA((reach,)),
            pltpu.SemaphoreType.DMA((reach,)),
            pltpu.SemaphoreType.DMA((2,)),
            *extra,
        ],
        compiler_params=pltpu.CompilerParams(collective_id=2, has_side_effects=True, vmem_limit_bytes=60 << 20),
    )(marks, tok, ids, dist, rest, enter, g, gains, vec, wout, x0, base, car, u, n1, heads, *ups, *downs, win, proj)


def reduce_plain(n, grads, small_a, small_b, out, gtok):
    both = lax.psum_scatter(grads.astype(F32), "ch", scatter_dimension=1, tiled=False)
    total = lax.psum_scatter(both, "seq", scatter_dimension=1, tiled=True)
    total = jnp.transpose(total, (1, 0, 2))
    used = len(MIX_ORDERS) * LANES
    total = jnp.concatenate([total[:, :TILES].reshape(total.shape[0], -1), total[:, TILES:, :used].reshape(total.shape[0], -1)], axis=1)
    swap = lambda whole: lax.all_to_all(whole, "ch", split_axis=1, concat_axis=0, tiled=True)
    small_a, small_b = lax.psum((small_a, small_b), ("seq", "ch"))
    return total, small_a, small_b, swap(out), swap(gtok)


def finish_kernel(total, small_a, small_b, gains, vec, table, w1, b1, w2, out, gtok,
                  out_o, gtok_o, gain_one_o, in_o, short_o, w1_o, b1_o, w2_o, w3_o, bias_o, tgain_o, trate_o,
                  outw_o, gain_two_o, up_o, down_o, out_v, gtok_v, sem):
    full = gains.shape[1]
    width, hidden = full // 2, up_o.shape[1]
    loads = [pltpu.make_async_copy(src, dst, sem.at[k]) for k, (src, dst) in enumerate(((out, out_v), (gtok, gtok_v)))]
    saves = [pltpu.make_async_copy(src, dst, sem.at[2 + k]) for k, (src, dst) in enumerate(((out_v, out_o), (gtok_v, gtok_o)))]
    for copy in loads:
        copy.start()

    def natural(rows):
        blocks = [rows[:, b * LANES : (b + 1) * LANES] for b in range(full // LANES)]
        return jnp.concatenate(blocks[0::2] + blocks[1::2], axis=1)

    raw = natural(small_a[0:FIR, :]) * filter_window(0, full, full)
    pre_one, hidden_one, pre_two, hidden_two = filter_layers(table[...], w1[...], b1[...], w2[...])

    def exact(left, right, dims):
        return lax.dot_general(left, right, (dims, ((), ())), precision=HIGHEST, preferred_element_type=F32)

    w3_o[...] = exact(hidden_two, raw, ((0,), (0,)))
    pre_two_grad = exact(raw, gains[8:, :], ((1,), (1,))) * jnp.cos(pre_two)
    w2_o[...] = exact(hidden_one, pre_two_grad, ((0,), (0,)))
    pre_one_grad = exact(pre_two_grad, w2[...], ((1,), (1,))) * jnp.cos(pre_one)
    w1_o[...] = exact(table[...], pre_one_grad, ((0,), (0,)))
    b1_o[...] = jnp.sum(pre_one_grad, axis=0, keepdims=True).reshape(b1_o.shape)

    for copy, following in zip(loads, saves):
        copy.wait()
        following.start()

    last = [small_b[10 + k : 11 + k, full - BLOCK : full] for k in range(full // BLOCK)]
    gain_one_o[...] = jnp.concatenate(last, axis=1).reshape(full)
    gain_two_o[...] = small_a[FIR : FIR + 1, :].reshape(full)
    bias_o[...] = natural(small_a[FIR + 1 : FIR + 2, :]).reshape(full)
    long_car, rate, nu = small_a[FIR + 2 : FIR + 3, :], vec[4:5, :], vec[5:6, :]
    factor = jnp.exp(-rate)
    tgain_o[...] = natural(nu * long_car).reshape(full)
    trate_o[...] = natural(vec[3:4, :] * long_car * factor * factor / nu - small_b[9:10, :]).reshape(full)
    short = natural(small_b[0:9, :])
    for j in range(3):
        for s in range(3):
            short_o[j, s : s + 1, :] = short[3 * j + s : 3 * j + s + 1, :]
    for k in range(TILES):
        up_o[:, k * PART : (k + 1) * PART] = total[:, k * TILE : k * TILE + PART]
        down_o[:, k * PART : (k + 1) * PART] = total[:, k * TILE + PART : (k + 1) * TILE]
    outw_o[...] = total[:, TILES * TILE : TILES * TILE + width]
    for i in range(width // LANES):
        for s in range(3):
            at = TILES * TILE + (1 + i) * len(MIX_ORDERS) * LANES + s * LANES
            in_o[s, :, i * LANES : (i + 1) * LANES] = total[:, at : at + LANES]
    for copy in saves:
        copy.wait()


def finish(total, small_a, small_b, gains, vec, table, w1, b1, w2, out, gtok):
    full, rows = gains.shape[1], total.shape[0]
    width, hidden = full // 2, TILES * PART
    shape = jax.ShapeDtypeStruct
    vmem, anywhere = pl.BlockSpec(memory_space=pltpu.VMEM), pl.BlockSpec(memory_space=pl.ANY)
    vector = shape((full,), F32)
    return pl.pallas_call(
        finish_kernel,
        name="finish",
        out_shape=(
            shape(out.shape, F32), shape(gtok.shape, F32), vector, shape((3, rows, width), F32), shape((3, 3, full), F32),
            shape(w1.shape, F32), shape((b1.shape[1],), F32), shape(w2.shape, F32), shape((w2.shape[0], full), F32),
            vector, vector, vector, shape((rows, width), F32), vector, shape((rows, hidden), F32), shape((rows, hidden), F32),
        ),
        in_specs=[vmem] * 9 + [anywhere] * 2,
        out_specs=(anywhere, anywhere) + (vmem,) * 14,
        scratch_shapes=[pltpu.VMEM(out.shape, F32), pltpu.VMEM(gtok.shape, F32), pltpu.SemaphoreType.DMA((4,))],
        compiler_params=pltpu.CompilerParams(vmem_limit_bytes=VMEM_LIMIT),
    )(total, small_a, small_b, gains, vec, table, w1, b1, w2, out, gtok)


def on_device(tokens, seg_ids, norm1_gain, in_weight, short_weight, filt_w1, filt_b1, filt_w2, filt_w3,
              long_bias, tail_gain, tail_rate, out_weight, norm2_gain, up_weight, down_weight, grad_out):
    rows, width = tokens.shape
    full, block = 2 * width, rows // 2
    n = lax.axis_size("seq")
    devices = 2 * n
    me = 2 * lax.axis_index("seq") + lax.axis_index("ch")
    row_start = me * block
    total_rows = seg_ids.shape[0]
    length = min(SEQ_LEN, total_rows)

    keys = seg_ids + (jnp.arange(total_rows, dtype=jnp.int32) // length) * 65536
    padded = jnp.concatenate([jnp.full((BEFORE,), -1, jnp.int32), keys, jnp.full((block + AFTER,), -2, jnp.int32)])
    near = lax.dynamic_slice_in_dim(padded, row_start, BEFORE + block + AFTER)
    window = near
    ids = jnp.broadcast_to(window.astype(F32)[:, None], (window.shape[0], LANES))

    table = position_table(FIR, (filt_w1.shape[0] - 1) // 2)
    norm_tail = jnp.sqrt(-jnp.expm1(-2.0 * tail_rate))
    vectors = (norm1_gain, norm2_gain, long_bias, tail_gain, tail_rate, norm_tail, short_weight)
    filt_b1 = filt_b1[None, :]
    marks = jnp.concatenate([keys[::block], keys[block - 1 :: block]])
    (tok, g, win, wout, up_other, down_other, gains, vec, n1, proj, x0, u, heads, base, car, dist, rest, enter) = forward(
        n, marks, tokens, grad_out, jnp.transpose(in_weight, (1, 0, 2)), out_weight, up_weight, down_weight,
        filt_w3, table, filt_w1, filt_b1, filt_w2, vectors, ids)

    summed = n == 16
    results = backward(
        n, summed, marks, tok, ids, dist, rest, enter, g, gains, vec, wout, x0, base, car, u, n1, heads,
        (up_weight, up_other), (down_weight, down_other), win, proj)
    if not summed:
        results = reduce_plain(n, *results)
    total, small_a, small_b, out, gtok = results

    (out, gtok, gain_one, in_grad, short_grad, w1_grad, b1_grad, w2_grad, w3_grad, bias_grad, tail_gain_grad, rate_grad,
     out_grad, gain_two, up_grad, down_grad) = finish(
        total, small_a, small_b, gains, vec, table, filt_w1, filt_b1, filt_w2, out, gtok)
    return (
        out, gtok, gain_one, jnp.transpose(in_grad, (1, 0, 2)), short_grad, w1_grad, b1_grad, w2_grad, w3_grad, bias_grad,
        tail_gain_grad, rate_grad, out_grad.T, gain_two, up_grad, down_grad.T,
    )


def solution(mesh):
    placed = (
        P("seq", "ch"),
        P(),
        P("ch"),
        P(None, None, "ch"),
        P(None, None, "ch"),
        P(),
        P(),
        P(),
        P(None, "ch"),
        P("ch"),
        P("ch"),
        P("ch"),
        P("ch", None),
        P("ch"),
        P(None, "ch"),
        P("ch", None),
        P("seq", "ch"),
    )
    return jax.shard_map(
        on_device,
        mesh=mesh,
        in_specs=placed,
        out_specs=(
            P("seq", "ch"),
            P("seq", "ch"),
            P(),
            P("seq", None, "ch"),
            P(),
            P(),
            P(),
            P(),
            P(),
            P(),
            P(),
            P(),
            P("ch", "seq"),
            P(),
            P("seq", "ch"),
            P("ch", "seq"),
        ),
        check_vma=False,
    )
```

```python
import functools

import jax
import jax.numpy as jnp
import numpy as np
from jax import lax
from jax.experimental import pallas as pl
from jax.experimental.pallas import tpu as pltpu
from jax.sharding import PartitionSpec as P

FIR = 32
SEQ_LEN = 16384
DOC_MOST = 8192
EPSILON = 1e-05
FREQUENCY = 0.4
HIGHEST = lax.Precision.HIGHEST
MESH = pl.DeviceIdType.MESH
F32, BF16 = jnp.float32, jnp.bfloat16

BEFORE = 48
AFTER = 80
LANES = 128
BLOCK = 256
CHUNK = 64
SUMS = 48
HEAD = 16
VMEM_LIMIT = 56 << 20
ROOT_TWO_OVER_PI = 0.7978845608028654


def position_table(filter_len, band_count):
    places = np.arange(filter_len, dtype=np.float32)
    harmonics = np.arange(1, band_count + 1, dtype=np.float32)
    angles = (np.float32(FREQUENCY) * places[:, None] * harmonics[None, :]).astype(np.float64)
    table = np.concatenate([places[:, None] / filter_len, np.cos(angles), np.sin(angles)], axis=1)
    return jnp.asarray(table.astype(np.float32))


def filter_layers(table, w1, b1, w2):
    pre_one = jnp.dot(table, w1, precision=HIGHEST, preferred_element_type=F32) + b1
    hidden_one = jnp.sin(pre_one)
    pre_two = jnp.dot(hidden_one, w2, precision=HIGHEST, preferred_element_type=F32)
    return pre_one, hidden_one, pre_two, jnp.sin(pre_two)


def filter_window(start, count, full):
    channel = (start + lax.broadcasted_iota(jnp.int32, (FIR, count), 1)).astype(F32)
    place = lax.broadcasted_iota(jnp.int32, (FIR, count), 0).astype(F32)
    return jnp.exp(-(0.5 + 3.0 * channel / full) * place / FIR)


def device_of(index):
    return (index // 2, index % 2)


class Pushing:
    def __init__(self, n, reach, backward, source, slots, send_sem, recv_sem):
        self.total, self.reach = 2 * n, reach
        self.me = 2 * lax.axis_index("seq") + lax.axis_index("ch")
        self.ahead = -1 if backward else 1
        self.place = self.total - 1 - self.me if backward else self.me
        self.source, self.slots, self.send_sem, self.recv_sem = source, slots, send_sem, recv_sem

    def greet(self, barrier):
        for k in range(self.reach):

            @pl.when(self.place - 1 - k >= 0)
            def _():
                pl.semaphore_signal(
                    barrier, inc=1, device_id=device_of(self.me - self.ahead * (1 + k)), device_id_type=MESH)

    def await_greetings(self, barrier, others):
        following = self.total - 1 - self.place
        for count in range(0, self.reach + 1):
            if count + others:

                @pl.when((following >= count) if count == self.reach else (following == count))
                def _():
                    pl.semaphore_wait(barrier, count + others)

    def copy(self, k):
        return pltpu.make_async_remote_copy(
            src_ref=self.source, dst_ref=self.slots.at[k], send_sem=self.send_sem.at[k], recv_sem=self.recv_sem.at[k],
            device_id=device_of(self.me + self.ahead * (1 + k)), device_id_type=MESH)

    def start(self):
        for k in range(self.reach):

            @pl.when(self.place + 1 + k < self.total)
            def _():
                self.copy(k).start()

    def take(self, use):
        for k in range(self.reach):

            @pl.when(self.place - 1 - k >= 0)
            def _():
                self.copy(k).wait_recv()
                use(k, self.slots[k])

            @pl.when(self.place + 1 + k < self.total)
            def _():
                self.copy(k).wait_send()


def row_stats(values):
    center = jnp.mean(values, axis=1, keepdims=True)
    shifted = values - center
    inverse = lax.rsqrt(jnp.mean(shifted * shifted, axis=1, keepdims=True) + EPSILON)
    return shifted * inverse, inverse


def forward_kernel(n, rows, reach, marks, tokens, gout, w_in, w_out, w_up, w_down, filt_w3, table, filt_w1, filt_b1, filt_w2,
                   norms_a, norms_b, biases, tails, decays, nus, shorts, ids,
                   tok_o, g_o, in_o, out_o, up_o, down_o, gains_o, vec_o,
                   n1_o, proj_o, x0_o, u_o, heads_o, long_o, car_o, dist_o, rest_o, enter_o,
                   tok_v, g_v, in_v, out_v, gains_v, vec_v, gains, head, n1_s, proj_s, u_s, state_s, end_s, slots_s,
                   local_sem, store_sem, send_sem, recv_sem, push_send, push_recv):
    block, full = rows // 2, in_v.shape[1]
    width = full // 2
    steps = full // BLOCK
    two = range(BLOCK // LANES)
    step = pl.program_id(0)
    s, c = lax.axis_index("seq"), lax.axis_index("ch")
    barrier = pltpu.get_barrier_semaphore()
    pushing = Pushing(n, reach, False, end_s, slots_s, push_send, push_recv)
    partner = (s, 1 - c)
    cols = pl.ds(pl.multiple_of(c * width, width), width)
    early = [(gains, gains_v.at[pl.ds(0, 8), cols]), (filt_w3, gains_v.at[pl.ds(8, filt_w3.shape[0]), cols])]
    late = []
    for i in range(width // LANES):
        source = pl.ds(i * LANES, LANES)
        paired = pl.ds(pl.multiple_of((2 * i + c) * LANES, LANES), LANES)
        early += [
            (head.at[:, source], vec_v.at[pl.ds(0, HEAD), paired]),
            (w_in.at[:, :, source], in_v.at[:, :, paired]),
        ]
        late.append((w_out.at[source, :], out_v.at[paired, :]))

    def remote(src, dst, k, target=partner):
        return pltpu.make_async_remote_copy(
            src_ref=src, dst_ref=dst, send_sem=send_sem.at[k], recv_sem=recv_sem.at[k],
            device_id=target, device_id_type=MESH)

    halves = [(early[k], k) for k in range(len(early))] + [(late[k], len(early) + k) for k in range(len(late))]
    count = len(halves)
    far = [remote(w_up, up_o, count), remote(w_down, down_o, count + 1)]
    at_tokens = count + 2

    left, right = pl.ds(0, width), pl.ds(width, width)
    first, second = pl.ds(0, block), pl.ds(block, block)
    ahead, tail = pl.ds(block - BEFORE, block + BEFORE), pl.ds(rows - BEFORE, BEFORE)
    main = pl.ds(BEFORE, block)
    keeps = [
        [(tokens.at[first, :], tok_v.at[main, left]), (gout.at[first, :], g_v.at[:, left])],
        [(tokens.at[ahead, :], tok_v.at[:, right]), (gout.at[second, :], g_v.at[:, right])],
    ]
    sends = [
        [(tokens.at[ahead, :], tok_v.at[:, left]), (gout.at[second, :], g_v.at[:, left])],
        [(tokens.at[first, :], tok_v.at[main, right]), (gout.at[first, :], g_v.at[:, right])],
    ]

    def edge(which, target):
        return remote(
            tokens.at[tail, :], tok_v.at[pl.ds(0, BEFORE), (left, right)[which]], at_tokens + 2 + which, target)

    def for_core(action):
        for which in range(2):

            @pl.when(c == which)
            def _():
                action(which)

    stores = [(tok_v, tok_o), (gains_v, gains_o), (vec_v, vec_o), (in_v, in_o), (g_v, g_o), (out_v, out_o)]

    def store(k):
        return pltpu.make_async_copy(*stores[k], store_sem.at[k])

    @pl.when(step == 0)
    def _():
        pushing.greet(barrier)
        pl.semaphore_signal(barrier, inc=1, device_id=partner, device_id_type=MESH)

        @pl.when((c == 0) & (s > 0))
        def _():
            for k in range(2):
                pl.semaphore_signal(barrier, inc=1, device_id=(s - 1, k), device_id_type=MESH)

        gains[...] = jnp.zeros_like(gains)
        head[...] = jnp.zeros_like(head)
        for ref, row, value in ((gains, 0, norms_a), (gains, 1, norms_b), (head, 2, biases), (head, 3, tails),
                                (head, 4, decays), (head, 5, nus)):
            ref[row : row + 1, :] = value[...].reshape(1, width)
        for j in range(3):
            for t in range(3):
                head[6 + 3 * j + t : 7 + 3 * j + t, :] = shorts[j, t : t + 1, :]

        def begin_own(which):
            for k, (src, dst) in enumerate(keeps[which]):
                pltpu.make_async_copy(src, dst, local_sem.at[at_tokens + k]).start()

        for_core(begin_own)
        for (src, dst), k in halves:
            pltpu.make_async_copy(src, dst, local_sem.at[k]).start()

        @pl.when(s < n - 1)
        def _():
            pushing.await_greetings(barrier, 2)

        @pl.when(s == n - 1)
        def _():
            pushing.await_greetings(barrier, 1)

        def begin(which):
            remote(*sends[which][0], at_tokens).start()

            @pl.when(s < n - 1)
            def _():
                edge(which, (s + 1, 0)).start()

        for_core(begin)
        for (src, dst), k in halves[: len(early)]:
            remote(src, dst, k).start()
        for_core(lambda which: remote(*sends[which][1], at_tokens + 1).start())
        for (src, dst), k in halves[len(early) :]:
            remote(src, dst, k).start()
        for copy in far:
            copy.start()

        def distances(j, _):
            at = pl.ds(pl.multiple_of(j * 32, 32), 32)
            start = pl.multiple_of(BEFORE + j * 32, 16)
            own = ids[pl.ds(start, 32), :]
            before = after = jnp.zeros((32, LANES), F32)
            for k in range(1, FIR):
                before += jnp.where(own == ids[pl.ds(start - k, 32), :], 1.0, 0.0)
                after += jnp.where(own == ids[pl.ds(start + k, 32), :], 1.0, 0.0)
            dist_o[at, :] = before
            rest_o[at, :] = after
            return 0

        lax.fori_loop(0, block // 32, distances, 0)

        def take_tokens(which):
            remote(*sends[which][0], at_tokens).wait_send()
            remote(*sends[1 - which][0], at_tokens).wait_recv()
            pltpu.make_async_copy(*keeps[which][0], local_sem.at[at_tokens]).wait()

            @pl.when(s < n - 1)
            def _():
                edge(which, (s + 1, 0)).wait_send()

            if which == 0:

                @pl.when(s > 0)
                def _():
                    for k in range(2):
                        edge(k, partner).wait_recv()

        for_core(take_tokens)
        hidden_two = filter_layers(table[...], filt_w1[...], filt_b1[...], filt_w2[...])[3]
        for (src, dst), k in halves[:2]:
            pltpu.make_async_copy(src, dst, local_sem.at[k]).wait()
            remote(src, dst, k).wait()
        store(0).start()
        store(1).start()

        def normed(j, _):
            at = pl.ds(pl.multiple_of(j * 80, 16), 80)
            values = jnp.where(ids[at, 0:1] >= 0.0, tok_v[at, :].astype(F32), 0.0)
            n1_s[at, :] = (row_stats(values)[0] * gains_v[0:1, :]).astype(BF16)
            return 0

        lax.fori_loop(0, (BEFORE + block) // 80, normed, 0)
        n1_o[...] = n1_s[pl.ds(BEFORE, block), :]
        for (src, dst), k in halves[2 : len(early)]:
            pltpu.make_async_copy(src, dst, local_sem.at[k]).wait()
            remote(src, dst, k).wait()
        taps = jnp.dot(hidden_two, gains_v[8:, :], precision=HIGHEST, preferred_element_type=F32)
        taps *= filter_window(0, full, full)
        for i in range(width // LANES):
            for half in range(2):
                source = half * width + i * LANES
                vec_v[HEAD : HEAD + FIR, (2 * i + half) * LANES : (2 * i + half + 1) * LANES] = (
                    taps[:, source : source + LANES])
        store(2).start()
        store(3).start()

    @pl.when(step < steps)
    def _():
        lanes = [pl.ds(pl.multiple_of((2 * step + b) * LANES, LANES), LANES) for b in two]
        wide = pl.ds(pl.multiple_of(step * BLOCK, BLOCK), BLOCK)
        for t in range(3):
            part = jnp.dot(n1_s[...], in_v[t, :, wide], preferred_element_type=F32).astype(BF16)
            for b in two:
                proj_o[t, b] = part[:, b * LANES : (b + 1) * LANES]
                proj_s[t, b] = part[:, b * LANES : (b + 1) * LANES].astype(F32)

        def convolved(start, size):
            own = ids[pl.ds(start, size), :]
            same = [None] + [own == ids[pl.ds(start - j, size), :] for j in (1, 2)]
            results = []
            for b in two:
                streams = []
                for t in range(3):
                    value = vec_v[6 + t : 7 + t, lanes[b]] * proj_s[t, b, pl.ds(start, size), :]
                    for j in (1, 2):
                        tap = vec_v[6 + 3 * j + t : 7 + 3 * j + t, lanes[b]]
                        value += jnp.where(same[j], tap * proj_s[t, b, pl.ds(start - j, size), :], 0.0)
                    streams.append(value)
                gated = (streams[0] * streams[2]).astype(BF16).astype(F32)
                u_s[2 * step + b, pl.ds(start, size), :] = gated
                u_o[b, pl.ds(start, size), :] = gated
                results.append(streams)
            return results

        convolved(16, 32)
        for b, streams in enumerate(convolved(BEFORE, 8)):
            heads_o[0:8, b * LANES : (b + 1) * LANES] = streams[2]
            heads_o[8:16, b * LANES : (b + 1) * LANES] = streams[0]
            u_o[b, 0:16, :] = jnp.zeros((16, LANES), F32)
            u_s[2 * step + b, 0:16, :] = jnp.zeros((16, LANES), F32)

        def conv_chunk(j, _):
            start = pl.multiple_of(BEFORE + j * 32, 16)
            for b, streams in enumerate(convolved(start, 32)):
                x0_o[b, pl.ds(pl.multiple_of(j * 32, 32), 32), :] = streams[1]
            return 0

        lax.fori_loop(0, block // 32, conv_chunk, 0)

        row_id = lax.broadcasted_iota(jnp.int32, (8, LANES), 0)
        rates = [vec_v[4:5, lanes[b]] for b in two]
        powers = [jnp.exp(-rate * (row_id + 1).astype(F32)) for rate in rates]
        lams = [[jnp.exp(-rate * float(k)) for k in (1, 2, 4)] for rate in rates]
        for b in two:
            state_s[2 * step + b, 0:8, :] = jnp.zeros((8, LANES), F32)

        def scan_group(g, carry):
            start = pl.multiple_of(BEFORE + g * 8, 8)
            own = ids[pl.ds(start, 8), :]
            masks = [(own == ids[pl.ds(start - k, 8), :]) & (row_id >= k) for k in (1, 2, 4)]
            joined = own == jnp.broadcast_to(ids[pl.ds(start - 1, 1), :], (8, LANES))
            result = []
            for b in two:
                value = u_s[2 * step + b, pl.ds(start, 8), :]
                for mask, lam, k in zip(masks, lams[b], (1, 2, 4)):
                    value += jnp.where(mask, lam * pltpu.roll(value, k, 0), 0.0)
                value += jnp.where(joined, powers[b] * carry[b], 0.0)
                state_s[2 * step + b, pl.ds(pl.multiple_of(8 + g * 8, 8), 8), :] = value
                result.append(jnp.broadcast_to(value[7:8, :], (8, LANES)))
            return tuple(result)

        zero = jnp.zeros((8, LANES), F32)
        final = lax.fori_loop(0, block // 8, scan_group, (zero,) * len(two), unroll=8)
        for b in two:
            end_s[:, lanes[b]] = final[b][0:1, :]

    @pl.when(step == steps - 1)
    def _():
        pushing.start()

    @pl.when(step >= steps)
    def _():
        i = step - steps
        lanes = [pl.ds(pl.multiple_of((2 * i + b) * LANES, LANES), LANES) for b in two]
        lam = [jnp.exp(-vec_v[4:5, lanes[b]]) for b in two]
        tails = [vec_v[3:4, lanes[b]] * vec_v[5:6, lanes[b]] for b in two]

        def long_chunk(j, _):
            at = pl.ds(pl.multiple_of(j * 32, 32), 32)
            start = pl.multiple_of(BEFORE + j * 32, 16)
            near = dist_o[at, :]
            totals = []
            for b in two:
                previous = state_s[2 * i + b, pl.ds(7 + j * 32, 32), :]
                carried = jnp.where(near >= 1.0, lam[b] * previous, 0.0)
                car_o[b, at, :] = carried
                here = u_s[2 * i + b, pl.ds(start, 32), :]
                totals.append((vec_v[2:3, lanes[b]] + vec_v[16:17, lanes[b]]) * here + tails[b] * carried)
            for k in range(1, FIR):
                same = near >= float(k)
                for b in two:
                    term = vec_v[16 + k : 17 + k, lanes[b]] * u_s[2 * i + b, pl.ds(start - k, 32), :]
                    totals[b] += jnp.where(same, term, 0.0)
            for b in two:
                long_o[b, at, :] = totals[b]
            return 0

        lax.fori_loop(0, block // 32, long_chunk, 0)

    @pl.when(step == steps)
    def _():
        def take_rows(which):
            remote(*sends[which][1], at_tokens + 1).wait_send()
            remote(*sends[1 - which][1], at_tokens + 1).wait_recv()
            pltpu.make_async_copy(*keeps[which][1], local_sem.at[at_tokens + 1]).wait()

        for_core(take_rows)
        for (src, dst), k in halves[len(early) :]:
            pltpu.make_async_copy(src, dst, local_sem.at[k]).wait()
            remote(src, dst, k).wait()
        store(4).start()
        store(5).start()

    @pl.when(step == 2 * steps - 1)
    def _():
        enter_o[...] = jnp.zeros_like(enter_o)
        rate = vec_v[4:5, :]
        last = marks[2 * n + jnp.maximum(pushing.me - 1, 0)]

        def use(k, state):
            same = jnp.where(marks[2 * n + pushing.me - 1 - k] == last, 1.0, 0.0)
            enter_o[...] += same * jnp.exp(-rate * float(block * k)) * state

        pushing.take(use)
        for copy in far:
            copy.wait()
        for k in range(len(stores)):
            store(k).wait()


def forward(n, marks, tokens, gout, w_in, w_out, w_up, w_down, filt_w3, table, filt_w1, filt_b1, filt_w2, vectors, ids):
    rows, width = tokens.shape
    hidden = w_up.shape[1]
    full, block = 2 * width, rows // 2
    window = BEFORE + block
    steps, lane_blocks = full // BLOCK, full // LANES
    reach = min(DOC_MOST // block, 2 * n - 1)
    anywhere = pl.BlockSpec(memory_space=pl.ANY)
    whole = lambda *shape: pl.BlockSpec(shape, lambda i: (0,) * len(shape), pipeline_mode=pl.Buffered(1))
    soon, later = lambda i: jnp.minimum(i, steps - 1), lambda i: jnp.maximum(i - steps, 0)
    stacked = lambda count, place: pl.BlockSpec((BLOCK // LANES, count, LANES), lambda i: (place(i), 0, 0))
    shape = jax.ShapeDtypeStruct
    vmem = pltpu.VMEM
    far = 2 + 3 * (width // LANES) + 2 + 4
    dma = pltpu.SemaphoreType.DMA
    landing = [
        ((window, full), BF16), ((block, full), BF16), ((3, full, full), BF16), ((full, full), BF16),
        ((8 + filt_w3.shape[0], full), F32), ((HEAD + FIR, full), F32),
    ]
    return pl.pallas_call(
        functools.partial(forward_kernel, n, rows, reach),
        name="forward",
        grid=(2 * steps,),
        out_shape=(
            *[shape(*part) for part in landing[:4]],
            shape((full, hidden), BF16),
            shape((hidden, full), BF16),
            *[shape(*part) for part in landing[4:]],
            shape((block, full), BF16),
            shape((3, lane_blocks, window, LANES), BF16),
            shape((lane_blocks, block, LANES), F32),
            shape((lane_blocks, window, LANES), F32),
            shape((16, full), F32),
            shape((lane_blocks, block, LANES), F32),
            shape((lane_blocks, block, LANES), F32),
            shape((block, LANES), F32),
            shape((block, LANES), F32),
            shape((1, full), F32),
        ),
        in_specs=[pl.BlockSpec(memory_space=pltpu.SMEM)] + [anywhere] * 7 + [
            whole(*part.shape) for part in (table, filt_w1, filt_b1, filt_w2, *vectors, ids)],
        out_specs=(
            *[anywhere] * 8,
            whole(block, full),
            pl.BlockSpec((3, BLOCK // LANES, window, LANES), lambda i: (0, soon(i), 0, 0)),
            stacked(block, soon),
            stacked(window, soon),
            pl.BlockSpec((16, BLOCK), lambda i: (0, soon(i))),
            stacked(block, later),
            stacked(block, later),
            whole(block, LANES),
            whole(block, LANES),
            whole(1, full),
        ),
        scratch_shapes=[
            *[vmem(*part) for part in landing],
            vmem((8, width), F32),
            vmem((HEAD, width), F32),
            vmem((window, full), BF16),
            vmem((3, BLOCK // LANES, window, LANES), F32),
            vmem((lane_blocks, window, LANES), F32),
            vmem((lane_blocks, 8 + block, LANES), F32),
            vmem((1, full), F32),
            vmem((reach, 1, full), F32),
            dma((far,)), dma((6,)), dma((far,)), dma((far,)), dma((reach,)), dma((reach,)),
        ],
        compiler_params=pltpu.CompilerParams(collective_id=0, has_side_effects=True, vmem_limit_bytes=VMEM_LIMIT),
    )(marks, tokens, gout, w_in, w_out, w_up, w_down, filt_w3, table, filt_w1, filt_b1, filt_w2, *vectors, ids)


TILE = 512
PART = TILE // 2
STAGES = 5
FEED_ORDERS = ((0, 1, 2, 3), (0, 2, 3, 1), (1, 0, 2, 3), (1, 2, 3, 0))
MIX_ORDERS = ((0, 1, 2, 3), (1, 0, 2, 3), (2, 0, 1, 3))


class Summing:
    def __init__(self, slots, rows, staged, first, second, third, fourth, fifth, send_sem, recv_sem):
        self.slots, self.rows, self.staged = slots, rows, staged
        self.held = (first, second, third, fourth, fifth)
        self.send_sem, self.recv_sem = send_sem, recv_sem
        self.s, self.c = lax.axis_index("seq"), lax.axis_index("ch")
        self.bits = [(self.s // (1 << b)) % 2 for b in range(4)]
        self.peers = [(self.s + (1 - 2 * bit) * (1 << b), self.c) for b, bit in enumerate(self.bits)]
        self.partner = (self.s, 1 - self.c)

    @staticmethod
    def scratch(tiles, slots, rows):
        parts = len(FEED_ORDERS)
        return [
            pltpu.VMEM((2, 2, parts, 2, 2, 2, 2, rows, LANES), BF16),
            pltpu.VMEM((slots, parts, 2, 2, 2, 2, rows, LANES), BF16),
            pltpu.VMEM((slots, parts, 2, 2, 2, rows, LANES), BF16),
            pltpu.VMEM((slots, parts, 2, 2, rows, LANES), BF16),
            pltpu.VMEM((slots, parts, 2, rows, LANES), BF16),
            pltpu.VMEM((slots, parts, rows, LANES), BF16),
            pltpu.SemaphoreType.DMA((tiles, 1 + 4 * parts)),
            pltpu.SemaphoreType.DMA((tiles, 1 + 4 * parts)),
        ]

    def greet(self, barrier):
        for peer in [self.partner] + self.peers:
            pl.semaphore_signal(barrier, inc=1, device_id=peer, device_id_type=MESH)

    def remote(self, src, dst, tile, k, target):
        return pltpu.make_async_remote_copy(
            src_ref=src, dst_ref=dst, send_sem=self.send_sem.at[tile, k], recv_sem=self.recv_sem.at[tile, k],
            device_id=target, device_id_type=MESH)

    def stage_in(self, tile, whose, part, order, grad):
        for q in range(16):
            at = [(q >> bit) & 1 for bit in order]
            self.staged[(tile % 2, whose, part, *at)] = grad[q * self.rows : (q + 1) * self.rows]

    def copies(self, tile, stage, orders):
        slot = tile % self.slots
        if stage == 0:
            parts = pl.ds(0, len(orders))
            return [self.remote(self.staged.at[tile % 2, 1, parts], self.held[0].at[slot, parts], tile, 0, self.partner)]
        result = []
        for part, order in enumerate(orders):
            bit = order[stage - 1]
            src, dst = self.held[stage - 1].at[slot, part, 1 - self.bits[bit]], self.held[stage].at[slot, part]
            result.append(self.remote(src, dst, tile, 1 + 4 * (stage - 1) + part, self.peers[bit]))
        return result

    def start(self, tile, stage, orders):
        for copy in self.copies(tile, stage, orders):
            copy.start()

    def advance(self, tile, stage, orders, total):
        slot = tile % self.slots
        arriving = self.copies(tile, stage, orders)
        following = self.copies(tile, stage + 1, orders) if stage < STAGES - 1 else []
        if stage == 0:
            arriving[0].wait()
        for part, order in enumerate(orders):
            if stage == 0:

                def add(i, _):
                    for q in range(8):
                        at = (q >> 2 & 1, q >> 1 & 1, q & 1)
                        self.held[0][(slot, part, i, *at)] += self.staged[(tile % 2, 0, part, i, *at)]
                    return 0

                lax.fori_loop(0, 2, add, 0)
            else:
                arriving[part].wait()
                mine = self.bits[order[stage - 1]]
                for e in range(1 << (4 - stage)):
                    inner = [(e >> (3 - stage - k)) & 1 for k in range(4 - stage)]
                    source = self.held[stage - 1][(slot, part, mine, *inner)]
                    if stage == STAGES - 1:
                        total(tile, part, source.astype(F32) + self.held[stage][slot, part].astype(F32))
                    else:
                        self.held[stage][(slot, part, *inner)] += source
            if following:
                following[part].start()


class Joining:
    def __init__(self, sums, held, arrived, send_sem, recv_sem):
        self.held, self.arrived, self.send_sem, self.recv_sem = held, arrived, send_sem, recv_sem
        self.targets = [sums.partner] + sums.peers

    @staticmethod
    def scratch(*shape):
        return [pltpu.VMEM((STAGES,) + shape, F32), pltpu.VMEM((STAGES,) + shape, F32),
                pltpu.SemaphoreType.DMA((STAGES,)), pltpu.SemaphoreType.DMA((STAGES,))]

    def copy(self, stage):
        return pltpu.make_async_remote_copy(
            src_ref=self.held.at[stage], dst_ref=self.arrived.at[stage], send_sem=self.send_sem.at[stage],
            recv_sem=self.recv_sem.at[stage], device_id=self.targets[stage], device_id_type=MESH)

    def start(self, stage):
        self.copy(stage).start()

    def advance(self, stage, result):
        self.copy(stage).wait()
        total = self.held[stage] + self.arrived[stage]
        if stage == STAGES - 1:
            result(total)
        else:
            self.held[stage + 1] = total
            self.start(stage + 1)


def contract(left, right, dims):
    return lax.dot_general(left, right, (dims, ((), ())), preferred_element_type=F32)


def contract(left, right, dims):
    return lax.dot_general(left, right, (dims, ((), ())), preferred_element_type=F32)


TILES = 6
EPILOGUE, GATE, TAPS, BACK = TILES, TILES + 1, TILES + 2, TILES + 3
TURN_OF_BACK = TILES + 1
LAGS = (1, 3, 5, 6, 7)
HALO = 80


def when(condition):
    if isinstance(condition, bool):
        return lambda body: body() if condition else None
    return pl.when(condition)


def lanes_at(start):
    return pl.ds(start if isinstance(start, int) else pl.multiple_of(start, LANES), LANES)


def backward_kernel(n, block, reach, summed, marks, tok, ids, dist_s, rest_s, enter, g, gains, vec, wout, x0, base, car, u, n1, heads,
                    wup_a, wup_b, wdn_a, wdn_b, win, proj, *refs):
    full = g.shape[1]
    width, lane_blocks = full // 2, full // LANES
    steps = full // BLOCK
    last_back = BACK + steps - 1
    (grads_o, small_a, small_b, out_o, gtok_o), refs = refs[:5], refs[5:]
    (mixed_s, middle_s, n2_s, gn_s, gout_s, out_s, gmid_s, long_s, car_s, glong_s, q_s, gc_s, gp_s, proj_s,
     taps_s, first_s, slots_s, joined_s, halo_s, halo_r, head_s,
     push_send, push_recv, halo_sem, *buffers) = refs
    turn = pl.program_id(0)
    step = turn + (BACK - TURN_OF_BACK) * (turn // TURN_OF_BACK)
    groups = block // 32
    barrier = pltpu.get_barrier_semaphore()
    pushing = Pushing(n, reach, True, first_s, slots_s, push_send, push_recv)
    c = lax.axis_index("ch")
    lanes_of = lambda b: pl.ds(pl.multiple_of(b * LANES, LANES), LANES)
    if summed:
        sums = Summing(TILES, full // 16, *buffers[:8])
        held_b = buffers[12]
        joins = [(Joining(sums, *buffers[8:12]), lambda value: small_a.__setitem__(Ellipsis, value), TAPS)]
        for k in range(steps):
            at = slice(k * BLOCK, (k + 1) * BLOCK)
            joins.append((Joining(sums, *[ref.at[k] for ref in buffers[12:16]]),
                          lambda value, at=at: small_b.__setitem__((slice(None), at), value), BACK + k))
        local_sem, exchange_send, exchange_recv = buffers[16:]

        def shares(k, src, dst):
            at = pl.ds(pl.multiple_of(c * block, block), block)
            of_core = lambda which: src.at[:, pl.ds(pl.multiple_of(which * width, width), width)]
            return (
                pltpu.make_async_copy(of_core(c), dst.at[at, :], local_sem.at[k]),
                pltpu.make_async_remote_copy(
                    src_ref=of_core(1 - c), dst_ref=dst.at[at, :], send_sem=exchange_send.at[k],
                    recv_sem=exchange_recv.at[k], device_id=sums.partner, device_id_type=MESH),
            )

    halo_copy = pltpu.make_async_remote_copy(
        src_ref=halo_s, dst_ref=halo_r, send_sem=halo_sem.at[0], recv_sem=halo_sem.at[1],
        device_id=device_of(pushing.me - 1), device_id_type=MESH)

    @pl.when(step == 0)
    def _():
        pushing.greet(barrier)
        if summed:
            sums.greet(barrier)

        last = ids[pl.ds(BEFORE - 1, 1), :]
        for b in range(lane_blocks):
            lanes = slice(b * LANES, (b + 1) * LANES)
            rate, tail = vec[4:5, lanes], vec[3:4, lanes] * vec[5:6, lanes]
            state = enter[0:1, lanes]

            def mix(j, _):
                at = pl.ds(pl.multiple_of(j * 32, 32), 32)
                passed = (lax.broadcasted_iota(jnp.int32, (32, LANES), 0) + (j * 32 + 1)).astype(F32)
                same = ids[pl.ds(pl.multiple_of(BEFORE + j * 32, 16), 32), :] == last
                entered = jnp.where(same, jnp.exp(-rate * passed) * state, 0.0)
                car_s[b, at, :] = car[b, at, :] + entered
                long = base[b, at, :] + tail * entered
                long_s[b, at, :] = long
                mixed_s[at, lanes] = (long * x0[b, at, :]).astype(BF16)
                return 0

            lax.fori_loop(0, groups, mix, 0)
        middle_s[...] = jnp.dot(mixed_s[...], wout[...], preferred_element_type=F32)

        def norm(j, _):
            at = pl.ds(pl.multiple_of(j * 32, 32), 32)
            start = pl.multiple_of(BEFORE + j * 32, 16)
            values = middle_s[at, :] + tok[pl.ds(start, 32), :].astype(F32)
            middle_s[at, :] = values
            out_s[at, :] = values
            n2_s[at, :] = (row_stats(values)[0] * gains[1:2, :]).astype(BF16)
            gn_s[at, :] = jnp.zeros_like(values)
            return 0

        lax.fori_loop(0, groups, norm, 0)
        pushing.await_greetings(barrier, 5 if summed else 0)

    def put(tile, part, grad):
        for half in range(2):
            if summed:
                sums.stage_in(tile, (half + c) % 2, part, MIX_ORDERS[part], grad[half])
            else:
                grads_o[0, half, :, part * LANES : (part + 1) * LANES] = grad[half]

    def note(row, i, lanes, value):
        if summed:
            held_b[i, 0, row : row + 1, lanes] = value
        else:
            at = pl.ds(pl.multiple_of(i * BLOCK + lanes.start, LANES), lanes.stop - lanes.start)
            small_b[row : row + 1, at] = value

    def feed(half, wup, wdn):
        n2, rows = n2_s[...], g[...]
        up = jnp.dot(n2, wup[...], preferred_element_type=F32)
        pulled = contract(rows, wdn[...], ((1,), (1,)))
        square = up * up
        inner = ROOT_TWO_OVER_PI * up * (1.0 + 0.044715 * square)
        bent = jnp.tanh(inner)
        part = 0.5 * (1.0 + bent)
        active = (up * part).astype(BF16)
        slope = part + (0.5 * ROOT_TWO_OVER_PI) * up * (1.0 - bent * bent) * (1.0 + 0.134145 * square)
        g_up = (pulled * slope).astype(BF16)
        out_s[...] += jnp.dot(active, wdn[...], preferred_element_type=F32)
        gn_s[...] += contract(g_up, wup[...], ((1,), (1,)))
        pair = (contract(n2, g_up, ((0,), (0,))).astype(BF16), contract(rows, active, ((0,), (0,))).astype(BF16))
        for k in range(2):
            if summed:
                for j in range(2):
                    columns = pair[k][:, j * LANES : (j + 1) * LANES]
                    sums.stage_in(step, half, 2 * k + j, FEED_ORDERS[2 * k + j], columns)
            else:
                grads_o[0, (half + c) % 2, :, k * PART : (k + 1) * PART] = pair[k]

    row_id = lax.broadcasted_iota(jnp.int32, (8, LANES), 0)
    zero = jnp.zeros((8, LANES), F32)

    @pl.when(step < TILES)
    def _():
        feed(0, wup_a, wdn_a)

    @pl.when(step == EPILOGUE)
    def _():
        if summed:
            for copy in shares(0, out_s, out_o):
                copy.start()
        else:
            out_o[...] = out_s[...]

        def back(j, total):
            at = pl.ds(pl.multiple_of(j * 32, 32), 32)
            normal, inverse = row_stats(middle_s[at, :])
            grad = gn_s[at, :]
            total += jnp.sum(grad * normal, axis=0, keepdims=True)
            scaled = grad * gains[1:2, :]
            cross = jnp.mean(scaled * normal, axis=1, keepdims=True)
            result = g[at, :].astype(F32) + inverse * (
                scaled - jnp.mean(scaled, axis=1, keepdims=True) - normal * cross)
            gmid_s[at, :] = result
            gout_s[at, :] = result.astype(BF16)
            gn_s[at, :] = jnp.zeros_like(grad)
            return total

        gain_two = lax.fori_loop(0, groups, back, jnp.zeros((1, full), F32))
        head_s[...] = jnp.zeros_like(head_s)
        head_s[0:1, :] = gain_two
        for i in range(steps):
            gmix = contract(gout_s[...], wout[i * BLOCK : (i + 1) * BLOCK, :], ((1,), (1,)))
            for k in range(BLOCK // LANES):
                b = i * (BLOCK // LANES) + k
                part = gmix[:, k * LANES : (k + 1) * LANES]
                glong_s[b, 0:block, :] = part * x0[b]
                long_s[b] = part * long_s[b]

    @pl.when(step == BACK)
    def _():
        for i in range(steps):
            for row in range(10, 16):
                note(row, i, slice(0, BLOCK), jnp.zeros((1, BLOCK), F32))
        joined_s[...] = jnp.zeros_like(joined_s)
        rate = vec[4:5, :]
        following = 2 * n + jnp.minimum(pushing.me + 1, 2 * n - 1)
        lasts = (marks[2 * n + pushing.me], marks[following])

        def use(k, state):
            first = marks[pushing.me + 1 + k]
            for row in range(2):
                if k >= row:
                    same = jnp.where(first == lasts[row], 1.0, 0.0)
                    joined_s[row : row + 1, :] += same * jnp.exp(-rate * float(block * (k - row) + 1)) * state

        pushing.take(use)

        @pl.when(pushing.me > 0)
        def _():
            halo_copy.wait_send()

        @pl.when(pushing.me < 2 * n - 1)
        def _():
            halo_copy.wait_recv()

        for b in range(lane_blocks):
            glong_s[b, block : block + 48, :] = halo_r[0:48, b * LANES : (b + 1) * LANES]

    @pl.when((step >= BACK) & (step <= last_back))
    def _():
        i = step - BACK
        two = range(2)
        lanes = [lanes_of(2 * i + k) for k in two]
        rates = [vec[4:5, lanes[k]] for k in two]
        scales = [vec[2:3, lanes[k]] - vec[3:4, lanes[k]] * vec[5:6, lanes[k]] for k in two]
        mine = [joined_s[0:1, lanes[k]] for k in two]
        for k in two:
            for s in range(3):
                proj_s[s, k] = proj[s, k].astype(F32)
        last = ids[pl.ds(BEFORE + block - 1, 1), :]

        def conv_at(s, k, start, size, same):
            value = vec[6 + s : 7 + s, lanes[k]] * proj_s[s, k, pl.ds(start, size), :]
            for j in (1, 2):
                tap = vec[6 + 3 * j + s : 7 + 3 * j + s, lanes[k]]
                value += jnp.where(same[j - 1], tap * proj_s[s, k, pl.ds(start - j, size), :], 0.0)
            return value

        def chunk(j, totals):
            at = pl.ds(pl.multiple_of(j * 32, 32), 32)
            start = pl.multiple_of(BEFORE + j * 32, 16)
            own = ids[pl.ds(start, 32), :]
            left = (block - 1 - j * 32 - lax.broadcasted_iota(jnp.int32, (32, LANES), 0)).astype(F32)
            after = rest_s[at, :]
            near = dist_s[at, :]
            grads, result = [], []
            for k in two:
                b = 2 * i + k
                state = q_s[b, at, :] + jnp.where(own == last, jnp.exp(-rates[k] * left) * mine[k], 0.0)
                result.append(totals[k] + jnp.sum((car_s[b, at, :] * state).reshape(4, 8, LANES), axis=0))
                grads.append(scales[k] * glong_s[b, at, :] + state)
            for tap in range(FIR):
                same = after >= float(tap)
                for k in two:
                    term = vec[16 + tap : 17 + tap, lanes[k]] * glong_s[2 * i + k, pl.ds(j * 32 + tap, 32), :]
                    grads[k] += jnp.where(same, term, 0.0)
            same = [near >= 1.0, near >= 2.0]
            for k in two:
                gc_s[0, k, at, :] = grads[k] * conv_at(2, k, start, 32, same)
                gc_s[1, k, at, :] = long_s[2 * i + k, at, :]
                gc_s[2, k, at, :] = grads[k] * conv_at(0, k, start, 32, same)
            return tuple(result)

        crossed = lax.fori_loop(0, groups, chunk, (zero, zero))
        for k in two:
            note(9, i, slice(k * LANES, (k + 1) * LANES), jnp.sum(crossed[k], axis=0, keepdims=True))

    def fed(tile, part, value):
        grads_o[:, lanes_at(tile * TILE + part * LANES)] = value

    def mixed(tile, part, value):
        grads_o[:, lanes_at(TILES * TILE + (tile - TILES) * len(MIX_ORDERS) * LANES + part * LANES)] = value

    def advance(step):
        if not summed:
            return
        for stage in range(STAGES - 1, -1, -1):
            for join, result, begun in joins:

                @when(step - 1 - stage == begun)
                def _():
                    join.advance(stage, result)

        for stage in range(STAGES - 1, -1, -1):
            since, early = step - 1 - stage, step - LAGS[stage]

            @when((early >= 0) & (early < TILES))
            def _():
                sums.advance(early, stage, FEED_ORDERS, fed)

            @when((since == GATE) | ((since >= BACK) & (since <= last_back)))
            def _():
                sums.advance(since - 1 - since // BACK, stage, MIX_ORDERS, mixed)

    advance(step)

    @pl.when(step < TILES)
    def _():
        feed(1, wup_b, wdn_b)
        if summed:
            sums.start(step, 0, FEED_ORDERS)

    @pl.when(step == EPILOGUE)
    def _():
        for i in range(steps):
            piece = contract(gout_s[...], mixed_s[:, i * BLOCK : (i + 1) * BLOCK], ((0,), (0,))).astype(BF16)
            put(TILES, i, [piece[:, half * LANES : (half + 1) * LANES] for half in range(2)])
        if summed:
            sums.start(TILES, 0, MIX_ORDERS)
        advance(GATE)

    @pl.when(step == EPILOGUE)
    def _():
        rates = [vec[4:5, b * LANES : (b + 1) * LANES] for b in range(lane_blocks)]
        tails = [vec[3:4, b * LANES : (b + 1) * LANES] * vec[5:6, b * LANES : (b + 1) * LANES] for b in range(lane_blocks)]
        lams = [[jnp.exp(-rate * float(k)) for k in (1, 2, 4)] for rate in rates]
        powers = [jnp.exp(-rate * (8 - row_id).astype(F32)) for rate in rates]

        def scan_group(i, carry):
            at = block // 8 - 1 - i
            to = pl.ds(pl.multiple_of(at * 8, 8), 8)
            start = pl.multiple_of(BEFORE + at * 8, 8)
            own = ids[pl.ds(start, 8), :]
            masks = [(own == ids[pl.ds(start + k, 8), :]) & (row_id < 8 - k) for k in (1, 2, 4)]
            joined = own == jnp.broadcast_to(ids[pl.ds(start + 8, 1), :], (8, LANES))
            states, biases, carries = [], [], []
            for b in range(lane_blocks):
                grad = glong_s[b, to, :]
                value = grad * tails[b]
                for mask, lam, k in zip(masks, lams[b], (1, 2, 4)):
                    value += jnp.where(mask, lam * pltpu.roll(value, 8 - k, 0), 0.0)
                value += jnp.where(joined, powers[b] * carry[0][b], 0.0)
                q_s[b, to, :] = value
                states.append(jnp.broadcast_to(value[0:1, :], (8, LANES)))
                biases.append(carry[1][b] + grad * u[b, pl.ds(start, 8), :])
                carries.append(carry[2][b] + grad * car_s[b, to, :])
            return tuple(states), tuple(biases), tuple(carries)

        many = (zero,) * lane_blocks
        states, biases, carries = lax.fori_loop(0, block // 8, scan_group, (many, many, many), unroll=4)
        for b in range(lane_blocks):
            lanes = slice(b * LANES, (b + 1) * LANES)
            first_s[:, lanes] = states[b][0:1, :]
            head_s[1:2, lanes] = jnp.sum(biases[b], axis=0, keepdims=True)
            head_s[2:3, lanes] = jnp.sum(carries[b], axis=0, keepdims=True)
            halo_s[0:48, lanes] = glong_s[b, 0:48, :]
            halo_s[48:56, lanes] = q_s[b, 0:8, :]
            halo_s[72:80, lanes] = long_s[b, 0:8, :]
        halo_s[56:72, :] = heads[...]
        pushing.start()

        @pl.when(pushing.me > 0)
        def _():
            halo_copy.start()
        advance(TAPS)

    @pl.when(step == EPILOGUE)
    def _():
        taps_s[...] = jnp.zeros_like(taps_s)

        def pairs(p, _):
            def chunk(j, _):
                at = pl.ds(pl.multiple_of(j * 32, 32), 32)
                start = BEFORE + j * 32
                near = dist_s[at, :]
                here = [glong_s[2 * p + k, at, :] for k in range(2)]
                for tap in range(FIR):
                    same = near >= float(tap)
                    for k in range(2):
                        term = jnp.where(same, here[k] * u[2 * p + k, pl.ds(start - tap, 32), :], 0.0)
                        taps_s[2 * p + k, tap] += jnp.sum(term.reshape(4, 8, LANES), axis=0)
                return 0

            lax.fori_loop(0, groups, chunk, 0)
            return 0

        lax.fori_loop(0, lane_blocks // 2, pairs, 0)
        result = joins[0][0].held.at[0] if summed else small_a
        for b in range(lane_blocks):
            lanes = slice(b * LANES, (b + 1) * LANES)
            result[0:FIR, lanes] = jnp.sum(taps_s[b], axis=1)
        result[FIR : FIR + 8, :] = head_s[...]
        if summed:
            joins[0][0].start(0)

    @pl.when((step >= BACK) & (step <= last_back))
    def _():
        i = step - BACK
        two = range(2)
        lanes = [lanes_of(2 * i + k) for k in two]
        rates = [vec[4:5, lanes[k]] for k in two]
        scales = [vec[2:3, lanes[k]] - vec[3:4, lanes[k]] * vec[5:6, lanes[k]] for k in two]
        start = BEFORE + block
        own = ids[pl.ds(start, 8), :]
        end_id = marks[2 * n + jnp.minimum(pushing.me + 1, 2 * n - 1)].astype(F32)
        left = (block - 1 - row_id).astype(F32)
        for k in two:
            b = 2 * i + k
            entered = jnp.exp(-rates[k] * left) * joined_s[1:2, lanes[k]]
            grad = halo_r[48:56, lanes[k]] + jnp.where(own == end_id, entered, 0.0)
            grad += scales[k] * glong_s[b, block : block + 8, :]
            for tap in range(FIR):
                term = vec[16 + tap : 17 + tap, lanes[k]] * glong_s[b, block + tap : block + tap + 8, :]
                grad += jnp.where(own == ids[pl.ds(start + tap, 8), :], term, 0.0)
            gc_s[0, k, block : block + 8, :] = grad * halo_r[56:64, lanes[k]]
            gc_s[1, k, block : block + 8, :] = halo_r[72:80, lanes[k]]
            gc_s[2, k, block : block + 8, :] = grad * halo_r[64:72, lanes[k]]

        for k in two:

            def short(j, totals):
                at = pl.ds(pl.multiple_of(j * 32, 32), 32)
                start = pl.multiple_of(BEFORE + j * 32, 16)
                same = [dist_s[at, :] >= float(d) for d in (1, 2)]
                later = [rest_s[at, :] >= float(d) for d in (1, 2)]
                result = []
                for s in range(3):
                    here = gc_s[s, k, at, :]
                    value = vec[6 + s : 7 + s, lanes[k]] * here
                    for d in (1, 2):
                        tap = vec[6 + 3 * d + s : 7 + 3 * d + s, lanes[k]]
                        value += jnp.where(later[d - 1], tap * gc_s[s, k, pl.ds(j * 32 + d, 32), :], 0.0)
                    gp_s[s, at, k * LANES : (k + 1) * LANES] = value.astype(BF16)
                    for d in range(3):
                        term = here * proj_s[s, k, pl.ds(start - d, 32), :]
                        if d:
                            term = jnp.where(same[d - 1], term, 0.0)
                        result.append(totals[3 * s + d] + jnp.sum(term.reshape(4, 8, LANES), axis=0))
                return tuple(result)

            totals = lax.fori_loop(0, groups, short, (zero,) * 9)
            rows = [None] * 9
            for s in range(3):
                for d in range(3):
                    rows[3 * d + s] = jnp.sum(totals[3 * s + d], axis=0, keepdims=True)
            for row, value in enumerate(rows):
                note(row, i, slice(k * LANES, (k + 1) * LANES), value)

        tile = TILES + 1 + i
        pieces = [contract(n1[...], gp_s[s], ((0,), (0,))).astype(BF16) for s in range(3)]
        for s, piece in enumerate(pieces):
            put(tile, s, [piece[:, half * LANES : (half + 1) * LANES] for half in range(2)])
        if summed:
            sums.start(tile, 0, MIX_ORDERS)
        for s in range(3):
            gn_s[...] += contract(gp_s[s], win[s], ((1,), (1,)))

    @pl.when(step == last_back)
    def _():
        def back(j, total):
            at = pl.ds(pl.multiple_of(j * 32, 32), 32)
            normal, inverse = row_stats(tok[pl.ds(pl.multiple_of(BEFORE + j * 32, 16), 32), :].astype(F32))
            grad = gn_s[at, :]
            total += jnp.sum(grad * normal, axis=0, keepdims=True)
            scaled = grad * gains[0:1, :]
            cross = jnp.mean(scaled * normal, axis=1, keepdims=True)
            middle_s[at, :] = gmid_s[at, :] + inverse * (
                scaled - jnp.mean(scaled, axis=1, keepdims=True) - normal * cross)
            return total

        gain_one = lax.fori_loop(0, groups, back, jnp.zeros((1, full), F32))
        for k in range(steps):
            note(10 + k, steps - 1, slice(0, BLOCK), gain_one[:, k * BLOCK : (k + 1) * BLOCK])
        if summed:
            for copy in shares(1, middle_s, gtok_o):
                copy.start()
        else:
            gtok_o[...] = middle_s[...]

    if summed:
        for join, _, begun in joins[1:]:

            @pl.when(step == begun)
            def _():
                join.start(0)

        @pl.when(step == last_back + 1)
        def _():
            for drain in range(2, STAGES + 1):
                advance(last_back + drain)
            for k, (src, dst) in enumerate(((out_s, out_o), (middle_s, gtok_o))):
                for copy in shares(k, src, dst):
                    copy.wait()


def backward(n, summed, marks, tok, ids, dist, rest, enter, g, gains, vec, wout, x0, base, car, u, n1, heads, ups, downs,
             win, proj):
    block, full = g.shape
    rows, lane_blocks = BEFORE + block, full // LANES
    steps = full // BLOCK
    tiles = TILES + 1 + steps
    reach = min(DOC_MOST // block + 1, 2 * n - 1)
    whole = lambda *shape: pl.BlockSpec(shape, lambda i: (0,) * len(shape), pipeline_mode=pl.Buffered(1))
    tile = lambda i: jnp.minimum(i, TILES - 1)
    back = lambda i: jnp.clip(i - TURN_OF_BACK, 0, steps - 1)
    wide = lambda dtype: pltpu.VMEM((block, full), dtype)
    stacked = lambda count, dtype=F32: pltpu.VMEM((lane_blocks, count, LANES), dtype)
    shape = jax.ShapeDtypeStruct
    if summed:
        columns = TILES * TILE + (1 + steps) * len(MIX_ORDERS) * LANES
        out_shape = [shape((full // 16, columns), F32), shape((FIR + 8, full), F32), shape((16, full), F32)]
        out_shape += [shape((2 * block, full // 2), F32)] * 2
        out_specs = [whole(full // 16, columns), whole(FIR + 8, full), whole(16, full)]
        out_specs += [pl.BlockSpec(memory_space=pl.ANY)] * 2
        extra = Summing.scratch(tiles, TILES, full // 16) + Joining.scratch(FIR + 8, full)
        extra += [pltpu.VMEM((steps, STAGES, 16, BLOCK), F32)] * 2 + [pltpu.SemaphoreType.DMA((steps, STAGES))] * 2
        extra += [pltpu.SemaphoreType.DMA((2,))] * 3
    else:
        out_shape = [shape((tiles, 2, full, TILE), BF16), shape((FIR + 8, full), F32), shape((16, full), F32)]
        out_shape += [shape((block, full), F32)] * 2
        place = lambda i: jnp.minimum(i, TILES - 1) + jnp.clip(i - EPILOGUE + 1, 0, 1) + jnp.clip(i - TURN_OF_BACK + 1, 0, steps)
        out_specs = [pl.BlockSpec((1, 2, full, TILE), lambda i: (place(i), 0, 0, 0)), whole(FIR + 8, full), whole(16, full)]
        out_specs += [whole(block, full)] * 2
        extra = []
    return pl.pallas_call(
        functools.partial(backward_kernel, n, block, reach, summed),
        name="backward",
        grid=(TURN_OF_BACK + steps + (1 if summed else 0),),
        out_shape=out_shape,
        in_specs=[
            pl.BlockSpec(memory_space=pltpu.SMEM),
            whole(*tok.shape), whole(*ids.shape), whole(*dist.shape), whole(*rest.shape), whole(*enter.shape), whole(*g.shape), whole(*gains.shape),
            whole(*vec.shape), whole(*wout.shape), whole(*x0.shape), whole(*base.shape), whole(*car.shape),
            whole(*u.shape), whole(*n1.shape), whole(*heads.shape),
            *[pl.BlockSpec((full, PART), lambda i: (0, tile(i)))] * 2,
            *[pl.BlockSpec((PART, full), lambda i: (tile(i), 0))] * 2,
            pl.BlockSpec((3, full, BLOCK), lambda i: (0, 0, back(i))),
            pl.BlockSpec((3, BLOCK // LANES, rows, LANES), lambda i: (0, back(i), 0, 0)),
        ],
        out_specs=out_specs,
        scratch_shapes=[
            wide(BF16), wide(F32), wide(BF16), wide(F32), wide(BF16), wide(F32), wide(F32),
            stacked(block), stacked(block), stacked(block + 48), stacked(block),
            pltpu.VMEM((3, BLOCK // LANES, block + 8, LANES), F32),
            pltpu.VMEM((3, block, BLOCK), BF16),
            pltpu.VMEM((3, BLOCK // LANES, rows, LANES), F32),
            pltpu.VMEM((lane_blocks, FIR, 8, LANES), F32),
            pltpu.VMEM((1, full), F32),
            pltpu.VMEM((reach, 1, full), F32),
            pltpu.VMEM((2, full), F32),
            pltpu.VMEM((HALO, full), F32),
            pltpu.VMEM((HALO, full), F32),
            pltpu.VMEM((8, full), F32),
            pltpu.SemaphoreType.DMA((reach,)),
            pltpu.SemaphoreType.DMA((reach,)),
            pltpu.SemaphoreType.DMA((2,)),
            *extra,
        ],
        compiler_params=pltpu.CompilerParams(collective_id=2, has_side_effects=True, vmem_limit_bytes=60 << 20),
    )(marks, tok, ids, dist, rest, enter, g, gains, vec, wout, x0, base, car, u, n1, heads, *ups, *downs, win, proj)


def reduce_plain(n, grads, small_a, small_b, out, gtok):
    both = lax.psum_scatter(grads.astype(F32), "ch", scatter_dimension=1, tiled=False)
    total = lax.psum_scatter(both, "seq", scatter_dimension=1, tiled=True)
    total = jnp.transpose(total, (1, 0, 2))
    used = len(MIX_ORDERS) * LANES
    total = jnp.concatenate([total[:, :TILES].reshape(total.shape[0], -1), total[:, TILES:, :used].reshape(total.shape[0], -1)], axis=1)
    swap = lambda whole: lax.all_to_all(whole, "ch", split_axis=1, concat_axis=0, tiled=True)
    small_a, small_b = lax.psum((small_a, small_b), ("seq", "ch"))
    return total, small_a, small_b, swap(out), swap(gtok)


def finish_kernel(total, small_a, small_b, gains, vec, table, w1, b1, w2, out, gtok,
                  out_o, gtok_o, gain_one_o, in_o, short_o, w1_o, b1_o, w2_o, w3_o, bias_o, tgain_o, trate_o,
                  outw_o, gain_two_o, up_o, down_o, out_v, gtok_v, sem):
    full = gains.shape[1]
    width, hidden = full // 2, up_o.shape[1]
    loads = [pltpu.make_async_copy(src, dst, sem.at[k]) for k, (src, dst) in enumerate(((out, out_v), (gtok, gtok_v)))]
    saves = [pltpu.make_async_copy(src, dst, sem.at[2 + k]) for k, (src, dst) in enumerate(((out_v, out_o), (gtok_v, gtok_o)))]
    for copy in loads:
        copy.start()

    def natural(rows):
        blocks = [rows[:, b * LANES : (b + 1) * LANES] for b in range(full // LANES)]
        return jnp.concatenate(blocks[0::2] + blocks[1::2], axis=1)

    raw = natural(small_a[0:FIR, :]) * filter_window(0, full, full)
    pre_one, hidden_one, pre_two, hidden_two = filter_layers(table[...], w1[...], b1[...], w2[...])

    def exact(left, right, dims):
        return lax.dot_general(left, right, (dims, ((), ())), precision=HIGHEST, preferred_element_type=F32)

    w3_o[...] = exact(hidden_two, raw, ((0,), (0,)))
    pre_two_grad = exact(raw, gains[8:, :], ((1,), (1,))) * jnp.cos(pre_two)
    w2_o[...] = exact(hidden_one, pre_two_grad, ((0,), (0,)))
    pre_one_grad = exact(pre_two_grad, w2[...], ((1,), (1,))) * jnp.cos(pre_one)
    w1_o[...] = exact(table[...], pre_one_grad, ((0,), (0,)))
    b1_o[...] = jnp.sum(pre_one_grad, axis=0, keepdims=True).reshape(b1_o.shape)

    for copy, following in zip(loads, saves):
        copy.wait()
        following.start()

    last = [small_b[10 + k : 11 + k, full - BLOCK : full] for k in range(full // BLOCK)]
    gain_one_o[...] = jnp.concatenate(last, axis=1).reshape(full)
    gain_two_o[...] = small_a[FIR : FIR + 1, :].reshape(full)
    bias_o[...] = natural(small_a[FIR + 1 : FIR + 2, :]).reshape(full)
    long_car, rate, nu = small_a[FIR + 2 : FIR + 3, :], vec[4:5, :], vec[5:6, :]
    factor = jnp.exp(-rate)
    tgain_o[...] = natural(nu * long_car).reshape(full)
    trate_o[...] = natural(vec[3:4, :] * long_car * factor * factor / nu - small_b[9:10, :]).reshape(full)
    short = natural(small_b[0:9, :])
    for j in range(3):
        for s in range(3):
            short_o[j, s : s + 1, :] = short[3 * j + s : 3 * j + s + 1, :]
    for k in range(TILES):
        up_o[:, k * PART : (k + 1) * PART] = total[:, k * TILE : k * TILE + PART]
        down_o[:, k * PART : (k + 1) * PART] = total[:, k * TILE + PART : (k + 1) * TILE]
    outw_o[...] = total[:, TILES * TILE : TILES * TILE + width]
    for i in range(width // LANES):
        for s in range(3):
            at = TILES * TILE + (1 + i) * len(MIX_ORDERS) * LANES + s * LANES
            in_o[s, :, i * LANES : (i + 1) * LANES] = total[:, at : at + LANES]
    for copy in saves:
        copy.wait()


def finish(total, small_a, small_b, gains, vec, table, w1, b1, w2, out, gtok):
    full, rows = gains.shape[1], total.shape[0]
    width, hidden = full // 2, TILES * PART
    shape = jax.ShapeDtypeStruct
    vmem, anywhere = pl.BlockSpec(memory_space=pltpu.VMEM), pl.BlockSpec(memory_space=pl.ANY)
    vector = shape((full,), F32)
    return pl.pallas_call(
        finish_kernel,
        name="finish",
        out_shape=(
            shape(out.shape, F32), shape(gtok.shape, F32), vector, shape((3, rows, width), F32), shape((3, 3, full), F32),
            shape(w1.shape, F32), shape((b1.shape[1],), F32), shape(w2.shape, F32), shape((w2.shape[0], full), F32),
            vector, vector, vector, shape((rows, width), F32), vector, shape((rows, hidden), F32), shape((rows, hidden), F32),
        ),
        in_specs=[vmem] * 9 + [anywhere] * 2,
        out_specs=(anywhere, anywhere) + (vmem,) * 14,
        scratch_shapes=[pltpu.VMEM(out.shape, F32), pltpu.VMEM(gtok.shape, F32), pltpu.SemaphoreType.DMA((4,))],
        compiler_params=pltpu.CompilerParams(vmem_limit_bytes=VMEM_LIMIT),
    )(total, small_a, small_b, gains, vec, table, w1, b1, w2, out, gtok)


def on_device(tokens, seg_ids, norm1_gain, in_weight, short_weight, filt_w1, filt_b1, filt_w2, filt_w3,
              long_bias, tail_gain, tail_rate, out_weight, norm2_gain, up_weight, down_weight, grad_out):
    rows, width = tokens.shape
    full, block = 2 * width, rows // 2
    n = lax.axis_size("seq")
    devices = 2 * n
    me = 2 * lax.axis_index("seq") + lax.axis_index("ch")
    row_start = me * block
    total_rows = seg_ids.shape[0]
    length = min(SEQ_LEN, total_rows)

    keys = seg_ids + (jnp.arange(total_rows, dtype=jnp.int32) // length) * 65536
    padded = jnp.concatenate([jnp.full((BEFORE,), -1, jnp.int32), keys, jnp.full((block + AFTER,), -2, jnp.int32)])
    near = lax.dynamic_slice_in_dim(padded, row_start, BEFORE + block + AFTER)
    window = near
    ids = jnp.broadcast_to(window.astype(F32)[:, None], (window.shape[0], LANES))

    table = position_table(FIR, (filt_w1.shape[0] - 1) // 2)
    norm_tail = jnp.sqrt(-jnp.expm1(-2.0 * tail_rate))
    vectors = (norm1_gain, norm2_gain, long_bias, tail_gain, tail_rate, norm_tail, short_weight)
    filt_b1 = filt_b1[None, :]
    marks = jnp.concatenate([keys[::block], keys[block - 1 :: block]])
    (tok, g, win, wout, up_other, down_other, gains, vec, n1, proj, x0, u, heads, base, car, dist, rest, enter) = forward(
        n, marks, tokens, grad_out, jnp.transpose(in_weight, (1, 0, 2)), out_weight, up_weight, down_weight,
        filt_w3, table, filt_w1, filt_b1, filt_w2, vectors, ids)

    summed = n == 16
    results = backward(
        n, summed, marks, tok, ids, dist, rest, enter, g, gains, vec, wout, x0, base, car, u, n1, heads,
        (up_weight, up_other), (down_weight, down_other), win, proj)
    if not summed:
        results = reduce_plain(n, *results)
    total, small_a, small_b, out, gtok = results

    (out, gtok, gain_one, in_grad, short_grad, w1_grad, b1_grad, w2_grad, w3_grad, bias_grad, tail_gain_grad, rate_grad,
     out_grad, gain_two, up_grad, down_grad) = finish(
        total, small_a, small_b, gains, vec, table, filt_w1, filt_b1, filt_w2, out, gtok)
    return (
        out, gtok, gain_one, jnp.transpose(in_grad, (1, 0, 2)), short_grad, w1_grad, b1_grad, w2_grad, w3_grad, bias_grad,
        tail_gain_grad, rate_grad, out_grad.T, gain_two, up_grad, down_grad.T,
    )


def solution(mesh):
    placed = (
        P("seq", "ch"),
        P(),
        P("ch"),
        P(None, None, "ch"),
        P(None, None, "ch"),
        P(),
        P(),
        P(),
        P(None, "ch"),
        P("ch"),
        P("ch"),
        P("ch"),
        P("ch", None),
        P("ch"),
        P(None, "ch"),
        P("ch", None),
        P("seq", "ch"),
    )
    return jax.shard_map(
        on_device,
        mesh=mesh,
        in_specs=placed,
        out_specs=(
            P("seq", "ch"),
            P("seq", "ch"),
            P(),
            P("seq", None, "ch"),
            P(),
            P(),
            P(),
            P(),
            P(),
            P(),
            P(),
            P(),
            P("ch", "seq"),
            P(),
            P("seq", "ch"),
            P("ch", "seq"),
        ),
        check_vma=False,
    )
```
